32 devices in a mesh: shots: 2 (over x), gx: 8 (over z, y), gy: 2 (over core).
Axes of the slice: x: 2, y: 2, z: 4, core: 2. Of those that a mesh axis runs over, the one named last changes fastest.
Arguments:
- field_now: float32 [512, 96, 128], P(('shots', 'gx'), 'gy'), parts along dimension 0, may hold values from -6 to 6
- field_prev: float32 [512, 96, 128], P(('shots', 'gx'), 'gy'), parts along dimension 0, may hold values from -6 to 6
- courant_squared: float32 [256, 96, 128], P('gx', 'gy'), may hold values from 0.05 to 0.18, as said below
- source_cells: int32 [3, 16], P(None, 'shots'), parts along dimension 1, may hold values from 0 to 127, as said below
- source_wave: float32 [4, 16], P(None, 'shots'), parts along dimension 1, may hold values from -8 to 8
- receiver_cells: int32 [3, 512], P(None, 'shots'), parts along dimension 1, may hold values from 0 to 127, as said below
- receiver_wave: float32 [4, 512], P(None, 'shots'), parts along dimension 1, may hold values from -8 to 8
- snapshot_steps: int32 [4, 2], P('shots'), parts along dimension 0, may hold values from 1 to 4, as said below
- lag_offsets: int32 [17], replicated, may hold values from -8 to 8
Outputs:
- final_field: float32 [512, 96, 128], P(('shots', 'gx'), 'gy'), parts along dimension 0
- extended_image: float32 [256, 17, 1536], P(('shots', 'gx'), None, 'gy'), parts along dimension 0
The draws below stay inside these ranges and needn't reach their ends.
There are 2 independent parts, one for each index of `shots`. The reference program is written for one: setup_inputs(seed, part) draws one part's arguments, and reference() takes and returns one part's arrays. A program takes and returns all parts, laid end to end along the dimension named above; an argument that names none is the same for every part. Nothing has to cross between parts.
Inputs may be any that keep to these rules, and one draw needn't show every extreme that they name: `courant_squared`: both fields' rows of the same model cell hold the same value. `source_cells`: row 0 is an x cell below 128, row 1 a y cell below 96, row 2 a z cell below 128. `receiver_cells`: row 0 is an x cell below 128, row 1 a y cell below 96, row 2 a z cell below 128. `snapshot_steps`: column 0 lies in 1 to 2, column 1 in 3 to 4.
All inputs are finite; a program needn't handle non-finite values.
Results may differ from the reference program's by a relative error of at most 0.0003.
Values sent between devices are 32-bit elements; how exact they have to be, the bound alone decides.
No kernel may reach another device: no remote copies, remote signals or barrier semaphores. Data moves between devices by JAX's collectives and lax.ppermute only.
A program may use at most 64 MiB of HBM per device.

```python
import jax
import jax.numpy as jnp
from jax import lax

STEPS = 4
NSRC = 8
NREC = 256
LAGS = 17
LAGMAX = 8
NX = 128
NY = 96
NZ = 128


def place_positions(key, count):
    subkeys = jax.random.split(key, 4)
    columns = []
    for number, extent in enumerate((NX, NY, NZ)):
        drawn = jax.random.randint(subkeys[number], (count,), 0, extent)
        ranking = jax.random.permutation(jax.random.fold_in(subkeys[3], number), count)
        drawn = jnp.where(ranking == 0, extent - 1, jnp.where(ranking == 1, 0, drawn))
        columns.append(drawn)
    return jnp.stack(columns).astype(jnp.int32)


def draw_source_cells(key, part):
    return place_positions(jax.random.fold_in(key, 11), NSRC)


def draw_receiver_cells(key, part):
    return place_positions(jax.random.fold_in(key, 12), NREC)


def draw_courant_squared(key, part):
    uniform_draw = jax.random.uniform(jax.random.fold_in(key, 13), (NX, NY, NZ), jnp.float32)
    values = 0.05 + 0.13 * uniform_draw
    return jnp.concatenate([values[NX // 2:], values, values[:NX // 2]], axis=0).astype(jnp.float32)


def draw_snapshot_steps(key, part):
    subkeys = jax.random.split(jax.random.fold_in(key, 14), 4)
    early = jax.random.randint(subkeys[0], (2,), 1, STEPS // 2 + 1)
    later = jax.random.randint(subkeys[1], (2,), STEPS // 2 + 1, STEPS + 1)
    early_row = jax.random.randint(subkeys[2], (), 0, 2)
    later_row = jax.random.randint(subkeys[3], (), 0, 2)
    rows = jnp.arange(2)
    early = jnp.where(rows == early_row, 1, early)
    later = jnp.where(rows == later_row, STEPS, later)
    return jnp.stack([early, later], axis=1).astype(jnp.int32)


def draw_lag_offsets(key, part):
    subkeys = jax.random.split(jax.random.fold_in(key, 15), 2)
    values = jax.random.randint(subkeys[0], (LAGS,), -LAGMAX, LAGMAX + 1)
    ranking = jax.random.permutation(subkeys[1], LAGS)
    values = jnp.where(ranking == 0, -LAGMAX, jnp.where(ranking == 1, LAGMAX, values))
    return values.astype(jnp.int32)


def level_of(own_key, dims, cuts, low, high):
    level, own = 1.0, jax.random.fold_in(own_key, 6)
    for axis_at, shards_of in cuts:
        heights = jnp.exp(jax.random.uniform(jax.random.fold_in(own, axis_at), (shards_of,), jnp.float32, low / len(cuts), high / len(cuts)))
        level = level * jnp.repeat(heights, dims[axis_at] // shards_of).reshape([-1 if axis == axis_at else 1 for axis in range(len(dims))])
    return level


def noise(stream_key, dims, deviation, limit, cuts=(), dtype=jnp.bfloat16):
    values = deviation * jax.random.normal(stream_key, dims, jnp.float32)
    if cuts:
        values = values * level_of(stream_key, dims, cuts, -0.22, 0.18)
    return jnp.clip(values, -limit, limit).astype(dtype)


def setup_inputs(seed: int = 0, part: int = 0) -> dict:
    seeds = jax.random.split(jax.random.key(seed), 10)
    part_splits = jax.random.split(jax.random.fold_in(seeds[9], part), 10)
    return {
        "field_now": noise(part_splits[0], (2 * NX, NY, NZ), 1.0, 6.0, ((0, 8), (1, 2)), jnp.float32),
        "field_prev": noise(part_splits[1], (2 * NX, NY, NZ), 1.0, 6.0, ((0, 8), (1, 2)), jnp.float32),
        "courant_squared": draw_courant_squared(jax.random.fold_in(seeds[9], 71), part),
        "source_cells": draw_source_cells(jax.random.fold_in(jax.random.fold_in(seeds[9], part), 71), part),
        "source_wave": noise(part_splits[4], (STEPS, NSRC), 2.0, 8.0, (), jnp.float32),
        "receiver_cells": draw_receiver_cells(jax.random.fold_in(jax.random.fold_in(seeds[9], part), 71), part),
        "receiver_wave": noise(part_splits[6], (STEPS, NREC), 2.0, 8.0, (), jnp.float32),
        "snapshot_steps": draw_snapshot_steps(jax.random.fold_in(jax.random.fold_in(seeds[9], part), 71), part),
        "lag_offsets": draw_lag_offsets(jax.random.fold_in(seeds[9], 71), part),
    }


centre_weight = -205.0 / 72.0
stencil_weights = (1.6, -0.2, 8.0 / 315.0, -1.0 / 560.0)


def laplace_padded(padded, count_x, count_y, count_z):
    def window(shift_x, shift_y, shift_z):
        return padded[4 + shift_x:4 + shift_x + count_x, 4 + shift_y:4 + shift_y + count_y, 4 + shift_z:4 + shift_z + count_z]

    result = (3.0 * centre_weight) * window(0, 0, 0)
    for offset, weight in enumerate(stencil_weights, 1):
        paired = window(offset, 0, 0) + window(-offset, 0, 0)
        paired = paired + window(0, offset, 0) + window(0, -offset, 0)
        paired = paired + window(0, 0, offset) + window(0, 0, -offset)
        result = result + weight * paired
    return result


def march(current, previous, courant_half, positions, amounts, wanted):
    held = [jnp.zeros_like(current), jnp.zeros_like(current)]
    for number in range(STEPS):
        padded = jnp.pad(current, 4)
        advanced = 2.0 * current - previous + courant_half * laplace_padded(padded, NX, NY, NZ)
        advanced = advanced.at[positions[0], positions[1], positions[2]].add(amounts[number])
        held = [jnp.where(wanted[snapshot_slot] == number + 1, advanced, held[snapshot_slot]) for snapshot_slot in range(2)]
        previous, current = current, advanced
    return current, held


def source_rows(array):
    return array[NX // 2:NX // 2 + NX]


def receiver_rows(array):
    return jnp.concatenate([array[NX // 2 + NX:], array[:NX // 2]], axis=0)


def lag_products(source_even, receiver_even, lag_offsets, z_first, z_count):
    pad_width = ((0, 0), (0, 0), (LAGMAX, LAGMAX))
    source_pad = jnp.pad(source_even, pad_width)
    receiver_pad = jnp.pad(receiver_even, pad_width)

    def one_lag(offset):
        start_source = (z_first + LAGMAX - offset).astype(jnp.int32)
        start_receiver = (z_first + LAGMAX + offset).astype(jnp.int32)
        shifted_source = lax.dynamic_slice_in_dim(source_pad, start_source, 2 * z_count, 2)[:, :, ::2]
        shifted_receiver = lax.dynamic_slice_in_dim(receiver_pad, start_receiver, 2 * z_count, 2)[:, :, ::2]
        return shifted_source * shifted_receiver

    return lax.map(one_lag, lag_offsets)


def reference(field_now, field_prev, courant_squared, source_cells, source_wave, receiver_cells, receiver_wave, snapshot_steps, lag_offsets):
    source_final, source_held = march(source_rows(field_now), source_rows(field_prev), source_rows(courant_squared), source_cells, source_wave, snapshot_steps[0])
    receiver_final, receiver_held = march(receiver_rows(field_now), receiver_rows(field_prev), receiver_rows(courant_squared), receiver_cells, receiver_wave, snapshot_steps[1])
    final_field = jnp.concatenate([receiver_final[NX // 2:], source_final, receiver_final[:NX // 2]], axis=0)
    extended = lag_products(source_held[0][::2, ::2, :], receiver_held[0][::2, ::2, :], lag_offsets, 0, NZ // 2)
    extended = extended + lag_products(source_held[1][::2, ::2, :], receiver_held[1][::2, ::2, :], lag_offsets, 0, NZ // 2)
    quarter = NZ // 4
    upper_part = jnp.transpose(extended[:, :, :, :quarter], (1, 0, 2, 3)).reshape(NX // 2, LAGS, (NY // 2) * quarter)
    lower_part = jnp.transpose(extended[:, :, :, quarter:], (1, 0, 2, 3)).reshape(NX // 2, LAGS, (NY // 2) * quarter)
    extended_image = jnp.concatenate([lower_part[NX // 4:], upper_part, lower_part[:NX // 4]], axis=0)
    return final_field, extended_image
```

```python
import functools

import jax
import jax.numpy as jnp
from jax import lax
from jax.experimental import pallas as pl
from jax.experimental.pallas import tpu as pltpu
from jax.sharding import PartitionSpec as P

STEPS = 4
WIDTH = 4
LAGMAX = 8

SCALE = 5040.0
BAND = (8064.0, -1008.0, 128.0, -9.0)
CENTRE = 3.0 * (-205.0 / 72.0)
WEIGHTS = (1.6, -0.2, 8.0 / 315.0, -1.0 / 560.0)

VMEM = pltpu.VMEM
SMEM = pltpu.SMEM
GROUP = 4


def params(megabytes):
    return pltpu.CompilerParams(vmem_limit_bytes=megabytes << 20)


def spec(space):
    return pl.BlockSpec(memory_space=space)


def cost(count, flops_each, arrays):
    return pl.CostEstimate(
        flops=int(count * flops_each), bytes_accessed=int(4 * count * arrays), transcendentals=0
    )


def split3(values):
    high = values.astype(jnp.bfloat16)
    rest = values - high.astype(jnp.float32)
    middle = rest.astype(jnp.bfloat16)
    low = (rest - middle.astype(jnp.float32)).astype(jnp.bfloat16)
    return high, middle, low


def exact_dot(values, matrix):
    parts = [
        jnp.dot(part, matrix, preferred_element_type=jnp.float32) for part in split3(values)
    ]
    return (parts[2] + parts[1]) + parts[0]


def first_faces(info, field):
    count_x, count_y, count_z = field.shape

    def kernel(info_ref, field_ref, low_ref, high_ref, side_ref, sems):
        block = pl.multiple_of(info_ref[4], 8)
        copies = [
            pltpu.make_async_copy(field_ref.at[pl.ds(0, WIDTH)], low_ref, sems.at[0]),
            pltpu.make_async_copy(
                field_ref.at[pl.ds(count_x - WIDTH, WIDTH)], high_ref, sems.at[1]
            ),
            pltpu.make_async_copy(field_ref.at[:, pl.ds(block, 8)], side_ref, sems.at[2]),
        ]
        for copy in copies:
            copy.start()
        for copy in copies:
            copy.wait()

    return pl.pallas_call(
        kernel,
        out_shape=(
            jax.ShapeDtypeStruct((WIDTH, count_y, count_z), jnp.float32),
            jax.ShapeDtypeStruct((WIDTH, count_y, count_z), jnp.float32),
            jax.ShapeDtypeStruct((count_x, 8, count_z), jnp.float32),
        ),
        in_specs=[spec(SMEM), spec(pl.ANY)],
        out_specs=(spec(VMEM),) * 3,
        scratch_shapes=[pltpu.SemaphoreType.DMA((3,))],
        compiler_params=params(8),
        name="first_faces",
    )(info, field)


def gather_even(level_ref, offset_x, offset_y, count_a, count_b, out_ref):
    for b in range(count_b):
        for a in range(count_a):
            out_ref[b, pl.ds(a, 1), :] = level_ref[
                offset_x + 2 * a, pl.ds(offset_y + 2 * b, 1), :
            ]


def inner_step(
    number, info, cells, waves, current, faces, previous, courant, extras=()
):
    count_x, count_y, count_z = current.shape
    overlay = faces is not None
    pairs = ("early",) if "early" in extras else ()
    want_even = "even" in extras
    want_edges = "edges" in extras
    count_a, count_b = count_x // 2, count_y // 2

    def kernel(*refs):
        refs = list(refs)
        info_ref, source_ref, receiver_ref, swave_ref, rwave_ref = refs[:5]
        current_ref = refs[5]
        position = 6
        if overlay:
            low_ref, high_ref, side_ref = refs[6:9]
            position = 9
        previous_ref, courant_ref = refs[position : position + 2]
        position += 2
        next_ref, qx_ref, qy_ref = refs[position : position + 3]
        position += 3
        if overlay:
            whole_ref = refs[position]
            position += 1
        if want_edges:
            cx_ref, cy_ref = refs[position : position + 2]
            position += 2
        if want_even:
            even_ref = refs[position]
            position += 1
        if pairs:
            early_ref = refs[position]
            position += 1
        padded, zpart = refs[position : position + 2]

        anchor_x, anchor_y, is_source, block = info_ref[0], info_ref[1], info_ref[2], info_ref[4]
        block = pl.multiple_of(block, 8)
        rows = pl.ds(WIDTH, count_x)
        zero_x = jnp.zeros((WIDTH, count_y + 16, count_z), jnp.float32)
        padded[pl.ds(0, WIDTH)] = zero_x
        padded[pl.ds(count_x + WIDTH, WIDTH)] = zero_x
        zero_y = jnp.zeros((count_x, 8, count_z), jnp.float32)
        padded[rows, pl.ds(0, 8)] = zero_y
        padded[rows, pl.ds(count_y + 8, 8)] = zero_y
        padded[rows, pl.ds(8, count_y)] = current_ref[...]
        if overlay:
            padded[pl.ds(WIDTH, WIDTH), pl.ds(8, count_y)] = low_ref[...]
            padded[pl.ds(count_x, WIDTH), pl.ds(8, count_y)] = high_ref[...]
            padded[rows, pl.ds(pl.multiple_of(block + 8, 8), 8)] = side_ref[...]

        gap = jnp.abs(
            lax.broadcasted_iota(jnp.int32, (count_z, count_z), 0)
            - lax.broadcasted_iota(jnp.int32, (count_z, count_z), 1)
        )
        band = jnp.zeros((count_z, count_z), jnp.float32)
        for offset, weight in enumerate(BAND, 1):
            band = jnp.where(gap == offset, weight, band)
        band = band.astype(jnp.bfloat16)
        chunk = 8

        def multiply(index, _):
            start = pl.multiple_of(index * chunk, chunk)
            values = padded[pl.ds(start + WIDTH, chunk), pl.ds(8, count_y)]
            zpart[pl.ds(start, chunk)] = exact_dot(
                values.reshape(chunk * count_y, count_z), band
            ).reshape(chunk, count_y, count_z)
            return 0

        lax.fori_loop(0, count_x // chunk, multiply, 0)

        def row(x, _):
            middle = padded[x + WIDTH, pl.ds(8, count_y)]
            total = CENTRE * middle + (1.0 / SCALE) * zpart[x]
            for offset, weight in enumerate(WEIGHTS, 1):
                paired = (
                    padded[x + WIDTH + offset, pl.ds(8, count_y)]
                    + padded[x + WIDTH - offset, pl.ds(8, count_y)]
                )
                paired = paired + (
                    padded[x + WIDTH, pl.ds(8 + offset, count_y)]
                    + padded[x + WIDTH, pl.ds(8 - offset, count_y)]
                )
                total = total + weight * paired
            if overlay:
                whole_ref[x] = middle
            next_ref[x] = 2.0 * middle - previous_ref[x] + courant_ref[x] * total
            return 0

        lax.fori_loop(0, count_x, row, 0)

        lane = lax.broadcasted_iota(jnp.int32, (1, count_z), 1)

        def inject(cells_ref, wave_ref):
            def one(j, _):
                x = cells_ref[0, j] - anchor_x
                y = cells_ref[1, j] - anchor_y
                inside = (x >= 0) & (x < count_x) & (y >= 0) & (y < count_y)

                @pl.when(inside)
                def _():
                    old = next_ref[x, pl.ds(y, 1), :]
                    next_ref[x, pl.ds(y, 1), :] = old + jnp.where(
                        lane == cells_ref[2, j], wave_ref[number, j], 0.0
                    )

                return 0

            lax.fori_loop(0, cells_ref.shape[1], one, 0)

        @pl.when(is_source == 1)
        def _():
            inject(source_ref, swave_ref)

        @pl.when(is_source == 0)
        def _():
            inject(receiver_ref, rwave_ref)

        qx_ref[pl.ds(0, WIDTH)] = next_ref[pl.ds(0, WIDTH)]
        qx_ref[pl.ds(WIDTH, WIDTH)] = next_ref[pl.ds(count_x - WIDTH, WIDTH)]
        qy_ref[...] = next_ref[:, pl.ds(block, 8)]
        if want_edges:
            cx_ref[pl.ds(0, WIDTH)] = courant_ref[pl.ds(0, WIDTH)]
            cx_ref[pl.ds(WIDTH, WIDTH)] = courant_ref[pl.ds(count_x - WIDTH, WIDTH)]
            cy_ref[...] = courant_ref[:, pl.ds(block, 8)]
        if want_even:
            gather_even(padded, WIDTH, 8, count_a, count_b, even_ref)
        if pairs:
            wants_first = info_ref[5] == number - 1

            @pl.when(wants_first)
            def _():
                gather_even(previous_ref, 0, 0, count_a, count_b, early_ref)

            @pl.when(jnp.logical_not(wants_first))
            def _():
                gather_even(padded, WIDTH, 8, count_a, count_b, early_ref)

    full = jax.ShapeDtypeStruct((count_x, count_y, count_z), jnp.float32)
    slab = jax.ShapeDtypeStruct((2 * WIDTH, count_y, count_z), jnp.float32)
    side = jax.ShapeDtypeStruct((count_x, 8, count_z), jnp.float32)
    even = jax.ShapeDtypeStruct((count_b, count_a, count_z), jnp.float32)
    outs = [full, slab, side]
    if overlay:
        outs.append(full)
    if want_edges:
        outs += [slab, side]
    if want_even:
        outs.append(even)
    if pairs:
        outs.append(even)
    operands = [info, *cells, *waves, current]
    if overlay:
        operands += list(faces)
    operands += [previous, courant]
    return pl.pallas_call(
        kernel,
        out_shape=tuple(outs),
        in_specs=[spec(SMEM)] * 5 + [spec(VMEM)] * (len(operands) - 5),
        out_specs=(spec(VMEM),) * len(outs),
        scratch_shapes=[
            pltpu.VMEM((count_x + 2 * WIDTH, count_y + 16, count_z), jnp.float32),
            pltpu.VMEM((count_x, count_y, count_z), jnp.float32),
        ],
        compiler_params=params(20),
        cost_estimate=cost(count_x * count_y * count_z, 60, 6),
        name="inner_step",
    )(*operands)


def add_halo(info_ref, qx_ref, qy_ref, cx_ref, cy_ref, from_low, from_high, from_side, outs, pad):
    low_ref, high_ref, side_ref = outs
    count_y = qx_ref.shape[1]
    count_x, _, count_z = qy_ref.shape
    dev_y = info_ref[3]
    block = pl.multiple_of(info_ref[4], 8)
    pad[...] = jnp.zeros_like(pad)

    pad[:, pl.ds(pl.multiple_of((1 - dev_y) * 16, 8), 8)] = from_side[...]
    for r in range(WIDTH):
        total = None
        for k in range(r + 1, WIDTH + 1):
            term = WEIGHTS[k - 1] * from_low[WIDTH + r - k]
            total = term if total is None else total + term
        low_ref[r] = qx_ref[r] + cx_ref[r] * total
        total = None
        for k in range(WIDTH - r, WIDTH + 1):
            term = WEIGHTS[k - 1] * from_high[r + k - WIDTH]
            total = term if total is None else total + term
        high_ref[r] = qx_ref[WIDTH + r] + cx_ref[WIDTH + r] * total
    side_ref[pl.ds(WIDTH, count_x - 2 * WIDTH)] = qy_ref[pl.ds(WIDTH, count_x - 2 * WIDTH)]
    side_ref[pl.ds(0, WIDTH)] = low_ref[:, pl.ds(block, 8)]
    side_ref[pl.ds(count_x - WIDTH, WIDTH)] = high_ref[:, pl.ds(block, 8)]
    total = None
    for k in range(1, WIDTH + 1):
        term = WEIGHTS[k - 1] * (pad[:, pl.ds(8 + k, 8)] + pad[:, pl.ds(8 - k, 8)])
        total = term if total is None else total + term
    side_ref[...] = side_ref[...] + cy_ref[...] * total
    low_ref[:, pl.ds(block, 8)] = side_ref[pl.ds(0, WIDTH)]
    high_ref[:, pl.ds(block, 8)] = side_ref[pl.ds(count_x - WIDTH, WIDTH)]


def face_shapes(count_x, count_y, count_z):
    slab = jax.ShapeDtypeStruct((WIDTH, count_y, count_z), jnp.float32)
    side = jax.ShapeDtypeStruct((count_x, 8, count_z), jnp.float32)
    return slab, slab, side


def halo_step(info, qx, qy, cx, cy, halos):
    count_x, _, count_z = qy.shape
    count_y = qx.shape[1]

    def kernel(info_ref, qx_ref, qy_ref, cx_ref, cy_ref, a_ref, b_ref, s_ref, *rest):
        add_halo(info_ref, qx_ref, qy_ref, cx_ref, cy_ref, a_ref, b_ref, s_ref, rest[:3], rest[3])

    return pl.pallas_call(
        kernel,
        out_shape=face_shapes(count_x, count_y, count_z),
        in_specs=[spec(SMEM)] + [spec(VMEM)] * 7,
        out_specs=(spec(VMEM),) * 3,
        scratch_shapes=[pltpu.VMEM((count_x, 24, count_z), jnp.float32)],
        compiler_params=params(8),
        cost_estimate=cost(16 * count_y * count_z, 10, 6),
        name="halo_step",
    )(info, qx, qy, cx, cy, *halos)


def pack_matrix(window, count_z):
    half = count_z // 4
    reach = LAGMAX // 2
    size = GROUP * count_z
    row = lax.broadcasted_iota(jnp.int32, (size, 4 * count_z), 0)
    column = lax.broadcasted_iota(jnp.int32, (size, 4 * count_z), 1)
    row_b, row_z = row // count_z, row % count_z
    kind = column // count_z
    parity = kind % 2
    lane_b, lane_i = (column % count_z) // half, column % half
    main = (row_b == lane_b) & (row_z == 2 * (half * window + lane_i) + parity)
    is_low = window == 0
    wanted_b = jnp.where(is_low, lane_b + GROUP - 1, lane_b + 1) % GROUP
    wanted_z = 2 * (half * (1 - window) + lane_i) + parity
    useful = jnp.where(is_low, lane_i < reach, lane_i >= half - reach)
    edge = (row_b == wanted_b) & (row_z == wanted_z) & useful
    return jnp.where(kind < 2, main, edge).astype(jnp.bfloat16)


def packed(even_values, matrix, count_z):
    return exact_dot(even_values, matrix)


def pack(even, matrix):
    count_b, count_a, count_z = even.shape
    groups = count_b // GROUP

    def kernel(even_ref, matrix_ref, out_ref):
        pack_into(lambda b: even_ref[b], matrix_ref, out_ref, groups, count_a, count_z)

    return pl.pallas_call(
        kernel,
        out_shape=jax.ShapeDtypeStruct((4, groups * count_a, count_z), jnp.float32),
        in_specs=[spec(VMEM)] * 2,
        out_specs=spec(VMEM),
        compiler_params=params(8),
        cost_estimate=cost(count_b * count_a * count_z, 1024, 4),
        name="pack",
    )(even, matrix)


def pack_into(value, matrix_ref, out_ref, groups, count_a, count_z):
    lhs = jnp.concatenate(
        [
            jnp.concatenate([value(GROUP * g + b) for b in range(GROUP)], axis=1)
            for g in range(groups)
        ],
        axis=0,
    )
    result = exact_dot(lhs, matrix_ref[...])
    for kind in range(4):
        out_ref[kind] = result[:, kind * count_z : (kind + 1) * count_z]


def last_step(info, whole_before, even_before, current, qx, qy, cx, cy, halos, matrix):
    count_x, count_y, count_z = current.shape
    count_a, count_b = count_x // 2, count_y // 2
    groups = count_b // GROUP

    def kernel(
        info_ref, even_ref, current_ref, qx_ref, qy_ref, cx_ref, cy_ref, a_ref, b_ref, s_ref,
        matrix_ref, final_ref, late_ref, sent_ref, low_ref, high_ref, side_ref, pad,
    ):
        final_ref[...] = current_ref[...]
        block = pl.multiple_of(info_ref[4], 8)
        add_halo(
            info_ref, qx_ref, qy_ref, cx_ref, cy_ref, a_ref, b_ref, s_ref,
            (low_ref, high_ref, side_ref), pad,
        )
        final_ref[pl.ds(0, WIDTH)] = low_ref[...]
        final_ref[pl.ds(count_x - WIDTH, WIDTH)] = high_ref[...]
        final_ref[:, pl.ds(block, 8)] = side_ref[...]
        wants_last = info_ref[6] == STEPS

        @pl.when(wants_last)
        def _():
            gather_even(final_ref, 0, 0, count_a, count_b, late_ref)

        @pl.when(jnp.logical_not(wants_last))
        def _():
            late_ref[...] = even_ref[...]

        pack_into(lambda b: late_ref[b], matrix_ref, sent_ref, groups, count_a, count_z)

    slab, _, side = face_shapes(count_x, count_y, count_z)
    return pl.pallas_call(
        kernel,
        out_shape=(
            jax.ShapeDtypeStruct(current.shape, jnp.float32),
            jax.ShapeDtypeStruct((count_b, count_a, count_z), jnp.float32),
            jax.ShapeDtypeStruct((4, groups * count_a, count_z), jnp.float32),
        ),
        in_specs=[spec(SMEM)] + [spec(VMEM)] * 10,
        out_specs=(spec(VMEM),) * 3,
        scratch_shapes=[
            pltpu.VMEM(slab.shape, jnp.float32),
            pltpu.VMEM(slab.shape, jnp.float32),
            pltpu.VMEM(side.shape, jnp.float32),
            pltpu.VMEM((count_x, 24, count_z), jnp.float32),
        ],
        compiler_params=params(16),
        cost_estimate=cost(count_x * count_y * count_z, 10, 3),
        name="last_step",
    )(info, even_before, current, qx, qy, cx, cy, *halos, matrix)


def lag_image(info, lags, own, other, before, count_a):
    _, total_rows, count_z = own.shape
    groups = total_rows // count_a
    count_h = lags.shape[0]
    half = count_z // 4
    last = before is not None

    def kernel(*refs):
        info_ref, lags_ref, own_ref, other_ref = refs[:4]
        if last:
            before_ref, out_ref, store = refs[4:]
        else:
            out_ref = refs[4]
            store = out_ref
        is_source = info_ref[2] == 1
        lane = lax.broadcasted_iota(jnp.int32, (total_rows, count_z), 1) % half

        def moved(ref, parity, shift):
            mask = (lane < shift) | (lane >= half + shift)
            mixed = jnp.where(mask, ref[parity + 2], ref[parity])
            return pltpu.roll(mixed, (count_z - shift) % count_z, 1)

        def one(h, _):
            lag = lags_ref[h]
            parity = lag & 1
            source_shift = -((lag + parity) >> 1)
            receiver_shift = (lag - parity) >> 1
            own_shift = jnp.where(is_source, source_shift, receiver_shift)
            other_shift = jnp.where(is_source, receiver_shift, source_shift)
            product = moved(own_ref, parity, own_shift) * moved(other_ref, parity, other_shift)
            for g in range(groups):
                rows = pl.ds(pl.multiple_of(h * count_a, count_a), count_a)
                part = product[g * count_a : (g + 1) * count_a]
                if last:
                    part = part + before_ref[g, rows, :]
                store[g, rows, :] = part
            return 0

        lax.fori_loop(0, count_h, one, 0)
        if last:
            for a in range(count_a):
                for g in range(groups):
                    out_ref[a, :, pl.ds(g * count_z, count_z)] = store[
                        g, pl.ds(a, count_h, stride=count_a), :
                    ]

    ordered = (groups, count_h * count_a, count_z)
    out = (count_a, count_h, groups * count_z) if last else ordered
    operands = [info, lags, own, other] + ([before] if last else [])
    return pl.pallas_call(
        kernel,
        out_shape=jax.ShapeDtypeStruct(out, jnp.float32),
        in_specs=[spec(SMEM)] * 2 + [spec(VMEM)] * (len(operands) - 2),
        out_specs=spec(VMEM),
        scratch_shapes=[pltpu.VMEM(ordered, jnp.float32)] if last else [],
        compiler_params=params(12),
        cost_estimate=cost(count_h * total_rows * count_z, 10, 2),
        name="lag_image",
    )(*operands)


def body(
    field_now,
    field_prev,
    courant_squared,
    source_cells,
    source_wave,
    receiver_cells,
    receiver_wave,
    snapshot_steps,
    lag_offsets,
):
    count_x, count_y, count_z = field_now.shape
    loop_size = lax.axis_size("gx")
    half_size = loop_size // 2
    turn = loop_size // 4
    assert lax.axis_size("gy") == 2

    device_x = lax.axis_index("gx")
    relative = (device_x - turn + loop_size) % loop_size
    which_half = relative // half_size
    slab_index = relative % half_size
    device_y = lax.axis_index("gy")
    wanted = snapshot_steps[which_half]
    info = jnp.stack(
        [
            slab_index * count_x,
            device_y * count_y,
            (which_half == 0).astype(jnp.int32),
            device_y,
            (1 - device_y) * (count_y - 8),
            wanted[0],
            wanted[1],
        ]
    ).astype(jnp.int32)

    inside = [
        i for i in range(loop_size) if (i - turn) % loop_size % half_size != half_size - 1
    ]
    upward = [(i, (i + 1) % loop_size) for i in inside]
    downward = [(j, i) for i, j in upward]
    across = [(i, (i + half_size) % loop_size) for i in range(loop_size)]

    def exchange(faces):
        low, high, side = faces
        return (
            lax.ppermute(high, "gx", upward),
            lax.ppermute(low, "gx", downward),
            lax.ppermute(side, "gy", [(0, 1), (1, 0)]),
        )

    own_matrix = pack_matrix(which_half, count_z)
    sent_matrix = pack_matrix(1 - which_half, count_z)
    cells = (source_cells, receiver_cells)
    waves = (source_wave, receiver_wave)

    def step(number, *rest, extras=()):
        return inner_step(number, info, cells, waves, *rest, courant_squared, extras=extras)

    halos = exchange(first_faces(info, field_now))
    next1, qx, qy, cx, cy = step(0, field_now, None, field_prev, extras=("edges",))
    faces = halo_step(info, qx, qy, cx, cy, halos)
    halos = exchange(faces)
    next2, qx, qy, whole1 = step(1, next1, faces, field_now)
    faces = halo_step(info, qx, qy, cx, cy, halos)
    halos = exchange(faces)
    next3, qx, qy, whole2, early = step(2, next2, faces, whole1, extras=("early",))
    faces = halo_step(info, qx, qy, cx, cy, halos)
    halos = exchange(faces)
    own_early = pack(early, own_matrix)
    other_early = lax.ppermute(pack(early, sent_matrix), "gx", across)
    next4, qx, qy, whole3, even3 = step(3, next3, faces, whole2, extras=("even",))
    final, late, sent_late = last_step(
        info, whole3, even3, next4, qx, qy, cx, cy, halos, sent_matrix
    )
    other_late = lax.ppermute(sent_late, "gx", across)
    partial = lag_image(info, lag_offsets, own_early, other_early, None, count_x // 2)
    own_late = pack(late, own_matrix)
    image = lag_image(info, lag_offsets, own_late, other_late, partial, count_x // 2)
    return final, image


def solution(mesh):
    placed = (
        P(("shots", "gx"), "gy", None),
        P(("shots", "gx"), "gy", None),
        P("gx", "gy", None),
        P(None, "shots"),
        P(None, "shots"),
        P(None, "shots"),
        P(None, "shots"),
        P("shots", None),
        P(),
    )
    return jax.shard_map(
        body,
        mesh=mesh,
        in_specs=placed,
        out_specs=(P(("shots", "gx"), "gy", None), P(("shots", "gx"), None, "gy")),
        check_vma=False,
    )
```

```python
import jax
import jax.numpy as jnp
from jax import lax
from jax.experimental import pallas as pl
from jax.experimental.pallas import tpu as pltpu
from jax.sharding import PartitionSpec as P

STEPS = 4
WIDTH = 4
LAGMAX = 8
REACH = LAGMAX // 2
GROUP = 4
SIDE = 8

SCALE = 5040.0
BAND = (8064.0, -1008.0, 128.0, -9.0)
CENTRE = 3.0 * (-205.0 / 72.0)
WEIGHTS = (1.6, -0.2, 8.0 / 315.0, -1.0 / 560.0)

F32 = jnp.float32
BF16 = jnp.bfloat16


def shape(*dims, dtype=F32):
    return jax.ShapeDtypeStruct(dims, dtype)


def params(megabytes):
    return pltpu.CompilerParams(vmem_limit_bytes=megabytes << 20)


def spec(space):
    return pl.BlockSpec(memory_space=space)


def cost(count, flops_each, arrays):
    return pl.CostEstimate(
        flops=int(count * flops_each), bytes_accessed=int(4 * count * arrays), transcendentals=0
    )


def split3(values):
    high = values.astype(BF16)
    rest = values - high.astype(F32)
    middle = rest.astype(BF16)
    low = (rest - middle.astype(F32)).astype(BF16)
    return high, middle, low


def exact_dot(values, matrix):
    parts = [jnp.dot(part, matrix, preferred_element_type=F32) for part in split3(values)]
    return (parts[2] + parts[1]) + parts[0]


class Place:
    def __init__(self):
        loop_size = lax.axis_size("gx")
        self.half = loop_size // 2
        relative = lax.rem(lax.axis_index("gx") + loop_size - loop_size // 4, loop_size)
        self.field = relative // self.half
        self.slab = lax.rem(relative, self.half)
        self.even = lax.rem(self.slab, 2) == 0
        self.y = lax.axis_index("gy")

    def block(self, count_y):
        return pl.multiple_of((1 - self.y) * (count_y - SIDE), SIDE)


def first_faces(field):
    count_x, count_y, count_z = field.shape

    def kernel(field_ref, near_ref, far_ref, side_ref, sems):
        place = Place()
        top = count_x - WIDTH
        near_start = jnp.where(place.even, top, 0)
        copies = [
            pltpu.make_async_copy(field_ref.at[pl.ds(top - near_start, WIDTH)], far_ref, sems.at[0]),
            pltpu.make_async_copy(field_ref.at[pl.ds(near_start, WIDTH)], near_ref, sems.at[1]),
            pltpu.make_async_copy(
                field_ref.at[:, pl.ds(place.block(count_y), SIDE)], side_ref, sems.at[2]
            ),
        ]
        for copy in copies:
            copy.start()
        for copy in copies:
            copy.wait()

    return pl.pallas_call(
        kernel,
        out_shape=face_shapes(count_x, count_y, count_z),
        in_specs=[spec(pltpu.HBM)],
        out_specs=(spec(pltpu.VMEM),) * 3,
        scratch_shapes=[pltpu.SemaphoreType.DMA((3,))],
        compiler_params=params(8),
        name="first_faces",
    )(field)


def face_shapes(count_x, count_y, count_z):
    slab = shape(WIDTH, count_y, count_z)
    return slab, slab, shape(count_x, SIDE, count_z)


def even_rows(level_ref, offset_x, offset_y, count_a, b):
    rows, stride, lanes = level_ref.shape
    flat = level_ref.reshape(rows * stride, lanes)
    start = offset_x * stride + offset_y + 2 * b
    return flat[pl.ds(start, count_a, stride=2 * stride), :]


def inner_step(number, points, waves, current, faces, previous, courant, snapshots=None):
    count_x, count_y, count_z = current.shape
    count_a, count_b = count_x // 2, count_y // 2
    first = faces is None
    last = number == STEPS - 1
    snapshot = number == STEPS // 2
    count_j = points.shape[1]

    def kernel(*refs):
        refs = list(refs)
        take = lambda count: [refs.pop(0) for _ in range(count)]
        points_ref, waves_ref, current_ref = take(3)
        if not first:
            near_ref, far_ref, side_ref = take(3)
        previous_ref, courant_ref = take(2)
        if snapshot:
            (steps_ref,) = take(1)
        next_ref, qx_ref, qy_ref = take(3)
        if first:
            kept_ref, cx_ref, cy_ref = take(3)
        elif not last:
            (whole_ref,) = take(1)
        if snapshot or last:
            (even_ref,) = take(1)
        padded, zpart = take(2)
        if first:
            before_ref, sems = take(2)
        if snapshot:
            wanted, sems = take(2)

        place = Place()
        block = place.block(count_y)
        rows, columns = pl.ds(WIDTH, count_x), pl.ds(SIDE, count_y)
        if first:
            copies = [
                pltpu.make_async_copy(current_ref, padded.at[rows, columns], sems.at[0]),
                pltpu.make_async_copy(previous_ref, before_ref, sems.at[1]),
                pltpu.make_async_copy(courant_ref, kept_ref, sems.at[2]),
            ]
            for copy in copies:
                copy.start()
        else:
            before_ref, kept_ref = previous_ref, courant_ref
        if snapshot:
            copies = [pltpu.make_async_copy(steps_ref, wanted, sems.at[0])]
            copies[0].start()

        zero_x = jnp.zeros((WIDTH, count_y + 2 * SIDE, count_z), F32)
        padded[pl.ds(0, WIDTH)] = zero_x
        padded[pl.ds(count_x + WIDTH, WIDTH)] = zero_x
        zero_y = jnp.zeros((count_x, SIDE, count_z), F32)
        padded[rows, pl.ds(0, SIDE)] = zero_y
        padded[rows, pl.ds(count_y + SIDE, SIDE)] = zero_y

        px = points_ref[0:1, :] - place.slab * count_x
        py = points_ref[1:2, :] - place.y * count_y
        inside = (px >= 0) & (px < count_x) & (py >= 0) & (py < count_y)
        home = jnp.where(inside, px * count_y + py, -1)
        amounts = waves_ref[number : number + 1, :]
        spread = jnp.where(
            lax.broadcasted_iota(jnp.int32, (count_z, count_j), 0) == points_ref[2:3, :],
            amounts,
            0.0,
        )
        spread = split3(spread)

        gap = jnp.abs(
            lax.broadcasted_iota(jnp.int32, (count_z, count_z), 0)
            - lax.broadcasted_iota(jnp.int32, (count_z, count_z), 1)
        )
        band = jnp.zeros((count_z, count_z), F32)
        for offset, weight in enumerate(BAND, 1):
            band = jnp.where(gap == offset, weight, band)
        band = band.astype(BF16)

        if first:
            copies[0].wait()
        else:
            padded[rows, columns] = current_ref[...]
            low, high = pl.ds(WIDTH, WIDTH), pl.ds(count_x, WIDTH)

            @pl.when(place.even)
            def _():
                padded[high, columns] = near_ref[...]
                padded[low, columns] = far_ref[...]

            @pl.when(jnp.logical_not(place.even))
            def _():
                padded[low, columns] = near_ref[...]
                padded[high, columns] = far_ref[...]

            padded[rows, pl.ds(pl.multiple_of(block + SIDE, SIDE), SIDE)] = side_ref[...]

        chunk = 8

        def multiply(index, _):
            start = pl.multiple_of(index * chunk, chunk)
            values = padded[pl.ds(start + WIDTH, chunk), columns]
            zpart[pl.ds(start, chunk)] = exact_dot(
                values.reshape(chunk * count_y, count_z), band
            ).reshape(chunk, count_y, count_z)
            return 0

        lax.fori_loop(0, count_x // chunk, multiply, 0)
        if first:
            copies[1].wait()
            copies[2].wait()

        def row(x, _):
            middle = padded[x + WIDTH, columns]
            total = CENTRE * middle + (1.0 / SCALE) * zpart[x]
            for offset, weight in enumerate(WEIGHTS, 1):
                paired = padded[x + WIDTH + offset, columns] + padded[x + WIDTH - offset, columns]
                paired = paired + (
                    padded[x + WIDTH, pl.ds(SIDE + offset, count_y)]
                    + padded[x + WIDTH, pl.ds(SIDE - offset, count_y)]
                )
                total = total + weight * paired
            here = x * count_y + lax.broadcasted_iota(jnp.int32, (count_y, count_j), 0)
            hit = jnp.where(here == home, 1.0, 0.0).astype(BF16)
            added = [
                lax.dot_general(
                    hit, part, (((1,), (1,)), ((), ())), preferred_element_type=F32
                )
                for part in spread
            ]
            added = (added[2] + added[1]) + added[0]
            if not first and not last:
                whole_ref[x] = middle
            next_ref[x] = (2.0 * middle - before_ref[x] + kept_ref[x] * total) + added
            return 0

        lax.fori_loop(0, count_x, row, 0)

        qx_ref[pl.ds(0, WIDTH)] = next_ref[pl.ds(0, WIDTH)]
        qx_ref[pl.ds(WIDTH, WIDTH)] = next_ref[pl.ds(count_x - WIDTH, WIDTH)]
        qy_ref[...] = next_ref[:, pl.ds(block, SIDE)]
        if first:
            cx_ref[pl.ds(0, WIDTH)] = kept_ref[pl.ds(0, WIDTH)]
            cx_ref[pl.ds(WIDTH, WIDTH)] = kept_ref[pl.ds(count_x - WIDTH, WIDTH)]
            cy_ref[...] = kept_ref[:, pl.ds(block, SIDE)]
        if last:
            for b in range(count_b):
                even_ref[b] = even_rows(padded, WIDTH, SIDE, count_a, b)
        if snapshot:
            copies[0].wait()
            earlier = wanted[place.field, 0] == number - 1

            @pl.when(earlier)
            def _():
                for b in range(count_b):
                    even_ref[b] = even_rows(previous_ref, 0, 0, count_a, b)

            @pl.when(jnp.logical_not(earlier))
            def _():
                for b in range(count_b):
                    even_ref[b] = even_rows(padded, WIDTH, SIDE, count_a, b)

    full = shape(count_x, count_y, count_z)
    slab, side = shape(2 * WIDTH, count_y, count_z), shape(count_x, SIDE, count_z)
    even = shape(count_b, count_a, count_z)
    outs = [full, slab, side]
    if first:
        outs += [full, slab, side]
    elif not last:
        outs.append(full)
    if snapshot or last:
        outs.append(even)
    place_of = spec(pltpu.HBM) if first else spec(pltpu.VMEM)
    operands, specs = [points, waves, current], [spec(pltpu.VMEM)] * 2 + [place_of]
    if not first:
        operands += list(faces)
        specs += [spec(pltpu.VMEM)] * 3
    operands += [previous, courant]
    specs += [place_of] * 2
    scratch = [
        pltpu.VMEM((count_x + 2 * WIDTH, count_y + 2 * SIDE, count_z), F32),
        pltpu.VMEM(full.shape, F32),
    ]
    if first:
        scratch += [pltpu.VMEM(full.shape, F32), pltpu.SemaphoreType.DMA((3,))]
    if snapshot:
        operands.append(snapshots)
        specs.append(spec(pltpu.HBM))
        scratch += [
            pltpu.SMEM(snapshots.shape, jnp.int32),
            pltpu.SemaphoreType.DMA((1,)),
        ]
    return pl.pallas_call(
        kernel,
        out_shape=tuple(outs),
        in_specs=specs,
        out_specs=(spec(pltpu.VMEM),) * len(outs),
        scratch_shapes=scratch,
        compiler_params=params(20),
        cost_estimate=cost(count_x * count_y * count_z, 60, 6),
        name=f"inner_step_{number}",
    )(*operands)


def low_terms(halo_ref, r):
    total = None
    for k in range(r + 1, WIDTH + 1):
        term = WEIGHTS[k - 1] * halo_ref[WIDTH + r - k]
        total = term if total is None else total + term
    return total


def high_terms(halo_ref, r):
    total = None
    for k in range(WIDTH - r, WIDTH + 1):
        term = WEIGHTS[k - 1] * halo_ref[r + k - WIDTH]
        total = term if total is None else total + term
    return total


def add_halo(place, parts, halos, outs):
    qx_ref, qy_ref, cx_ref, cy_ref = parts
    near_in, far_in, side_in = halos
    near_out, far_out, side_out = outs
    count_y, count_x = qx_ref.shape[1], qy_ref.shape[0]
    block = place.block(count_y)

    def along_x(low_in, high_in, low_out, high_out):
        for r in range(WIDTH):
            low_out[r] = qx_ref[r] + cx_ref[r] * low_terms(low_in, r)
            high_out[r] = qx_ref[WIDTH + r] + cx_ref[WIDTH + r] * high_terms(high_in, r)
        side_out[pl.ds(0, WIDTH)] = low_out[:, pl.ds(block, SIDE)]
        side_out[pl.ds(count_x - WIDTH, WIDTH)] = high_out[:, pl.ds(block, SIDE)]

    inner = pl.ds(WIDTH, count_x - 2 * WIDTH)
    side_out[inner] = qy_ref[inner]

    @pl.when(place.even)
    def _():
        along_x(far_in, near_in, far_out, near_out)

    @pl.when(jnp.logical_not(place.even))
    def _():
        along_x(near_in, far_in, near_out, far_out)

    def along_y(shifts, masks):
        halo = side_in[...]
        depth, lanes = halo.shape[0], halo.shape[2]
        line = lax.broadcasted_iota(jnp.int32, (1, SIDE, lanes), 1)
        total = None
        for k in range(1, WIDTH + 1):
            weight = jnp.where(masks(line, k), WEIGHTS[k - 1], 0.0)
            term = weight * pltpu.roll(halo, shifts(k), 1)
            total = term if total is None else total + term
        side_out[...] = side_out[...] + cy_ref[...] * total

    @pl.when(place.y == 0)
    def _():
        along_y(lambda k: SIDE - k, lambda line, k: line >= SIDE - k)

    @pl.when(place.y != 0)
    def _():
        along_y(lambda k: k, lambda line, k: line < k)

    def corners(low_out, high_out):
        low_out[:, pl.ds(block, SIDE)] = side_out[pl.ds(0, WIDTH)]
        high_out[:, pl.ds(block, SIDE)] = side_out[pl.ds(count_x - WIDTH, WIDTH)]

    @pl.when(place.even)
    def _():
        corners(far_out, near_out)

    @pl.when(jnp.logical_not(place.even))
    def _():
        corners(near_out, far_out)


def halo_step(parts, halos):
    count_y, (count_x, _, count_z) = parts[0].shape[1], parts[1].shape

    def kernel(*refs):
        add_halo(Place(), refs[:4], refs[4:7], refs[7:])

    return pl.pallas_call(
        kernel,
        out_shape=face_shapes(count_x, count_y, count_z),
        in_specs=[spec(pltpu.VMEM)] * 7,
        out_specs=(spec(pltpu.VMEM),) * 3,
        compiler_params=params(8),
        cost_estimate=cost(16 * count_y * count_z, 10, 6),
        name="halo_step",
    )(*parts, *halos)


def pack_matrix(window, count_z):
    half = count_z // GROUP
    size = GROUP * count_z
    row = lax.broadcasted_iota(jnp.int32, (size, size), 0)
    column = lax.broadcasted_iota(jnp.int32, (size, size), 1)
    row_b, row_z = row // count_z, row % count_z
    kind = column // count_z
    parity = kind % 2
    lane_b, lane_i = (column % count_z) // half, column % half
    main = (row_b == lane_b) & (row_z == 2 * (half * window + lane_i) + parity)
    is_low = window == 0
    wanted_b = jnp.where(is_low, lane_b + GROUP - 1, lane_b + 1) % GROUP
    wanted_z = 2 * (half * (1 - window) + lane_i) + parity
    useful = jnp.where(is_low, lane_i < REACH, lane_i >= half - REACH)
    edge = (row_b == wanted_b) & (row_z == wanted_z) & useful
    return jnp.where(kind < 2, main, edge).astype(BF16)


def packed(even_ref, matrix_ref):
    count_b, _, count_z = even_ref.shape
    rows = [
        jnp.concatenate([even_ref[b + i] for i in range(GROUP)], axis=1)
        for b in range(0, count_b, GROUP)
    ]
    result = exact_dot(jnp.concatenate(rows, axis=0), matrix_ref[...])
    return [result[:, kind * count_z : (kind + 1) * count_z] for kind in range(4)]


def pack_own(even, matrix):
    count_b, count_a, count_z = even.shape
    total_rows = count_b // GROUP * count_a

    def kernel(even_ref, matrix_ref, out_ref):
        for kind, part in enumerate(packed(even_ref, matrix_ref)):
            out_ref[kind] = part

    return pl.pallas_call(
        kernel,
        out_shape=shape(4, total_rows, count_z),
        in_specs=[spec(pltpu.VMEM)] * 2,
        out_specs=spec(pltpu.VMEM),
        compiler_params=params(8),
        cost_estimate=cost(count_b * count_a * count_z, 1024, 4),
        name="pack_own",
    )(even, matrix)


def edge_slots(count_a, groups, count_z):
    fits = count_z // GROUP // REACH
    slots = []
    for index in range(2 * groups):
        slots.append((index // groups, index % groups, index // fits * count_a, index % fits * REACH))
    return slots, -(-2 * groups // fits) * count_a


def send_into(even_ref, matrix_ref, out_ref):
    count_b, count_a, count_z = even_ref.shape
    groups = count_b // GROUP
    total_rows = groups * count_a
    parts = packed(even_ref, matrix_ref)
    out_ref[pl.ds(0, total_rows), :] = parts[0]
    out_ref[pl.ds(total_rows, total_rows), :] = parts[1]
    slots, _ = edge_slots(count_a, groups, count_z)
    sums = {}
    for parity, g, row, shift in slots:
        part = parts[2 + parity][g * count_a : (g + 1) * count_a]
        part = pltpu.roll(part, shift, 1) if shift else part
        sums[row] = sums[row] + part if row in sums else part
    for row, part in sums.items():
        out_ref[pl.ds(2 * total_rows + row, count_a), :] = part


def sent_shape(count_a, count_b, count_z):
    groups = count_b // GROUP
    _, extra = edge_slots(count_a, groups, count_z)
    return shape(2 * groups * count_a + extra, count_z)


def pack_sent(even, matrix):
    count_b, count_a, count_z = even.shape

    def kernel(even_ref, matrix_ref, out_ref):
        send_into(even_ref, matrix_ref, out_ref)

    return pl.pallas_call(
        kernel,
        out_shape=sent_shape(count_a, count_b, count_z),
        in_specs=[spec(pltpu.VMEM)] * 2,
        out_specs=spec(pltpu.VMEM),
        compiler_params=params(8),
        cost_estimate=cost(count_b * count_a * count_z, 1024, 4),
        name="pack_sent",
    )(even, matrix)


def last_step(snapshots, even_before, current, parts, halos, matrix):
    count_x, count_y, count_z = current.shape
    count_a, count_b = count_x // 2, count_y // 2

    def kernel(
        steps_ref, even_ref, current_ref, qx_ref, qy_ref, cx_ref, cy_ref, near_ref, far_ref,
        side_ref, matrix_ref, final_ref, late_ref, sent_ref, near_out, far_out, side_out,
        wanted, sems,
    ):
        place = Place()
        copy = pltpu.make_async_copy(steps_ref, wanted, sems.at[0])
        copy.start()
        add_halo(
            place, (qx_ref, qy_ref, cx_ref, cy_ref), (near_ref, far_ref, side_ref),
            (near_out, far_out, side_out),
        )
        low, high = pl.ds(0, WIDTH), pl.ds(count_x - WIDTH, WIDTH)

        @pl.when(place.even)
        def _():
            final_ref[high] = near_out[...]
            final_ref[low] = far_out[...]

        @pl.when(jnp.logical_not(place.even))
        def _():
            final_ref[low] = near_out[...]
            final_ref[high] = far_out[...]

        final_ref[:, pl.ds(place.block(count_y), SIDE)] = side_out[...]
        copy.wait()
        wants_last = wanted[place.field, 1] == STEPS

        @pl.when(wants_last)
        def _():
            for b in range(count_b):
                late_ref[b] = even_rows(final_ref, 0, 0, count_a, b)

        @pl.when(jnp.logical_not(wants_last))
        def _():
            late_ref[...] = even_ref[...]

        send_into(late_ref, matrix_ref, sent_ref)

    slab, _, side = face_shapes(count_x, count_y, count_z)
    return pl.pallas_call(
        kernel,
        out_shape=(
            shape(*current.shape),
            shape(count_b, count_a, count_z),
            sent_shape(count_a, count_b, count_z),
        ),
        in_specs=[spec(pltpu.HBM)] + [spec(pltpu.VMEM)] * 10,
        out_specs=(spec(pltpu.VMEM),) * 3,
        scratch_shapes=[
            pltpu.VMEM(slab.shape, F32),
            pltpu.VMEM(slab.shape, F32),
            pltpu.VMEM(side.shape, F32),
            pltpu.SMEM(snapshots.shape, jnp.int32),
            pltpu.SemaphoreType.DMA((1,)),
        ],
        input_output_aliases={2: 0},
        compiler_params=params(12),
        cost_estimate=cost(count_x * count_y * count_z, 10, 3),
        name="last_step",
    )(snapshots, even_before, current, *parts, *halos, matrix)


def write_out(level):
    def kernel(level_ref, out_ref, sem):
        copy = pltpu.make_async_copy(level_ref, out_ref, sem)
        copy.start()
        copy.wait()

    return pl.pallas_call(
        kernel,
        out_shape=shape(*level.shape),
        in_specs=[spec(pltpu.VMEM)],
        out_specs=spec(pltpu.HBM),
        scratch_shapes=[pltpu.SemaphoreType.DMA],
        compiler_params=params(4),
        cost_estimate=cost(level.size, 0, 2),
        name="write_out",
    )(level)


def lag_image(lags, own, other, before, count_a):
    _, total_rows, count_z = own.shape
    groups = total_rows // count_a
    count_h = lags.shape[0]
    half = count_z // GROUP
    last = before is not None

    def kernel(*refs):
        refs = list(refs)
        take = lambda count: [refs.pop(0) for _ in range(count)]
        lags_ref, own_ref, other_ref = take(3)
        if last:
            (before_ref,) = take(1)
        (out_ref,) = take(1)
        edges, lag_of, sems = take(3)
        if last:
            (store,) = take(1)
        else:
            store = out_ref
        place = Place()
        copy = pltpu.make_async_copy(lags_ref, lag_of, sems.at[0])
        copy.start()
        is_source = place.field == 0
        lane = lax.broadcasted_iota(jnp.int32, (count_a, count_z), 1) % half
        useful = jnp.where(is_source, lane, half - 1 - lane) < REACH
        slots, _ = edge_slots(count_a, groups, count_z)
        for parity, g, row, shift in slots:
            part = other_ref[pl.ds(2 * total_rows + row, count_a), :]
            part = pltpu.roll(part, count_z - shift, 1) if shift else part
            edges[parity, pl.ds(g * count_a, count_a), :] = jnp.where(useful, part, 0.0)
        copy.wait()
        lane = lax.broadcasted_iota(jnp.int32, (1, count_z), 1) % half

        def moved(main, edge, shift):
            mask = (lane < shift) | (lane >= half + shift)
            return pltpu.roll(jnp.where(mask, edge, main), (count_z - shift) & (count_z - 1), 1)

        def one(h, _):
            lag = lag_of[h]
            parity = lag & 1
            source_shift = -((lag + parity) >> 1)
            receiver_shift = (lag - parity) >> 1
            own_shift = jnp.where(is_source, source_shift, receiver_shift)
            other_shift = jnp.where(is_source, receiver_shift, source_shift)
            other_rows = pl.ds(pl.multiple_of(parity * total_rows, 8), total_rows)
            product = moved(own_ref[parity], own_ref[2 + parity], own_shift)
            product = product * moved(other_ref[other_rows, :], edges[parity], other_shift)
            for g in range(groups):
                part = product[g * count_a : (g + 1) * count_a]
                lanes = pl.ds(g * count_z, count_z)
                if last:
                    part = part + before_ref[h, :, lanes]
                store[h, :, lanes] = part
            if last:
                pltpu.make_async_copy(store.at[h], out_ref.at[h], sems.at[1]).start()
            return 0

        lax.fori_loop(0, count_h, one, 0)
        if last:
            pltpu.make_async_copy(store, out_ref, sems.at[1]).wait()

    out = (count_h, count_a, groups * count_z)
    operands = [lags, own, other] + ([before] if last else [])
    return pl.pallas_call(
        kernel,
        out_shape=shape(*out),
        in_specs=[spec(pltpu.HBM)] + [spec(pltpu.VMEM)] * (len(operands) - 1),
        out_specs=spec(pltpu.HBM if last else pltpu.VMEM),
        scratch_shapes=[
            pltpu.VMEM((2, total_rows, count_z), F32),
            pltpu.SMEM((count_h,), jnp.int32),
            pltpu.SemaphoreType.DMA((2,)),
        ]
        + ([pltpu.VMEM(out, F32)] if last else []),
        compiler_params=params(12),
        cost_estimate=cost(count_h * total_rows * count_z, 10, 2),
        name="lag_image",
    )(*operands)


def body(
    field_now,
    field_prev,
    courant_squared,
    source_cells,
    source_wave,
    receiver_cells,
    receiver_wave,
    snapshot_steps,
    lag_offsets,
):
    count_x, count_y, count_z = field_now.shape
    loop_size = lax.axis_size("gx")
    half_size = loop_size // 2
    turn = loop_size // 4
    assert lax.axis_size("gy") == 2 and half_size % 2 == 0

    field = ((lax.axis_index("gx") - turn + loop_size) % loop_size) // half_size
    slabs = [(i - turn) % loop_size % half_size for i in range(loop_size)]

    def pairs(odd):
        found = []
        for i, slab in enumerate(slabs):
            if slab % 2 == odd and slab != half_size - 1:
                j = (i + 1) % loop_size
                found += [(i, j), (j, i)]
        return found

    near_pairs, far_pairs = pairs(0), pairs(1)
    across = [(i, (i + half_size) % loop_size) for i in range(loop_size)]

    def exchange(faces):
        near, far, side = faces
        far_in = lax.ppermute(far, "gx", far_pairs)
        near_in = lax.ppermute(near, "gx", near_pairs)
        return near_in, far_in, lax.ppermute(side, "gy", [(0, 1), (1, 0)])

    most = -(-max(source_cells.shape[1], receiver_cells.shape[1]) // 128) * 128

    def chosen(source, receiver, empty):
        source, receiver = (
            jnp.pad(array, ((0, 0), (0, most - array.shape[1])), constant_values=empty)
            for array in (source, receiver)
        )
        return jnp.where(field == 0, source, receiver)

    points = chosen(source_cells, receiver_cells, -1)
    waves = chosen(source_wave, receiver_wave, 0.0)
    own_matrix = pack_matrix(field, count_z)
    sent_matrix = pack_matrix(1 - field, count_z)

    halos = exchange(first_faces(field_now))
    next1, qx, qy, courant, cx, cy = inner_step(
        0, points, waves, field_now, None, field_prev, courant_squared
    )
    faces = halo_step((qx, qy, cx, cy), halos)
    halos = exchange(faces)
    next2, qx, qy, whole1 = inner_step(1, points, waves, next1, faces, field_now, courant)
    faces = halo_step((qx, qy, cx, cy), halos)
    halos = exchange(faces)
    next3, qx, qy, whole2, early = inner_step(
        2, points, waves, next2, faces, whole1, courant, snapshot_steps
    )
    faces = halo_step((qx, qy, cx, cy), halos)
    halos = exchange(faces)
    other_early = lax.ppermute(pack_sent(early, sent_matrix), "gx", across)
    own_early = pack_own(early, own_matrix)
    next4, qx, qy, even3 = inner_step(3, points, waves, next3, faces, whole2, courant)
    final, late, sent_late = last_step(
        snapshot_steps, even3, next4, (qx, qy, cx, cy), halos, sent_matrix
    )
    other_late = lax.ppermute(sent_late, "gx", across)
    partial = lag_image(lag_offsets, own_early, other_early, None, count_x // 2)
    own_late = pack_own(late, own_matrix)
    image = lag_image(lag_offsets, own_late, other_late, partial, count_x // 2)
    return write_out(final), jnp.transpose(image, (1, 0, 2))


def solution(mesh):
    placed = (
        P(("shots", "gx"), "gy", None),
        P(("shots", "gx"), "gy", None),
        P("gx", "gy", None),
        P(None, "shots"),
        P(None, "shots"),
        P(None, "shots"),
        P(None, "shots"),
        P("shots", None),
        P(),
    )
    return jax.shard_map(
        body,
        mesh=mesh,
        in_specs=placed,
        out_specs=(P(("shots", "gx"), "gy", None), P(("shots", "gx"), None, "gy")),
        check_vma=False,
    )
```

```python
import jax
import jax.numpy as jnp
from jax import lax
from jax.experimental import pallas as pl
from jax.experimental.pallas import tpu as pltpu
from jax.sharding import PartitionSpec as P

STEPS = 4
WIDTH = 4
LAGMAX = 8
REACH = LAGMAX // 2
GROUP = 4
SIDE = 8

SCALE = 5040.0
BAND = (8064.0, -1008.0, 128.0, -9.0)
CENTRE = 3.0 * (-205.0 / 72.0)
WEIGHTS = (1.6, -0.2, 8.0 / 315.0, -1.0 / 560.0)

F32 = jnp.float32
BF16 = jnp.bfloat16


def shape(*dims, dtype=F32):
    return jax.ShapeDtypeStruct(dims, dtype)


def params(megabytes):
    return pltpu.CompilerParams(vmem_limit_bytes=megabytes << 20)


def spec(space):
    return pl.BlockSpec(memory_space=space)


def cost(count, flops_each, arrays):
    return pl.CostEstimate(
        flops=int(count * flops_each), bytes_accessed=int(4 * count * arrays), transcendentals=0
    )


def split3(values):
    high = values.astype(BF16)
    rest = values - high.astype(F32)
    middle = rest.astype(BF16)
    low = (rest - middle.astype(F32)).astype(BF16)
    return high, middle, low


def exact_dot(values, matrix):
    parts = [jnp.dot(part, matrix, preferred_element_type=F32) for part in split3(values)]
    return (parts[2] + parts[1]) + parts[0]


class Place:
    def __init__(self):
        loop_size = lax.axis_size("gx")
        self.half = loop_size // 2
        relative = lax.rem(lax.axis_index("gx") + loop_size - loop_size // 4, loop_size)
        self.field = relative // self.half
        self.slab = lax.rem(relative, self.half)
        self.even = lax.rem(self.slab, 2) == 0
        self.y = lax.axis_index("gy")

    def block(self, count_y):
        return pl.multiple_of((1 - self.y) * (count_y - SIDE), SIDE)


def first_faces(field):
    count_x, count_y, count_z = field.shape

    def kernel(field_ref, near_ref, far_ref, side_ref, sems):
        place = Place()
        top = count_x - WIDTH
        near_start = jnp.where(place.even, top, 0)
        copies = [
            pltpu.make_async_copy(field_ref.at[pl.ds(top - near_start, WIDTH)], far_ref, sems.at[0]),
            pltpu.make_async_copy(field_ref.at[pl.ds(near_start, WIDTH)], near_ref, sems.at[1]),
            pltpu.make_async_copy(
                field_ref.at[:, pl.ds(place.block(count_y), SIDE)], side_ref, sems.at[2]
            ),
        ]
        for copy in copies:
            copy.start()
        for copy in copies:
            copy.wait()

    return pl.pallas_call(
        kernel,
        out_shape=face_shapes(count_x, count_y, count_z),
        in_specs=[spec(pltpu.HBM)],
        out_specs=(spec(pltpu.VMEM),) * 3,
        scratch_shapes=[pltpu.SemaphoreType.DMA((3,))],
        compiler_params=params(8),
        name="first_faces",
    )(field)


def face_shapes(count_x, count_y, count_z):
    slab = shape(WIDTH, count_y, count_z)
    return slab, slab, shape(count_x, SIDE, count_z)


def even_rows(level_ref, offset_x, offset_y, count_a, b):
    rows, stride, lanes = level_ref.shape
    flat = level_ref.reshape(rows * stride, lanes)
    start = offset_x * stride + offset_y + 2 * b
    return flat[pl.ds(start, count_a, stride=2 * stride), :]


def inner_step(number, points, waves, current, faces, previous, courant, snapshots=None):
    count_x, count_y, count_z = current.shape
    count_a, count_b = count_x // 2, count_y // 2
    first = faces is None
    last = number == STEPS - 1
    snapshot = number == STEPS // 2
    count_j = points.shape[1]

    def kernel(*refs):
        refs = list(refs)
        take = lambda count: [refs.pop(0) for _ in range(count)]
        points_ref, waves_ref, current_ref = take(3)
        if not first:
            near_ref, far_ref, side_ref = take(3)
        previous_ref, courant_ref = take(2)
        if snapshot:
            (steps_ref,) = take(1)
        next_ref, qx_ref, qy_ref = take(3)
        if first:
            kept_ref, cx_ref, cy_ref = take(3)
        elif not last:
            (whole_ref,) = take(1)
        if snapshot or last:
            (even_ref,) = take(1)
        padded, zpart, addpart = take(3)
        if first:
            before_ref, sems = take(2)
        if snapshot:
            wanted, sems = take(2)

        place = Place()
        block = place.block(count_y)
        rows, columns = pl.ds(WIDTH, count_x), pl.ds(SIDE, count_y)
        if first:
            copies = [
                pltpu.make_async_copy(current_ref, padded.at[rows, columns], sems.at[0]),
                pltpu.make_async_copy(previous_ref, before_ref, sems.at[1]),
                pltpu.make_async_copy(courant_ref, kept_ref, sems.at[2]),
            ]
            for copy in copies:
                copy.start()
        else:
            before_ref, kept_ref = previous_ref, courant_ref
        if snapshot:
            copies = [pltpu.make_async_copy(steps_ref, wanted, sems.at[0])]
            copies[0].start()

        zero_x = jnp.zeros((WIDTH, count_y + 2 * SIDE, count_z), F32)
        padded[pl.ds(0, WIDTH)] = zero_x
        padded[pl.ds(count_x + WIDTH, WIDTH)] = zero_x
        zero_y = jnp.zeros((count_x, SIDE, count_z), F32)
        padded[rows, pl.ds(0, SIDE)] = zero_y
        padded[rows, pl.ds(count_y + SIDE, SIDE)] = zero_y

        px = points_ref[0:1, :] - place.slab * count_x
        py = points_ref[1:2, :] - place.y * count_y
        inside = (px >= 0) & (px < count_x) & (py >= 0) & (py < count_y)
        home = jnp.where(inside, px * count_y + py, -1)
        amounts = waves_ref[number : number + 1, :]
        spread = jnp.where(
            lax.broadcasted_iota(jnp.int32, (count_z, count_j), 0) == points_ref[2:3, :],
            amounts,
            0.0,
        )
        spread = split3(spread)

        gap = jnp.abs(
            lax.broadcasted_iota(jnp.int32, (count_z, count_z), 0)
            - lax.broadcasted_iota(jnp.int32, (count_z, count_z), 1)
        )
        band = jnp.zeros((count_z, count_z), F32)
        for offset, weight in enumerate(BAND, 1):
            band = jnp.where(gap == offset, weight, band)
        band = band.astype(BF16)

        if first:
            copies[0].wait()
        else:
            padded[rows, columns] = current_ref[...]
            low, high = pl.ds(WIDTH, WIDTH), pl.ds(count_x, WIDTH)

            @pl.when(place.even)
            def _():
                padded[high, columns] = near_ref[...]
                padded[low, columns] = far_ref[...]

            @pl.when(jnp.logical_not(place.even))
            def _():
                padded[low, columns] = near_ref[...]
                padded[high, columns] = far_ref[...]

            padded[rows, pl.ds(pl.multiple_of(block + SIDE, SIDE), SIDE)] = side_ref[...]

        chunk = 8

        def multiply(index, _):
            start = pl.multiple_of(index * chunk, chunk)
            values = padded[pl.ds(start + WIDTH, chunk), columns]
            zpart[pl.ds(start, chunk)] = exact_dot(
                values.reshape(chunk * count_y, count_z), band
            ).reshape(chunk, count_y, count_z)
            here = start * count_y + lax.broadcasted_iota(
                jnp.int32, (chunk * count_y, count_j), 0
            )
            hit = jnp.where(here == home, 1.0, 0.0).astype(BF16)
            added = [
                lax.dot_general(hit, part, (((1,), (1,)), ((), ())), preferred_element_type=F32)
                for part in spread
            ]
            added = (added[2] + added[1]) + added[0]
            addpart[pl.ds(start, chunk)] = added.reshape(chunk, count_y, count_z)
            return 0

        lax.fori_loop(0, count_x // chunk, multiply, 0)
        if first:
            copies[1].wait()
            copies[2].wait()

        def row(x, _):
            middle = padded[x + WIDTH, columns]
            total = CENTRE * middle + (1.0 / SCALE) * zpart[x]
            for offset, weight in enumerate(WEIGHTS, 1):
                paired = padded[x + WIDTH + offset, columns] + padded[x + WIDTH - offset, columns]
                paired = paired + (
                    padded[x + WIDTH, pl.ds(SIDE + offset, count_y)]
                    + padded[x + WIDTH, pl.ds(SIDE - offset, count_y)]
                )
                total = total + weight * paired
            if not first and not last:
                whole_ref[x] = middle
            next_ref[x] = (2.0 * middle - before_ref[x] + kept_ref[x] * total) + addpart[x]
            return 0

        lax.fori_loop(0, count_x, row, 0, unroll=4)

        qx_ref[pl.ds(0, WIDTH)] = next_ref[pl.ds(0, WIDTH)]
        qx_ref[pl.ds(WIDTH, WIDTH)] = next_ref[pl.ds(count_x - WIDTH, WIDTH)]
        qy_ref[...] = next_ref[:, pl.ds(block, SIDE)]
        if first:
            cx_ref[pl.ds(0, WIDTH)] = kept_ref[pl.ds(0, WIDTH)]
            cx_ref[pl.ds(WIDTH, WIDTH)] = kept_ref[pl.ds(count_x - WIDTH, WIDTH)]
            cy_ref[...] = kept_ref[:, pl.ds(block, SIDE)]
        if last:
            for b in range(count_b):
                even_ref[b] = even_rows(padded, WIDTH, SIDE, count_a, b)
        if snapshot:
            copies[0].wait()
            earlier = wanted[place.field, 0] == number - 1

            @pl.when(earlier)
            def _():
                for b in range(count_b):
                    even_ref[b] = even_rows(previous_ref, 0, 0, count_a, b)

            @pl.when(jnp.logical_not(earlier))
            def _():
                for b in range(count_b):
                    even_ref[b] = even_rows(padded, WIDTH, SIDE, count_a, b)

    full = shape(count_x, count_y, count_z)
    slab, side = shape(2 * WIDTH, count_y, count_z), shape(count_x, SIDE, count_z)
    even = shape(count_b, count_a, count_z)
    outs = [full, slab, side]
    if first:
        outs += [full, slab, side]
    elif not last:
        outs.append(full)
    if snapshot or last:
        outs.append(even)
    place_of = spec(pltpu.HBM) if first else spec(pltpu.VMEM)
    operands, specs = [points, waves, current], [spec(pltpu.VMEM)] * 2 + [place_of]
    if not first:
        operands += list(faces)
        specs += [spec(pltpu.VMEM)] * 3
    operands += [previous, courant]
    specs += [place_of] * 2
    scratch = [
        pltpu.VMEM((count_x + 2 * WIDTH, count_y + 2 * SIDE, count_z), F32),
        pltpu.VMEM(full.shape, F32),
        pltpu.VMEM(full.shape, F32),
    ]
    if first:
        scratch += [pltpu.VMEM(full.shape, F32), pltpu.SemaphoreType.DMA((3,))]
    if snapshot:
        operands.append(snapshots)
        specs.append(spec(pltpu.HBM))
        scratch += [
            pltpu.SMEM(snapshots.shape, jnp.int32),
            pltpu.SemaphoreType.DMA((1,)),
        ]
    return pl.pallas_call(
        kernel,
        out_shape=tuple(outs),
        in_specs=specs,
        out_specs=(spec(pltpu.VMEM),) * len(outs),
        scratch_shapes=scratch,
        compiler_params=params(20),
        cost_estimate=cost(count_x * count_y * count_z, 60, 6),
        name=f"inner_step_{number}",
    )(*operands)


def low_terms(halo_ref, r):
    total = None
    for k in range(r + 1, WIDTH + 1):
        term = WEIGHTS[k - 1] * halo_ref[WIDTH + r - k]
        total = term if total is None else total + term
    return total


def high_terms(halo_ref, r):
    total = None
    for k in range(WIDTH - r, WIDTH + 1):
        term = WEIGHTS[k - 1] * halo_ref[r + k - WIDTH]
        total = term if total is None else total + term
    return total


def add_halo(place, parts, halos, outs):
    qx_ref, qy_ref, cx_ref, cy_ref = parts
    near_in, far_in, side_in = halos
    near_out, far_out, side_out = outs
    count_y, count_x = qx_ref.shape[1], qy_ref.shape[0]
    block = place.block(count_y)

    def along_x(low_in, high_in, low_out, high_out):
        for r in range(WIDTH):
            low_out[r] = qx_ref[r] + cx_ref[r] * low_terms(low_in, r)
            high_out[r] = qx_ref[WIDTH + r] + cx_ref[WIDTH + r] * high_terms(high_in, r)
        side_out[pl.ds(0, WIDTH)] = low_out[:, pl.ds(block, SIDE)]
        side_out[pl.ds(count_x - WIDTH, WIDTH)] = high_out[:, pl.ds(block, SIDE)]

    inner = pl.ds(WIDTH, count_x - 2 * WIDTH)
    side_out[inner] = qy_ref[inner]

    @pl.when(place.even)
    def _():
        along_x(far_in, near_in, far_out, near_out)

    @pl.when(jnp.logical_not(place.even))
    def _():
        along_x(near_in, far_in, near_out, far_out)

    def along_y(shifts, masks):
        halo = side_in[...]
        depth, lanes = halo.shape[0], halo.shape[2]
        line = lax.broadcasted_iota(jnp.int32, (1, SIDE, lanes), 1)
        total = None
        for k in range(1, WIDTH + 1):
            weight = jnp.where(masks(line, k), WEIGHTS[k - 1], 0.0)
            term = weight * pltpu.roll(halo, shifts(k), 1)
            total = term if total is None else total + term
        side_out[...] = side_out[...] + cy_ref[...] * total

    @pl.when(place.y == 0)
    def _():
        along_y(lambda k: SIDE - k, lambda line, k: line >= SIDE - k)

    @pl.when(place.y != 0)
    def _():
        along_y(lambda k: k, lambda line, k: line < k)

    def corners(low_out, high_out):
        low_out[:, pl.ds(block, SIDE)] = side_out[pl.ds(0, WIDTH)]
        high_out[:, pl.ds(block, SIDE)] = side_out[pl.ds(count_x - WIDTH, WIDTH)]

    @pl.when(place.even)
    def _():
        corners(far_out, near_out)

    @pl.when(jnp.logical_not(place.even))
    def _():
        corners(near_out, far_out)


def halo_step(parts, halos):
    count_y, (count_x, _, count_z) = parts[0].shape[1], parts[1].shape

    def kernel(*refs):
        add_halo(Place(), refs[:4], refs[4:7], refs[7:])

    return pl.pallas_call(
        kernel,
        out_shape=face_shapes(count_x, count_y, count_z),
        in_specs=[spec(pltpu.VMEM)] * 7,
        out_specs=(spec(pltpu.VMEM),) * 3,
        compiler_params=params(8),
        cost_estimate=cost(16 * count_y * count_z, 10, 6),
        name="halo_step",
    )(*parts, *halos)


def pack_matrix(window, count_z):
    half = count_z // GROUP
    size = GROUP * count_z
    row = lax.broadcasted_iota(jnp.int32, (size, size), 0)
    column = lax.broadcasted_iota(jnp.int32, (size, size), 1)
    row_b, row_z = row // count_z, row % count_z
    kind = column // count_z
    parity = kind % 2
    lane_b, lane_i = (column % count_z) // half, column % half
    main = (row_b == lane_b) & (row_z == 2 * (half * window + lane_i) + parity)
    is_low = window == 0
    wanted_b = jnp.where(is_low, lane_b + GROUP - 1, lane_b + 1) % GROUP
    wanted_z = 2 * (half * (1 - window) + lane_i) + parity
    useful = jnp.where(is_low, lane_i < REACH, lane_i >= half - REACH)
    edge = (row_b == wanted_b) & (row_z == wanted_z) & useful
    return jnp.where(kind < 2, main, edge).astype(BF16)


def packed(even_ref, matrix_ref):
    count_b, _, count_z = even_ref.shape
    rows = [
        jnp.concatenate([even_ref[b + i] for i in range(GROUP)], axis=1)
        for b in range(0, count_b, GROUP)
    ]
    result = exact_dot(jnp.concatenate(rows, axis=0), matrix_ref[...])
    return [result[:, kind * count_z : (kind + 1) * count_z] for kind in range(4)]


def pack_own(even, matrix):
    count_b, count_a, count_z = even.shape
    total_rows = count_b // GROUP * count_a

    def kernel(even_ref, matrix_ref, out_ref):
        for kind, part in enumerate(packed(even_ref, matrix_ref)):
            out_ref[kind] = part

    return pl.pallas_call(
        kernel,
        out_shape=shape(4, total_rows, count_z),
        in_specs=[spec(pltpu.VMEM)] * 2,
        out_specs=spec(pltpu.VMEM),
        compiler_params=params(8),
        cost_estimate=cost(count_b * count_a * count_z, 1024, 4),
        name="pack_own",
    )(even, matrix)


def edge_slots(count_a, groups, count_z):
    fits = count_z // GROUP // REACH
    slots = []
    for index in range(2 * groups):
        slots.append((index // groups, index % groups, index // fits * count_a, index % fits * REACH))
    return slots, -(-2 * groups // fits) * count_a


def send_into(even_ref, matrix_ref, out_ref):
    count_b, count_a, count_z = even_ref.shape
    groups = count_b // GROUP
    total_rows = groups * count_a
    parts = packed(even_ref, matrix_ref)
    out_ref[pl.ds(0, total_rows), :] = parts[0]
    out_ref[pl.ds(total_rows, total_rows), :] = parts[1]
    slots, _ = edge_slots(count_a, groups, count_z)
    sums = {}
    for parity, g, row, shift in slots:
        part = parts[2 + parity][g * count_a : (g + 1) * count_a]
        part = pltpu.roll(part, shift, 1) if shift else part
        sums[row] = sums[row] + part if row in sums else part
    for row, part in sums.items():
        out_ref[pl.ds(2 * total_rows + row, count_a), :] = part


def sent_shape(count_a, count_b, count_z):
    groups = count_b // GROUP
    _, extra = edge_slots(count_a, groups, count_z)
    return shape(2 * groups * count_a + extra, count_z)


def pack_sent(even, matrix):
    count_b, count_a, count_z = even.shape

    def kernel(even_ref, matrix_ref, out_ref):
        send_into(even_ref, matrix_ref, out_ref)

    return pl.pallas_call(
        kernel,
        out_shape=sent_shape(count_a, count_b, count_z),
        in_specs=[spec(pltpu.VMEM)] * 2,
        out_specs=spec(pltpu.VMEM),
        compiler_params=params(8),
        cost_estimate=cost(count_b * count_a * count_z, 1024, 4),
        name="pack_sent",
    )(even, matrix)


def last_step(snapshots, even_before, current, parts, halos, matrix):
    count_x, count_y, count_z = current.shape
    count_a, count_b = count_x // 2, count_y // 2

    def kernel(
        steps_ref, even_ref, current_ref, qx_ref, qy_ref, cx_ref, cy_ref, near_ref, far_ref,
        side_ref, matrix_ref, final_ref, late_ref, sent_ref, near_out, far_out, side_out,
        wanted, sems,
    ):
        place = Place()
        copy = pltpu.make_async_copy(steps_ref, wanted, sems.at[0])
        copy.start()
        add_halo(
            place, (qx_ref, qy_ref, cx_ref, cy_ref), (near_ref, far_ref, side_ref),
            (near_out, far_out, side_out),
        )
        low, high = pl.ds(0, WIDTH), pl.ds(count_x - WIDTH, WIDTH)

        @pl.when(place.even)
        def _():
            final_ref[high] = near_out[...]
            final_ref[low] = far_out[...]

        @pl.when(jnp.logical_not(place.even))
        def _():
            final_ref[low] = near_out[...]
            final_ref[high] = far_out[...]

        final_ref[:, pl.ds(place.block(count_y), SIDE)] = side_out[...]
        copy.wait()
        wants_last = wanted[place.field, 1] == STEPS

        @pl.when(wants_last)
        def _():
            for b in range(count_b):
                late_ref[b] = even_rows(final_ref, 0, 0, count_a, b)

        @pl.when(jnp.logical_not(wants_last))
        def _():
            late_ref[...] = even_ref[...]

        send_into(late_ref, matrix_ref, sent_ref)

    slab, _, side = face_shapes(count_x, count_y, count_z)
    return pl.pallas_call(
        kernel,
        out_shape=(
            shape(*current.shape),
            shape(count_b, count_a, count_z),
            sent_shape(count_a, count_b, count_z),
        ),
        in_specs=[spec(pltpu.HBM)] + [spec(pltpu.VMEM)] * 10,
        out_specs=(spec(pltpu.VMEM),) * 3,
        scratch_shapes=[
            pltpu.VMEM(slab.shape, F32),
            pltpu.VMEM(slab.shape, F32),
            pltpu.VMEM(side.shape, F32),
            pltpu.SMEM(snapshots.shape, jnp.int32),
            pltpu.SemaphoreType.DMA((1,)),
        ],
        input_output_aliases={2: 0},
        compiler_params=params(12),
        cost_estimate=cost(count_x * count_y * count_z, 10, 3),
        name="last_step",
    )(snapshots, even_before, current, *parts, *halos, matrix)


def write_out(level):
    def kernel(level_ref, out_ref, sem):
        copy = pltpu.make_async_copy(level_ref, out_ref, sem)
        copy.start()
        copy.wait()

    return pl.pallas_call(
        kernel,
        out_shape=shape(*level.shape),
        in_specs=[spec(pltpu.VMEM)],
        out_specs=spec(pltpu.HBM),
        scratch_shapes=[pltpu.SemaphoreType.DMA],
        compiler_params=params(4),
        cost_estimate=cost(level.size, 0, 2),
        name="write_out",
    )(level)


def lag_image(lags, own, other, before, count_a):
    _, total_rows, count_z = own.shape
    groups = total_rows // count_a
    count_h = lags.shape[0]
    half = count_z // GROUP
    last = before is not None

    def kernel(*refs):
        refs = list(refs)
        take = lambda count: [refs.pop(0) for _ in range(count)]
        lags_ref, own_ref, other_ref = take(3)
        if last:
            (before_ref,) = take(1)
        (out_ref,) = take(1)
        edges, lag_of, sems = take(3)
        if last:
            (store,) = take(1)
        else:
            store = out_ref
        place = Place()
        copy = pltpu.make_async_copy(lags_ref, lag_of, sems.at[0])
        copy.start()
        is_source = place.field == 0
        lane = lax.broadcasted_iota(jnp.int32, (count_a, count_z), 1) % half
        useful = jnp.where(is_source, lane, half - 1 - lane) < REACH
        slots, _ = edge_slots(count_a, groups, count_z)
        for parity, g, row, shift in slots:
            part = other_ref[pl.ds(2 * total_rows + row, count_a), :]
            part = pltpu.roll(part, count_z - shift, 1) if shift else part
            edges[parity, pl.ds(g * count_a, count_a), :] = jnp.where(useful, part, 0.0)
        copy.wait()
        lane = lax.broadcasted_iota(jnp.int32, (1, count_z), 1) % half

        def moved(main, edge, shift):
            mask = (lane < shift) | (lane >= half + shift)
            return pltpu.roll(jnp.where(mask, edge, main), (count_z - shift) & (count_z - 1), 1)

        def one(h, _):
            lag = lag_of[h]
            parity = lag & 1
            source_shift = -((lag + parity) >> 1)
            receiver_shift = (lag - parity) >> 1
            own_shift = jnp.where(is_source, source_shift, receiver_shift)
            other_shift = jnp.where(is_source, receiver_shift, source_shift)
            other_rows = pl.ds(pl.multiple_of(parity * total_rows, 8), total_rows)
            product = moved(own_ref[parity], own_ref[2 + parity], own_shift)
            product = product * moved(other_ref[other_rows, :], edges[parity], other_shift)
            for g in range(groups):
                part = product[g * count_a : (g + 1) * count_a]
                lanes = pl.ds(g * count_z, count_z)
                if last:
                    part = part + before_ref[h, :, lanes]
                store[h, :, lanes] = part
            if last:
                pltpu.make_async_copy(store.at[h], out_ref.at[h], sems.at[1]).start()
            return 0

        lax.fori_loop(0, count_h, one, 0, unroll=True)
        if last:
            pltpu.make_async_copy(store, out_ref, sems.at[1]).wait()

    out = (count_h, count_a, groups * count_z)
    operands = [lags, own, other] + ([before] if last else [])
    return pl.pallas_call(
        kernel,
        out_shape=shape(*out),
        in_specs=[spec(pltpu.HBM)] + [spec(pltpu.VMEM)] * (len(operands) - 1),
        out_specs=spec(pltpu.HBM if last else pltpu.VMEM),
        scratch_shapes=[
            pltpu.VMEM((2, total_rows, count_z), F32),
            pltpu.SMEM((count_h,), jnp.int32),
            pltpu.SemaphoreType.DMA((2,)),
        ]
        + ([pltpu.VMEM(out, F32)] if last else []),
        compiler_params=params(12),
        cost_estimate=cost(count_h * total_rows * count_z, 10, 2),
        name="lag_image",
    )(*operands)


def body(
    field_now,
    field_prev,
    courant_squared,
    source_cells,
    source_wave,
    receiver_cells,
    receiver_wave,
    snapshot_steps,
    lag_offsets,
):
    count_x, count_y, count_z = field_now.shape
    loop_size = lax.axis_size("gx")
    half_size = loop_size // 2
    turn = loop_size // 4
    assert lax.axis_size("gy") == 2 and half_size % 2 == 0

    field = ((lax.axis_index("gx") - turn + loop_size) % loop_size) // half_size
    slabs = [(i - turn) % loop_size % half_size for i in range(loop_size)]

    def pairs(odd):
        found = []
        for i, slab in enumerate(slabs):
            if slab % 2 == odd and slab != half_size - 1:
                j = (i + 1) % loop_size
                found += [(i, j), (j, i)]
        return found

    near_pairs, far_pairs = pairs(0), pairs(1)
    across = [(i, (i + half_size) % loop_size) for i in range(loop_size)]

    def exchange(faces):
        near, far, side = faces
        far_in = lax.ppermute(far, "gx", far_pairs)
        near_in = lax.ppermute(near, "gx", near_pairs)
        return near_in, far_in, lax.ppermute(side, "gy", [(0, 1), (1, 0)])

    most = -(-max(source_cells.shape[1], receiver_cells.shape[1]) // 128) * 128

    def chosen(source, receiver, empty):
        source, receiver = (
            jnp.pad(array, ((0, 0), (0, most - array.shape[1])), constant_values=empty)
            for array in (source, receiver)
        )
        return jnp.where(field == 0, source, receiver)

    points = chosen(source_cells, receiver_cells, -1)
    waves = chosen(source_wave, receiver_wave, 0.0)
    own_matrix = pack_matrix(field, count_z)
    sent_matrix = pack_matrix(1 - field, count_z)

    field_now, field_prev, courant_squared = (
        pltpu.with_memory_space_constraint(array, pltpu.HBM)
        for array in (field_now, field_prev, courant_squared)
    )
    halos = exchange(first_faces(field_now))
    next1, qx, qy, courant, cx, cy = inner_step(
        0, points, waves, field_now, None, field_prev, courant_squared
    )
    faces = halo_step((qx, qy, cx, cy), halos)
    halos = exchange(faces)
    next2, qx, qy, whole1 = inner_step(1, points, waves, next1, faces, field_now, courant)
    faces = halo_step((qx, qy, cx, cy), halos)
    halos = exchange(faces)
    next3, qx, qy, whole2, early = inner_step(
        2, points, waves, next2, faces, whole1, courant, snapshot_steps
    )
    faces = halo_step((qx, qy, cx, cy), halos)
    halos = exchange(faces)
    other_early = lax.ppermute(pack_sent(early, sent_matrix), "gx", across)
    own_early = pack_own(early, own_matrix)
    next4, qx, qy, even3 = inner_step(3, points, waves, next3, faces, whole2, courant)
    final, late, sent_late = last_step(
        snapshot_steps, even3, next4, (qx, qy, cx, cy), halos, sent_matrix
    )
    other_late = lax.ppermute(sent_late, "gx", across)
    partial = lag_image(lag_offsets, own_early, other_early, None, count_x // 2)
    own_late = pack_own(late, own_matrix)
    image = lag_image(lag_offsets, own_late, other_late, partial, count_x // 2)
    return write_out(final), jnp.transpose(image, (1, 0, 2))


def solution(mesh):
    placed = (
        P(("shots", "gx"), "gy", None),
        P(("shots", "gx"), "gy", None),
        P("gx", "gy", None),
        P(None, "shots"),
        P(None, "shots"),
        P(None, "shots"),
        P(None, "shots"),
        P("shots", None),
        P(),
    )
    return jax.shard_map(
        body,
        mesh=mesh,
        in_specs=placed,
        out_specs=(P(("shots", "gx"), "gy", None), P(("shots", "gx"), None, "gy")),
        check_vma=False,
    )
```

```python
import jax
import jax.numpy as jnp
import numpy as np
from jax import lax
from jax.experimental import pallas as pl
from jax.experimental.pallas import tpu as pltpu
from jax.sharding import PartitionSpec as P

STEPS = 4
WIDTH = 4
LAGMAX = 8
REACH = LAGMAX // 2
GROUP = 4
SIDE = 8

SCALE = 5040.0
BAND = (8064.0, -1008.0, 128.0, -9.0)
CENTRE = 3.0 * (-205.0 / 72.0)
WEIGHTS = (1.6, -0.2, 8.0 / 315.0, -1.0 / 560.0)

F32 = jnp.float32
BF16 = jnp.bfloat16


def shape(*dims, dtype=F32):
    return jax.ShapeDtypeStruct(dims, dtype)


def params(megabytes):
    return pltpu.CompilerParams(vmem_limit_bytes=megabytes << 20)


def spec(space):
    return pl.BlockSpec(memory_space=space)


def cost(count, flops_each, arrays):
    return pl.CostEstimate(
        flops=int(count * flops_each), bytes_accessed=int(4 * count * arrays), transcendentals=0
    )


def split3(values):
    high = values.astype(BF16)
    rest = values - high.astype(F32)
    middle = rest.astype(BF16)
    low = (rest - middle.astype(F32)).astype(BF16)
    return high, middle, low


def exact_dot(values, matrix):
    parts = [jnp.dot(part, matrix, preferred_element_type=F32) for part in split3(values)]
    return (parts[2] + parts[1]) + parts[0]


class Place:
    def __init__(self):
        loop_size = lax.axis_size("gx")
        self.half = loop_size // 2
        relative = lax.rem(lax.axis_index("gx") + loop_size - loop_size // 4, loop_size)
        self.field = relative // self.half
        self.slab = lax.rem(relative, self.half)
        self.even = lax.rem(self.slab, 2) == 0
        self.y = lax.axis_index("gy")

    def block(self, count_y):
        return pl.multiple_of((1 - self.y) * (count_y - SIDE), SIDE)


def first_far(field):
    count_x, count_y, count_z = field.shape

    def kernel(field_ref, far_ref, sem):
        start = jnp.where(Place().even, 0, count_x - WIDTH)
        copy = pltpu.make_async_copy(field_ref.at[pl.ds(start, WIDTH)], far_ref, sem)
        copy.start()
        copy.wait()

    return pl.pallas_call(
        kernel,
        out_shape=shape(WIDTH, count_y, count_z),
        in_specs=[spec(pltpu.HBM)],
        out_specs=spec(pltpu.VMEM),
        scratch_shapes=[pltpu.SemaphoreType.DMA],
        compiler_params=params(8),
        name="first_far",
    )(field)


def first_near(field):
    count_x, count_y, count_z = field.shape

    def kernel(field_ref, near_ref, side_ref, sems):
        place = Place()
        start = jnp.where(place.even, count_x - WIDTH, 0)
        copies = [
            pltpu.make_async_copy(field_ref.at[pl.ds(start, WIDTH)], near_ref, sems.at[0]),
            pltpu.make_async_copy(
                field_ref.at[:, pl.ds(place.block(count_y), SIDE)], side_ref, sems.at[1]
            ),
        ]
        for copy in copies:
            copy.start()
        for copy in copies:
            copy.wait()

    return pl.pallas_call(
        kernel,
        out_shape=face_shapes(count_x, count_y, count_z)[1:],
        in_specs=[spec(pltpu.HBM)],
        out_specs=(spec(pltpu.VMEM),) * 2,
        scratch_shapes=[pltpu.SemaphoreType.DMA((2,))],
        compiler_params=params(8),
        name="first_near",
    )(field)


def face_shapes(count_x, count_y, count_z):
    slab = shape(WIDTH, count_y, count_z)
    return slab, slab, shape(count_x, SIDE, count_z)


def even_rows(level_ref, offset_x, offset_y, count_a, b):
    rows, stride, lanes = level_ref.shape
    flat = level_ref.reshape(rows * stride, lanes)
    start = offset_x * stride + offset_y + 2 * b
    return flat[pl.ds(start, count_a, stride=2 * stride), :]


def inner_step(number, points, waves, current, faces, previous, courant, snapshots=None, matrices=None):
    count_x, count_y, count_z = current.shape
    count_a, count_b = count_x // 2, count_y // 2
    first = faces is None
    last = number == STEPS - 1
    snapshot = number == STEPS // 2
    count_j = points.shape[1]

    def kernel(*refs):
        refs = list(refs)
        take = lambda count: [refs.pop(0) for _ in range(count)]
        points_ref, waves_ref, current_ref = take(3)
        if not first:
            far_ref, near_ref, side_ref = take(3)
        previous_ref, courant_ref = take(2)
        if snapshot:
            steps_ref, matrices_ref = take(2)
        next_ref, qx_ref, qy_ref = take(3)
        if first:
            kept_ref, cx_ref, cy_ref = take(3)
        if not last:
            (whole_ref,) = take(1)
        if snapshot:
            own_out, sent_out, own_matrix, sent_matrix, flag_ref = take(5)
        if last:
            (even_ref,) = take(1)
        padded, zpart, addpart = take(3)
        if first:
            before_ref, sems = take(2)
        if snapshot:
            even_ref, wanted, sems = take(3)

        place = Place()
        block = place.block(count_y)
        rows, columns = pl.ds(WIDTH, count_x), pl.ds(SIDE, count_y)
        if first:
            copies = [
                pltpu.make_async_copy(current_ref, padded.at[rows, columns], sems.at[0]),
                pltpu.make_async_copy(previous_ref, before_ref, sems.at[1]),
                pltpu.make_async_copy(courant_ref, kept_ref, sems.at[2]),
            ]
            for copy in copies:
                copy.start()
        else:
            before_ref, kept_ref = previous_ref, courant_ref
        if snapshot:
            copies = [
                pltpu.make_async_copy(steps_ref, wanted, sems.at[0]),
                pltpu.make_async_copy(matrices_ref.at[place.field], own_matrix, sems.at[1]),
                pltpu.make_async_copy(matrices_ref.at[1 - place.field], sent_matrix, sems.at[2]),
            ]
            for copy in copies:
                copy.start()

        zero_x = jnp.zeros((WIDTH, count_y + 2 * SIDE, count_z), F32)
        padded[pl.ds(0, WIDTH)] = zero_x
        padded[pl.ds(count_x + WIDTH, WIDTH)] = zero_x
        zero_y = jnp.zeros((count_x, SIDE, count_z), F32)
        padded[rows, pl.ds(0, SIDE)] = zero_y
        padded[rows, pl.ds(count_y + SIDE, SIDE)] = zero_y

        px = points_ref[0:1, :] - place.slab * count_x
        py = points_ref[1:2, :] - place.y * count_y
        inside = (px >= 0) & (px < count_x) & (py >= 0) & (py < count_y)
        home = jnp.where(inside, px * count_y + py, -1)
        amounts = waves_ref[number : number + 1, :]
        spread = jnp.where(
            lax.broadcasted_iota(jnp.int32, (count_z, count_j), 0) == points_ref[2:3, :],
            amounts,
            0.0,
        )
        spread = split3(spread)

        gap = jnp.abs(
            lax.broadcasted_iota(jnp.int32, (count_z, count_z), 0)
            - lax.broadcasted_iota(jnp.int32, (count_z, count_z), 1)
        )
        band = jnp.zeros((count_z, count_z), F32)
        for offset, weight in enumerate(BAND, 1):
            band = jnp.where(gap == offset, weight, band)
        band = band.astype(BF16)

        if first:
            copies[0].wait()
        else:
            padded[rows, columns] = current_ref[...]
            low, high = pl.ds(WIDTH, WIDTH), pl.ds(count_x, WIDTH)

            @pl.when(place.even)
            def _():
                padded[high, columns] = near_ref[...]
                padded[low, columns] = far_ref[...]

            @pl.when(jnp.logical_not(place.even))
            def _():
                padded[low, columns] = near_ref[...]
                padded[high, columns] = far_ref[...]

            padded[rows, pl.ds(pl.multiple_of(block + SIDE, SIDE), SIDE)] = side_ref[...]

        chunk = 8

        def multiply(index, _):
            start = pl.multiple_of(index * chunk, chunk)
            values = padded[pl.ds(start + WIDTH, chunk), columns]
            zpart[pl.ds(start, chunk)] = exact_dot(
                values.reshape(chunk * count_y, count_z), band
            ).reshape(chunk, count_y, count_z)
            here = start * count_y + lax.broadcasted_iota(
                jnp.int32, (chunk * count_y, count_j), 0
            )
            hit = jnp.where(here == home, 1.0, 0.0).astype(BF16)
            added = [
                lax.dot_general(hit, part, (((1,), (1,)), ((), ())), preferred_element_type=F32)
                for part in spread
            ]
            added = (added[2] + added[1]) + added[0]
            addpart[pl.ds(start, chunk)] = added.reshape(chunk, count_y, count_z)
            return 0

        lax.fori_loop(0, count_x // chunk, multiply, 0)
        if first:
            copies[1].wait()
            copies[2].wait()

        def row(x, _):
            middle = padded[x + WIDTH, columns]
            total = CENTRE * middle + (1.0 / SCALE) * zpart[x]
            for offset, weight in enumerate(WEIGHTS, 1):
                paired = padded[x + WIDTH + offset, columns] + padded[x + WIDTH - offset, columns]
                paired = paired + (
                    padded[x + WIDTH, pl.ds(SIDE + offset, count_y)]
                    + padded[x + WIDTH, pl.ds(SIDE - offset, count_y)]
                )
                total = total + weight * paired
            if not last:
                whole_ref[x] = middle
            next_ref[x] = (2.0 * middle - before_ref[x] + kept_ref[x] * total) + addpart[x]
            return 0

        lax.fori_loop(0, count_x, row, 0, unroll=4)

        qx_ref[pl.ds(0, WIDTH)] = next_ref[pl.ds(0, WIDTH)]
        qx_ref[pl.ds(WIDTH, WIDTH)] = next_ref[pl.ds(count_x - WIDTH, WIDTH)]
        qy_ref[...] = next_ref[:, pl.ds(block, SIDE)]
        if first:
            cx_ref[pl.ds(0, WIDTH)] = kept_ref[pl.ds(0, WIDTH)]
            cx_ref[pl.ds(WIDTH, WIDTH)] = kept_ref[pl.ds(count_x - WIDTH, WIDTH)]
            cy_ref[...] = kept_ref[:, pl.ds(block, SIDE)]
        if last:
            for b in range(count_b):
                even_ref[b] = even_rows(padded, WIDTH, SIDE, count_a, b)
        if snapshot:
            for copy in copies:
                copy.wait()
            flag_ref[...] = jnp.where(
                wanted[place.field, 1] == STEPS, jnp.ones(flag_ref.shape, F32), 0.0
            )
            earlier = wanted[place.field, 0] == number - 1

            @pl.when(earlier)
            def _():
                for b in range(count_b):
                    even_ref[b] = even_rows(previous_ref, 0, 0, count_a, b)

            @pl.when(jnp.logical_not(earlier))
            def _():
                for b in range(count_b):
                    even_ref[b] = even_rows(padded, WIDTH, SIDE, count_a, b)

            for kind, part in enumerate(packed(even_ref, own_matrix)):
                own_out[kind] = part
            send_into(even_ref, sent_matrix, sent_out)

    full = shape(count_x, count_y, count_z)
    slab, side = shape(2 * WIDTH, count_y, count_z), shape(count_x, SIDE, count_z)
    even = shape(count_b, count_a, count_z)
    outs = [full, slab, side]
    if first:
        outs += [full, slab, side]
    if not last:
        outs.append(full)
    if snapshot:
        size = GROUP * count_z
        outs += [
            shape(4, count_b // GROUP * count_a, count_z),
            sent_shape(count_a, count_b, count_z),
            shape(size, size, dtype=BF16),
            shape(size, size, dtype=BF16),
            shape(8, count_z),
        ]
    if last:
        outs.append(even)
    place_of = spec(pltpu.HBM) if first else spec(pltpu.VMEM)
    operands, specs = [points, waves, current], [spec(pltpu.VMEM)] * 2 + [place_of]
    if not first:
        operands += list(faces)
        specs += [spec(pltpu.VMEM)] * 3
    operands += [previous, courant]
    specs += [place_of] * 2
    scratch = [
        pltpu.VMEM((count_x + 2 * WIDTH, count_y + 2 * SIDE, count_z), F32),
        pltpu.VMEM(full.shape, F32),
        pltpu.VMEM(full.shape, F32),
    ]
    if first:
        scratch += [pltpu.VMEM(full.shape, F32), pltpu.SemaphoreType.DMA((3,))]
    if snapshot:
        operands += [snapshots, matrices]
        specs += [spec(pltpu.HBM)] * 2
        scratch += [
            pltpu.VMEM(even.shape, F32),
            pltpu.SMEM(snapshots.shape, jnp.int32),
            pltpu.SemaphoreType.DMA((3,)),
        ]
    return pl.pallas_call(
        kernel,
        out_shape=tuple(outs),
        in_specs=specs,
        out_specs=(spec(pltpu.VMEM),) * len(outs),
        scratch_shapes=scratch,
        compiler_params=params(20),
        cost_estimate=cost(count_x * count_y * count_z, 60, 6),
    )(*operands)


def low_terms(halo_ref, r):
    total = None
    for k in range(r + 1, WIDTH + 1):
        term = WEIGHTS[k - 1] * halo_ref[WIDTH + r - k]
        total = term if total is None else total + term
    return total


def high_terms(halo_ref, r):
    total = None
    for k in range(WIDTH - r, WIDTH + 1):
        term = WEIGHTS[k - 1] * halo_ref[r + k - WIDTH]
        total = term if total is None else total + term
    return total


def add_halo(place, parts, halos, outs):
    qx_ref, qy_ref, cx_ref, cy_ref = parts
    far_in, near_in, side_in = halos
    far_out, near_out, side_out = outs
    count_y, count_x = qx_ref.shape[1], qy_ref.shape[0]
    block = place.block(count_y)

    def along_x(low_in, high_in, low_out, high_out):
        for r in range(WIDTH):
            low_out[r] = qx_ref[r] + cx_ref[r] * low_terms(low_in, r)
            high_out[r] = qx_ref[WIDTH + r] + cx_ref[WIDTH + r] * high_terms(high_in, r)
        side_out[pl.ds(0, WIDTH)] = low_out[:, pl.ds(block, SIDE)]
        side_out[pl.ds(count_x - WIDTH, WIDTH)] = high_out[:, pl.ds(block, SIDE)]

    inner = pl.ds(WIDTH, count_x - 2 * WIDTH)
    side_out[inner] = qy_ref[inner]

    @pl.when(place.even)
    def _():
        along_x(far_in, near_in, far_out, near_out)

    @pl.when(jnp.logical_not(place.even))
    def _():
        along_x(near_in, far_in, near_out, far_out)

    def along_y(shifts, masks):
        halo = side_in[...]
        lanes = halo.shape[2]
        line = lax.broadcasted_iota(jnp.int32, (1, SIDE, lanes), 1)
        total = None
        for k in range(1, WIDTH + 1):
            weight = jnp.where(masks(line, k), WEIGHTS[k - 1], 0.0)
            term = weight * pltpu.roll(halo, shifts(k), 1)
            total = term if total is None else total + term
        side_out[...] = side_out[...] + cy_ref[...] * total

    @pl.when(place.y == 0)
    def _():
        along_y(lambda k: SIDE - k, lambda line, k: line >= SIDE - k)

    @pl.when(place.y != 0)
    def _():
        along_y(lambda k: k, lambda line, k: line < k)

    def corners(low_out, high_out):
        low_out[:, pl.ds(block, SIDE)] = side_out[pl.ds(0, WIDTH)]
        high_out[:, pl.ds(block, SIDE)] = side_out[pl.ds(count_x - WIDTH, WIDTH)]

    @pl.when(place.even)
    def _():
        corners(far_out, near_out)

    @pl.when(jnp.logical_not(place.even))
    def _():
        corners(near_out, far_out)


def halo_step(parts, halos):
    count_y, (count_x, _, count_z) = parts[0].shape[1], parts[1].shape

    def kernel(*refs):
        add_halo(Place(), refs[:4], refs[4:7], refs[7:])

    return pl.pallas_call(
        kernel,
        out_shape=face_shapes(count_x, count_y, count_z),
        in_specs=[spec(pltpu.VMEM)] * 7,
        out_specs=(spec(pltpu.VMEM),) * 3,
        compiler_params=params(8),
        cost_estimate=cost(16 * count_y * count_z, 10, 6),
        name="halo_step",
    )(*parts, *halos)


def pack_matrix(window, count_z):
    half = count_z // GROUP
    size = GROUP * count_z
    row, column = np.arange(size)[:, None], np.arange(size)[None, :]
    row_b, row_z = row // count_z, row % count_z
    kind = column // count_z
    parity = kind % 2
    lane_b, lane_i = (column % count_z) // half, column % half
    main = (row_b == lane_b) & (row_z == 2 * (half * window + lane_i) + parity)
    wanted_b = (lane_b + (GROUP - 1 if window == 0 else 1)) % GROUP
    wanted_z = 2 * (half * (1 - window) + lane_i) + parity
    useful = lane_i < REACH if window == 0 else lane_i >= half - REACH
    edge = (row_b == wanted_b) & (row_z == wanted_z) & useful
    return np.where(kind < 2, main, edge).astype(np.float32)


def packed(even_ref, matrix_ref):
    count_b, _, count_z = even_ref.shape
    rows = [
        jnp.concatenate([even_ref[b + i] for i in range(GROUP)], axis=1)
        for b in range(0, count_b, GROUP)
    ]
    result = exact_dot(jnp.concatenate(rows, axis=0), matrix_ref[...])
    return [result[:, kind * count_z : (kind + 1) * count_z] for kind in range(4)]


def pack_own(even, matrix):
    count_b, count_a, count_z = even.shape
    total_rows = count_b // GROUP * count_a

    def kernel(even_ref, matrix_ref, out_ref):
        for kind, part in enumerate(packed(even_ref, matrix_ref)):
            out_ref[kind] = part

    return pl.pallas_call(
        kernel,
        out_shape=shape(4, total_rows, count_z),
        in_specs=[spec(pltpu.VMEM)] * 2,
        out_specs=spec(pltpu.VMEM),
        compiler_params=params(8),
        cost_estimate=cost(count_b * count_a * count_z, 1024, 4),
        name="pack_own",
    )(even, matrix)


def edge_slots(count_a, groups, count_z):
    fits = count_z // GROUP // REACH
    slots = []
    for index in range(2 * groups):
        slots.append((index // groups, index % groups, index // fits * count_a, index % fits * REACH))
    return slots, -(-2 * groups // fits) * count_a


def send_into(even_ref, matrix_ref, out_ref):
    count_b, count_a, count_z = even_ref.shape
    groups = count_b // GROUP
    total_rows = groups * count_a
    parts = packed(even_ref, matrix_ref)
    out_ref[pl.ds(0, total_rows), :] = parts[0]
    out_ref[pl.ds(total_rows, total_rows), :] = parts[1]
    slots, _ = edge_slots(count_a, groups, count_z)
    sums = {}
    for parity, g, row, shift in slots:
        part = parts[2 + parity][g * count_a : (g + 1) * count_a]
        part = pltpu.roll(part, shift, 1) if shift else part
        sums[row] = sums[row] + part if row in sums else part
    for row, part in sums.items():
        out_ref[pl.ds(2 * total_rows + row, count_a), :] = part


def sent_shape(count_a, count_b, count_z):
    groups = count_b // GROUP
    _, extra = edge_slots(count_a, groups, count_z)
    return shape(2 * groups * count_a + extra, count_z)


def last_step(flag, even_before, current, parts, halos, matrix):
    count_x, count_y, count_z = current.shape
    count_a, count_b = count_x // 2, count_y // 2

    def kernel(
        flag_ref, even_ref, current_ref, qx_ref, qy_ref, cx_ref, cy_ref, far_ref, near_ref,
        side_ref, matrix_ref, final_ref, late_ref, sent_ref, far_out, near_out, side_out,
    ):
        place = Place()
        add_halo(
            place, (qx_ref, qy_ref, cx_ref, cy_ref), (far_ref, near_ref, side_ref),
            (far_out, near_out, side_out),
        )
        low, high = pl.ds(0, WIDTH), pl.ds(count_x - WIDTH, WIDTH)

        @pl.when(place.even)
        def _():
            final_ref[high] = near_out[...]
            final_ref[low] = far_out[...]

        @pl.when(jnp.logical_not(place.even))
        def _():
            final_ref[low] = near_out[...]
            final_ref[high] = far_out[...]

        final_ref[:, pl.ds(place.block(count_y), SIDE)] = side_out[...]
        wants_last = jnp.broadcast_to(flag_ref[0:1, :], (count_a, count_z)) > 0.5
        for b in range(count_b):
            late_ref[b] = jnp.where(
                wants_last, even_rows(final_ref, 0, 0, count_a, b), even_ref[b]
            )
        send_into(late_ref, matrix_ref, sent_ref)

    slab, _, side = face_shapes(count_x, count_y, count_z)
    return pl.pallas_call(
        kernel,
        out_shape=(
            shape(*current.shape),
            shape(count_b, count_a, count_z),
            sent_shape(count_a, count_b, count_z),
        ),
        in_specs=[spec(pltpu.VMEM)] * 11,
        out_specs=(spec(pltpu.VMEM),) * 3,
        scratch_shapes=[
            pltpu.VMEM(slab.shape, F32),
            pltpu.VMEM(slab.shape, F32),
            pltpu.VMEM(side.shape, F32),
        ],
        input_output_aliases={2: 0},
        compiler_params=params(12),
        cost_estimate=cost(count_x * count_y * count_z, 10, 3),
        name="last_step",
    )(flag, even_before, current, *parts, *halos, matrix)


def write_out(level):
    def kernel(level_ref, out_ref, sem):
        copy = pltpu.make_async_copy(level_ref, out_ref, sem)
        copy.start()
        copy.wait()

    return pl.pallas_call(
        kernel,
        out_shape=shape(*level.shape),
        in_specs=[spec(pltpu.VMEM)],
        out_specs=spec(pltpu.HBM),
        scratch_shapes=[pltpu.SemaphoreType.DMA],
        compiler_params=params(4),
        cost_estimate=cost(level.size, 0, 2),
        name="write_out",
    )(level)


def lag_image(lags, own, other, before, count_a):
    _, total_rows, count_z = own.shape
    groups = total_rows // count_a
    count_h = lags.shape[0]
    half = count_z // GROUP
    last = before is not None

    def kernel(*refs):
        refs = list(refs)
        take = lambda count: [refs.pop(0) for _ in range(count)]
        lags_ref, own_ref, other_ref = take(3)
        if last:
            (before_ref,) = take(1)
        (out_ref,) = take(1)
        edges, lag_of, sems = take(3)
        if last:
            (store,) = take(1)
        else:
            store = out_ref
        place = Place()
        copy = pltpu.make_async_copy(lags_ref, lag_of, sems.at[0])
        copy.start()
        is_source = place.field == 0
        lane = lax.broadcasted_iota(jnp.int32, (count_a, count_z), 1) % half
        useful = jnp.where(is_source, lane, half - 1 - lane) < REACH
        slots, _ = edge_slots(count_a, groups, count_z)
        for parity, g, row, shift in slots:
            part = other_ref[pl.ds(2 * total_rows + row, count_a), :]
            part = pltpu.roll(part, count_z - shift, 1) if shift else part
            edges[parity, pl.ds(g * count_a, count_a), :] = jnp.where(useful, part, 0.0)
        copy.wait()
        lane = lax.broadcasted_iota(jnp.int32, (1, count_z), 1) % half

        def moved(main, edge, shift):
            mask = (lane < shift) | (lane >= half + shift)
            return pltpu.roll(jnp.where(mask, edge, main), (count_z - shift) & (count_z - 1), 1)

        def one(h, _):
            lag = lag_of[h]
            parity = lag & 1
            source_shift = -((lag + parity) >> 1)
            receiver_shift = (lag - parity) >> 1
            own_shift = jnp.where(is_source, source_shift, receiver_shift)
            other_shift = jnp.where(is_source, receiver_shift, source_shift)
            other_rows = pl.ds(pl.multiple_of(parity * total_rows, 8), total_rows)
            product = moved(own_ref[parity], own_ref[2 + parity], own_shift)
            product = product * moved(other_ref[other_rows, :], edges[parity], other_shift)
            for g in range(groups):
                part = product[g * count_a : (g + 1) * count_a]
                lanes = pl.ds(g * count_z, count_z)
                if last:
                    part = part + before_ref[h, :, lanes]
                store[h, :, lanes] = part
            if last:
                pltpu.make_async_copy(store.at[h], out_ref.at[h], sems.at[1]).start()
            return 0

        lax.fori_loop(0, count_h, one, 0, unroll=True)
        if last:
            pltpu.make_async_copy(store, out_ref, sems.at[1]).wait()

    out = (count_h, count_a, groups * count_z)
    operands = [lags, own, other] + ([before] if last else [])
    return pl.pallas_call(
        kernel,
        out_shape=shape(*out),
        in_specs=[spec(pltpu.HBM)] + [spec(pltpu.VMEM)] * (len(operands) - 1),
        out_specs=spec(pltpu.HBM if last else pltpu.VMEM),
        scratch_shapes=[
            pltpu.VMEM((2, total_rows, count_z), F32),
            pltpu.SMEM((count_h,), jnp.int32),
            pltpu.SemaphoreType.DMA((2,)),
        ]
        + ([pltpu.VMEM(out, F32)] if last else []),
        compiler_params=params(12),
        cost_estimate=cost(count_h * total_rows * count_z, 10, 2),
        name="lag_image",
    )(*operands)


def body(
    field_now,
    field_prev,
    courant_squared,
    source_cells,
    source_wave,
    receiver_cells,
    receiver_wave,
    snapshot_steps,
    lag_offsets,
):
    count_x, _, count_z = field_now.shape
    loop_size = lax.axis_size("gx")
    half_size = loop_size // 2
    turn = loop_size // 4
    assert lax.axis_size("gy") == 2 and half_size % 2 == 0

    field = ((lax.axis_index("gx") - turn + loop_size) % loop_size) // half_size
    slabs = [(i - turn) % loop_size % half_size for i in range(loop_size)]

    def pairs(odd):
        found = []
        for i, slab in enumerate(slabs):
            if slab % 2 == odd and slab != half_size - 1:
                j = (i + 1) % loop_size
                found += [(i, j), (j, i)]
        return found

    near_pairs, far_pairs = pairs(0), pairs(1)
    across = [(i, (i + half_size) % loop_size) for i in range(loop_size)]

    def send_far(far):
        return lax.ppermute(far, "gx", far_pairs)

    def send_near(near, side):
        near = lax.ppermute(near, "gx", near_pairs)
        return near, lax.ppermute(side, "gy", [(0, 1), (1, 0)])

    def exchange(faces):
        far, near, side = faces
        return (send_far(far), *send_near(near, side))

    most = -(-max(source_cells.shape[1], receiver_cells.shape[1]) // 128) * 128

    def chosen(source, receiver, empty):
        source, receiver = (
            jnp.pad(array, ((0, 0), (0, most - array.shape[1])), constant_values=empty)
            for array in (source, receiver)
        )
        return jnp.where(field == 0, source, receiver)

    points = chosen(source_cells, receiver_cells, -1)
    waves = chosen(source_wave, receiver_wave, 0.0)
    matrices = jnp.asarray(
        np.stack([pack_matrix(window, count_z) for window in (0, 1)]), dtype=BF16
    )
    field_now, field_prev, courant_squared, matrices = (
        pltpu.with_memory_space_constraint(array, pltpu.HBM)
        for array in (field_now, field_prev, courant_squared, matrices)
    )
    far = send_far(first_far(field_now))
    faces = first_near(field_now)
    halos = (far, *send_near(*faces))
    next1, qx, qy, courant, cx, cy, whole0 = inner_step(
        0, points, waves, field_now, None, field_prev, courant_squared
    )
    faces = halo_step((qx, qy, cx, cy), halos)
    halos = exchange(faces)
    next2, qx, qy, whole1 = inner_step(1, points, waves, next1, faces, whole0, courant)
    faces = halo_step((qx, qy, cx, cy), halos)
    halos = exchange(faces)
    next3, qx, qy, whole2, own_early, sent_early, own_matrix, sent_matrix, flag = inner_step(
        2, points, waves, next2, faces, whole1, courant, snapshot_steps, matrices
    )
    faces = halo_step((qx, qy, cx, cy), halos)
    halos = exchange(faces)
    other_early = lax.ppermute(sent_early, "gx", across)
    next4, qx, qy, even3 = inner_step(3, points, waves, next3, faces, whole2, courant)
    final, late, sent_late = last_step(
        flag, even3, next4, (qx, qy, cx, cy), halos, sent_matrix
    )
    other_late = lax.ppermute(sent_late, "gx", across)
    partial = lag_image(lag_offsets, own_early, other_early, None, count_x // 2)
    own_late = pack_own(late, own_matrix)
    image = lag_image(lag_offsets, own_late, other_late, partial, count_x // 2)
    return write_out(final), jnp.transpose(image, (1, 0, 2))


def solution(mesh):
    placed = (
        P(("shots", "gx"), "gy", None),
        P(("shots", "gx"), "gy", None),
        P("gx", "gy", None),
        P(None, "shots"),
        P(None, "shots"),
        P(None, "shots"),
        P(None, "shots"),
        P("shots", None),
        P(),
    )
    return jax.shard_map(
        body,
        mesh=mesh,
        in_specs=placed,
        out_specs=(P(("shots", "gx"), "gy", None), P(("shots", "gx"), None, "gy")),
        check_vma=False,
    )
```

```python
import jax
import jax.numpy as jnp
import numpy as np
from jax import lax
from jax.experimental import pallas as pl
from jax.experimental.pallas import tpu as pltpu
from jax.sharding import PartitionSpec as P

STEPS = 4
WIDTH = 4
LAGMAX = 8
REACH = LAGMAX // 2
GROUP = 4
SIDE = 8

SCALE = 5040.0
BAND = (8064.0, -1008.0, 128.0, -9.0)
CENTRE = 3.0 * (-205.0 / 72.0)
WEIGHTS = (1.6, -0.2, 8.0 / 315.0, -1.0 / 560.0)

F32 = jnp.float32
BF16 = jnp.bfloat16


def shape(*dims, dtype=F32):
    return jax.ShapeDtypeStruct(dims, dtype)


def params(megabytes):
    return pltpu.CompilerParams(vmem_limit_bytes=megabytes << 20)


def spec(space):
    return pl.BlockSpec(memory_space=space)


def cost(count, flops_each, arrays):
    return pl.CostEstimate(
        flops=int(count * flops_each), bytes_accessed=int(4 * count * arrays), transcendentals=0
    )


def split3(values):
    high = values.astype(BF16)
    rest = values - high.astype(F32)
    middle = rest.astype(BF16)
    low = (rest - middle.astype(F32)).astype(BF16)
    return high, middle, low


def exact_dot(values, matrix):
    parts = [jnp.dot(part, matrix, preferred_element_type=F32) for part in split3(values)]
    return (parts[2] + parts[1]) + parts[0]


class Place:
    def __init__(self):
        loop_size = lax.axis_size("gx")
        self.half = loop_size // 2
        relative = lax.rem(lax.axis_index("gx") + loop_size - loop_size // 4, loop_size)
        self.field = relative // self.half
        self.slab = lax.rem(relative, self.half)
        self.even = lax.rem(self.slab, 2) == 0
        self.y = lax.axis_index("gy")

    def block(self, count_y):
        return pl.multiple_of((1 - self.y) * (count_y - SIDE), SIDE)


def first_faces(field):
    count_x, count_y, count_z = field.shape
    top = count_x - WIDTH

    def kernel(field_ref, far_ref, near_ref, side_ref, whole_ref, sems):
        place = Place()
        far = jnp.where(place.even, 0, top)
        sources = [
            field_ref.at[pl.ds(far, WIDTH)],
            field_ref.at[pl.ds(top - far, WIDTH)],
            field_ref.at[:, pl.ds(place.block(count_y), SIDE)],
            field_ref,
        ]
        copies = [
            pltpu.make_async_copy(source, target, sems.at[index])
            for index, (source, target) in enumerate(
                zip(sources, (far_ref, near_ref, side_ref, whole_ref))
            )
        ]
        for copy in copies:
            copy.start()
        for copy in copies:
            copy.wait()

    return pl.pallas_call(
        kernel,
        out_shape=(*face_shapes(count_x, count_y, count_z), shape(*field.shape)),
        in_specs=[spec(pltpu.HBM)],
        out_specs=(spec(pltpu.VMEM),) * 4,
        scratch_shapes=[pltpu.SemaphoreType.DMA((4,))],
        compiler_params=params(8),
        name="first_faces",
    )(field)


def face_shapes(count_x, count_y, count_z):
    slab = shape(WIDTH, count_y, count_z)
    return slab, slab, shape(count_x, SIDE, count_z)


def even_rows(level_ref, offset_x, offset_y, count_a, b):
    rows, stride, lanes = level_ref.shape
    flat = level_ref.reshape(rows * stride, lanes)
    start = offset_x * stride + offset_y + 2 * b
    return flat[pl.ds(start, count_a, stride=2 * stride), :]


def inner_step(number, points, waves, current, faces, previous, courant, snapshots=None, matrices=None):
    count_x, count_y, count_z = current.shape
    count_a, count_b = count_x // 2, count_y // 2
    first = faces is None
    last = number == STEPS - 1
    snapshot = number == STEPS // 2
    if first:
        count_j = -(-max(array.shape[1] for array in points) // 128) * 128
    else:
        count_j = points.shape[1]

    def kernel(*refs):
        refs = list(refs)
        take = lambda count: [refs.pop(0) for _ in range(count)]
        if first:
            raw_refs = take(4)
        else:
            points_ref, waves_ref = take(2)
        (current_ref,) = take(1)
        if not first:
            far_ref, near_ref, side_ref = take(3)
        previous_ref, courant_ref = take(2)
        if snapshot:
            steps_ref, matrices_ref = take(2)
        next_ref, qx_ref, qy_ref = take(3)
        if first:
            kept_ref, cx_ref, cy_ref, points_ref, waves_ref = take(5)
        elif not last:
            (whole_ref,) = take(1)
        if snapshot:
            own_out, sent_out, own_matrix, sent_matrix, flag_ref = take(5)
        if last:
            (even_ref,) = take(1)
        padded, zpart, addpart = take(3)
        if first:
            before_ref = take(1)[0]
            raw_refs_in, raw_refs = raw_refs, take(4)
            (sems,) = take(1)
        if snapshot:
            even_ref, wanted, sems = take(3)

        place = Place()
        block = place.block(count_y)
        rows, columns = pl.ds(WIDTH, count_x), pl.ds(SIDE, count_y)
        if first:
            copies = [
                pltpu.make_async_copy(source, target, sems.at[index])
                for index, (source, target) in enumerate(
                    zip(
                        (*raw_refs_in, previous_ref, courant_ref),
                        (*raw_refs, before_ref, kept_ref),
                    )
                )
            ]
            for copy in copies:
                copy.start()
        else:
            before_ref, kept_ref = previous_ref, courant_ref
        if snapshot:
            copies = [
                pltpu.make_async_copy(steps_ref, wanted, sems.at[0]),
                pltpu.make_async_copy(matrices_ref.at[place.field], own_matrix, sems.at[1]),
                pltpu.make_async_copy(matrices_ref.at[1 - place.field], sent_matrix, sems.at[2]),
            ]
            for copy in copies:
                copy.start()

        zero_x = jnp.zeros((WIDTH, count_y + 2 * SIDE, count_z), F32)
        padded[pl.ds(0, WIDTH)] = zero_x
        padded[pl.ds(count_x + WIDTH, WIDTH)] = zero_x
        zero_y = jnp.zeros((count_x, SIDE, count_z), F32)
        padded[rows, pl.ds(0, SIDE)] = zero_y
        padded[rows, pl.ds(count_y + SIDE, SIDE)] = zero_y

        padded[rows, columns] = current_ref[...]
        if not first:
            low, high = pl.ds(WIDTH, WIDTH), pl.ds(count_x, WIDTH)

            @pl.when(place.even)
            def _():
                padded[high, columns] = near_ref[...]
                padded[low, columns] = far_ref[...]

            @pl.when(jnp.logical_not(place.even))
            def _():
                padded[low, columns] = near_ref[...]
                padded[high, columns] = far_ref[...]

            padded[rows, pl.ds(pl.multiple_of(block + SIDE, SIDE), SIDE)] = side_ref[...]

        if first:
            for copy in copies[:4]:
                copy.wait()
            points_ref[...] = jnp.full(points_ref.shape, -1, jnp.int32)
            waves_ref[...] = jnp.zeros(waves_ref.shape, F32)

            def choose(cells_ref, wave_ref):
                count = cells_ref.shape[1]
                points_ref[pl.ds(0, 3), pl.ds(0, count)] = cells_ref[...]
                waves_ref[pl.ds(0, STEPS), pl.ds(0, count)] = wave_ref[...]

            @pl.when(place.field == 0)
            def _():
                choose(raw_refs[0], raw_refs[1])

            @pl.when(place.field != 0)
            def _():
                choose(raw_refs[2], raw_refs[3])

        px = points_ref[0:1, :] - place.slab * count_x
        py = points_ref[1:2, :] - place.y * count_y
        inside = (px >= 0) & (px < count_x) & (py >= 0) & (py < count_y)
        home = jnp.where(inside, px * count_y + py, -1)
        amounts = waves_ref[number : number + 1, :]
        spread = jnp.where(
            lax.broadcasted_iota(jnp.int32, (count_z, count_j), 0) == points_ref[2:3, :],
            amounts,
            0.0,
        )
        spread = split3(spread)

        gap = jnp.abs(
            lax.broadcasted_iota(jnp.int32, (count_z, count_z), 0)
            - lax.broadcasted_iota(jnp.int32, (count_z, count_z), 1)
        )
        band = jnp.zeros((count_z, count_z), F32)
        for offset, weight in enumerate(BAND, 1):
            band = jnp.where(gap == offset, weight, band)
        band = band.astype(BF16)

        chunk = 8

        def multiply(index, _):
            start = pl.multiple_of(index * chunk, chunk)
            values = padded[pl.ds(start + WIDTH, chunk), columns]
            zpart[pl.ds(start, chunk)] = exact_dot(
                values.reshape(chunk * count_y, count_z), band
            ).reshape(chunk, count_y, count_z)
            here = start * count_y + lax.broadcasted_iota(
                jnp.int32, (chunk * count_y, count_j), 0
            )
            hit = jnp.where(here == home, 1.0, 0.0).astype(BF16)
            added = [
                lax.dot_general(hit, part, (((1,), (1,)), ((), ())), preferred_element_type=F32)
                for part in spread
            ]
            added = (added[2] + added[1]) + added[0]
            addpart[pl.ds(start, chunk)] = added.reshape(chunk, count_y, count_z)
            return 0

        lax.fori_loop(0, count_x // chunk, multiply, 0)
        if first:
            for copy in copies[4:]:
                copy.wait()

        def row(x, _):
            middle = padded[x + WIDTH, columns]
            total = CENTRE * middle + (1.0 / SCALE) * zpart[x]
            for offset, weight in enumerate(WEIGHTS, 1):
                paired = padded[x + WIDTH + offset, columns] + padded[x + WIDTH - offset, columns]
                paired = paired + (
                    padded[x + WIDTH, pl.ds(SIDE + offset, count_y)]
                    + padded[x + WIDTH, pl.ds(SIDE - offset, count_y)]
                )
                total = total + weight * paired
            if not first and not last:
                whole_ref[x] = middle
            next_ref[x] = (2.0 * middle - before_ref[x] + kept_ref[x] * total) + addpart[x]
            return 0

        lax.fori_loop(0, count_x, row, 0, unroll=4)

        qx_ref[pl.ds(0, WIDTH)] = next_ref[pl.ds(0, WIDTH)]
        qx_ref[pl.ds(WIDTH, WIDTH)] = next_ref[pl.ds(count_x - WIDTH, WIDTH)]
        qy_ref[...] = next_ref[:, pl.ds(block, SIDE)]
        if first:
            cx_ref[pl.ds(0, WIDTH)] = kept_ref[pl.ds(0, WIDTH)]
            cx_ref[pl.ds(WIDTH, WIDTH)] = kept_ref[pl.ds(count_x - WIDTH, WIDTH)]
            cy_ref[...] = kept_ref[:, pl.ds(block, SIDE)]
        if last:
            for b in range(count_b):
                even_ref[b] = even_rows(padded, WIDTH, SIDE, count_a, b)
        if snapshot:
            for copy in copies:
                copy.wait()
            flag_ref[...] = jnp.where(
                wanted[place.field, 1] == STEPS, jnp.ones(flag_ref.shape, F32), 0.0
            )
            earlier = wanted[place.field, 0] == number - 1

            @pl.when(earlier)
            def _():
                for b in range(count_b):
                    even_ref[b] = even_rows(previous_ref, 0, 0, count_a, b)

            @pl.when(jnp.logical_not(earlier))
            def _():
                for b in range(count_b):
                    even_ref[b] = even_rows(padded, WIDTH, SIDE, count_a, b)

            for kind, part in enumerate(packed(even_ref, own_matrix)):
                own_out[kind] = part
            send_into(even_ref, sent_matrix, sent_out)

    full = shape(count_x, count_y, count_z)
    slab, side = shape(2 * WIDTH, count_y, count_z), shape(count_x, SIDE, count_z)
    even = shape(count_b, count_a, count_z)
    outs = [full, slab, side]
    if first:
        outs += [full, slab, side, shape(8, count_j, dtype=jnp.int32), shape(8, count_j)]
    elif not last:
        outs.append(full)
    if snapshot:
        size = GROUP * count_z
        outs += [
            shape(4, count_b // GROUP * count_a, count_z),
            sent_shape(count_a, count_b, count_z),
            shape(size, size, dtype=BF16),
            shape(size, size, dtype=BF16),
            shape(8, count_z),
        ]
    if last:
        outs.append(even)
    place_of = spec(pltpu.HBM) if first else spec(pltpu.VMEM)
    operands = [*points, current] if first else [points, waves, current]
    specs = [place_of] * (len(operands) - 1) + [spec(pltpu.VMEM)]
    if not first:
        operands += list(faces)
        specs += [spec(pltpu.VMEM)] * 3
    operands += [previous, courant]
    specs += [place_of] * 2
    scratch = [
        pltpu.VMEM((count_x + 2 * WIDTH, count_y + 2 * SIDE, count_z), F32),
        pltpu.VMEM(full.shape, F32),
        pltpu.VMEM(full.shape, F32),
    ]
    if first:
        scratch.append(pltpu.VMEM(full.shape, F32))
        scratch += [pltpu.VMEM(array.shape, array.dtype) for array in points]
        scratch.append(pltpu.SemaphoreType.DMA((6,)))
    if snapshot:
        operands += [snapshots, matrices]
        specs += [spec(pltpu.HBM)] * 2
        scratch += [
            pltpu.VMEM(even.shape, F32),
            pltpu.SMEM(snapshots.shape, jnp.int32),
            pltpu.SemaphoreType.DMA((3,)),
        ]
    return pl.pallas_call(
        kernel,
        out_shape=tuple(outs),
        in_specs=specs,
        out_specs=(spec(pltpu.VMEM),) * len(outs),
        scratch_shapes=scratch,
        compiler_params=params(20),
        cost_estimate=cost(count_x * count_y * count_z, 60, 6),
    )(*operands)


def low_terms(halo_ref, r):
    total = None
    for k in range(r + 1, WIDTH + 1):
        term = WEIGHTS[k - 1] * halo_ref[WIDTH + r - k]
        total = term if total is None else total + term
    return total


def high_terms(halo_ref, r):
    total = None
    for k in range(WIDTH - r, WIDTH + 1):
        term = WEIGHTS[k - 1] * halo_ref[r + k - WIDTH]
        total = term if total is None else total + term
    return total


def add_halo(place, parts, halos, outs):
    qx_ref, qy_ref, cx_ref, cy_ref = parts
    far_in, near_in, side_in = halos
    far_out, near_out, side_out = outs
    count_y, count_x = qx_ref.shape[1], qy_ref.shape[0]
    block = place.block(count_y)

    def along_x(low_in, high_in, low_out, high_out):
        for r in range(WIDTH):
            low_out[r] = qx_ref[r] + cx_ref[r] * low_terms(low_in, r)
            high_out[r] = qx_ref[WIDTH + r] + cx_ref[WIDTH + r] * high_terms(high_in, r)
        side_out[pl.ds(0, WIDTH)] = low_out[:, pl.ds(block, SIDE)]
        side_out[pl.ds(count_x - WIDTH, WIDTH)] = high_out[:, pl.ds(block, SIDE)]

    inner = pl.ds(WIDTH, count_x - 2 * WIDTH)
    side_out[inner] = qy_ref[inner]

    @pl.when(place.even)
    def _():
        along_x(far_in, near_in, far_out, near_out)

    @pl.when(jnp.logical_not(place.even))
    def _():
        along_x(near_in, far_in, near_out, far_out)

    def along_y(shifts, masks):
        halo = side_in[...]
        lanes = halo.shape[2]
        line = lax.broadcasted_iota(jnp.int32, (1, SIDE, lanes), 1)
        total = None
        for k in range(1, WIDTH + 1):
            weight = jnp.where(masks(line, k), WEIGHTS[k - 1], 0.0)
            term = weight * pltpu.roll(halo, shifts(k), 1)
            total = term if total is None else total + term
        side_out[...] = side_out[...] + cy_ref[...] * total

    @pl.when(place.y == 0)
    def _():
        along_y(lambda k: SIDE - k, lambda line, k: line >= SIDE - k)

    @pl.when(place.y != 0)
    def _():
        along_y(lambda k: k, lambda line, k: line < k)

    def corners(low_out, high_out):
        low_out[:, pl.ds(block, SIDE)] = side_out[pl.ds(0, WIDTH)]
        high_out[:, pl.ds(block, SIDE)] = side_out[pl.ds(count_x - WIDTH, WIDTH)]

    @pl.when(place.even)
    def _():
        corners(far_out, near_out)

    @pl.when(jnp.logical_not(place.even))
    def _():
        corners(near_out, far_out)


def halo_step(parts, halos):
    count_y, (count_x, _, count_z) = parts[0].shape[1], parts[1].shape

    def kernel(*refs):
        add_halo(Place(), refs[:4], refs[4:7], refs[7:])

    return pl.pallas_call(
        kernel,
        out_shape=face_shapes(count_x, count_y, count_z),
        in_specs=[spec(pltpu.VMEM)] * 7,
        out_specs=(spec(pltpu.VMEM),) * 3,
        compiler_params=params(8),
        cost_estimate=cost(16 * count_y * count_z, 10, 6),
        name="halo_step",
    )(*parts, *halos)


def pack_matrix(window, count_z):
    half = count_z // GROUP
    size = GROUP * count_z
    row, column = np.arange(size)[:, None], np.arange(size)[None, :]
    row_b, row_z = row // count_z, row % count_z
    kind = column // count_z
    parity = kind % 2
    lane_b, lane_i = (column % count_z) // half, column % half
    main = (row_b == lane_b) & (row_z == 2 * (half * window + lane_i) + parity)
    wanted_b = (lane_b + (GROUP - 1 if window == 0 else 1)) % GROUP
    wanted_z = 2 * (half * (1 - window) + lane_i) + parity
    useful = lane_i < REACH if window == 0 else lane_i >= half - REACH
    edge = (row_b == wanted_b) & (row_z == wanted_z) & useful
    return np.where(kind < 2, main, edge).astype(np.float32)


def packed(even_ref, matrix_ref):
    count_b, _, count_z = even_ref.shape
    rows = [
        jnp.concatenate([even_ref[b + i] for i in range(GROUP)], axis=1)
        for b in range(0, count_b, GROUP)
    ]
    result = exact_dot(jnp.concatenate(rows, axis=0), matrix_ref[...])
    return [result[:, kind * count_z : (kind + 1) * count_z] for kind in range(4)]


def pack_own(even, matrix):
    count_b, count_a, count_z = even.shape
    total_rows = count_b // GROUP * count_a

    def kernel(even_ref, matrix_ref, out_ref):
        for kind, part in enumerate(packed(even_ref, matrix_ref)):
            out_ref[kind] = part

    return pl.pallas_call(
        kernel,
        out_shape=shape(4, total_rows, count_z),
        in_specs=[spec(pltpu.VMEM)] * 2,
        out_specs=spec(pltpu.VMEM),
        compiler_params=params(8),
        cost_estimate=cost(count_b * count_a * count_z, 1024, 4),
        name="pack_own",
    )(even, matrix)


def edge_slots(count_a, groups, count_z):
    fits = count_z // GROUP // REACH
    slots = []
    for index in range(2 * groups):
        slots.append((index // groups, index % groups, index // fits * count_a, index % fits * REACH))
    return slots, -(-2 * groups // fits) * count_a


def send_into(even_ref, matrix_ref, out_ref):
    count_b, count_a, count_z = even_ref.shape
    groups = count_b // GROUP
    total_rows = groups * count_a
    parts = packed(even_ref, matrix_ref)
    out_ref[pl.ds(0, total_rows), :] = parts[0]
    out_ref[pl.ds(total_rows, total_rows), :] = parts[1]
    slots, _ = edge_slots(count_a, groups, count_z)
    sums = {}
    for parity, g, row, shift in slots:
        part = parts[2 + parity][g * count_a : (g + 1) * count_a]
        part = pltpu.roll(part, shift, 1) if shift else part
        sums[row] = sums[row] + part if row in sums else part
    for row, part in sums.items():
        out_ref[pl.ds(2 * total_rows + row, count_a), :] = part


def sent_shape(count_a, count_b, count_z):
    groups = count_b // GROUP
    _, extra = edge_slots(count_a, groups, count_z)
    return shape(2 * groups * count_a + extra, count_z)


def last_step(flag, even_before, current, parts, halos, matrix):
    count_x, count_y, count_z = current.shape
    count_a, count_b = count_x // 2, count_y // 2

    def kernel(
        flag_ref, even_ref, current_ref, qx_ref, qy_ref, cx_ref, cy_ref, far_ref, near_ref,
        side_ref, matrix_ref, final_ref, late_ref, sent_ref, far_out, near_out, side_out,
    ):
        place = Place()
        add_halo(
            place, (qx_ref, qy_ref, cx_ref, cy_ref), (far_ref, near_ref, side_ref),
            (far_out, near_out, side_out),
        )
        low, high = pl.ds(0, WIDTH), pl.ds(count_x - WIDTH, WIDTH)

        @pl.when(place.even)
        def _():
            final_ref[high] = near_out[...]
            final_ref[low] = far_out[...]

        @pl.when(jnp.logical_not(place.even))
        def _():
            final_ref[low] = near_out[...]
            final_ref[high] = far_out[...]

        final_ref[:, pl.ds(place.block(count_y), SIDE)] = side_out[...]
        wants_last = jnp.broadcast_to(flag_ref[0:1, :], (count_a, count_z)) > 0.5
        for b in range(count_b):
            late_ref[b] = jnp.where(
                wants_last, even_rows(final_ref, 0, 0, count_a, b), even_ref[b]
            )
        send_into(late_ref, matrix_ref, sent_ref)

    slab, _, side = face_shapes(count_x, count_y, count_z)
    return pl.pallas_call(
        kernel,
        out_shape=(
            shape(*current.shape),
            shape(count_b, count_a, count_z),
            sent_shape(count_a, count_b, count_z),
        ),
        in_specs=[spec(pltpu.VMEM)] * 11,
        out_specs=(spec(pltpu.VMEM),) * 3,
        scratch_shapes=[
            pltpu.VMEM(slab.shape, F32),
            pltpu.VMEM(slab.shape, F32),
            pltpu.VMEM(side.shape, F32),
        ],
        input_output_aliases={2: 0},
        compiler_params=params(12),
        cost_estimate=cost(count_x * count_y * count_z, 10, 3),
        name="last_step",
    )(flag, even_before, current, *parts, *halos, matrix)


def write_out(level):
    def kernel(level_ref, out_ref, sem):
        copy = pltpu.make_async_copy(level_ref, out_ref, sem)
        copy.start()
        copy.wait()

    return pl.pallas_call(
        kernel,
        out_shape=shape(*level.shape),
        in_specs=[spec(pltpu.VMEM)],
        out_specs=spec(pltpu.HBM),
        scratch_shapes=[pltpu.SemaphoreType.DMA],
        compiler_params=params(4),
        cost_estimate=cost(level.size, 0, 2),
        name="write_out",
    )(level)


def lag_image(lags, own, other, before, count_a):
    _, total_rows, count_z = own.shape
    groups = total_rows // count_a
    count_h = lags.shape[0]
    half = count_z // GROUP
    last = before is not None

    def kernel(*refs):
        refs = list(refs)
        take = lambda count: [refs.pop(0) for _ in range(count)]
        lags_ref, own_ref, other_ref = take(3)
        if last:
            (before_ref,) = take(1)
        (out_ref,) = take(1)
        edges, lag_of, sems = take(3)
        if last:
            (store,) = take(1)
        else:
            store = out_ref
        place = Place()
        copy = pltpu.make_async_copy(lags_ref, lag_of, sems.at[0])
        copy.start()
        is_source = place.field == 0
        lane = lax.broadcasted_iota(jnp.int32, (count_a, count_z), 1) % half
        useful = jnp.where(is_source, lane, half - 1 - lane) < REACH
        slots, _ = edge_slots(count_a, groups, count_z)
        for parity, g, row, shift in slots:
            part = other_ref[pl.ds(2 * total_rows + row, count_a), :]
            part = pltpu.roll(part, count_z - shift, 1) if shift else part
            edges[parity, pl.ds(g * count_a, count_a), :] = jnp.where(useful, part, 0.0)
        copy.wait()
        lane = lax.broadcasted_iota(jnp.int32, (1, count_z), 1) % half

        def moved(main, edge, shift):
            mask = (lane < shift) | (lane >= half + shift)
            return pltpu.roll(jnp.where(mask, edge, main), (count_z - shift) & (count_z - 1), 1)

        def one(h, _):
            lag = lag_of[h]
            parity = lag & 1
            source_shift = -((lag + parity) >> 1)
            receiver_shift = (lag - parity) >> 1
            own_shift = jnp.where(is_source, source_shift, receiver_shift)
            other_shift = jnp.where(is_source, receiver_shift, source_shift)
            other_rows = pl.ds(pl.multiple_of(parity * total_rows, 8), total_rows)
            product = moved(own_ref[parity], own_ref[2 + parity], own_shift)
            product = product * moved(other_ref[other_rows, :], edges[parity], other_shift)
            for g in range(groups):
                part = product[g * count_a : (g + 1) * count_a]
                lanes = pl.ds(g * count_z, count_z)
                if last:
                    part = part + before_ref[h, :, lanes]
                store[h, :, lanes] = part
            if last:
                pltpu.make_async_copy(store.at[h], out_ref.at[h], sems.at[1]).start()
            return 0

        lax.fori_loop(0, count_h, one, 0, unroll=True)
        if last:
            pltpu.make_async_copy(store, out_ref, sems.at[1]).wait()

    out = (count_h, count_a, groups * count_z)
    operands = [lags, own, other] + ([before] if last else [])
    return pl.pallas_call(
        kernel,
        out_shape=shape(*out),
        in_specs=[spec(pltpu.HBM)] + [spec(pltpu.VMEM)] * (len(operands) - 1),
        out_specs=spec(pltpu.HBM if last else pltpu.VMEM),
        scratch_shapes=[
            pltpu.VMEM((2, total_rows, count_z), F32),
            pltpu.SMEM((count_h,), jnp.int32),
            pltpu.SemaphoreType.DMA((2,)),
        ]
        + ([pltpu.VMEM(out, F32)] if last else []),
        compiler_params=params(12),
        cost_estimate=cost(count_h * total_rows * count_z, 10, 2),
        name="lag_image",
    )(*operands)


def body(
    field_now,
    field_prev,
    courant_squared,
    source_cells,
    source_wave,
    receiver_cells,
    receiver_wave,
    snapshot_steps,
    lag_offsets,
):
    count_x, _, count_z = field_now.shape
    loop_size = lax.axis_size("gx")
    half_size = loop_size // 2
    turn = loop_size // 4
    assert lax.axis_size("gy") == 2 and half_size % 2 == 0

    slabs = [(i - turn) % loop_size % half_size for i in range(loop_size)]

    def pairs(odd):
        found = []
        for i, slab in enumerate(slabs):
            if slab % 2 == odd and slab != half_size - 1:
                j = (i + 1) % loop_size
                found += [(i, j), (j, i)]
        return found

    near_pairs, far_pairs = pairs(0), pairs(1)
    across = [(i, (i + half_size) % loop_size) for i in range(loop_size)]

    def send_far(far):
        return lax.ppermute(far, "gx", far_pairs)

    def send_near(near, side):
        near = lax.ppermute(near, "gx", near_pairs)
        return near, lax.ppermute(side, "gy", [(0, 1), (1, 0)])

    def exchange(faces):
        far, near, side = faces
        return (send_far(far), *send_near(near, side))

    matrices = jnp.asarray(
        np.stack([pack_matrix(window, count_z) for window in (0, 1)]), dtype=BF16
    )
    raw = (source_cells, source_wave, receiver_cells, receiver_wave)
    field_now, field_prev, courant_squared, matrices, snapshot_steps, lag_offsets, *raw = (
        pltpu.with_memory_space_constraint(array, pltpu.HBM)
        for array in (
            field_now, field_prev, courant_squared, matrices, snapshot_steps, lag_offsets, *raw
        )
    )
    *faces, whole0 = first_faces(field_now)
    halos = exchange(faces)
    next1, qx, qy, courant, cx, cy, points, waves = inner_step(
        0, raw, None, whole0, None, field_prev, courant_squared
    )
    faces = halo_step((qx, qy, cx, cy), halos)
    halos = exchange(faces)
    next2, qx, qy, whole1 = inner_step(1, points, waves, next1, faces, whole0, courant)
    faces = halo_step((qx, qy, cx, cy), halos)
    halos = exchange(faces)
    next3, qx, qy, whole2, own_early, sent_early, own_matrix, sent_matrix, flag = inner_step(
        2, points, waves, next2, faces, whole1, courant, snapshot_steps, matrices
    )
    other_early = lax.ppermute(sent_early, "gx", across)
    faces = halo_step((qx, qy, cx, cy), halos)
    halos = exchange(faces)
    next4, qx, qy, even3 = inner_step(3, points, waves, next3, faces, whole2, courant)
    final, late, sent_late = last_step(
        flag, even3, next4, (qx, qy, cx, cy), halos, sent_matrix
    )
    other_late = lax.ppermute(sent_late, "gx", across)
    partial = lag_image(lag_offsets, own_early, other_early, None, count_x // 2)
    own_late = pack_own(late, own_matrix)
    image = lag_image(lag_offsets, own_late, other_late, partial, count_x // 2)
    return write_out(final), jnp.transpose(image, (1, 0, 2))


def solution(mesh):
    placed = (
        P(("shots", "gx"), "gy", None),
        P(("shots", "gx"), "gy", None),
        P("gx", "gy", None),
        P(None, "shots"),
        P(None, "shots"),
        P(None, "shots"),
        P(None, "shots"),
        P("shots", None),
        P(),
    )
    return jax.shard_map(
        body,
        mesh=mesh,
        in_specs=placed,
        out_specs=(P(("shots", "gx"), "gy", None), P(("shots", "gx"), None, "gy")),
        check_vma=False,
    )
```

```python
import jax
import jax.numpy as jnp
import numpy as np
from jax import lax
from jax.experimental import pallas as pl
from jax.experimental.pallas import tpu as pltpu
from jax.sharding import PartitionSpec as P

STEPS = 4
WIDTH = 4
LAGMAX = 8
REACH = LAGMAX // 2
GROUP = 4
SIDE = 8

SCALE = 5040.0
BAND = (8064.0, -1008.0, 128.0, -9.0)
CENTRE = 3.0 * (-205.0 / 72.0)
WEIGHTS = (1.6, -0.2, 8.0 / 315.0, -1.0 / 560.0)

F32 = jnp.float32
BF16 = jnp.bfloat16


def shape(*dims, dtype=F32):
    return jax.ShapeDtypeStruct(dims, dtype)


def params(megabytes):
    return pltpu.CompilerParams(vmem_limit_bytes=megabytes << 20)


def spec(space):
    return pl.BlockSpec(memory_space=space)


def cost(count, flops_each, arrays):
    return pl.CostEstimate(
        flops=int(count * flops_each), bytes_accessed=int(4 * count * arrays), transcendentals=0
    )


def split3(values):
    high = values.astype(BF16)
    rest = values - high.astype(F32)
    middle = rest.astype(BF16)
    low = (rest - middle.astype(F32)).astype(BF16)
    return high, middle, low


def exact_dot(values, matrix):
    parts = [jnp.dot(part, matrix, preferred_element_type=F32) for part in split3(values)]
    return (parts[2] + parts[1]) + parts[0]


class Place:
    def __init__(self):
        loop_size = lax.axis_size("gx")
        self.half = loop_size // 2
        relative = lax.rem(lax.axis_index("gx") + loop_size - loop_size // 4, loop_size)
        self.field = relative // self.half
        self.slab = lax.rem(relative, self.half)
        self.even = lax.rem(self.slab, 2) == 0
        self.y = lax.axis_index("gy")

    def block(self, count_y):
        return pl.multiple_of((1 - self.y) * (count_y - SIDE), SIDE)


def first_faces(field):
    count_x, count_y, count_z = field.shape
    top = count_x - WIDTH

    def kernel(field_ref, far_ref, near_ref, side_ref, sems):
        place = Place()
        far = jnp.where(place.even, 0, top)
        sources = [
            field_ref.at[pl.ds(far, WIDTH)],
            field_ref.at[pl.ds(top - far, WIDTH)],
            field_ref.at[:, pl.ds(place.block(count_y), SIDE)],
        ]
        copies = [
            pltpu.make_async_copy(source, target, sems.at[index])
            for index, (source, target) in enumerate(zip(sources, (far_ref, near_ref, side_ref)))
        ]
        for copy in copies:
            copy.start()
        for copy in copies:
            copy.wait()

    return pl.pallas_call(
        kernel,
        out_shape=face_shapes(count_x, count_y, count_z),
        in_specs=[spec(pltpu.HBM)],
        out_specs=(spec(pltpu.VMEM),) * 3,
        scratch_shapes=[pltpu.SemaphoreType.DMA((3,))],
        compiler_params=params(8),
        name="first_faces",
    )(field)


def face_shapes(count_x, count_y, count_z):
    slab = shape(WIDTH, count_y, count_z)
    return slab, slab, shape(count_x, SIDE, count_z)


def even_rows(level_ref, offset_x, offset_y, count_a, b):
    rows, stride, lanes = level_ref.shape
    flat = level_ref.reshape(rows * stride, lanes)
    start = offset_x * stride + offset_y + 2 * b
    return flat[pl.ds(start, count_a, stride=2 * stride), :]


def inner_step(number, points, waves, current, faces, previous, courant, snapshots=None, matrices=None):
    count_x, count_y, count_z = current.shape
    count_a, count_b = count_x // 2, count_y // 2
    first = faces is None
    last = number == STEPS - 1
    snapshot = number == STEPS // 2
    if first:
        count_j = -(-max(array.shape[1] for array in points) // 128) * 128
    else:
        count_j = points.shape[1]

    def kernel(*refs):
        refs = list(refs)
        take = lambda count: [refs.pop(0) for _ in range(count)]
        if first:
            raw_refs = take(4)
        else:
            points_ref, waves_ref = take(2)
        (current_ref,) = take(1)
        if not first:
            far_ref, near_ref, side_ref = take(3)
        previous_ref, courant_ref = take(2)
        if snapshot:
            steps_ref, matrices_ref = take(2)
        next_ref, qx_ref, qy_ref = take(3)
        if first:
            kept_ref, cx_ref, cy_ref, points_ref, waves_ref = take(5)
        if not last:
            (whole_ref,) = take(1)
        if snapshot:
            own_out, sent_out, own_matrix, sent_matrix, flag_ref = take(5)
        if last:
            (even_ref,) = take(1)
        padded, zpart, addpart = take(3)
        if first:
            before_ref = take(1)[0]
            raw_refs_in, raw_refs = raw_refs, take(4)
            (sems,) = take(1)
        if snapshot:
            even_ref, wanted, sems = take(3)

        place = Place()
        block = place.block(count_y)
        rows, columns = pl.ds(WIDTH, count_x), pl.ds(SIDE, count_y)
        if first:
            copies = [
                pltpu.make_async_copy(source, target, sems.at[index])
                for index, (source, target) in enumerate(
                    zip(
                        (*raw_refs_in, current_ref, previous_ref, courant_ref),
                        (*raw_refs, padded.at[rows, columns], before_ref, kept_ref),
                    )
                )
            ]
            for copy in copies:
                copy.start()
        else:
            before_ref, kept_ref = previous_ref, courant_ref
        if snapshot:
            copies = [
                pltpu.make_async_copy(steps_ref, wanted, sems.at[0]),
                pltpu.make_async_copy(matrices_ref.at[place.field], own_matrix, sems.at[1]),
                pltpu.make_async_copy(matrices_ref.at[1 - place.field], sent_matrix, sems.at[2]),
            ]
            for copy in copies:
                copy.start()

        zero_x = jnp.zeros((WIDTH, count_y + 2 * SIDE, count_z), F32)
        padded[pl.ds(0, WIDTH)] = zero_x
        padded[pl.ds(count_x + WIDTH, WIDTH)] = zero_x
        zero_y = jnp.zeros((count_x, SIDE, count_z), F32)
        padded[rows, pl.ds(0, SIDE)] = zero_y
        padded[rows, pl.ds(count_y + SIDE, SIDE)] = zero_y

        if not first:
            padded[rows, columns] = current_ref[...]
            low, high = pl.ds(WIDTH, WIDTH), pl.ds(count_x, WIDTH)

            @pl.when(place.even)
            def _():
                padded[high, columns] = near_ref[...]
                padded[low, columns] = far_ref[...]

            @pl.when(jnp.logical_not(place.even))
            def _():
                padded[low, columns] = near_ref[...]
                padded[high, columns] = far_ref[...]

            padded[rows, pl.ds(pl.multiple_of(block + SIDE, SIDE), SIDE)] = side_ref[...]

        if first:
            for copy in copies[:4]:
                copy.wait()
            points_ref[...] = jnp.full(points_ref.shape, -1, jnp.int32)
            waves_ref[...] = jnp.zeros(waves_ref.shape, F32)

            def choose(cells_ref, wave_ref):
                count = cells_ref.shape[1]
                points_ref[pl.ds(0, 3), pl.ds(0, count)] = cells_ref[...]
                waves_ref[pl.ds(0, STEPS), pl.ds(0, count)] = wave_ref[...]

            @pl.when(place.field == 0)
            def _():
                choose(raw_refs[0], raw_refs[1])

            @pl.when(place.field != 0)
            def _():
                choose(raw_refs[2], raw_refs[3])

        px = points_ref[0:1, :] - place.slab * count_x
        py = points_ref[1:2, :] - place.y * count_y
        inside = (px >= 0) & (px < count_x) & (py >= 0) & (py < count_y)
        home = jnp.where(inside, px * count_y + py, -1)
        amounts = waves_ref[number : number + 1, :]
        spread = jnp.where(
            lax.broadcasted_iota(jnp.int32, (count_z, count_j), 0) == points_ref[2:3, :],
            amounts,
            0.0,
        )
        spread = split3(spread)

        gap = jnp.abs(
            lax.broadcasted_iota(jnp.int32, (count_z, count_z), 0)
            - lax.broadcasted_iota(jnp.int32, (count_z, count_z), 1)
        )
        band = jnp.zeros((count_z, count_z), F32)
        for offset, weight in enumerate(BAND, 1):
            band = jnp.where(gap == offset, weight, band)
        band = band.astype(BF16)

        if first:
            copies[4].wait()
        chunk = 8

        def multiply(index, _):
            start = pl.multiple_of(index * chunk, chunk)
            values = padded[pl.ds(start + WIDTH, chunk), columns]
            zpart[pl.ds(start, chunk)] = exact_dot(
                values.reshape(chunk * count_y, count_z), band
            ).reshape(chunk, count_y, count_z)
            here = start * count_y + lax.broadcasted_iota(
                jnp.int32, (chunk * count_y, count_j), 0
            )
            hit = jnp.where(here == home, 1.0, 0.0).astype(BF16)
            added = [
                lax.dot_general(hit, part, (((1,), (1,)), ((), ())), preferred_element_type=F32)
                for part in spread
            ]
            added = (added[2] + added[1]) + added[0]
            addpart[pl.ds(start, chunk)] = added.reshape(chunk, count_y, count_z)
            return 0

        lax.fori_loop(0, count_x // chunk, multiply, 0)
        if first:
            for copy in copies[5:]:
                copy.wait()

        def row(x, _):
            middle = padded[x + WIDTH, columns]
            total = CENTRE * middle + (1.0 / SCALE) * zpart[x]
            for offset, weight in enumerate(WEIGHTS, 1):
                paired = padded[x + WIDTH + offset, columns] + padded[x + WIDTH - offset, columns]
                paired = paired + (
                    padded[x + WIDTH, pl.ds(SIDE + offset, count_y)]
                    + padded[x + WIDTH, pl.ds(SIDE - offset, count_y)]
                )
                total = total + weight * paired
            if not last:
                whole_ref[x] = middle
            next_ref[x] = (2.0 * middle - before_ref[x] + kept_ref[x] * total) + addpart[x]
            return 0

        lax.fori_loop(0, count_x, row, 0, unroll=4)

        qx_ref[pl.ds(0, WIDTH)] = next_ref[pl.ds(0, WIDTH)]
        qx_ref[pl.ds(WIDTH, WIDTH)] = next_ref[pl.ds(count_x - WIDTH, WIDTH)]
        qy_ref[...] = next_ref[:, pl.ds(block, SIDE)]
        if first:
            cx_ref[pl.ds(0, WIDTH)] = kept_ref[pl.ds(0, WIDTH)]
            cx_ref[pl.ds(WIDTH, WIDTH)] = kept_ref[pl.ds(count_x - WIDTH, WIDTH)]
            cy_ref[...] = kept_ref[:, pl.ds(block, SIDE)]
        if last:
            for b in range(count_b):
                even_ref[b] = even_rows(padded, WIDTH, SIDE, count_a, b)
        if snapshot:
            for copy in copies:
                copy.wait()
            flag_ref[...] = jnp.where(
                wanted[place.field, 1] == STEPS, jnp.ones(flag_ref.shape, F32), 0.0
            )
            earlier = wanted[place.field, 0] == number - 1

            @pl.when(earlier)
            def _():
                for b in range(count_b):
                    even_ref[b] = even_rows(previous_ref, 0, 0, count_a, b)

            @pl.when(jnp.logical_not(earlier))
            def _():
                for b in range(count_b):
                    even_ref[b] = even_rows(padded, WIDTH, SIDE, count_a, b)

            for kind, part in enumerate(packed(even_ref, own_matrix)):
                own_out[kind] = part
            send_into(even_ref, sent_matrix, sent_out)

    full = shape(count_x, count_y, count_z)
    slab, side = shape(2 * WIDTH, count_y, count_z), shape(count_x, SIDE, count_z)
    even = shape(count_b, count_a, count_z)
    outs = [full, slab, side]
    if first:
        outs += [full, slab, side, shape(8, count_j, dtype=jnp.int32), shape(8, count_j)]
    if not last:
        outs.append(full)
    if snapshot:
        size = GROUP * count_z
        outs += [
            shape(4, count_b // GROUP * count_a, count_z),
            sent_shape(count_a, count_b, count_z),
            shape(size, size, dtype=BF16),
            shape(size, size, dtype=BF16),
            shape(8, count_z),
        ]
    if last:
        outs.append(even)
    place_of = spec(pltpu.HBM) if first else spec(pltpu.VMEM)
    operands = [*points, current] if first else [points, waves, current]
    specs = [place_of] * len(operands)
    if not first:
        operands += list(faces)
        specs += [spec(pltpu.VMEM)] * 3
    operands += [previous, courant]
    specs += [place_of] * 2
    scratch = [
        pltpu.VMEM((count_x + 2 * WIDTH, count_y + 2 * SIDE, count_z), F32),
        pltpu.VMEM(full.shape, F32),
        pltpu.VMEM(full.shape, F32),
    ]
    if first:
        scratch.append(pltpu.VMEM(full.shape, F32))
        scratch += [pltpu.VMEM(array.shape, array.dtype) for array in points]
        scratch.append(pltpu.SemaphoreType.DMA((7,)))
    if snapshot:
        operands += [snapshots, matrices]
        specs += [spec(pltpu.HBM)] * 2
        scratch += [
            pltpu.VMEM(even.shape, F32),
            pltpu.SMEM(snapshots.shape, jnp.int32),
            pltpu.SemaphoreType.DMA((3,)),
        ]
    return pl.pallas_call(
        kernel,
        out_shape=tuple(outs),
        in_specs=specs,
        out_specs=(spec(pltpu.VMEM),) * len(outs),
        scratch_shapes=scratch,
        compiler_params=params(20),
        cost_estimate=cost(count_x * count_y * count_z, 60, 6),
    )(*operands)


def low_terms(halo_ref, r):
    total = None
    for k in range(r + 1, WIDTH + 1):
        term = WEIGHTS[k - 1] * halo_ref[WIDTH + r - k]
        total = term if total is None else total + term
    return total


def high_terms(halo_ref, r):
    total = None
    for k in range(WIDTH - r, WIDTH + 1):
        term = WEIGHTS[k - 1] * halo_ref[r + k - WIDTH]
        total = term if total is None else total + term
    return total


def add_halo(place, parts, halos, outs):
    qx_ref, qy_ref, cx_ref, cy_ref = parts
    far_in, near_in, side_in = halos
    far_out, near_out, side_out = outs
    count_y, count_x = qx_ref.shape[1], qy_ref.shape[0]
    block = place.block(count_y)

    def along_x(low_in, high_in, low_out, high_out):
        for r in range(WIDTH):
            low_out[r] = qx_ref[r] + cx_ref[r] * low_terms(low_in, r)
            high_out[r] = qx_ref[WIDTH + r] + cx_ref[WIDTH + r] * high_terms(high_in, r)
        side_out[pl.ds(0, WIDTH)] = low_out[:, pl.ds(block, SIDE)]
        side_out[pl.ds(count_x - WIDTH, WIDTH)] = high_out[:, pl.ds(block, SIDE)]

    inner = pl.ds(WIDTH, count_x - 2 * WIDTH)
    side_out[inner] = qy_ref[inner]

    @pl.when(place.even)
    def _():
        along_x(far_in, near_in, far_out, near_out)

    @pl.when(jnp.logical_not(place.even))
    def _():
        along_x(near_in, far_in, near_out, far_out)

    def along_y(shifts, masks):
        halo = side_in[...]
        lanes = halo.shape[2]
        line = lax.broadcasted_iota(jnp.int32, (1, SIDE, lanes), 1)
        total = None
        for k in range(1, WIDTH + 1):
            weight = jnp.where(masks(line, k), WEIGHTS[k - 1], 0.0)
            term = weight * pltpu.roll(halo, shifts(k), 1)
            total = term if total is None else total + term
        side_out[...] = side_out[...] + cy_ref[...] * total

    @pl.when(place.y == 0)
    def _():
        along_y(lambda k: SIDE - k, lambda line, k: line >= SIDE - k)

    @pl.when(place.y != 0)
    def _():
        along_y(lambda k: k, lambda line, k: line < k)

    def corners(low_out, high_out):
        low_out[:, pl.ds(block, SIDE)] = side_out[pl.ds(0, WIDTH)]
        high_out[:, pl.ds(block, SIDE)] = side_out[pl.ds(count_x - WIDTH, WIDTH)]

    @pl.when(place.even)
    def _():
        corners(far_out, near_out)

    @pl.when(jnp.logical_not(place.even))
    def _():
        corners(near_out, far_out)


def halo_step(parts, halos):
    count_y, (count_x, _, count_z) = parts[0].shape[1], parts[1].shape

    def kernel(*refs):
        add_halo(Place(), refs[:4], refs[4:7], refs[7:])

    return pl.pallas_call(
        kernel,
        out_shape=face_shapes(count_x, count_y, count_z),
        in_specs=[spec(pltpu.VMEM)] * 7,
        out_specs=(spec(pltpu.VMEM),) * 3,
        compiler_params=params(8),
        cost_estimate=cost(16 * count_y * count_z, 10, 6),
        name="halo_step",
    )(*parts, *halos)


def pack_matrix(window, count_z):
    half = count_z // GROUP
    size = GROUP * count_z
    row, column = np.arange(size)[:, None], np.arange(size)[None, :]
    row_b, row_z = row // count_z, row % count_z
    kind = column // count_z
    parity = kind % 2
    lane_b, lane_i = (column % count_z) // half, column % half
    main = (row_b == lane_b) & (row_z == 2 * (half * window + lane_i) + parity)
    wanted_b = (lane_b + (GROUP - 1 if window == 0 else 1)) % GROUP
    wanted_z = 2 * (half * (1 - window) + lane_i) + parity
    useful = lane_i < REACH if window == 0 else lane_i >= half - REACH
    edge = (row_b == wanted_b) & (row_z == wanted_z) & useful
    return np.where(kind < 2, main, edge).astype(np.float32)


def packed(even_ref, matrix_ref):
    count_b, _, count_z = even_ref.shape
    rows = [
        jnp.concatenate([even_ref[b + i] for i in range(GROUP)], axis=1)
        for b in range(0, count_b, GROUP)
    ]
    result = exact_dot(jnp.concatenate(rows, axis=0), matrix_ref[...])
    return [result[:, kind * count_z : (kind + 1) * count_z] for kind in range(4)]


def pack_own(even, matrix):
    count_b, count_a, count_z = even.shape
    total_rows = count_b // GROUP * count_a

    def kernel(even_ref, matrix_ref, out_ref):
        for kind, part in enumerate(packed(even_ref, matrix_ref)):
            out_ref[kind] = part

    return pl.pallas_call(
        kernel,
        out_shape=shape(4, total_rows, count_z),
        in_specs=[spec(pltpu.VMEM)] * 2,
        out_specs=spec(pltpu.VMEM),
        compiler_params=params(8),
        cost_estimate=cost(count_b * count_a * count_z, 1024, 4),
        name="pack_own",
    )(even, matrix)


def edge_slots(count_a, groups, count_z):
    fits = count_z // GROUP // REACH
    slots = []
    for index in range(2 * groups):
        slots.append((index // groups, index % groups, index // fits * count_a, index % fits * REACH))
    return slots, -(-2 * groups // fits) * count_a


def send_into(even_ref, matrix_ref, out_ref):
    count_b, count_a, count_z = even_ref.shape
    groups = count_b // GROUP
    total_rows = groups * count_a
    parts = packed(even_ref, matrix_ref)
    out_ref[pl.ds(0, total_rows), :] = parts[0]
    out_ref[pl.ds(total_rows, total_rows), :] = parts[1]
    slots, _ = edge_slots(count_a, groups, count_z)
    sums = {}
    for parity, g, row, shift in slots:
        part = parts[2 + parity][g * count_a : (g + 1) * count_a]
        part = pltpu.roll(part, shift, 1) if shift else part
        sums[row] = sums[row] + part if row in sums else part
    for row, part in sums.items():
        out_ref[pl.ds(2 * total_rows + row, count_a), :] = part


def sent_shape(count_a, count_b, count_z):
    groups = count_b // GROUP
    _, extra = edge_slots(count_a, groups, count_z)
    return shape(2 * groups * count_a + extra, count_z)


def last_step(which, flag, even_before, current, late, parts, halos, matrix):
    count_x, count_y, count_z = current.shape
    count_a, count_b = count_x // 2, count_y // 2
    keep = late is not None

    def kernel(*refs):
        refs = list(refs)
        take = lambda count: [refs.pop(0) for _ in range(count)]
        flag_ref, even_ref, _ = take(3)
        if keep:
            take(1)
        parts_in, halos_in = take(4), take(3)
        matrix_ref, final_ref, late_ref, sent_ref = take(4)
        faces = take(3)
        place = Place()

        @pl.when(place.field == which)
        def _():
            add_halo(place, parts_in, halos_in, faces)
            far_out, near_out, side_out = faces
            low, high = pl.ds(0, WIDTH), pl.ds(count_x - WIDTH, WIDTH)

            @pl.when(place.even)
            def _():
                final_ref[high] = near_out[...]
                final_ref[low] = far_out[...]

            @pl.when(jnp.logical_not(place.even))
            def _():
                final_ref[low] = near_out[...]
                final_ref[high] = far_out[...]

            final_ref[:, pl.ds(place.block(count_y), SIDE)] = side_out[...]
            wants_last = jnp.broadcast_to(flag_ref[0:1, :], (count_a, count_z)) > 0.5
            for b in range(count_b):
                late_ref[b] = jnp.where(
                    wants_last, even_rows(final_ref, 0, 0, count_a, b), even_ref[b]
                )
            send_into(late_ref, matrix_ref, sent_ref)

    slab, _, side = face_shapes(count_x, count_y, count_z)
    operands = [flag, even_before, current, *([late] if keep else []), *parts, *halos, matrix]
    return pl.pallas_call(
        kernel,
        out_shape=(
            shape(*current.shape),
            shape(count_b, count_a, count_z),
            sent_shape(count_a, count_b, count_z),
        ),
        in_specs=[spec(pltpu.VMEM)] * len(operands),
        out_specs=(spec(pltpu.VMEM),) * 3,
        scratch_shapes=[
            pltpu.VMEM(slab.shape, F32),
            pltpu.VMEM(slab.shape, F32),
            pltpu.VMEM(side.shape, F32),
        ],
        input_output_aliases={2: 0, 3: 1} if keep else {2: 0},
        compiler_params=params(12),
        cost_estimate=cost(count_x * count_y * count_z, 10, 3),
    )(*operands)


def lag_image(count_a, lags, own, others, before=None, level=None):
    _, total_rows, count_z = own.shape
    count_h = lags.shape[1]
    half = count_z // GROUP
    last = before is not None
    width = total_rows // count_a * count_z
    groups = total_rows // count_a

    def kernel(*refs):
        refs = list(refs)
        take = lambda count: [refs.pop(0) for _ in range(count)]
        lags_ref, own_ref = take(2)
        other_refs = take(len(others))
        if last:
            before_ref, level_ref = take(2)
        (out_ref,) = take(1)
        if last:
            (final_ref,) = take(1)
        mains, edges = take(2)
        if last:
            store, sems = take(2)
        else:
            store = out_ref
        place = Place()
        if last:
            final = pltpu.make_async_copy(level_ref, final_ref, sems.at[0])
            final.start()
        is_source = place.field == 0
        lane = lax.broadcasted_iota(jnp.int32, (count_a, count_z), 1) % half
        useful = jnp.where(is_source, lane, half - 1 - lane) < REACH
        slots, _ = edge_slots(count_a, groups, count_z)

        def unpack(other_ref):
            for parity in range(2):
                mains[parity] = other_ref[pl.ds(parity * total_rows, total_rows), :]
            for parity, g, row, shift in slots:
                part = other_ref[pl.ds(2 * total_rows + row, count_a), :]
                part = pltpu.roll(part, count_z - shift, 1) if shift else part
                edges[parity, pl.ds(g * count_a, count_a), :] = jnp.where(useful, part, 0.0)

        if len(other_refs) == 1:
            unpack(other_refs[0])
        else:
            for which, other_ref in enumerate(other_refs):
                pl.when(place.field == which)(lambda other_ref=other_ref: unpack(other_ref))

        lane = lax.broadcasted_iota(jnp.int32, (1, count_z), 1) % half
        all_lags = lags_ref[...]

        def moved(main, edge, shift):
            mask = (lane < shift) | (lane >= half + shift)
            return pltpu.roll(jnp.where(mask, edge, main), (count_z - shift) & (count_z - 1), 1)

        for h in range(count_h):
            lag = all_lags[0, h]
            parity = lag & 1
            source_shift = -((lag + parity) >> 1)
            receiver_shift = (lag - parity) >> 1
            own_shift = jnp.where(is_source, source_shift, receiver_shift)
            other_shift = jnp.where(is_source, receiver_shift, source_shift)
            product = moved(own_ref[parity], own_ref[2 + parity], own_shift)
            product = product * moved(mains[parity], edges[parity], other_shift)
            for g in range(groups):
                part = product[g * count_a : (g + 1) * count_a]
                lanes = pl.ds(g * count_z, count_z)
                if last:
                    part = part + before_ref[h, :, lanes]
                store[h, :, lanes] = part
            if last:
                pltpu.make_async_copy(store.at[h], out_ref.at[h], sems.at[1]).start()
        if last:
            pltpu.make_async_copy(store, out_ref, sems.at[1]).wait()
            final.wait()

    image = shape(count_h, count_a, width)
    operands = [lags, own, *others] + ([before, level] if last else [])
    scratch = [pltpu.VMEM((2, total_rows, count_z), F32)] * 2
    if last:
        scratch += [pltpu.VMEM(image.shape, F32), pltpu.SemaphoreType.DMA((2,))]
    return pl.pallas_call(
        kernel,
        out_shape=(image, shape(*level.shape)) if last else image,
        in_specs=[spec(pltpu.VMEM)] * len(operands),
        out_specs=(spec(pltpu.HBM),) * 2 if last else spec(pltpu.VMEM),
        scratch_shapes=scratch,
        compiler_params=params(12),
        cost_estimate=cost(count_h * total_rows * count_z, 10, 2),
        name="last_image" if last else "early_image",
    )(*operands)


def body(
    field_now,
    field_prev,
    courant_squared,
    source_cells,
    source_wave,
    receiver_cells,
    receiver_wave,
    snapshot_steps,
    lag_offsets,
):
    count_x, _, count_z = field_now.shape
    loop_size = lax.axis_size("gx")
    half_size = loop_size // 2
    turn = loop_size // 4
    assert lax.axis_size("gy") == 2 and half_size % 2 == 0

    slabs = [(i - turn) % loop_size % half_size for i in range(loop_size)]

    def pairs(odd):
        found = []
        for i, slab in enumerate(slabs):
            if slab % 2 == odd and slab != half_size - 1:
                j = (i + 1) % loop_size
                found += [(i, j), (j, i)]
        return found

    near_pairs, far_pairs = pairs(0), pairs(1)
    across = [(i, (i + half_size) % loop_size) for i in range(loop_size)]
    fields = [(i - turn) % loop_size // half_size for i in range(loop_size)]

    def of(which, found):
        return [(i, j) for i, j in found if fields[i] == which]

    def send_far(far, which=None):
        if which is None:
            return lax.ppermute(far, "gx", far_pairs)
        return lax.ppermute(far, "gx", of(which, far_pairs))

    def send_near(near, side):
        near = lax.ppermute(near, "gx", near_pairs)
        return near, lax.ppermute(side, "gy", [(0, 1), (1, 0)])

    def exchange(faces):
        far, near, side = faces
        return (send_far(far), *send_near(near, side))

    matrices = jnp.asarray(
        np.stack([pack_matrix(window, count_z) for window in (0, 1)]), dtype=BF16
    )
    raw = (source_cells, source_wave, receiver_cells, receiver_wave)
    lags = lag_offsets.reshape(1, -1)
    field_now, field_prev, courant_squared, matrices, snapshot_steps, *raw = (
        pltpu.with_memory_space_constraint(array, pltpu.HBM)
        for array in (field_now, field_prev, courant_squared, matrices, snapshot_steps, *raw)
    )
    halos = exchange(first_faces(field_now))
    next1, qx, qy, courant, cx, cy, points, waves, whole0 = inner_step(
        0, raw, None, field_now, None, field_prev, courant_squared
    )
    faces = halo_step((qx, qy, cx, cy), halos)
    halos = exchange(faces)
    next2, qx, qy, whole1 = inner_step(1, points, waves, next1, faces, whole0, courant)
    faces = halo_step((qx, qy, cx, cy), halos)
    halos = exchange(faces)
    next3, qx, qy, whole2, own_early, sent_early, own_matrix, sent_matrix, flag = inner_step(
        2, points, waves, next2, faces, whole1, courant, snapshot_steps, matrices
    )
    other_early = lax.ppermute(sent_early, "gx", across)
    faces = halo_step((qx, qy, cx, cy), halos)
    far, near, side = faces
    near, side = send_near(near, side)
    fars = send_far(far, 0), send_far(far, 1)
    next4, qx, qy, even3 = inner_step(3, points, waves, next3, faces, whole2, courant)
    parts = (qx, qy, cx, cy)
    final, late, sent = last_step(
        0, flag, even3, next4, None, parts, (fars[0], near, side), sent_matrix
    )
    from_source = lax.ppermute(sent, "gx", of(0, across))
    partial = lag_image(count_x // 2, lags, own_early, [other_early])
    final, late, sent = last_step(
        1, flag, even3, final, late, parts, (fars[1], near, side), sent_matrix
    )
    from_receiver = lax.ppermute(sent, "gx", of(1, across))
    own_late = pack_own(late, own_matrix)
    image, final = lag_image(
        count_x // 2, lags, own_late, [from_receiver, from_source], partial, final
    )
    return final, jnp.transpose(image, (1, 0, 2))


def solution(mesh):
    placed = (
        P(("shots", "gx"), "gy", None),
        P(("shots", "gx"), "gy", None),
        P("gx", "gy", None),
        P(None, "shots"),
        P(None, "shots"),
        P(None, "shots"),
        P(None, "shots"),
        P("shots", None),
        P(),
    )
    return jax.shard_map(
        body,
        mesh=mesh,
        in_specs=placed,
        out_specs=(P(("shots", "gx"), "gy", None), P(("shots", "gx"), None, "gy")),
        check_vma=False,
    )
```

```python
import jax
import jax.numpy as jnp
import numpy as np
from jax import lax
from jax.experimental import pallas as pl
from jax.experimental.pallas import tpu as pltpu
from jax.sharding import PartitionSpec as P

STEPS = 4
WIDTH = 4
LAGMAX = 8
REACH = LAGMAX // 2
GROUP = 4
SIDE = 8

SCALE = 5040.0
BAND = (8064.0, -1008.0, 128.0, -9.0)
CENTRE = 3.0 * (-205.0 / 72.0)
WEIGHTS = (1.6, -0.2, 8.0 / 315.0, -1.0 / 560.0)

F32 = jnp.float32
BF16 = jnp.bfloat16


def shape(*dims, dtype=F32):
    return jax.ShapeDtypeStruct(dims, dtype)


def params(megabytes):
    return pltpu.CompilerParams(vmem_limit_bytes=megabytes << 20)


def spec(space):
    return pl.BlockSpec(memory_space=space)


def cost(count, flops_each, arrays):
    return pl.CostEstimate(
        flops=int(count * flops_each), bytes_accessed=int(4 * count * arrays), transcendentals=0
    )


def split3(values):
    high = values.astype(BF16)
    rest = values - high.astype(F32)
    middle = rest.astype(BF16)
    low = (rest - middle.astype(F32)).astype(BF16)
    return high, middle, low


def exact_dot(values, matrix):
    rows = values.shape[0]
    stacked = jnp.concatenate(split3(values), axis=0)
    result = jnp.dot(stacked, matrix, preferred_element_type=F32)
    return (result[2 * rows :] + result[rows : 2 * rows]) + result[:rows]


class Place:
    def __init__(self):
        loop_size = lax.axis_size("gx")
        self.half = loop_size // 2
        relative = lax.rem(lax.axis_index("gx") + loop_size - loop_size // 4, loop_size)
        self.field = relative // self.half
        self.slab = lax.rem(relative, self.half)
        self.even = lax.rem(self.slab, 2) == 0
        self.y = lax.axis_index("gy")

    def block(self, count_y):
        return pl.multiple_of((1 - self.y) * (count_y - SIDE), SIDE)


def first_faces(field):
    count_x, count_y, count_z = field.shape
    top = count_x - WIDTH

    def kernel(field_ref, far_ref, near_ref, side_ref, whole_ref, sems):
        place = Place()
        far = jnp.where(place.even, 0, top)
        sources = [
            field_ref.at[pl.ds(far, WIDTH)],
            field_ref.at[pl.ds(top - far, WIDTH)],
            field_ref.at[:, pl.ds(place.block(count_y), SIDE)],
            field_ref,
        ]
        copies = [
            pltpu.make_async_copy(source, target, sems.at[index])
            for index, (source, target) in enumerate(
                zip(sources, (far_ref, near_ref, side_ref, whole_ref))
            )
        ]
        for copy in copies:
            copy.start()
        for copy in copies:
            copy.wait()

    return pl.pallas_call(
        kernel,
        out_shape=(*face_shapes(count_x, count_y, count_z), shape(*field.shape)),
        in_specs=[spec(pltpu.HBM)],
        out_specs=(spec(pltpu.VMEM),) * 4,
        scratch_shapes=[pltpu.SemaphoreType.DMA((4,))],
        compiler_params=params(8),
        name="first_faces",
    )(field)


def face_shapes(count_x, count_y, count_z):
    slab = shape(WIDTH, count_y, count_z)
    return slab, slab, shape(count_x, SIDE, count_z)


def even_rows(level_ref, offset_x, offset_y, count_a, b):
    rows, stride, lanes = level_ref.shape
    flat = level_ref.reshape(rows * stride, lanes)
    start = offset_x * stride + offset_y + 2 * b
    return flat[pl.ds(start, count_a, stride=2 * stride), :]


def inner_step(number, points, waves, current, faces, previous, courant, snapshots=None, matrices=None):
    count_x, count_y, count_z = current.shape
    count_a, count_b = count_x // 2, count_y // 2
    first = faces is None
    last = number == STEPS - 1
    snapshot = number == STEPS // 2
    if first:
        count_j = -(-max(array.shape[1] for array in points) // 128) * 128
    else:
        count_j = points.shape[1]

    def kernel(*refs):
        refs = list(refs)
        take = lambda count: [refs.pop(0) for _ in range(count)]
        if first:
            raw_refs = take(4)
        else:
            points_ref, waves_ref = take(2)
        (current_ref,) = take(1)
        if not first:
            far_ref, near_ref, side_ref = take(3)
        previous_ref, courant_ref = take(2)
        if snapshot:
            steps_ref, matrices_ref = take(2)
        next_ref, qx_ref, qy_ref = take(3)
        if first:
            kept_ref, cx_ref, cy_ref, points_ref, waves_ref = take(5)
        elif not last:
            (whole_ref,) = take(1)
        if snapshot:
            own_out, sent_out, own_matrix, sent_matrix, flag_ref = take(5)
        if last:
            (even_ref,) = take(1)
        padded, zpart, addpart = take(3)
        if first:
            before_ref = take(1)[0]
            raw_refs_in, raw_refs = raw_refs, take(4)
            (sems,) = take(1)
        if snapshot:
            even_ref, wanted, sems = take(3)

        place = Place()
        block = place.block(count_y)
        rows, columns = pl.ds(WIDTH, count_x), pl.ds(SIDE, count_y)
        if first:
            copies = [
                pltpu.make_async_copy(source, target, sems.at[index])
                for index, (source, target) in enumerate(
                    zip(
                        (*raw_refs_in, previous_ref, courant_ref),
                        (*raw_refs, before_ref, kept_ref),
                    )
                )
            ]
            for copy in copies:
                copy.start()
        else:
            before_ref, kept_ref = previous_ref, courant_ref
        if snapshot:
            copies = [
                pltpu.make_async_copy(steps_ref, wanted, sems.at[0]),
                pltpu.make_async_copy(matrices_ref.at[place.field], own_matrix, sems.at[1]),
                pltpu.make_async_copy(matrices_ref.at[1 - place.field], sent_matrix, sems.at[2]),
            ]
            for copy in copies:
                copy.start()

        zero_x = jnp.zeros((WIDTH, count_y + 2 * SIDE, count_z), F32)
        padded[pl.ds(0, WIDTH)] = zero_x
        padded[pl.ds(count_x + WIDTH, WIDTH)] = zero_x
        zero_y = jnp.zeros((count_x, SIDE, count_z), F32)
        padded[rows, pl.ds(0, SIDE)] = zero_y
        padded[rows, pl.ds(count_y + SIDE, SIDE)] = zero_y

        padded[rows, columns] = current_ref[...]
        if not first:
            low, high = pl.ds(WIDTH, WIDTH), pl.ds(count_x, WIDTH)

            @pl.when(place.even)
            def _():
                padded[high, columns] = near_ref[...]
                padded[low, columns] = far_ref[...]

            @pl.when(jnp.logical_not(place.even))
            def _():
                padded[low, columns] = near_ref[...]
                padded[high, columns] = far_ref[...]

            padded[rows, pl.ds(pl.multiple_of(block + SIDE, SIDE), SIDE)] = side_ref[...]

        if first:
            for copy in copies[:4]:
                copy.wait()
            points_ref[...] = jnp.full(points_ref.shape, -1, jnp.int32)
            waves_ref[...] = jnp.zeros(waves_ref.shape, F32)

            def choose(cells_ref, wave_ref):
                count = cells_ref.shape[1]
                points_ref[pl.ds(0, 3), pl.ds(0, count)] = cells_ref[...]
                waves_ref[pl.ds(0, STEPS), pl.ds(0, count)] = wave_ref[...]

            @pl.when(place.field == 0)
            def _():
                choose(raw_refs[0], raw_refs[1])

            @pl.when(place.field != 0)
            def _():
                choose(raw_refs[2], raw_refs[3])

        px = points_ref[0:1, :] - place.slab * count_x
        py = points_ref[1:2, :] - place.y * count_y
        inside = (px >= 0) & (px < count_x) & (py >= 0) & (py < count_y)
        home = jnp.where(inside, px * count_y + py, -1)
        amounts = waves_ref[number : number + 1, :]
        spread = jnp.where(
            lax.broadcasted_iota(jnp.int32, (count_z, count_j), 0) == points_ref[2:3, :],
            amounts,
            0.0,
        )
        spread = split3(spread)

        gap = jnp.abs(
            lax.broadcasted_iota(jnp.int32, (count_z, count_z), 0)
            - lax.broadcasted_iota(jnp.int32, (count_z, count_z), 1)
        )
        band = jnp.zeros((count_z, count_z), F32)
        for offset, weight in enumerate(BAND, 1):
            band = jnp.where(gap == offset, weight, band)
        band = band.astype(BF16)

        chunk = 8

        def multiply(index, _):
            start = pl.multiple_of(index * chunk, chunk)
            values = padded[pl.ds(start + WIDTH, chunk), columns]
            zpart[pl.ds(start, chunk)] = exact_dot(
                values.reshape(chunk * count_y, count_z), band
            ).reshape(chunk, count_y, count_z)
            here = start * count_y + lax.broadcasted_iota(
                jnp.int32, (chunk * count_y, count_j), 0
            )
            hit = jnp.where(here == home, 1.0, 0.0).astype(BF16)
            added = [
                lax.dot_general(hit, part, (((1,), (1,)), ((), ())), preferred_element_type=F32)
                for part in spread
            ]
            added = (added[2] + added[1]) + added[0]
            addpart[pl.ds(start, chunk)] = added.reshape(chunk, count_y, count_z)
            return 0

        lax.fori_loop(0, count_x // chunk, multiply, 0)
        if first:
            for copy in copies[4:]:
                copy.wait()

        def row(x, _):
            middle = padded[x + WIDTH, columns]
            total = CENTRE * middle + (1.0 / SCALE) * zpart[x]
            for offset, weight in enumerate(WEIGHTS, 1):
                paired = padded[x + WIDTH + offset, columns] + padded[x + WIDTH - offset, columns]
                paired = paired + (
                    padded[x + WIDTH, pl.ds(SIDE + offset, count_y)]
                    + padded[x + WIDTH, pl.ds(SIDE - offset, count_y)]
                )
                total = total + weight * paired
            if not first and not last:
                whole_ref[x] = middle
            next_ref[x] = (2.0 * middle - before_ref[x] + kept_ref[x] * total) + addpart[x]
            return 0

        lax.fori_loop(0, count_x, row, 0, unroll=4)

        qx_ref[pl.ds(0, WIDTH)] = next_ref[pl.ds(0, WIDTH)]
        qx_ref[pl.ds(WIDTH, WIDTH)] = next_ref[pl.ds(count_x - WIDTH, WIDTH)]
        qy_ref[...] = next_ref[:, pl.ds(block, SIDE)]
        if first:
            cx_ref[pl.ds(0, WIDTH)] = kept_ref[pl.ds(0, WIDTH)]
            cx_ref[pl.ds(WIDTH, WIDTH)] = kept_ref[pl.ds(count_x - WIDTH, WIDTH)]
            cy_ref[...] = kept_ref[:, pl.ds(block, SIDE)]
        if last:
            for b in range(count_b):
                even_ref[b] = even_rows(padded, WIDTH, SIDE, count_a, b)
        if snapshot:
            for copy in copies:
                copy.wait()
            flag_ref[...] = jnp.where(
                wanted[place.field, 1] == STEPS, jnp.ones(flag_ref.shape, F32), 0.0
            )
            earlier = wanted[place.field, 0] == number - 1

            @pl.when(earlier)
            def _():
                for b in range(count_b):
                    even_ref[b] = even_rows(previous_ref, 0, 0, count_a, b)

            @pl.when(jnp.logical_not(earlier))
            def _():
                for b in range(count_b):
                    even_ref[b] = even_rows(padded, WIDTH, SIDE, count_a, b)

            for kind, part in enumerate(packed(even_ref, own_matrix)):
                own_out[kind] = part
            send_into(even_ref, sent_matrix, sent_out)

    full = shape(count_x, count_y, count_z)
    slab, side = shape(2 * WIDTH, count_y, count_z), shape(count_x, SIDE, count_z)
    even = shape(count_b, count_a, count_z)
    outs = [full, slab, side]
    if first:
        outs += [full, slab, side, shape(8, count_j, dtype=jnp.int32), shape(8, count_j)]
    elif not last:
        outs.append(full)
    if snapshot:
        size = GROUP * count_z
        outs += [
            shape(4, count_b // GROUP * count_a, count_z),
            sent_shape(count_a, count_b, count_z),
            shape(size, size, dtype=BF16),
            shape(size, size, dtype=BF16),
            shape(8, count_z),
        ]
    if last:
        outs.append(even)
    place_of = spec(pltpu.HBM) if first else spec(pltpu.VMEM)
    operands = [*points, current] if first else [points, waves, current]
    specs = [place_of] * (len(operands) - 1) + [spec(pltpu.VMEM)]
    if not first:
        operands += list(faces)
        specs += [spec(pltpu.VMEM)] * 3
    operands += [previous, courant]
    specs += [place_of] * 2
    scratch = [
        pltpu.VMEM((count_x + 2 * WIDTH, count_y + 2 * SIDE, count_z), F32),
        pltpu.VMEM(full.shape, F32),
        pltpu.VMEM(full.shape, F32),
    ]
    if first:
        scratch.append(pltpu.VMEM(full.shape, F32))
        scratch += [pltpu.VMEM(array.shape, array.dtype) for array in points]
        scratch.append(pltpu.SemaphoreType.DMA((6,)))
    if snapshot:
        operands += [snapshots, matrices]
        specs += [spec(pltpu.HBM)] * 2
        scratch += [
            pltpu.VMEM(even.shape, F32),
            pltpu.SMEM(snapshots.shape, jnp.int32),
            pltpu.SemaphoreType.DMA((3,)),
        ]
    return pl.pallas_call(
        kernel,
        out_shape=tuple(outs),
        in_specs=specs,
        out_specs=(spec(pltpu.VMEM),) * len(outs),
        scratch_shapes=scratch,
        compiler_params=params(20),
        cost_estimate=cost(count_x * count_y * count_z, 60, 6),
    )(*operands)


def low_terms(halo_ref, r):
    total = None
    for k in range(r + 1, WIDTH + 1):
        term = WEIGHTS[k - 1] * halo_ref[WIDTH + r - k]
        total = term if total is None else total + term
    return total


def high_terms(halo_ref, r):
    total = None
    for k in range(WIDTH - r, WIDTH + 1):
        term = WEIGHTS[k - 1] * halo_ref[r + k - WIDTH]
        total = term if total is None else total + term
    return total


def add_halo(place, parts, halos, outs):
    qx_ref, qy_ref, cx_ref, cy_ref = parts
    far_in, near_in, side_in = halos
    far_out, near_out, side_out = outs
    count_y, count_x = qx_ref.shape[1], qy_ref.shape[0]
    block = place.block(count_y)

    def along_x(low_in, high_in, low_out, high_out):
        for r in range(WIDTH):
            low, high = qx_ref[r], qx_ref[WIDTH + r]
            if low_in is not None:
                low = low + cx_ref[r] * low_terms(low_in, r)
            if high_in is not None:
                high = high + cx_ref[WIDTH + r] * high_terms(high_in, r)
            low_out[r], high_out[r] = low, high
        side_out[pl.ds(0, WIDTH)] = low_out[:, pl.ds(block, SIDE)]
        side_out[pl.ds(count_x - WIDTH, WIDTH)] = high_out[:, pl.ds(block, SIDE)]

    inner = pl.ds(WIDTH, count_x - 2 * WIDTH)
    side_out[inner] = qy_ref[inner]

    @pl.when(place.even)
    def _():
        along_x(far_in, near_in, far_out, near_out)

    @pl.when(jnp.logical_not(place.even))
    def _():
        along_x(near_in, far_in, near_out, far_out)

    def along_y(shifts, masks):
        halo = side_in[...]
        lanes = halo.shape[2]
        line = lax.broadcasted_iota(jnp.int32, (1, SIDE, lanes), 1)
        total = None
        for k in range(1, WIDTH + 1):
            weight = jnp.where(masks(line, k), WEIGHTS[k - 1], 0.0)
            term = weight * pltpu.roll(halo, shifts(k), 1)
            total = term if total is None else total + term
        side_out[...] = side_out[...] + cy_ref[...] * total

    @pl.when(place.y == 0)
    def _():
        along_y(lambda k: SIDE - k, lambda line, k: line >= SIDE - k)

    @pl.when(place.y != 0)
    def _():
        along_y(lambda k: k, lambda line, k: line < k)

    def corners(low_out, high_out):
        low_out[:, pl.ds(block, SIDE)] = side_out[pl.ds(0, WIDTH)]
        high_out[:, pl.ds(block, SIDE)] = side_out[pl.ds(count_x - WIDTH, WIDTH)]

    @pl.when(place.even)
    def _():
        corners(far_out, near_out)

    @pl.when(jnp.logical_not(place.even))
    def _():
        corners(near_out, far_out)


def halo_step(parts, halos):
    count_y, (count_x, _, count_z) = parts[0].shape[1], parts[1].shape

    def kernel(*refs):
        add_halo(Place(), refs[:4], refs[4:7], refs[7:])

    return pl.pallas_call(
        kernel,
        out_shape=face_shapes(count_x, count_y, count_z),
        in_specs=[spec(pltpu.VMEM)] * 7,
        out_specs=(spec(pltpu.VMEM),) * 3,
        compiler_params=params(8),
        cost_estimate=cost(16 * count_y * count_z, 10, 6),
        name="halo_step",
    )(*parts, *halos)


def pack_matrix(window, count_z):
    half = count_z // GROUP
    size = GROUP * count_z
    row, column = np.arange(size)[:, None], np.arange(size)[None, :]
    row_b, row_z = row // count_z, row % count_z
    kind = column // count_z
    parity = kind % 2
    lane_b, lane_i = (column % count_z) // half, column % half
    main = (row_b == lane_b) & (row_z == 2 * (half * window + lane_i) + parity)
    wanted_b = (lane_b + (GROUP - 1 if window == 0 else 1)) % GROUP
    wanted_z = 2 * (half * (1 - window) + lane_i) + parity
    useful = lane_i < REACH if window == 0 else lane_i >= half - REACH
    edge = (row_b == wanted_b) & (row_z == wanted_z) & useful
    return np.where(kind < 2, main, edge).astype(np.float32)


def packed(even_ref, matrix_ref):
    count_b, _, count_z = even_ref.shape
    rows = [
        jnp.concatenate([even_ref[b + i] for i in range(GROUP)], axis=1)
        for b in range(0, count_b, GROUP)
    ]
    result = exact_dot(jnp.concatenate(rows, axis=0), matrix_ref[...])
    return [result[:, kind * count_z : (kind + 1) * count_z] for kind in range(4)]


def pack_own(even, matrix):
    count_b, count_a, count_z = even.shape
    total_rows = count_b // GROUP * count_a

    def kernel(even_ref, matrix_ref, out_ref):
        for kind, part in enumerate(packed(even_ref, matrix_ref)):
            out_ref[kind] = part

    return pl.pallas_call(
        kernel,
        out_shape=shape(4, total_rows, count_z),
        in_specs=[spec(pltpu.VMEM)] * 2,
        out_specs=spec(pltpu.VMEM),
        compiler_params=params(8),
        cost_estimate=cost(count_b * count_a * count_z, 1024, 4),
        name="pack_own",
    )(even, matrix)


def edge_slots(count_a, groups, count_z):
    fits = count_z // GROUP // REACH
    slots = []
    for index in range(2 * groups):
        slots.append((index // groups, index % groups, index // fits * count_a, index % fits * REACH))
    return slots, -(-2 * groups // fits) * count_a


def send_into(even_ref, matrix_ref, out_ref):
    count_b, count_a, count_z = even_ref.shape
    groups = count_b // GROUP
    total_rows = groups * count_a
    parts = packed(even_ref, matrix_ref)
    out_ref[pl.ds(0, total_rows), :] = parts[0]
    out_ref[pl.ds(total_rows, total_rows), :] = parts[1]
    slots, _ = edge_slots(count_a, groups, count_z)
    sums = {}
    for parity, g, row, shift in slots:
        part = parts[2 + parity][g * count_a : (g + 1) * count_a]
        part = pltpu.roll(part, shift, 1) if shift else part
        sums[row] = sums[row] + part if row in sums else part
    for row, part in sums.items():
        out_ref[pl.ds(2 * total_rows + row, count_a), :] = part


def sent_shape(count_a, count_b, count_z):
    groups = count_b // GROUP
    _, extra = edge_slots(count_a, groups, count_z)
    return shape(2 * groups * count_a + extra, count_z)


def last_step(flag, even_before, current, parts, near, side, matrix):
    count_x, count_y, count_z = current.shape
    count_a, count_b = count_x // 2, count_y // 2

    def kernel(
        flag_ref, even_ref, current_ref, qx_ref, qy_ref, cx_ref, cy_ref, near_ref, side_ref,
        matrix_ref, final_ref, late_ref, sent_ref, far_out, near_out, side_out,
    ):
        place = Place()
        add_halo(
            place, (qx_ref, qy_ref, cx_ref, cy_ref), (None, near_ref, side_ref),
            (far_out, near_out, side_out),
        )
        low, high = pl.ds(0, WIDTH), pl.ds(count_x - WIDTH, WIDTH)

        @pl.when(place.even)
        def _():
            final_ref[high] = near_out[...]
            final_ref[low] = far_out[...]

        @pl.when(jnp.logical_not(place.even))
        def _():
            final_ref[low] = near_out[...]
            final_ref[high] = far_out[...]

        final_ref[:, pl.ds(place.block(count_y), SIDE)] = side_out[...]
        wants_last = jnp.broadcast_to(flag_ref[0:1, :], (count_a, count_z)) > 0.5
        for b in range(count_b):
            late_ref[b] = jnp.where(
                wants_last, even_rows(final_ref, 0, 0, count_a, b), even_ref[b]
            )
        send_into(late_ref, matrix_ref, sent_ref)

    slab, _, side_shape = face_shapes(count_x, count_y, count_z)
    return pl.pallas_call(
        kernel,
        out_shape=(
            shape(*current.shape),
            shape(count_b, count_a, count_z),
            sent_shape(count_a, count_b, count_z),
        ),
        in_specs=[spec(pltpu.VMEM)] * 10,
        out_specs=(spec(pltpu.VMEM),) * 3,
        scratch_shapes=[
            pltpu.VMEM(slab.shape, F32),
            pltpu.VMEM(slab.shape, F32),
            pltpu.VMEM(side_shape.shape, F32),
        ],
        input_output_aliases={2: 0},
        compiler_params=params(12),
        cost_estimate=cost(count_x * count_y * count_z, 10, 3),
        name="last_step",
    )(flag, even_before, current, *parts, near, side, matrix)


def far_rows(count_b):
    return -(-2 * (count_b // GROUP) // 16) * 16


def last_far(flag, final, late, cx, far, matrix):
    count_x, count_y, count_z = final.shape
    count_b, count_a, _ = late.shape
    rows, pair = far_rows(count_b), WIDTH // 2

    def kernel(
        flag_ref, final_in, late_in, cx_ref, far_ref, matrix_ref, final_ref, late_ref, sent_ref, lhs,
    ):
        place = Place()
        wants_last = jnp.broadcast_to(flag_ref[0:1, :], (1, count_z)) > 0.5
        lhs[...] = jnp.zeros_like(lhs)

        def correct(first_x, first_c, first_a, terms):
            for r in range(WIDTH):
                final_ref[first_x + r] = final_ref[first_x + r] + cx_ref[first_c + r] * terms(
                    far_ref, r
                )
            for b in range(count_b):
                for i in range(pair):
                    value = jnp.where(
                        wants_last,
                        final_ref[first_x + 2 * i, pl.ds(2 * b, 1), :],
                        late_ref[b, pl.ds(first_a + i, 1), :],
                    )
                    late_ref[b, pl.ds(first_a + i, 1), :] = value
                    lanes = pl.ds(b % GROUP * count_z, count_z)
                    lhs[pl.ds(b // GROUP * pair + i, 1), lanes] = value

        @pl.when(place.even)
        def _():
            correct(0, 0, 0, low_terms)

        @pl.when(jnp.logical_not(place.even))
        def _():
            correct(count_x - WIDTH, WIDTH, count_a - pair, high_terms)

        result = exact_dot(lhs[...], matrix_ref[...])
        parts = [result[:, kind * count_z : (kind + 1) * count_z] for kind in range(4)]
        sent_ref[pl.ds(0, rows), :] = parts[0]
        sent_ref[pl.ds(rows, rows), :] = parts[1]
        sent_ref[pl.ds(2 * rows, rows), :] = parts[2] + pltpu.roll(parts[3], REACH, 1)

    return pl.pallas_call(
        kernel,
        out_shape=(shape(*final.shape), shape(*late.shape), shape(3 * rows, count_z)),
        in_specs=[spec(pltpu.VMEM)] * 6,
        out_specs=(spec(pltpu.VMEM),) * 3,
        scratch_shapes=[pltpu.VMEM((rows, GROUP * count_z), F32)],
        input_output_aliases={1: 0, 2: 1},
        compiler_params=params(12),
        cost_estimate=cost(WIDTH * count_y * count_z, 20, 3),
        name="last_far",
    )(flag, final, late, cx, far, matrix)


def write_out(level):
    def kernel(level_ref, out_ref, sem):
        copy = pltpu.make_async_copy(level_ref, out_ref, sem)
        copy.start()
        copy.wait()

    return pl.pallas_call(
        kernel,
        out_shape=shape(*level.shape),
        in_specs=[spec(pltpu.VMEM)],
        out_specs=spec(pltpu.HBM),
        scratch_shapes=[pltpu.SemaphoreType.DMA],
        compiler_params=params(4),
        cost_estimate=cost(level.size, 0, 2),
        name="write_out",
    )(level)


CODE_BITS = 5
PER_CODE = 6


def lag_image(count_a, lags, own, other, extra=None, before=None):
    _, total_rows, count_z = own.shape
    groups = total_rows // count_a
    half = count_z // GROUP
    last = before is not None
    count_h = before.shape[0] if last else lags.shape[0]
    codes = -(-count_h // PER_CODE)
    pair = WIDTH // 2

    def kernel(*refs):
        refs = list(refs)
        take = lambda count: [refs.pop(0) for _ in range(count)]
        lags_ref, own_ref, other_ref = take(3)
        if last:
            extra_ref, before_ref = take(2)
        (out_ref,) = take(1)
        if not last:
            (codes_ref,) = take(1)
        mains, edges = take(2)
        if last:
            store, sem = take(2)
        else:
            store = out_ref
            lag_of, sem = take(2)
        place = Place()
        if last:
            packed_lags = [lags_ref[k : k + 1, :][0, 0] for k in range(codes)]
            mask = (1 << CODE_BITS) - 1
            lag_list = [
                ((packed_lags[h // PER_CODE] >> (h % PER_CODE * CODE_BITS)) & mask) - LAGMAX
                for h in range(count_h)
            ]
        else:
            copy = pltpu.make_async_copy(lags_ref, lag_of, sem)
            copy.start()
        is_source = place.field == 0

        def useful(rows):
            lane = lax.broadcasted_iota(jnp.int32, (rows, count_z), 1) % half
            return jnp.where(is_source, lane, half - 1 - lane) < REACH

        slots, _ = edge_slots(count_a, groups, count_z)
        for parity in range(2):
            mains[parity] = other_ref[pl.ds(parity * total_rows, total_rows), :]
        for parity, g, row, shift in slots:
            part = other_ref[pl.ds(2 * total_rows + row, count_a), :]
            part = pltpu.roll(part, count_z - shift, 1) if shift else part
            edges[parity, pl.ds(g * count_a, count_a), :] = jnp.where(useful(count_a), part, 0.0)
        if last:
            rows = extra_ref.shape[0] // 3
            border = extra_ref[pl.ds(2 * rows, rows), :]
            borders = [
                jnp.where(useful(rows), part, 0.0)
                for part in (border, pltpu.roll(border, count_z - REACH, 1))
            ]

            def overwrite(first_a):
                for g in range(groups):
                    target = pl.ds(g * count_a + first_a, pair)
                    for parity in range(2):
                        mains[parity, target, :] = extra_ref[
                            pl.ds(parity * rows + g * pair, pair), :
                        ]
                        edges[parity, target, :] = borders[parity][g * pair : (g + 1) * pair]

            pl.when(place.even)(lambda: overwrite(0))
            pl.when(jnp.logical_not(place.even))(lambda: overwrite(count_a - pair))
        else:
            copy.wait()
            lag_list = [lag_of[h] for h in range(count_h)]
            for k in range(codes):
                code = jnp.int32(0)
                for h in range(k * PER_CODE, min((k + 1) * PER_CODE, count_h)):
                    code = code | ((lag_list[h] + LAGMAX) << (h % PER_CODE * CODE_BITS))
                codes_ref[k : k + 1, :] = jnp.full((1, count_z), code, jnp.int32)
        lane = lax.broadcasted_iota(jnp.int32, (1, count_z), 1) % half

        def moved(main, edge, shift):
            mask = (lane < shift) | (lane >= half + shift)
            return pltpu.roll(jnp.where(mask, edge, main), (count_z - shift) & (count_z - 1), 1)

        for h, lag in enumerate(lag_list):
            parity = lag & 1
            source_shift = -((lag + parity) >> 1)
            receiver_shift = (lag - parity) >> 1
            own_shift = jnp.where(is_source, source_shift, receiver_shift)
            other_shift = jnp.where(is_source, receiver_shift, source_shift)
            product = moved(own_ref[parity], own_ref[2 + parity], own_shift)
            product = product * moved(mains[parity], edges[parity], other_shift)
            for g in range(groups):
                part = product[g * count_a : (g + 1) * count_a]
                lanes = pl.ds(g * count_z, count_z)
                if last:
                    part = part + before_ref[h, :, lanes]
                store[h, :, lanes] = part
            if last:
                pltpu.make_async_copy(store.at[h], out_ref.at[h], sem).start()
        if last:
            pltpu.make_async_copy(store, out_ref, sem).wait()

    image = shape(count_h, count_a, groups * count_z)
    operands = [lags, own, other] + ([extra, before] if last else [])
    scratch = [pltpu.VMEM((2, total_rows, count_z), F32)] * 2
    scratch.append(pltpu.VMEM(image.shape, F32) if last else pltpu.SMEM((count_h,), jnp.int32))
    scratch.append(pltpu.SemaphoreType.DMA)
    return pl.pallas_call(
        kernel,
        out_shape=image if last else (image, shape(8, count_z, dtype=jnp.int32)),
        in_specs=[spec(pltpu.VMEM if last else pltpu.HBM)]
        + [spec(pltpu.VMEM)] * (len(operands) - 1),
        out_specs=spec(pltpu.HBM) if last else (spec(pltpu.VMEM),) * 2,
        scratch_shapes=scratch,
        compiler_params=params(12),
        cost_estimate=cost(count_h * total_rows * count_z, 10, 2),
        name="last_image" if last else "early_image",
    )(*operands)


def body(
    field_now,
    field_prev,
    courant_squared,
    source_cells,
    source_wave,
    receiver_cells,
    receiver_wave,
    snapshot_steps,
    lag_offsets,
):
    count_x, _, count_z = field_now.shape
    loop_size = lax.axis_size("gx")
    half_size = loop_size // 2
    turn = loop_size // 4
    assert lax.axis_size("gy") == 2 and half_size % 2 == 0

    slabs = [(i - turn) % loop_size % half_size for i in range(loop_size)]

    def pairs(odd):
        found = []
        for i, slab in enumerate(slabs):
            if slab % 2 == odd and slab != half_size - 1:
                j = (i + 1) % loop_size
                found += [(i, j), (j, i)]
        return found

    near_pairs, far_pairs = pairs(0), pairs(1)
    across = [(i, (i + half_size) % loop_size) for i in range(loop_size)]

    def send_far(far):
        return lax.ppermute(far, "gx", far_pairs)

    def send_near(near, side):
        near = lax.ppermute(near, "gx", near_pairs)
        return near, lax.ppermute(side, "gy", [(0, 1), (1, 0)])

    def exchange(faces):
        far, near, side = faces
        return (send_far(far), *send_near(near, side))

    matrices = jnp.asarray(
        np.stack([pack_matrix(window, count_z) for window in (0, 1)]), dtype=BF16
    )
    raw = (source_cells, source_wave, receiver_cells, receiver_wave)
    field_now, field_prev, courant_squared, matrices, snapshot_steps, lag_offsets, *raw = (
        pltpu.with_memory_space_constraint(array, pltpu.HBM)
        for array in (
            field_now, field_prev, courant_squared, matrices, snapshot_steps, lag_offsets, *raw
        )
    )
    *faces, whole0 = first_faces(field_now)
    halos = exchange(faces)
    next1, qx, qy, courant, cx, cy, points, waves = inner_step(
        0, raw, None, whole0, None, field_prev, courant_squared
    )
    faces = halo_step((qx, qy, cx, cy), halos)
    halos = exchange(faces)
    next2, qx, qy, whole1 = inner_step(1, points, waves, next1, faces, whole0, courant)
    faces = halo_step((qx, qy, cx, cy), halos)
    halos = exchange(faces)
    next3, qx, qy, whole2, own_early, sent_early, own_matrix, sent_matrix, flag = inner_step(
        2, points, waves, next2, faces, whole1, courant, snapshot_steps, matrices
    )
    other_early = lax.ppermute(sent_early, "gx", across)
    faces = halo_step((qx, qy, cx, cy), halos)
    far, near, side = exchange(faces)
    next4, qx, qy, even3 = inner_step(3, points, waves, next3, faces, whole2, courant)
    final, late, sent_late = last_step(
        flag, even3, next4, (qx, qy, cx, cy), near, side, sent_matrix
    )
    other_late = lax.ppermute(sent_late, "gx", across)
    partial, codes = lag_image(count_x // 2, lag_offsets, own_early, other_early)
    final, late, sent_far = last_far(flag, final, late, cx, far, sent_matrix)
    extra = lax.ppermute(sent_far, "gx", across)
    own_late = pack_own(late, own_matrix)
    image = lag_image(count_x // 2, codes, own_late, other_late, extra, partial)
    return write_out(final), jnp.transpose(image, (1, 0, 2))


def solution(mesh):
    placed = (
        P(("shots", "gx"), "gy", None),
        P(("shots", "gx"), "gy", None),
        P("gx", "gy", None),
        P(None, "shots"),
        P(None, "shots"),
        P(None, "shots"),
        P(None, "shots"),
        P("shots", None),
        P(),
    )
    return jax.shard_map(
        body,
        mesh=mesh,
        in_specs=placed,
        out_specs=(P(("shots", "gx"), "gy", None), P(("shots", "gx"), None, "gy")),
        check_vma=False,
    )
```

```python
import jax
import jax.numpy as jnp
import numpy as np
from jax import lax
from jax.experimental import pallas as pl
from jax.experimental.pallas import tpu as pltpu
from jax.sharding import PartitionSpec as P

STEPS = 4
WIDTH = 4
LAGMAX = 8
REACH = LAGMAX // 2
GROUP = 4
SIDE = 8

SCALE = 5040.0
BAND = (8064.0, -1008.0, 128.0, -9.0)
CENTRE = 3.0 * (-205.0 / 72.0)
WEIGHTS = (1.6, -0.2, 8.0 / 315.0, -1.0 / 560.0)

F32 = jnp.float32
BF16 = jnp.bfloat16


def shape(*dims, dtype=F32):
    return jax.ShapeDtypeStruct(dims, dtype)


def params(megabytes):
    return pltpu.CompilerParams(vmem_limit_bytes=megabytes << 20)


def spec(space):
    return pl.BlockSpec(memory_space=space)


def cost(count, flops_each, arrays):
    return pl.CostEstimate(
        flops=int(count * flops_each), bytes_accessed=int(4 * count * arrays), transcendentals=0
    )


def split3(values):
    high = values.astype(BF16)
    rest = values - high.astype(F32)
    middle = rest.astype(BF16)
    low = (rest - middle.astype(F32)).astype(BF16)
    return high, middle, low


def exact_dot(values, matrix):
    rows = values.shape[0]
    stacked = jnp.concatenate(split3(values), axis=0)
    result = jnp.dot(stacked, matrix, preferred_element_type=F32)
    return (result[2 * rows :] + result[rows : 2 * rows]) + result[:rows]


class Place:
    def __init__(self):
        loop_size = lax.axis_size("gx")
        self.half = loop_size // 2
        relative = lax.rem(lax.axis_index("gx") + loop_size - loop_size // 4, loop_size)
        self.field = relative // self.half
        self.slab = lax.rem(relative, self.half)
        self.even = lax.rem(self.slab, 2) == 0
        self.y = lax.axis_index("gy")

    def block(self, count_y):
        return pl.multiple_of((1 - self.y) * (count_y - SIDE), SIDE)


def first_faces(field):
    count_x, count_y, count_z = field.shape
    top = count_x - WIDTH

    def kernel(field_ref, far_ref, near_ref, side_ref, whole_ref, sems):
        place = Place()
        far = jnp.where(place.even, 0, top)
        sources = [
            field_ref.at[pl.ds(far, WIDTH)],
            field_ref.at[pl.ds(top - far, WIDTH)],
            field_ref.at[:, pl.ds(place.block(count_y), SIDE)],
            field_ref,
        ]
        copies = [
            pltpu.make_async_copy(source, target, sems.at[index])
            for index, (source, target) in enumerate(
                zip(sources, (far_ref, near_ref, side_ref, whole_ref))
            )
        ]
        for copy in copies:
            copy.start()
        for copy in copies:
            copy.wait()

    return pl.pallas_call(
        kernel,
        out_shape=(*face_shapes(count_x, count_y, count_z), shape(*field.shape)),
        in_specs=[spec(pltpu.HBM)],
        out_specs=(spec(pltpu.VMEM),) * 4,
        scratch_shapes=[pltpu.SemaphoreType.DMA((4,))],
        compiler_params=params(8),
        name="first_faces",
    )(field)


def face_shapes(count_x, count_y, count_z):
    slab = shape(WIDTH, count_y, count_z)
    return slab, slab, shape(count_x, SIDE, count_z)


def even_rows(level_ref, offset_x, offset_y, count_a, b):
    rows, stride, lanes = level_ref.shape
    flat = level_ref.reshape(rows * stride, lanes)
    start = offset_x * stride + offset_y + 2 * b
    return flat[pl.ds(start, count_a, stride=2 * stride), :]


def inner_step(number, points, waves, current, faces, previous, courant, snapshots=None, matrices=None):
    count_x, count_y, count_z = current.shape
    count_a, count_b = count_x // 2, count_y // 2
    first = faces is None
    last = number == STEPS - 1
    snapshot = number == STEPS // 2
    ahead = number == 1
    if last:
        count_j = 0
    elif first:
        count_j = -(-max(array.shape[1] for array in points) // 128) * 128
    else:
        count_j = points.shape[1]

    def kernel(*refs):
        refs = list(refs)
        take = lambda count: [refs.pop(0) for _ in range(count)]
        if first:
            raw_refs = take(4)
        elif last:
            (added_ref,) = take(1)
        else:
            points_ref, waves_ref = take(2)
        (current_ref,) = take(1)
        if not first:
            far_ref, near_ref, side_ref = take(3)
        previous_ref, courant_ref = take(2)
        if snapshot:
            steps_ref, matrices_ref = take(2)
        next_ref, qx_ref, qy_ref = take(3)
        if first:
            kept_ref, cx_ref, cy_ref, points_ref, waves_ref = take(5)
        elif not last:
            (whole_ref,) = take(1)
        if snapshot:
            own_out, sent_out, own_matrix, sent_matrix, flag_ref = take(5)
        if ahead:
            (ahead_ref,) = take(1)
        if last:
            (even_ref,) = take(1)
        padded, zpart, addpart = take(3)
        if last:
            addpart = added_ref
        if first:
            before_ref = take(1)[0]
            raw_refs_in, raw_refs = raw_refs, take(4)
            (sems,) = take(1)
        if snapshot:
            even_ref, wanted, sems = take(3)

        place = Place()
        block = place.block(count_y)
        rows, columns = pl.ds(WIDTH, count_x), pl.ds(SIDE, count_y)
        if first:
            copies = [
                pltpu.make_async_copy(source, target, sems.at[index])
                for index, (source, target) in enumerate(
                    zip(
                        (*raw_refs_in, previous_ref, courant_ref),
                        (*raw_refs, before_ref, kept_ref),
                    )
                )
            ]
            for copy in copies:
                copy.start()
        else:
            before_ref, kept_ref = previous_ref, courant_ref
        if snapshot:
            copies = [
                pltpu.make_async_copy(steps_ref, wanted, sems.at[0]),
                pltpu.make_async_copy(matrices_ref.at[place.field], own_matrix, sems.at[1]),
                pltpu.make_async_copy(matrices_ref.at[1 - place.field], sent_matrix, sems.at[2]),
            ]
            for copy in copies:
                copy.start()

        zero_x = jnp.zeros((WIDTH, count_y + 2 * SIDE, count_z), F32)
        padded[pl.ds(0, WIDTH)] = zero_x
        padded[pl.ds(count_x + WIDTH, WIDTH)] = zero_x
        zero_y = jnp.zeros((count_x, SIDE, count_z), F32)
        padded[rows, pl.ds(0, SIDE)] = zero_y
        padded[rows, pl.ds(count_y + SIDE, SIDE)] = zero_y

        padded[rows, columns] = current_ref[...]
        if not first:
            low, high = pl.ds(WIDTH, WIDTH), pl.ds(count_x, WIDTH)

            @pl.when(place.even)
            def _():
                padded[high, columns] = near_ref[...]
                padded[low, columns] = far_ref[...]

            @pl.when(jnp.logical_not(place.even))
            def _():
                padded[low, columns] = near_ref[...]
                padded[high, columns] = far_ref[...]

            padded[rows, pl.ds(pl.multiple_of(block + SIDE, SIDE), SIDE)] = side_ref[...]

        if first:
            for copy in copies[:4]:
                copy.wait()
            points_ref[...] = jnp.full(points_ref.shape, -1, jnp.int32)
            waves_ref[...] = jnp.zeros(waves_ref.shape, F32)

            def choose(cells_ref, wave_ref):
                count = cells_ref.shape[1]
                points_ref[pl.ds(0, 3), pl.ds(0, count)] = cells_ref[...]
                waves_ref[pl.ds(0, STEPS), pl.ds(0, count)] = wave_ref[...]

            @pl.when(place.field == 0)
            def _():
                choose(raw_refs[0], raw_refs[1])

            @pl.when(place.field != 0)
            def _():
                choose(raw_refs[2], raw_refs[3])

        if not last:
            px = points_ref[0:1, :] - place.slab * count_x
            py = points_ref[1:2, :] - place.y * count_y
            inside = (px >= 0) & (px < count_x) & (py >= 0) & (py < count_y)
            home = jnp.where(inside, px * count_y + py, -1)
            at_z = (
                lax.broadcasted_iota(jnp.int32, (count_z, count_j), 0) == points_ref[2:3, :]
            )

            def spread_of(step):
                return split3(jnp.where(at_z, waves_ref[step : step + 1, :], 0.0))

            spreads = [(addpart, spread_of(number))]
            if ahead:
                spreads.append((ahead_ref, spread_of(STEPS - 1)))

        gap = jnp.abs(
            lax.broadcasted_iota(jnp.int32, (count_z, count_z), 0)
            - lax.broadcasted_iota(jnp.int32, (count_z, count_z), 1)
        )
        band = jnp.zeros((count_z, count_z), F32)
        for offset, weight in enumerate(BAND, 1):
            band = jnp.where(gap == offset, weight, band)
        band = band.astype(BF16)

        chunk = 8

        def multiply(index, _):
            start = pl.multiple_of(index * chunk, chunk)
            values = padded[pl.ds(start + WIDTH, chunk), columns]
            zpart[pl.ds(start, chunk)] = exact_dot(
                values.reshape(chunk * count_y, count_z), band
            ).reshape(chunk, count_y, count_z)
            if last:
                return 0
            here = start * count_y + lax.broadcasted_iota(
                jnp.int32, (chunk * count_y, count_j), 0
            )
            hit = jnp.where(here == home, 1.0, 0.0).astype(BF16)
            for target, spread in spreads:
                added = [
                    lax.dot_general(
                        hit, part, (((1,), (1,)), ((), ())), preferred_element_type=F32
                    )
                    for part in spread
                ]
                added = (added[2] + added[1]) + added[0]
                target[pl.ds(start, chunk)] = added.reshape(chunk, count_y, count_z)
            return 0

        lax.fori_loop(0, count_x // chunk, multiply, 0)
        if first:
            for copy in copies[4:]:
                copy.wait()

        def row(x, _):
            middle = padded[x + WIDTH, columns]
            total = CENTRE * middle + (1.0 / SCALE) * zpart[x]
            for offset, weight in enumerate(WEIGHTS, 1):
                paired = padded[x + WIDTH + offset, columns] + padded[x + WIDTH - offset, columns]
                paired = paired + (
                    padded[x + WIDTH, pl.ds(SIDE + offset, count_y)]
                    + padded[x + WIDTH, pl.ds(SIDE - offset, count_y)]
                )
                total = total + weight * paired
            if not first and not last:
                whole_ref[x] = middle
            next_ref[x] = (2.0 * middle - before_ref[x] + kept_ref[x] * total) + addpart[x]
            return 0

        lax.fori_loop(0, count_x, row, 0, unroll=4)

        qx_ref[pl.ds(0, WIDTH)] = next_ref[pl.ds(0, WIDTH)]
        qx_ref[pl.ds(WIDTH, WIDTH)] = next_ref[pl.ds(count_x - WIDTH, WIDTH)]
        qy_ref[...] = next_ref[:, pl.ds(block, SIDE)]
        if first:
            cx_ref[pl.ds(0, WIDTH)] = kept_ref[pl.ds(0, WIDTH)]
            cx_ref[pl.ds(WIDTH, WIDTH)] = kept_ref[pl.ds(count_x - WIDTH, WIDTH)]
            cy_ref[...] = kept_ref[:, pl.ds(block, SIDE)]
        if last:
            for b in range(count_b):
                even_ref[b] = even_rows(padded, WIDTH, SIDE, count_a, b)
        if snapshot:
            for copy in copies:
                copy.wait()
            flag_ref[...] = jnp.where(
                wanted[place.field, 1] == STEPS, jnp.ones(flag_ref.shape, F32), 0.0
            )
            earlier = wanted[place.field, 0] == number - 1

            @pl.when(earlier)
            def _():
                for b in range(count_b):
                    even_ref[b] = even_rows(previous_ref, 0, 0, count_a, b)

            @pl.when(jnp.logical_not(earlier))
            def _():
                for b in range(count_b):
                    even_ref[b] = even_rows(padded, WIDTH, SIDE, count_a, b)

            for kind, part in enumerate(packed(even_ref, own_matrix)):
                own_out[kind] = part
            send_into(even_ref, sent_matrix, sent_out)

    full = shape(count_x, count_y, count_z)
    slab, side = shape(2 * WIDTH, count_y, count_z), shape(count_x, SIDE, count_z)
    even = shape(count_b, count_a, count_z)
    outs = [full, slab, side]
    if first:
        outs += [full, slab, side, shape(8, count_j, dtype=jnp.int32), shape(8, count_j)]
    elif not last:
        outs.append(full)
    if snapshot:
        size = GROUP * count_z
        outs += [
            shape(4, count_b // GROUP * count_a, count_z),
            sent_shape(count_a, count_b, count_z),
            shape(size, size, dtype=BF16),
            shape(size, size, dtype=BF16),
            shape(8, count_z),
        ]
    if ahead:
        outs.append(full)
    if last:
        outs.append(even)
    place_of = spec(pltpu.HBM) if first else spec(pltpu.VMEM)
    if first:
        operands = [*points, current]
    elif last:
        operands = [points, current]
    else:
        operands = [points, waves, current]
    specs = [place_of] * (len(operands) - 1) + [spec(pltpu.VMEM)]
    if not first:
        operands += list(faces)
        specs += [spec(pltpu.VMEM)] * 3
    operands += [previous, courant]
    specs += [place_of] * 2
    scratch = [
        pltpu.VMEM((count_x + 2 * WIDTH, count_y + 2 * SIDE, count_z), F32),
        pltpu.VMEM(full.shape, F32),
        pltpu.VMEM(full.shape, F32),
    ]
    if first:
        scratch.append(pltpu.VMEM(full.shape, F32))
        scratch += [pltpu.VMEM(array.shape, array.dtype) for array in points]
        scratch.append(pltpu.SemaphoreType.DMA((6,)))
    if snapshot:
        operands += [snapshots, matrices]
        specs += [spec(pltpu.HBM)] * 2
        scratch += [
            pltpu.VMEM(even.shape, F32),
            pltpu.SMEM(snapshots.shape, jnp.int32),
            pltpu.SemaphoreType.DMA((3,)),
        ]
    return pl.pallas_call(
        kernel,
        out_shape=tuple(outs),
        in_specs=specs,
        out_specs=(spec(pltpu.VMEM),) * len(outs),
        scratch_shapes=scratch,
        compiler_params=params(20),
        cost_estimate=cost(count_x * count_y * count_z, 60, 6),
    )(*operands)


def low_terms(halo_ref, r):
    total = None
    for k in range(r + 1, WIDTH + 1):
        term = WEIGHTS[k - 1] * halo_ref[WIDTH + r - k]
        total = term if total is None else total + term
    return total


def high_terms(halo_ref, r):
    total = None
    for k in range(WIDTH - r, WIDTH + 1):
        term = WEIGHTS[k - 1] * halo_ref[r + k - WIDTH]
        total = term if total is None else total + term
    return total


def add_halo(place, parts, halos, outs):
    qx_ref, qy_ref, cx_ref, cy_ref = parts
    far_in, near_in, side_in = halos
    far_out, near_out, side_out = outs
    count_y, count_x = qx_ref.shape[1], qy_ref.shape[0]
    block = place.block(count_y)

    def along_x(low_in, high_in, low_out, high_out):
        for r in range(WIDTH):
            low, high = qx_ref[r], qx_ref[WIDTH + r]
            if low_in is not None:
                low = low + cx_ref[r] * low_terms(low_in, r)
            if high_in is not None:
                high = high + cx_ref[WIDTH + r] * high_terms(high_in, r)
            low_out[r], high_out[r] = low, high
        side_out[pl.ds(0, WIDTH)] = low_out[:, pl.ds(block, SIDE)]
        side_out[pl.ds(count_x - WIDTH, WIDTH)] = high_out[:, pl.ds(block, SIDE)]

    inner = pl.ds(WIDTH, count_x - 2 * WIDTH)
    side_out[inner] = qy_ref[inner]

    @pl.when(place.even)
    def _():
        along_x(far_in, near_in, far_out, near_out)

    @pl.when(jnp.logical_not(place.even))
    def _():
        along_x(near_in, far_in, near_out, far_out)

    def along_y(shifts, masks):
        halo = side_in[...]
        lanes = halo.shape[2]
        line = lax.broadcasted_iota(jnp.int32, (1, SIDE, lanes), 1)
        total = None
        for k in range(1, WIDTH + 1):
            weight = jnp.where(masks(line, k), WEIGHTS[k - 1], 0.0)
            term = weight * pltpu.roll(halo, shifts(k), 1)
            total = term if total is None else total + term
        side_out[...] = side_out[...] + cy_ref[...] * total

    @pl.when(place.y == 0)
    def _():
        along_y(lambda k: SIDE - k, lambda line, k: line >= SIDE - k)

    @pl.when(place.y != 0)
    def _():
        along_y(lambda k: k, lambda line, k: line < k)

    def corners(low_out, high_out):
        low_out[:, pl.ds(block, SIDE)] = side_out[pl.ds(0, WIDTH)]
        high_out[:, pl.ds(block, SIDE)] = side_out[pl.ds(count_x - WIDTH, WIDTH)]

    @pl.when(place.even)
    def _():
        corners(far_out, near_out)

    @pl.when(jnp.logical_not(place.even))
    def _():
        corners(near_out, far_out)


def halo_step(parts, halos):
    count_y, (count_x, _, count_z) = parts[0].shape[1], parts[1].shape

    def kernel(*refs):
        add_halo(Place(), refs[:4], refs[4:7], refs[7:])

    return pl.pallas_call(
        kernel,
        out_shape=face_shapes(count_x, count_y, count_z),
        in_specs=[spec(pltpu.VMEM)] * 7,
        out_specs=(spec(pltpu.VMEM),) * 3,
        compiler_params=params(8),
        cost_estimate=cost(16 * count_y * count_z, 10, 6),
        name="halo_step",
    )(*parts, *halos)


def pack_matrix(window, count_z):
    half = count_z // GROUP
    size = GROUP * count_z
    row, column = np.arange(size)[:, None], np.arange(size)[None, :]
    row_b, row_z = row // count_z, row % count_z
    kind = column // count_z
    parity = kind % 2
    lane_b, lane_i = (column % count_z) // half, column % half
    main = (row_b == lane_b) & (row_z == 2 * (half * window + lane_i) + parity)
    wanted_b = (lane_b + (GROUP - 1 if window == 0 else 1)) % GROUP
    wanted_z = 2 * (half * (1 - window) + lane_i) + parity
    useful = lane_i < REACH if window == 0 else lane_i >= half - REACH
    edge = (row_b == wanted_b) & (row_z == wanted_z) & useful
    return np.where(kind < 2, main, edge).astype(np.float32)


def packed(even_ref, matrix_ref):
    count_b, _, count_z = even_ref.shape
    rows = [
        jnp.concatenate([even_ref[b + i] for i in range(GROUP)], axis=1)
        for b in range(0, count_b, GROUP)
    ]
    result = exact_dot(jnp.concatenate(rows, axis=0), matrix_ref[...])
    return [result[:, kind * count_z : (kind + 1) * count_z] for kind in range(4)]


def pack_own(even, matrix):
    count_b, count_a, count_z = even.shape
    total_rows = count_b // GROUP * count_a

    def kernel(even_ref, matrix_ref, out_ref):
        for kind, part in enumerate(packed(even_ref, matrix_ref)):
            out_ref[kind] = part

    return pl.pallas_call(
        kernel,
        out_shape=shape(4, total_rows, count_z),
        in_specs=[spec(pltpu.VMEM)] * 2,
        out_specs=spec(pltpu.VMEM),
        compiler_params=params(8),
        cost_estimate=cost(count_b * count_a * count_z, 1024, 4),
        name="pack_own",
    )(even, matrix)


def edge_slots(count_a, groups, count_z):
    fits = count_z // GROUP // REACH
    slots = []
    for index in range(2 * groups):
        slots.append((index // groups, index % groups, index // fits * count_a, index % fits * REACH))
    return slots, -(-2 * groups // fits) * count_a


def send_into(even_ref, matrix_ref, out_ref):
    count_b, count_a, count_z = even_ref.shape
    groups = count_b // GROUP
    total_rows = groups * count_a
    parts = packed(even_ref, matrix_ref)
    out_ref[pl.ds(0, total_rows), :] = parts[0]
    out_ref[pl.ds(total_rows, total_rows), :] = parts[1]
    slots, _ = edge_slots(count_a, groups, count_z)
    sums = {}
    for parity, g, row, shift in slots:
        part = parts[2 + parity][g * count_a : (g + 1) * count_a]
        part = pltpu.roll(part, shift, 1) if shift else part
        sums[row] = sums[row] + part if row in sums else part
    for row, part in sums.items():
        out_ref[pl.ds(2 * total_rows + row, count_a), :] = part


def sent_shape(count_a, count_b, count_z):
    groups = count_b // GROUP
    _, extra = edge_slots(count_a, groups, count_z)
    return shape(2 * groups * count_a + extra, count_z)


def last_step(flag, even_before, current, parts, near, side, matrix):
    count_x, count_y, count_z = current.shape
    count_a, count_b = count_x // 2, count_y // 2

    def kernel(
        flag_ref, even_ref, current_ref, qx_ref, qy_ref, cx_ref, cy_ref, near_ref, side_ref,
        matrix_ref, final_ref, late_ref, sent_ref, far_out, near_out, side_out,
    ):
        place = Place()
        add_halo(
            place, (qx_ref, qy_ref, cx_ref, cy_ref), (None, near_ref, side_ref),
            (far_out, near_out, side_out),
        )
        low, high = pl.ds(0, WIDTH), pl.ds(count_x - WIDTH, WIDTH)

        @pl.when(place.even)
        def _():
            final_ref[high] = near_out[...]
            final_ref[low] = far_out[...]

        @pl.when(jnp.logical_not(place.even))
        def _():
            final_ref[low] = near_out[...]
            final_ref[high] = far_out[...]

        final_ref[:, pl.ds(place.block(count_y), SIDE)] = side_out[...]
        wants_last = jnp.broadcast_to(flag_ref[0:1, :], (count_a, count_z)) > 0.5
        for b in range(count_b):
            late_ref[b] = jnp.where(
                wants_last, even_rows(final_ref, 0, 0, count_a, b), even_ref[b]
            )
        send_into(late_ref, matrix_ref, sent_ref)

    slab, _, side_shape = face_shapes(count_x, count_y, count_z)
    return pl.pallas_call(
        kernel,
        out_shape=(
            shape(*current.shape),
            shape(count_b, count_a, count_z),
            sent_shape(count_a, count_b, count_z),
        ),
        in_specs=[spec(pltpu.VMEM)] * 10,
        out_specs=(spec(pltpu.VMEM),) * 3,
        scratch_shapes=[
            pltpu.VMEM(slab.shape, F32),
            pltpu.VMEM(slab.shape, F32),
            pltpu.VMEM(side_shape.shape, F32),
        ],
        input_output_aliases={2: 0},
        compiler_params=params(12),
        cost_estimate=cost(count_x * count_y * count_z, 10, 3),
        name="last_step",
    )(flag, even_before, current, *parts, near, side, matrix)


def far_rows(count_b):
    return -(-2 * (count_b // GROUP) // 16) * 16


def last_far(flag, final, late, cx, far, matrix):
    count_x, count_y, count_z = final.shape
    count_b, count_a, _ = late.shape
    rows, pair = far_rows(count_b), WIDTH // 2

    def kernel(
        flag_ref, final_in, late_in, cx_ref, far_ref, matrix_ref, final_ref, late_ref, sent_ref, lhs,
    ):
        place = Place()
        wants_last = jnp.broadcast_to(flag_ref[0:1, :], (1, count_z)) > 0.5
        lhs[...] = jnp.zeros_like(lhs)

        def correct(first_x, first_c, first_a, terms):
            for r in range(WIDTH):
                final_ref[first_x + r] = final_ref[first_x + r] + cx_ref[first_c + r] * terms(
                    far_ref, r
                )
            for b in range(count_b):
                for i in range(pair):
                    value = jnp.where(
                        wants_last,
                        final_ref[first_x + 2 * i, pl.ds(2 * b, 1), :],
                        late_ref[b, pl.ds(first_a + i, 1), :],
                    )
                    late_ref[b, pl.ds(first_a + i, 1), :] = value
                    lanes = pl.ds(b % GROUP * count_z, count_z)
                    lhs[pl.ds(b // GROUP * pair + i, 1), lanes] = value

        @pl.when(place.even)
        def _():
            correct(0, 0, 0, low_terms)

        @pl.when(jnp.logical_not(place.even))
        def _():
            correct(count_x - WIDTH, WIDTH, count_a - pair, high_terms)

        result = exact_dot(lhs[...], matrix_ref[...])
        parts = [result[:, kind * count_z : (kind + 1) * count_z] for kind in range(4)]
        sent_ref[pl.ds(0, rows), :] = parts[0]
        sent_ref[pl.ds(rows, rows), :] = parts[1]
        sent_ref[pl.ds(2 * rows, rows), :] = parts[2] + pltpu.roll(parts[3], REACH, 1)

    return pl.pallas_call(
        kernel,
        out_shape=(shape(*final.shape), shape(*late.shape), shape(3 * rows, count_z)),
        in_specs=[spec(pltpu.VMEM)] * 6,
        out_specs=(spec(pltpu.VMEM),) * 3,
        scratch_shapes=[pltpu.VMEM((rows, GROUP * count_z), F32)],
        input_output_aliases={1: 0, 2: 1},
        compiler_params=params(12),
        cost_estimate=cost(WIDTH * count_y * count_z, 20, 3),
        name="last_far",
    )(flag, final, late, cx, far, matrix)


def write_out(level):
    def kernel(level_ref, out_ref, sem):
        copy = pltpu.make_async_copy(level_ref, out_ref, sem)
        copy.start()
        copy.wait()

    return pl.pallas_call(
        kernel,
        out_shape=shape(*level.shape),
        in_specs=[spec(pltpu.VMEM)],
        out_specs=spec(pltpu.HBM),
        scratch_shapes=[pltpu.SemaphoreType.DMA],
        compiler_params=params(4),
        cost_estimate=cost(level.size, 0, 2),
        name="write_out",
    )(level)


CODE_BITS = 5
PER_CODE = 6


def lag_image(count_a, lags, own, other, extra=None, before=None):
    _, total_rows, count_z = own.shape
    groups = total_rows // count_a
    half = count_z // GROUP
    last = before is not None
    count_h = before.shape[0] if last else lags.shape[0]
    codes = -(-count_h // PER_CODE)
    pair = WIDTH // 2

    def kernel(*refs):
        refs = list(refs)
        take = lambda count: [refs.pop(0) for _ in range(count)]
        lags_ref, own_ref, other_ref = take(3)
        if last:
            extra_ref, before_ref = take(2)
        (out_ref,) = take(1)
        if not last:
            (codes_ref,) = take(1)
        mains, edges = take(2)
        if last:
            store, sem = take(2)
        else:
            store = out_ref
            lag_of, sem = take(2)
        place = Place()
        if last:
            packed_lags = [lags_ref[k : k + 1, :][0, 0] for k in range(codes)]
            mask = (1 << CODE_BITS) - 1
            lag_list = [
                ((packed_lags[h // PER_CODE] >> (h % PER_CODE * CODE_BITS)) & mask) - LAGMAX
                for h in range(count_h)
            ]
        else:
            copy = pltpu.make_async_copy(lags_ref, lag_of, sem)
            copy.start()
        is_source = place.field == 0

        def useful(rows):
            lane = lax.broadcasted_iota(jnp.int32, (rows, count_z), 1) % half
            return jnp.where(is_source, lane, half - 1 - lane) < REACH

        slots, _ = edge_slots(count_a, groups, count_z)
        for parity in range(2):
            mains[parity] = other_ref[pl.ds(parity * total_rows, total_rows), :]
        for parity, g, row, shift in slots:
            part = other_ref[pl.ds(2 * total_rows + row, count_a), :]
            part = pltpu.roll(part, count_z - shift, 1) if shift else part
            edges[parity, pl.ds(g * count_a, count_a), :] = jnp.where(useful(count_a), part, 0.0)
        if last:
            rows = extra_ref.shape[0] // 3
            border = extra_ref[pl.ds(2 * rows, rows), :]
            borders = [
                jnp.where(useful(rows), part, 0.0)
                for part in (border, pltpu.roll(border, count_z - REACH, 1))
            ]

            def overwrite(first_a):
                for g in range(groups):
                    target = pl.ds(g * count_a + first_a, pair)
                    for parity in range(2):
                        mains[parity, target, :] = extra_ref[
                            pl.ds(parity * rows + g * pair, pair), :
                        ]
                        edges[parity, target, :] = borders[parity][g * pair : (g + 1) * pair]

            pl.when(place.even)(lambda: overwrite(0))
            pl.when(jnp.logical_not(place.even))(lambda: overwrite(count_a - pair))
        else:
            copy.wait()
            lag_list = [lag_of[h] for h in range(count_h)]
            for k in range(codes):
                code = jnp.int32(0)
                for h in range(k * PER_CODE, min((k + 1) * PER_CODE, count_h)):
                    code = code | ((lag_list[h] + LAGMAX) << (h % PER_CODE * CODE_BITS))
                codes_ref[k : k + 1, :] = jnp.full((1, count_z), code, jnp.int32)
        lane = lax.broadcasted_iota(jnp.int32, (1, count_z), 1) % half

        def moved(main, edge, shift):
            mask = (lane < shift) | (lane >= half + shift)
            return pltpu.roll(jnp.where(mask, edge, main), (count_z - shift) & (count_z - 1), 1)

        for h, lag in enumerate(lag_list):
            parity = lag & 1
            source_shift = -((lag + parity) >> 1)
            receiver_shift = (lag - parity) >> 1
            own_shift = jnp.where(is_source, source_shift, receiver_shift)
            other_shift = jnp.where(is_source, receiver_shift, source_shift)
            product = moved(own_ref[parity], own_ref[2 + parity], own_shift)
            product = product * moved(mains[parity], edges[parity], other_shift)
            for g in range(groups):
                part = product[g * count_a : (g + 1) * count_a]
                lanes = pl.ds(g * count_z, count_z)
                if last:
                    part = part + before_ref[h, :, lanes]
                store[h, :, lanes] = part
            if last:
                pltpu.make_async_copy(store.at[h], out_ref.at[h], sem).start()
        if last:
            pltpu.make_async_copy(store, out_ref, sem).wait()

    image = shape(count_h, count_a, groups * count_z)
    operands = [lags, own, other] + ([extra, before] if last else [])
    scratch = [pltpu.VMEM((2, total_rows, count_z), F32)] * 2
    scratch.append(pltpu.VMEM(image.shape, F32) if last else pltpu.SMEM((count_h,), jnp.int32))
    scratch.append(pltpu.SemaphoreType.DMA)
    return pl.pallas_call(
        kernel,
        out_shape=image if last else (image, shape(8, count_z, dtype=jnp.int32)),
        in_specs=[spec(pltpu.VMEM if last else pltpu.HBM)]
        + [spec(pltpu.VMEM)] * (len(operands) - 1),
        out_specs=spec(pltpu.HBM) if last else (spec(pltpu.VMEM),) * 2,
        scratch_shapes=scratch,
        compiler_params=params(12),
        cost_estimate=cost(count_h * total_rows * count_z, 10, 2),
        name="last_image" if last else "early_image",
    )(*operands)


def body(
    field_now,
    field_prev,
    courant_squared,
    source_cells,
    source_wave,
    receiver_cells,
    receiver_wave,
    snapshot_steps,
    lag_offsets,
):
    count_x, _, count_z = field_now.shape
    loop_size = lax.axis_size("gx")
    half_size = loop_size // 2
    turn = loop_size // 4
    assert lax.axis_size("gy") == 2 and half_size % 2 == 0

    slabs = [(i - turn) % loop_size % half_size for i in range(loop_size)]

    def pairs(odd):
        found = []
        for i, slab in enumerate(slabs):
            if slab % 2 == odd and slab != half_size - 1:
                j = (i + 1) % loop_size
                found += [(i, j), (j, i)]
        return found

    near_pairs, far_pairs = pairs(0), pairs(1)
    across = [(i, (i + half_size) % loop_size) for i in range(loop_size)]

    def send_far(far):
        return lax.ppermute(far, "gx", far_pairs)

    def send_near(near, side):
        near = lax.ppermute(near, "gx", near_pairs)
        return near, lax.ppermute(side, "gy", [(0, 1), (1, 0)])

    def exchange(faces):
        far, near, side = faces
        return (send_far(far), *send_near(near, side))

    matrices = jnp.asarray(
        np.stack([pack_matrix(window, count_z) for window in (0, 1)]), dtype=BF16
    )
    raw = (source_cells, source_wave, receiver_cells, receiver_wave)
    field_now, field_prev, courant_squared, matrices, snapshot_steps, lag_offsets, *raw = (
        pltpu.with_memory_space_constraint(array, pltpu.HBM)
        for array in (
            field_now, field_prev, courant_squared, matrices, snapshot_steps, lag_offsets, *raw
        )
    )
    *faces, whole0 = first_faces(field_now)
    halos = exchange(faces)
    next1, qx, qy, courant, cx, cy, points, waves = inner_step(
        0, raw, None, whole0, None, field_prev, courant_squared
    )
    faces = halo_step((qx, qy, cx, cy), halos)
    halos = exchange(faces)
    next2, qx, qy, whole1, added = inner_step(1, points, waves, next1, faces, whole0, courant)
    faces = halo_step((qx, qy, cx, cy), halos)
    halos = exchange(faces)
    next3, qx, qy, whole2, own_early, sent_early, own_matrix, sent_matrix, flag = inner_step(
        2, points, waves, next2, faces, whole1, courant, snapshot_steps, matrices
    )
    other_early = lax.ppermute(sent_early, "gx", across)
    faces = halo_step((qx, qy, cx, cy), halos)
    far, near, side = exchange(faces)
    next4, qx, qy, even3 = inner_step(3, added, None, next3, faces, whole2, courant)
    final, late, sent_late = last_step(
        flag, even3, next4, (qx, qy, cx, cy), near, side, sent_matrix
    )
    other_late = lax.ppermute(sent_late, "gx", across)
    partial, codes = lag_image(count_x // 2, lag_offsets, own_early, other_early)
    final, late, sent_far = last_far(flag, final, late, cx, far, sent_matrix)
    extra = lax.ppermute(sent_far, "gx", across)
    own_late = pack_own(late, own_matrix)
    image = lag_image(count_x // 2, codes, own_late, other_late, extra, partial)
    return write_out(final), jnp.transpose(image, (1, 0, 2))


def solution(mesh):
    placed = (
        P(("shots", "gx"), "gy", None),
        P(("shots", "gx"), "gy", None),
        P("gx", "gy", None),
        P(None, "shots"),
        P(None, "shots"),
        P(None, "shots"),
        P(None, "shots"),
        P("shots", None),
        P(),
    )
    return jax.shard_map(
        body,
        mesh=mesh,
        in_specs=placed,
        out_specs=(P(("shots", "gx"), "gy", None), P(("shots", "gx"), None, "gy")),
        check_vma=False,
    )
```

```python
import jax
import jax.numpy as jnp
import numpy as np
from jax import lax
from jax.experimental import pallas as pl
from jax.experimental.pallas import tpu as pltpu
from jax.sharding import PartitionSpec as P

STEPS = 4
WIDTH = 4
LAGMAX = 8
REACH = LAGMAX // 2
GROUP = 4
SIDE = 8

SCALE = 5040.0
BAND = (8064.0, -1008.0, 128.0, -9.0)
CENTRE = 3.0 * (-205.0 / 72.0)
WEIGHTS = (1.6, -0.2, 8.0 / 315.0, -1.0 / 560.0)

F32 = jnp.float32
BF16 = jnp.bfloat16


def shape(*dims, dtype=F32):
    return jax.ShapeDtypeStruct(dims, dtype)


def params(megabytes):
    return pltpu.CompilerParams(vmem_limit_bytes=megabytes << 20)


def spec(space):
    return pl.BlockSpec(memory_space=space)


def cost(count, flops_each, arrays):
    return pl.CostEstimate(
        flops=int(count * flops_each), bytes_accessed=int(4 * count * arrays), transcendentals=0
    )


def split3(values):
    high = values.astype(BF16)
    rest = values - high.astype(F32)
    middle = rest.astype(BF16)
    low = (rest - middle.astype(F32)).astype(BF16)
    return high, middle, low


def exact_dot(values, matrix):
    rows = values.shape[0]
    stacked = jnp.concatenate(split3(values), axis=0)
    result = jnp.dot(stacked, matrix, preferred_element_type=F32)
    return (result[2 * rows :] + result[rows : 2 * rows]) + result[:rows]


class Place:
    def __init__(self):
        loop_size = lax.axis_size("gx")
        self.half = loop_size // 2
        relative = lax.rem(lax.axis_index("gx") + loop_size - loop_size // 4, loop_size)
        self.field = relative // self.half
        self.slab = lax.rem(relative, self.half)
        self.even = lax.rem(self.slab, 2) == 0
        self.y = lax.axis_index("gy")

    def block(self, count_y):
        return pl.multiple_of((1 - self.y) * (count_y - SIDE), SIDE)


def first_faces(field):
    count_x, count_y, count_z = field.shape
    top = count_x - WIDTH

    def kernel(field_ref, far_ref, near_ref, side_ref, sems):
        place = Place()
        far = jnp.where(place.even, 0, top)
        sources = [
            field_ref.at[pl.ds(far, WIDTH)],
            field_ref.at[pl.ds(top - far, WIDTH)],
            field_ref.at[:, pl.ds(place.block(count_y), SIDE)],
        ]
        copies = [
            pltpu.make_async_copy(source, target, sems.at[index])
            for index, (source, target) in enumerate(zip(sources, (far_ref, near_ref, side_ref)))
        ]
        for copy in copies:
            copy.start()
        for copy in copies:
            copy.wait()

    return pl.pallas_call(
        kernel,
        out_shape=face_shapes(count_x, count_y, count_z),
        in_specs=[spec(pltpu.HBM)],
        out_specs=(spec(pltpu.VMEM),) * 3,
        scratch_shapes=[pltpu.SemaphoreType.DMA((3,))],
        compiler_params=params(8),
        name="first_faces",
    )(field)


def face_shapes(count_x, count_y, count_z):
    slab = shape(WIDTH, count_y, count_z)
    return slab, slab, shape(count_x, SIDE, count_z)


def even_rows(level_ref, offset_x, offset_y, count_a, b):
    rows, stride, lanes = level_ref.shape
    flat = level_ref.reshape(rows * stride, lanes)
    start = offset_x * stride + offset_y + 2 * b
    return flat[pl.ds(start, count_a, stride=2 * stride), :]


def inner_step(number, points, waves, current, faces, previous, courant, snapshots=None, matrices=None):
    count_x, count_y, count_z = current.shape
    count_a, count_b = count_x // 2, count_y // 2
    first = faces is None
    last = number == STEPS - 1
    snapshot = number == STEPS // 2
    ahead = number == 1
    if last:
        count_j = 0
    elif first:
        count_j = -(-max(array.shape[1] for array in points) // 128) * 128
    else:
        count_j = points.shape[1]

    def kernel(*refs):
        refs = list(refs)
        take = lambda count: [refs.pop(0) for _ in range(count)]
        if first:
            raw_refs = take(4)
        elif last:
            (added_ref,) = take(1)
        else:
            points_ref, waves_ref = take(2)
        (current_ref,) = take(1)
        if not first:
            far_ref, near_ref, side_ref = take(3)
        previous_ref, courant_ref = take(2)
        if snapshot:
            steps_ref, matrices_ref = take(2)
        next_ref, qx_ref, qy_ref = take(3)
        if first:
            kept_ref, cx_ref, cy_ref, points_ref, waves_ref = take(5)
        if not last:
            (whole_ref,) = take(1)
        if snapshot:
            own_out, sent_out, own_matrix, sent_matrix, flag_ref = take(5)
        if ahead:
            (ahead_ref,) = take(1)
        if last:
            (even_ref,) = take(1)
        padded, zpart, addpart = take(3)
        if last:
            addpart = added_ref
        if first:
            before_ref = take(1)[0]
            raw_refs_in, raw_refs = raw_refs, take(4)
            (sems,) = take(1)
        if snapshot:
            even_ref, wanted, sems = take(3)

        place = Place()
        block = place.block(count_y)
        rows, columns = pl.ds(WIDTH, count_x), pl.ds(SIDE, count_y)
        if first:
            copies = [
                pltpu.make_async_copy(source, target, sems.at[index])
                for index, (source, target) in enumerate(
                    zip(
                        (*raw_refs_in, previous_ref, courant_ref),
                        (*raw_refs, before_ref, kept_ref),
                    )
                )
            ]
            for copy in copies:
                copy.start()
        else:
            before_ref, kept_ref = previous_ref, courant_ref
        if snapshot:
            copies = [
                pltpu.make_async_copy(steps_ref, wanted, sems.at[0]),
                pltpu.make_async_copy(matrices_ref.at[place.field], own_matrix, sems.at[1]),
                pltpu.make_async_copy(matrices_ref.at[1 - place.field], sent_matrix, sems.at[2]),
            ]
            for copy in copies:
                copy.start()

        zero_x = jnp.zeros((WIDTH, count_y + 2 * SIDE, count_z), F32)
        padded[pl.ds(0, WIDTH)] = zero_x
        padded[pl.ds(count_x + WIDTH, WIDTH)] = zero_x
        zero_y = jnp.zeros((count_x, SIDE, count_z), F32)
        padded[rows, pl.ds(0, SIDE)] = zero_y
        padded[rows, pl.ds(count_y + SIDE, SIDE)] = zero_y

        padded[rows, columns] = current_ref[...]
        if not first:
            low, high = pl.ds(WIDTH, WIDTH), pl.ds(count_x, WIDTH)

            @pl.when(place.even)
            def _():
                padded[high, columns] = near_ref[...]
                padded[low, columns] = far_ref[...]

            @pl.when(jnp.logical_not(place.even))
            def _():
                padded[low, columns] = near_ref[...]
                padded[high, columns] = far_ref[...]

            padded[rows, pl.ds(pl.multiple_of(block + SIDE, SIDE), SIDE)] = side_ref[...]

        gap = jnp.abs(
            lax.broadcasted_iota(jnp.int32, (count_z, count_z), 0)
            - lax.broadcasted_iota(jnp.int32, (count_z, count_z), 1)
        )
        band = jnp.zeros((count_z, count_z), F32)
        for offset, weight in enumerate(BAND, 1):
            band = jnp.where(gap == offset, weight, band)
        band = band.astype(BF16)

        chunk = 8

        def multiply(index, _):
            start = pl.multiple_of(index * chunk, chunk)
            values = padded[pl.ds(start + WIDTH, chunk), columns]
            zpart[pl.ds(start, chunk)] = exact_dot(
                values.reshape(chunk * count_y, count_z), band
            ).reshape(chunk, count_y, count_z)
            return 0

        lax.fori_loop(0, count_x // chunk, multiply, 0)

        if first:
            for copy in copies[:4]:
                copy.wait()
            points_ref[...] = jnp.full(points_ref.shape, -1, jnp.int32)
            waves_ref[...] = jnp.zeros(waves_ref.shape, F32)

            def choose(cells_ref, wave_ref):
                count = cells_ref.shape[1]
                points_ref[pl.ds(0, 3), pl.ds(0, count)] = cells_ref[...]
                waves_ref[pl.ds(0, STEPS), pl.ds(0, count)] = wave_ref[...]

            @pl.when(place.field == 0)
            def _():
                choose(raw_refs[0], raw_refs[1])

            @pl.when(place.field != 0)
            def _():
                choose(raw_refs[2], raw_refs[3])

        if not last:
            px = points_ref[0:1, :] - place.slab * count_x
            py = points_ref[1:2, :] - place.y * count_y
            inside = (px >= 0) & (px < count_x) & (py >= 0) & (py < count_y)
            home = jnp.where(inside, px * count_y + py, -1)
            at_z = (
                lax.broadcasted_iota(jnp.int32, (count_z, count_j), 0) == points_ref[2:3, :]
            )

            def spread_of(step):
                return split3(jnp.where(at_z, waves_ref[step : step + 1, :], 0.0))

            spreads = [(addpart, spread_of(number))]
            if ahead:
                spreads.append((ahead_ref, spread_of(STEPS - 1)))

        def inject(index, _):
            start = pl.multiple_of(index * chunk, chunk)
            here = start * count_y + lax.broadcasted_iota(
                jnp.int32, (chunk * count_y, count_j), 0
            )
            hit = jnp.where(here == home, 1.0, 0.0).astype(BF16)
            for target, spread in spreads:
                added = [
                    lax.dot_general(
                        hit, part, (((1,), (1,)), ((), ())), preferred_element_type=F32
                    )
                    for part in spread
                ]
                added = (added[2] + added[1]) + added[0]
                target[pl.ds(start, chunk)] = added.reshape(chunk, count_y, count_z)
            return 0

        if not last:
            lax.fori_loop(0, count_x // chunk, inject, 0)
        if first:
            for copy in copies[4:]:
                copy.wait()

        def row(x, _):
            middle = padded[x + WIDTH, columns]
            total = CENTRE * middle + (1.0 / SCALE) * zpart[x]
            for offset, weight in enumerate(WEIGHTS, 1):
                paired = padded[x + WIDTH + offset, columns] + padded[x + WIDTH - offset, columns]
                paired = paired + (
                    padded[x + WIDTH, pl.ds(SIDE + offset, count_y)]
                    + padded[x + WIDTH, pl.ds(SIDE - offset, count_y)]
                )
                total = total + weight * paired
            if not last:
                whole_ref[x] = middle
            next_ref[x] = (2.0 * middle - before_ref[x] + kept_ref[x] * total) + addpart[x]
            return 0

        lax.fori_loop(0, count_x, row, 0, unroll=4)

        qx_ref[pl.ds(0, WIDTH)] = next_ref[pl.ds(0, WIDTH)]
        qx_ref[pl.ds(WIDTH, WIDTH)] = next_ref[pl.ds(count_x - WIDTH, WIDTH)]
        qy_ref[...] = next_ref[:, pl.ds(block, SIDE)]
        if first:
            cx_ref[pl.ds(0, WIDTH)] = kept_ref[pl.ds(0, WIDTH)]
            cx_ref[pl.ds(WIDTH, WIDTH)] = kept_ref[pl.ds(count_x - WIDTH, WIDTH)]
            cy_ref[...] = kept_ref[:, pl.ds(block, SIDE)]
        if last:
            for b in range(count_b):
                even_ref[b] = even_rows(padded, WIDTH, SIDE, count_a, b)
        if snapshot:
            for copy in copies:
                copy.wait()
            flag_ref[...] = jnp.where(
                wanted[place.field, 1] == STEPS, jnp.ones(flag_ref.shape, F32), 0.0
            )
            earlier = wanted[place.field, 0] == number - 1

            @pl.when(earlier)
            def _():
                for b in range(count_b):
                    even_ref[b] = even_rows(previous_ref, 0, 0, count_a, b)

            @pl.when(jnp.logical_not(earlier))
            def _():
                for b in range(count_b):
                    even_ref[b] = even_rows(padded, WIDTH, SIDE, count_a, b)

            for kind, part in enumerate(packed(even_ref, own_matrix)):
                own_out[kind] = part
            send_into(even_ref, sent_matrix, sent_out)

    full = shape(count_x, count_y, count_z)
    slab, side = shape(2 * WIDTH, count_y, count_z), shape(count_x, SIDE, count_z)
    even = shape(count_b, count_a, count_z)
    outs = [full, slab, side]
    if first:
        outs += [full, slab, side, shape(8, count_j, dtype=jnp.int32), shape(8, count_j)]
    if not last:
        outs.append(full)
    if snapshot:
        size = GROUP * count_z
        outs += [
            shape(4, count_b // GROUP * count_a, count_z),
            sent_shape(count_a, count_b, count_z),
            shape(size, size, dtype=BF16),
            shape(size, size, dtype=BF16),
            shape(8, count_z),
        ]
    if ahead:
        outs.append(full)
    if last:
        outs.append(even)
    place_of = spec(pltpu.HBM) if first else spec(pltpu.VMEM)
    if first:
        operands = [*points, current]
    elif last:
        operands = [points, current]
    else:
        operands = [points, waves, current]
    specs = [place_of] * (len(operands) - 1) + [spec(pltpu.VMEM)]
    if not first:
        operands += list(faces)
        specs += [spec(pltpu.VMEM)] * 3
    operands += [previous, courant]
    specs += [place_of] * 2
    scratch = [
        pltpu.VMEM((count_x + 2 * WIDTH, count_y + 2 * SIDE, count_z), F32),
        pltpu.VMEM(full.shape, F32),
        pltpu.VMEM(full.shape, F32),
    ]
    if first:
        scratch.append(pltpu.VMEM(full.shape, F32))
        scratch += [pltpu.VMEM(array.shape, array.dtype) for array in points]
        scratch.append(pltpu.SemaphoreType.DMA((6,)))
    if snapshot:
        operands += [snapshots, matrices]
        specs += [spec(pltpu.HBM)] * 2
        scratch += [
            pltpu.VMEM(even.shape, F32),
            pltpu.SMEM(snapshots.shape, jnp.int32),
            pltpu.SemaphoreType.DMA((3,)),
        ]
    return pl.pallas_call(
        kernel,
        out_shape=tuple(outs),
        in_specs=specs,
        out_specs=(spec(pltpu.VMEM),) * len(outs),
        scratch_shapes=scratch,
        compiler_params=params(20),
        cost_estimate=cost(count_x * count_y * count_z, 60, 6),
    )(*operands)


def low_terms(halo_ref, r):
    total = None
    for k in range(r + 1, WIDTH + 1):
        term = WEIGHTS[k - 1] * halo_ref[WIDTH + r - k]
        total = term if total is None else total + term
    return total


def high_terms(halo_ref, r):
    total = None
    for k in range(WIDTH - r, WIDTH + 1):
        term = WEIGHTS[k - 1] * halo_ref[r + k - WIDTH]
        total = term if total is None else total + term
    return total


def add_halo(place, parts, halos, outs):
    qx_ref, qy_ref, cx_ref, cy_ref = parts
    far_in, near_in, side_in = halos
    far_out, near_out, side_out = outs
    count_y, count_x = qx_ref.shape[1], qy_ref.shape[0]
    block = place.block(count_y)

    def along_x(low_in, high_in, low_out, high_out):
        for r in range(WIDTH):
            low, high = qx_ref[r], qx_ref[WIDTH + r]
            if low_in is not None:
                low = low + cx_ref[r] * low_terms(low_in, r)
            if high_in is not None:
                high = high + cx_ref[WIDTH + r] * high_terms(high_in, r)
            low_out[r], high_out[r] = low, high
        side_out[pl.ds(0, WIDTH)] = low_out[:, pl.ds(block, SIDE)]
        side_out[pl.ds(count_x - WIDTH, WIDTH)] = high_out[:, pl.ds(block, SIDE)]

    inner = pl.ds(WIDTH, count_x - 2 * WIDTH)
    side_out[inner] = qy_ref[inner]

    @pl.when(place.even)
    def _():
        along_x(far_in, near_in, far_out, near_out)

    @pl.when(jnp.logical_not(place.even))
    def _():
        along_x(near_in, far_in, near_out, far_out)

    def along_y(shifts, masks):
        halo = side_in[...]
        lanes = halo.shape[2]
        line = lax.broadcasted_iota(jnp.int32, (1, SIDE, lanes), 1)
        total = None
        for k in range(1, WIDTH + 1):
            weight = jnp.where(masks(line, k), WEIGHTS[k - 1], 0.0)
            term = weight * pltpu.roll(halo, shifts(k), 1)
            total = term if total is None else total + term
        side_out[...] = side_out[...] + cy_ref[...] * total

    @pl.when(place.y == 0)
    def _():
        along_y(lambda k: SIDE - k, lambda line, k: line >= SIDE - k)

    @pl.when(place.y != 0)
    def _():
        along_y(lambda k: k, lambda line, k: line < k)

    def corners(low_out, high_out):
        low_out[:, pl.ds(block, SIDE)] = side_out[pl.ds(0, WIDTH)]
        high_out[:, pl.ds(block, SIDE)] = side_out[pl.ds(count_x - WIDTH, WIDTH)]

    @pl.when(place.even)
    def _():
        corners(far_out, near_out)

    @pl.when(jnp.logical_not(place.even))
    def _():
        corners(near_out, far_out)


def halo_step(parts, halos):
    count_y, (count_x, _, count_z) = parts[0].shape[1], parts[1].shape

    def kernel(*refs):
        add_halo(Place(), refs[:4], refs[4:7], refs[7:])

    return pl.pallas_call(
        kernel,
        out_shape=face_shapes(count_x, count_y, count_z),
        in_specs=[spec(pltpu.VMEM)] * 7,
        out_specs=(spec(pltpu.VMEM),) * 3,
        compiler_params=params(8),
        cost_estimate=cost(16 * count_y * count_z, 10, 6),
        name="halo_step",
    )(*parts, *halos)


def pack_matrix(window, count_z):
    half = count_z // GROUP
    size = GROUP * count_z
    row, column = np.arange(size)[:, None], np.arange(size)[None, :]
    row_b, row_z = row // count_z, row % count_z
    kind = column // count_z
    parity = kind % 2
    lane_b, lane_i = (column % count_z) // half, column % half
    main = (row_b == lane_b) & (row_z == 2 * (half * window + lane_i) + parity)
    wanted_b = (lane_b + (GROUP - 1 if window == 0 else 1)) % GROUP
    wanted_z = 2 * (half * (1 - window) + lane_i) + parity
    useful = lane_i < REACH if window == 0 else lane_i >= half - REACH
    edge = (row_b == wanted_b) & (row_z == wanted_z) & useful
    return np.where(kind < 2, main, edge).astype(np.float32)


def packed(even_ref, matrix_ref):
    count_b, _, count_z = even_ref.shape
    rows = [
        jnp.concatenate([even_ref[b + i] for i in range(GROUP)], axis=1)
        for b in range(0, count_b, GROUP)
    ]
    result = exact_dot(jnp.concatenate(rows, axis=0), matrix_ref[...])
    return [result[:, kind * count_z : (kind + 1) * count_z] for kind in range(4)]


def lag_shifts(lag, is_source):
    parity = lag & 1
    source_shift = -((lag + parity) >> 1)
    receiver_shift = (lag - parity) >> 1
    return (
        parity,
        jnp.where(is_source, source_shift, receiver_shift),
        jnp.where(is_source, receiver_shift, source_shift),
    )


def moved(main, edge, shift):
    count_z = main.shape[1]
    half = count_z // GROUP
    lane = lax.broadcasted_iota(jnp.int32, (1, count_z), 1) % half
    mask = (lane < shift) | (lane >= half + shift)
    return pltpu.roll(jnp.where(mask, edge, main), (count_z - shift) & (count_z - 1), 1)


def pack_own(lags, even, matrix):
    count_b, count_a, count_z = even.shape
    total_rows = count_b // GROUP * count_a
    (count_h,) = lags.shape

    def kernel(lags_ref, even_ref, matrix_ref, out_ref, windows, lag_of, sem):
        copy = pltpu.make_async_copy(lags_ref, lag_of, sem)
        copy.start()
        place = Place()
        for kind, part in enumerate(packed(even_ref, matrix_ref)):
            windows[kind] = part
        copy.wait()
        for h in range(count_h):
            parity, shift, _ = lag_shifts(lag_of[h], place.field == 0)
            out_ref[h] = moved(windows[parity], windows[2 + parity], shift)

    return pl.pallas_call(
        kernel,
        out_shape=shape(count_h, total_rows, count_z),
        in_specs=[spec(pltpu.HBM)] + [spec(pltpu.VMEM)] * 2,
        out_specs=spec(pltpu.VMEM),
        scratch_shapes=[
            pltpu.VMEM((4, total_rows, count_z), F32),
            pltpu.SMEM((count_h,), jnp.int32),
            pltpu.SemaphoreType.DMA,
        ],
        compiler_params=params(8),
        cost_estimate=cost(count_b * count_a * count_z, 1024, 4),
        name="pack_own",
    )(lags, even, matrix)


def edge_slots(count_a, groups, count_z):
    fits = count_z // GROUP // REACH
    slots = []
    for index in range(2 * groups):
        slots.append((index // groups, index % groups, index // fits * count_a, index % fits * REACH))
    return slots, -(-2 * groups // fits) * count_a


def send_into(even_ref, matrix_ref, out_ref):
    count_b, count_a, count_z = even_ref.shape
    groups = count_b // GROUP
    total_rows = groups * count_a
    parts = packed(even_ref, matrix_ref)
    out_ref[pl.ds(0, total_rows), :] = parts[0]
    out_ref[pl.ds(total_rows, total_rows), :] = parts[1]
    slots, _ = edge_slots(count_a, groups, count_z)
    sums = {}
    for parity, g, row, shift in slots:
        part = parts[2 + parity][g * count_a : (g + 1) * count_a]
        part = pltpu.roll(part, shift, 1) if shift else part
        sums[row] = sums[row] + part if row in sums else part
    for row, part in sums.items():
        out_ref[pl.ds(2 * total_rows + row, count_a), :] = part


def sent_shape(count_a, count_b, count_z):
    groups = count_b // GROUP
    _, extra = edge_slots(count_a, groups, count_z)
    return shape(2 * groups * count_a + extra, count_z)


def last_step(flag, even_before, current, parts, near, side, matrix):
    count_x, count_y, count_z = current.shape
    count_a, count_b = count_x // 2, count_y // 2

    def kernel(
        flag_ref, even_ref, current_ref, qx_ref, qy_ref, cx_ref, cy_ref, near_ref, side_ref,
        matrix_ref, final_ref, late_ref, sent_ref, far_out, near_out, side_out,
    ):
        place = Place()
        add_halo(
            place, (qx_ref, qy_ref, cx_ref, cy_ref), (None, near_ref, side_ref),
            (far_out, near_out, side_out),
        )
        low, high = pl.ds(0, WIDTH), pl.ds(count_x - WIDTH, WIDTH)

        @pl.when(place.even)
        def _():
            final_ref[high] = near_out[...]
            final_ref[low] = far_out[...]

        @pl.when(jnp.logical_not(place.even))
        def _():
            final_ref[low] = near_out[...]
            final_ref[high] = far_out[...]

        final_ref[:, pl.ds(place.block(count_y), SIDE)] = side_out[...]
        wants_last = jnp.broadcast_to(flag_ref[0:1, :], (count_a, count_z)) > 0.5
        for b in range(count_b):
            late_ref[b] = jnp.where(
                wants_last, even_rows(final_ref, 0, 0, count_a, b), even_ref[b]
            )
        send_into(late_ref, matrix_ref, sent_ref)

    slab, _, side_shape = face_shapes(count_x, count_y, count_z)
    return pl.pallas_call(
        kernel,
        out_shape=(
            shape(*current.shape),
            shape(count_b, count_a, count_z),
            sent_shape(count_a, count_b, count_z),
        ),
        in_specs=[spec(pltpu.VMEM)] * 10,
        out_specs=(spec(pltpu.VMEM),) * 3,
        scratch_shapes=[
            pltpu.VMEM(slab.shape, F32),
            pltpu.VMEM(slab.shape, F32),
            pltpu.VMEM(side_shape.shape, F32),
        ],
        input_output_aliases={2: 0},
        compiler_params=params(12),
        cost_estimate=cost(count_x * count_y * count_z, 10, 3),
        name="last_step",
    )(flag, even_before, current, *parts, near, side, matrix)


def far_rows(count_b):
    return -(-2 * (count_b // GROUP) // 16) * 16


def last_far(flag, final, late, cx, far, matrix):
    count_x, count_y, count_z = final.shape
    count_b, count_a, _ = late.shape
    rows, pair = far_rows(count_b), WIDTH // 2

    def kernel(
        flag_ref, final_in, late_in, cx_ref, far_ref, matrix_ref, final_ref, late_ref, sent_ref, lhs,
    ):
        place = Place()
        wants_last = jnp.broadcast_to(flag_ref[0:1, :], (1, count_z)) > 0.5
        lhs[...] = jnp.zeros_like(lhs)

        def correct(first_x, first_c, first_a, terms):
            for r in range(WIDTH):
                final_ref[first_x + r] = final_ref[first_x + r] + cx_ref[first_c + r] * terms(
                    far_ref, r
                )
            for b in range(count_b):
                for i in range(pair):
                    value = jnp.where(
                        wants_last,
                        final_ref[first_x + 2 * i, pl.ds(2 * b, 1), :],
                        late_ref[b, pl.ds(first_a + i, 1), :],
                    )
                    late_ref[b, pl.ds(first_a + i, 1), :] = value
                    lanes = pl.ds(b % GROUP * count_z, count_z)
                    lhs[pl.ds(b // GROUP * pair + i, 1), lanes] = value

        @pl.when(place.even)
        def _():
            correct(0, 0, 0, low_terms)

        @pl.when(jnp.logical_not(place.even))
        def _():
            correct(count_x - WIDTH, WIDTH, count_a - pair, high_terms)

        result = exact_dot(lhs[...], matrix_ref[...])
        parts = [result[:, kind * count_z : (kind + 1) * count_z] for kind in range(4)]
        sent_ref[pl.ds(0, rows), :] = parts[0]
        sent_ref[pl.ds(rows, rows), :] = parts[1]
        sent_ref[pl.ds(2 * rows, rows), :] = parts[2] + pltpu.roll(parts[3], REACH, 1)

    return pl.pallas_call(
        kernel,
        out_shape=(shape(*final.shape), shape(*late.shape), shape(3 * rows, count_z)),
        in_specs=[spec(pltpu.VMEM)] * 6,
        out_specs=(spec(pltpu.VMEM),) * 3,
        scratch_shapes=[pltpu.VMEM((rows, GROUP * count_z), F32)],
        input_output_aliases={1: 0, 2: 1},
        compiler_params=params(12),
        cost_estimate=cost(WIDTH * count_y * count_z, 20, 3),
        name="last_far",
    )(flag, final, late, cx, far, matrix)


def write_out(level):
    def kernel(level_ref, out_ref, sem):
        copy = pltpu.make_async_copy(level_ref, out_ref, sem)
        copy.start()
        copy.wait()

    return pl.pallas_call(
        kernel,
        out_shape=shape(*level.shape),
        in_specs=[spec(pltpu.VMEM)],
        out_specs=spec(pltpu.HBM),
        scratch_shapes=[pltpu.SemaphoreType.DMA],
        compiler_params=params(4),
        cost_estimate=cost(level.size, 0, 2),
        name="write_out",
    )(level)


CODE_BITS = 5
PER_CODE = 6


def lag_image(count_a, lags, own, other, extra=None, before=None):
    _, total_rows, count_z = own.shape
    groups = total_rows // count_a
    half = count_z // GROUP
    last = before is not None
    count_h = before.shape[0] if last else lags.shape[0]
    codes = -(-count_h // PER_CODE)
    pair = WIDTH // 2

    def kernel(*refs):
        refs = list(refs)
        take = lambda count: [refs.pop(0) for _ in range(count)]
        lags_ref, own_ref, other_ref = take(3)
        if last:
            extra_ref, before_ref = take(2)
        (out_ref,) = take(1)
        if not last:
            (codes_ref,) = take(1)
        mains, edges = take(2)
        if last:
            store, sem = take(2)
        else:
            store = out_ref
            lag_of, sem = take(2)
        place = Place()
        if last:
            packed_lags = [lags_ref[k : k + 1, :][0, 0] for k in range(codes)]
            mask = (1 << CODE_BITS) - 1
            lag_list = [
                ((packed_lags[h // PER_CODE] >> (h % PER_CODE * CODE_BITS)) & mask) - LAGMAX
                for h in range(count_h)
            ]
        else:
            copy = pltpu.make_async_copy(lags_ref, lag_of, sem)
            copy.start()
        is_source = place.field == 0

        def useful(rows):
            lane = lax.broadcasted_iota(jnp.int32, (rows, count_z), 1) % half
            return jnp.where(is_source, lane, half - 1 - lane) < REACH

        slots, _ = edge_slots(count_a, groups, count_z)
        for parity in range(2):
            mains[parity] = other_ref[pl.ds(parity * total_rows, total_rows), :]
        for parity, g, row, shift in slots:
            part = other_ref[pl.ds(2 * total_rows + row, count_a), :]
            part = pltpu.roll(part, count_z - shift, 1) if shift else part
            edges[parity, pl.ds(g * count_a, count_a), :] = jnp.where(useful(count_a), part, 0.0)
        if last:
            rows = extra_ref.shape[0] // 3
            border = extra_ref[pl.ds(2 * rows, rows), :]
            borders = [
                jnp.where(useful(rows), part, 0.0)
                for part in (border, pltpu.roll(border, count_z - REACH, 1))
            ]

            def overwrite(first_a):
                for g in range(groups):
                    target = pl.ds(g * count_a + first_a, pair)
                    for parity in range(2):
                        mains[parity, target, :] = extra_ref[
                            pl.ds(parity * rows + g * pair, pair), :
                        ]
                        edges[parity, target, :] = borders[parity][g * pair : (g + 1) * pair]

            pl.when(place.even)(lambda: overwrite(0))
            pl.when(jnp.logical_not(place.even))(lambda: overwrite(count_a - pair))
        else:
            copy.wait()
            lag_list = [lag_of[h] for h in range(count_h)]
            for k in range(codes):
                code = jnp.int32(0)
                for h in range(k * PER_CODE, min((k + 1) * PER_CODE, count_h)):
                    code = code | ((lag_list[h] + LAGMAX) << (h % PER_CODE * CODE_BITS))
                codes_ref[k : k + 1, :] = jnp.full((1, count_z), code, jnp.int32)
        for h, lag in enumerate(lag_list):
            parity, own_shift, other_shift = lag_shifts(lag, is_source)
            product = moved(mains[parity], edges[parity], other_shift)
            if last:
                product = product * own_ref[h]
            else:
                product = product * moved(own_ref[parity], own_ref[2 + parity], own_shift)
            for g in range(groups):
                part = product[g * count_a : (g + 1) * count_a]
                lanes = pl.ds(g * count_z, count_z)
                if last:
                    part = part + before_ref[h, :, lanes]
                store[h, :, lanes] = part
            if last:
                pltpu.make_async_copy(store.at[h], out_ref.at[h], sem).start()
        if last:
            pltpu.make_async_copy(store, out_ref, sem).wait()

    image = shape(count_h, count_a, groups * count_z)
    operands = [lags, own, other] + ([extra, before] if last else [])
    scratch = [pltpu.VMEM((2, total_rows, count_z), F32)] * 2
    scratch.append(pltpu.VMEM(image.shape, F32) if last else pltpu.SMEM((count_h,), jnp.int32))
    scratch.append(pltpu.SemaphoreType.DMA)
    return pl.pallas_call(
        kernel,
        out_shape=image if last else (image, shape(8, count_z, dtype=jnp.int32)),
        in_specs=[spec(pltpu.VMEM if last else pltpu.HBM)]
        + [spec(pltpu.VMEM)] * (len(operands) - 1),
        out_specs=spec(pltpu.HBM) if last else (spec(pltpu.VMEM),) * 2,
        scratch_shapes=scratch,
        compiler_params=params(12),
        cost_estimate=cost(count_h * total_rows * count_z, 10, 2),
        name="last_image" if last else "early_image",
    )(*operands)


def body(
    field_now,
    field_prev,
    courant_squared,
    source_cells,
    source_wave,
    receiver_cells,
    receiver_wave,
    snapshot_steps,
    lag_offsets,
):
    count_x, _, count_z = field_now.shape
    loop_size = lax.axis_size("gx")
    half_size = loop_size // 2
    turn = loop_size // 4
    assert lax.axis_size("gy") == 2 and half_size % 2 == 0

    slabs = [(i - turn) % loop_size % half_size for i in range(loop_size)]

    def pairs(odd):
        found = []
        for i, slab in enumerate(slabs):
            if slab % 2 == odd and slab != half_size - 1:
                j = (i + 1) % loop_size
                found += [(i, j), (j, i)]
        return found

    near_pairs, far_pairs = pairs(0), pairs(1)
    across = [(i, (i + half_size) % loop_size) for i in range(loop_size)]

    def send_far(far):
        return lax.ppermute(far, "gx", far_pairs)

    def send_near(near, side):
        near = lax.ppermute(near, "gx", near_pairs)
        return near, lax.ppermute(side, "gy", [(0, 1), (1, 0)])

    def exchange(faces):
        far, near, side = faces
        return (send_far(far), *send_near(near, side))

    matrices = jnp.asarray(
        np.stack([pack_matrix(window, count_z) for window in (0, 1)]), dtype=BF16
    )
    raw = (source_cells, source_wave, receiver_cells, receiver_wave)
    field_kept, field_prev, courant_squared, matrices, snapshot_steps, lag_offsets, *raw = (
        pltpu.with_memory_space_constraint(array, pltpu.HBM)
        for array in (
            field_now, field_prev, courant_squared, matrices, snapshot_steps, lag_offsets, *raw
        )
    )
    halos = exchange(first_faces(field_kept))
    next1, qx, qy, courant, cx, cy, points, waves, whole0 = inner_step(
        0, raw, None, field_now, None, field_prev, courant_squared
    )
    faces = halo_step((qx, qy, cx, cy), halos)
    halos = exchange(faces)
    next2, qx, qy, whole1, added = inner_step(1, points, waves, next1, faces, whole0, courant)
    faces = halo_step((qx, qy, cx, cy), halos)
    halos = exchange(faces)
    next3, qx, qy, whole2, own_early, sent_early, own_matrix, sent_matrix, flag = inner_step(
        2, points, waves, next2, faces, whole1, courant, snapshot_steps, matrices
    )
    other_early = lax.ppermute(sent_early, "gx", across)
    faces = halo_step((qx, qy, cx, cy), halos)
    far, near, side = exchange(faces)
    next4, qx, qy, even3 = inner_step(3, added, None, next3, faces, whole2, courant)
    final, late, sent_late = last_step(
        flag, even3, next4, (qx, qy, cx, cy), near, side, sent_matrix
    )
    other_late = lax.ppermute(sent_late, "gx", across)
    partial, codes = lag_image(count_x // 2, lag_offsets, own_early, other_early)
    final, late, sent_far = last_far(flag, final, late, cx, far, sent_matrix)
    extra = lax.ppermute(sent_far, "gx", across)
    own_late = pack_own(lag_offsets, late, own_matrix)
    image = lag_image(count_x // 2, codes, own_late, other_late, extra, partial)
    return write_out(final), jnp.transpose(image, (1, 0, 2))


def solution(mesh):
    placed = (
        P(("shots", "gx"), "gy", None),
        P(("shots", "gx"), "gy", None),
        P("gx", "gy", None),
        P(None, "shots"),
        P(None, "shots"),
        P(None, "shots"),
        P(None, "shots"),
        P("shots", None),
        P(),
    )
    return jax.shard_map(
        body,
        mesh=mesh,
        in_specs=placed,
        out_specs=(P(("shots", "gx"), "gy", None), P(("shots", "gx"), None, "gy")),
        check_vma=False,
    )
```

```python
import jax
import jax.numpy as jnp
import numpy as np
from jax import lax
from jax.experimental import pallas as pl
from jax.experimental.pallas import tpu as pltpu
from jax.sharding import PartitionSpec as P

STEPS = 4
WIDTH = 4
LAGMAX = 8
REACH = LAGMAX // 2
GROUP = 4
SIDE = 8

SCALE = 5040.0
BAND = (8064.0, -1008.0, 128.0, -9.0)
CENTRE = 3.0 * (-205.0 / 72.0)
WEIGHTS = (1.6, -0.2, 8.0 / 315.0, -1.0 / 560.0)

F32 = jnp.float32
BF16 = jnp.bfloat16


def shape(*dims, dtype=F32):
    return jax.ShapeDtypeStruct(dims, dtype)


def params(megabytes):
    return pltpu.CompilerParams(vmem_limit_bytes=megabytes << 20)


def spec(space):
    return pl.BlockSpec(memory_space=space)


def cost(count, flops_each, arrays):
    return pl.CostEstimate(
        flops=int(count * flops_each), bytes_accessed=int(4 * count * arrays), transcendentals=0
    )


def split3(values):
    high = values.astype(BF16)
    rest = values - high.astype(F32)
    middle = rest.astype(BF16)
    low = (rest - middle.astype(F32)).astype(BF16)
    return high, middle, low


def exact_dot(values, matrix):
    rows = values.shape[0]
    stacked = jnp.concatenate(split3(values), axis=0)
    result = jnp.dot(stacked, matrix, preferred_element_type=F32)
    return (result[2 * rows :] + result[rows : 2 * rows]) + result[:rows]


class Place:
    def __init__(self):
        loop_size = lax.axis_size("gx")
        self.half = loop_size // 2
        relative = lax.rem(lax.axis_index("gx") + loop_size - loop_size // 4, loop_size)
        self.field = relative // self.half
        self.slab = lax.rem(relative, self.half)
        self.even = lax.rem(self.slab, 2) == 0
        self.y = lax.axis_index("gy")

    def block(self, count_y):
        return pl.multiple_of((1 - self.y) * (count_y - SIDE), SIDE)


def first_faces(field):
    count_x, count_y, count_z = field.shape
    top = count_x - WIDTH

    def kernel(field_ref, far_ref, near_ref, side_ref, sems):
        place = Place()
        far = jnp.where(place.even, 0, top)
        sources = [
            field_ref.at[pl.ds(far, WIDTH)],
            field_ref.at[pl.ds(top - far, WIDTH)],
            field_ref.at[:, pl.ds(place.block(count_y), SIDE)],
        ]
        copies = [
            pltpu.make_async_copy(source, target, sems.at[index])
            for index, (source, target) in enumerate(zip(sources, (far_ref, near_ref, side_ref)))
        ]
        for copy in copies:
            copy.start()
        for copy in copies:
            copy.wait()

    return pl.pallas_call(
        kernel,
        out_shape=face_shapes(count_x, count_y, count_z),
        in_specs=[spec(pltpu.HBM)],
        out_specs=(spec(pltpu.VMEM),) * 3,
        scratch_shapes=[pltpu.SemaphoreType.DMA((3,))],
        compiler_params=params(8),
        name="first_faces",
    )(field)


def face_shapes(count_x, count_y, count_z):
    slab = shape(WIDTH, count_y, count_z)
    return slab, slab, shape(count_x, SIDE, count_z)


def even_rows(level_ref, offset_x, offset_y, count_a, b):
    rows, stride, lanes = level_ref.shape
    flat = level_ref.reshape(rows * stride, lanes)
    start = offset_x * stride + offset_y + 2 * b
    return flat[pl.ds(start, count_a, stride=2 * stride), :]


def inner_step(number, points, waves, current, faces, previous, courant, snapshots=None, matrices=None):
    count_x, count_y, count_z = current.shape
    count_a, count_b = count_x // 2, count_y // 2
    first = faces is None
    last = number == STEPS - 1
    snapshot = number == STEPS // 2
    ahead = number == 1
    if last:
        count_j = 0
    elif first:
        count_j = -(-max(array.shape[1] for array in points) // 128) * 128
    else:
        count_j = points.shape[1]

    def kernel(*refs):
        refs = list(refs)
        take = lambda count: [refs.pop(0) for _ in range(count)]
        if first:
            raw_refs = take(4)
        elif last:
            (added_ref,) = take(1)
        else:
            points_ref, waves_ref = take(2)
        (current_ref,) = take(1)
        if not first:
            far_ref, near_ref, side_ref = take(3)
        previous_ref, courant_ref = take(2)
        if snapshot:
            steps_ref, matrices_ref = take(2)
        next_ref, qx_ref, qy_ref = take(3)
        if first:
            kept_ref, cx_ref, cy_ref, points_ref, waves_ref = take(5)
        if not last:
            (whole_ref,) = take(1)
        if snapshot:
            own_out, sent_out, own_matrix, sent_matrix, flag_ref = take(5)
        if ahead:
            (ahead_ref,) = take(1)
        if last:
            (even_ref,) = take(1)
        padded, zpart, addpart = take(3)
        if last:
            addpart = added_ref
        if first:
            before_ref = take(1)[0]
            raw_refs_in, raw_refs = raw_refs, take(4)
            (sems,) = take(1)
        if snapshot:
            even_ref, wanted, sems = take(3)

        place = Place()
        block = place.block(count_y)
        rows, columns = pl.ds(WIDTH, count_x), pl.ds(SIDE, count_y)
        if first:
            copies = [
                pltpu.make_async_copy(source, target, sems.at[index])
                for index, (source, target) in enumerate(
                    zip(
                        (*raw_refs_in, previous_ref, courant_ref),
                        (*raw_refs, before_ref, kept_ref),
                    )
                )
            ]
            for copy in copies:
                copy.start()
        else:
            before_ref, kept_ref = previous_ref, courant_ref
        if snapshot:
            copies = [
                pltpu.make_async_copy(steps_ref, wanted, sems.at[0]),
                pltpu.make_async_copy(matrices_ref.at[place.field], own_matrix, sems.at[1]),
                pltpu.make_async_copy(matrices_ref.at[1 - place.field], sent_matrix, sems.at[2]),
            ]
            for copy in copies:
                copy.start()

        zero_x = jnp.zeros((WIDTH, count_y + 2 * SIDE, count_z), F32)
        padded[pl.ds(0, WIDTH)] = zero_x
        padded[pl.ds(count_x + WIDTH, WIDTH)] = zero_x
        zero_y = jnp.zeros((count_x, SIDE, count_z), F32)
        padded[rows, pl.ds(0, SIDE)] = zero_y
        padded[rows, pl.ds(count_y + SIDE, SIDE)] = zero_y

        padded[rows, columns] = current_ref[...]
        if not first:
            low, high = pl.ds(WIDTH, WIDTH), pl.ds(count_x, WIDTH)

            @pl.when(place.even)
            def _():
                padded[high, columns] = near_ref[...]
                padded[low, columns] = far_ref[...]

            @pl.when(jnp.logical_not(place.even))
            def _():
                padded[low, columns] = near_ref[...]
                padded[high, columns] = far_ref[...]

            padded[rows, pl.ds(pl.multiple_of(block + SIDE, SIDE), SIDE)] = side_ref[...]

        gap = jnp.abs(
            lax.broadcasted_iota(jnp.int32, (count_z, count_z), 0)
            - lax.broadcasted_iota(jnp.int32, (count_z, count_z), 1)
        )
        band = jnp.zeros((count_z, count_z), F32)
        for offset, weight in enumerate(BAND, 1):
            band = jnp.where(gap == offset, weight, band)
        band = band.astype(BF16)

        chunk = 8

        def multiply(index, _):
            start = pl.multiple_of(index * chunk, chunk)
            values = padded[pl.ds(start + WIDTH, chunk), columns]
            zpart[pl.ds(start, chunk)] = exact_dot(
                values.reshape(chunk * count_y, count_z), band
            ).reshape(chunk, count_y, count_z)
            return 0

        chunks = count_x // chunk
        if last:
            lax.fori_loop(0, chunks, multiply, 0)
        else:
            multiply(0, 0)

        if first:
            for copy in copies[:4]:
                copy.wait()
            points_ref[...] = jnp.full(points_ref.shape, -1, jnp.int32)
            waves_ref[...] = jnp.zeros(waves_ref.shape, F32)

            def choose(cells_ref, wave_ref):
                count = cells_ref.shape[1]
                points_ref[pl.ds(0, 3), pl.ds(0, count)] = cells_ref[...]
                waves_ref[pl.ds(0, STEPS), pl.ds(0, count)] = wave_ref[...]

            @pl.when(place.field == 0)
            def _():
                choose(raw_refs[0], raw_refs[1])

            @pl.when(place.field != 0)
            def _():
                choose(raw_refs[2], raw_refs[3])

        if not last:
            px = points_ref[0:1, :] - place.slab * count_x
            py = points_ref[1:2, :] - place.y * count_y
            inside = (px >= 0) & (px < count_x) & (py >= 0) & (py < count_y)
            home = jnp.where(inside, px * count_y + py, -1)
            at_z = (
                lax.broadcasted_iota(jnp.int32, (count_z, count_j), 0) == points_ref[2:3, :]
            )

            def spread_of(step):
                return split3(jnp.where(at_z, waves_ref[step : step + 1, :], 0.0))

            spreads = [(addpart, spread_of(number))]
            if ahead:
                spreads.append((ahead_ref, spread_of(STEPS - 1)))

        def inject(index):
            start = pl.multiple_of(index * chunk, chunk)
            here = start * count_y + lax.broadcasted_iota(
                jnp.int32, (chunk * count_y, count_j), 0
            )
            hit = jnp.where(here == home, 1.0, 0.0).astype(BF16)
            for target, spread in spreads:
                added = [
                    lax.dot_general(
                        hit, part, (((1,), (1,)), ((), ())), preferred_element_type=F32
                    )
                    for part in spread
                ]
                added = (added[2] + added[1]) + added[0]
                target[pl.ds(start, chunk)] = added.reshape(chunk, count_y, count_z)
            return 0

        def both(index, _):
            inject(index)
            return multiply(index + 1, 0)

        if not last:
            lax.fori_loop(0, chunks - 1, both, 0)
            inject(chunks - 1)
        if first:
            for copy in copies[4:]:
                copy.wait()

        def row(x, _):
            middle = padded[x + WIDTH, columns]
            total = CENTRE * middle + (1.0 / SCALE) * zpart[x]
            for offset, weight in enumerate(WEIGHTS, 1):
                paired = padded[x + WIDTH + offset, columns] + padded[x + WIDTH - offset, columns]
                paired = paired + (
                    padded[x + WIDTH, pl.ds(SIDE + offset, count_y)]
                    + padded[x + WIDTH, pl.ds(SIDE - offset, count_y)]
                )
                total = total + weight * paired
            if not last:
                whole_ref[x] = middle
            next_ref[x] = (2.0 * middle - before_ref[x] + kept_ref[x] * total) + addpart[x]
            return 0

        lax.fori_loop(0, count_x, row, 0, unroll=4)

        qx_ref[pl.ds(0, WIDTH)] = next_ref[pl.ds(0, WIDTH)]
        qx_ref[pl.ds(WIDTH, WIDTH)] = next_ref[pl.ds(count_x - WIDTH, WIDTH)]
        qy_ref[...] = next_ref[:, pl.ds(block, SIDE)]
        if first:
            cx_ref[pl.ds(0, WIDTH)] = kept_ref[pl.ds(0, WIDTH)]
            cx_ref[pl.ds(WIDTH, WIDTH)] = kept_ref[pl.ds(count_x - WIDTH, WIDTH)]
            cy_ref[...] = kept_ref[:, pl.ds(block, SIDE)]
        if last:
            for b in range(count_b):
                even_ref[b] = even_rows(padded, WIDTH, SIDE, count_a, b)
        if snapshot:
            for copy in copies:
                copy.wait()
            flag_ref[...] = jnp.where(
                wanted[place.field, 1] == STEPS, jnp.ones(flag_ref.shape, F32), 0.0
            )
            earlier = wanted[place.field, 0] == number - 1

            @pl.when(earlier)
            def _():
                for b in range(count_b):
                    even_ref[b] = even_rows(previous_ref, 0, 0, count_a, b)

            @pl.when(jnp.logical_not(earlier))
            def _():
                for b in range(count_b):
                    even_ref[b] = even_rows(padded, WIDTH, SIDE, count_a, b)

            for kind, part in enumerate(packed(even_ref, own_matrix)):
                own_out[kind] = part
            send_into(even_ref, sent_matrix, sent_out)

    full = shape(count_x, count_y, count_z)
    slab, side = shape(2 * WIDTH, count_y, count_z), shape(count_x, SIDE, count_z)
    even = shape(count_b, count_a, count_z)
    outs = [full, slab, side]
    if first:
        outs += [full, slab, side, shape(8, count_j, dtype=jnp.int32), shape(8, count_j)]
    if not last:
        outs.append(full)
    if snapshot:
        size = GROUP * count_z
        outs += [
            shape(4, count_b // GROUP * count_a, count_z),
            sent_shape(count_a, count_b, count_z),
            shape(size, size, dtype=BF16),
            shape(size, size, dtype=BF16),
            shape(8, count_z),
        ]
    if ahead:
        outs.append(full)
    if last:
        outs.append(even)
    place_of = spec(pltpu.HBM) if first else spec(pltpu.VMEM)
    if first:
        operands = [*points, current]
    elif last:
        operands = [points, current]
    else:
        operands = [points, waves, current]
    specs = [place_of] * (len(operands) - 1) + [spec(pltpu.VMEM)]
    if not first:
        operands += list(faces)
        specs += [spec(pltpu.VMEM)] * 3
    operands += [previous, courant]
    specs += [place_of] * 2
    scratch = [
        pltpu.VMEM((count_x + 2 * WIDTH, count_y + 2 * SIDE, count_z), F32),
        pltpu.VMEM(full.shape, F32),
        pltpu.VMEM(full.shape, F32),
    ]
    if first:
        scratch.append(pltpu.VMEM(full.shape, F32))
        scratch += [pltpu.VMEM(array.shape, array.dtype) for array in points]
        scratch.append(pltpu.SemaphoreType.DMA((6,)))
    if snapshot:
        operands += [snapshots, matrices]
        specs += [spec(pltpu.HBM)] * 2
        scratch += [
            pltpu.VMEM(even.shape, F32),
            pltpu.SMEM(snapshots.shape, jnp.int32),
            pltpu.SemaphoreType.DMA((3,)),
        ]
    return pl.pallas_call(
        kernel,
        out_shape=tuple(outs),
        in_specs=specs,
        out_specs=(spec(pltpu.VMEM),) * len(outs),
        scratch_shapes=scratch,
        compiler_params=params(20),
        cost_estimate=cost(count_x * count_y * count_z, 60, 6),
    )(*operands)


def low_terms(halo_ref, r):
    total = None
    for k in range(r + 1, WIDTH + 1):
        term = WEIGHTS[k - 1] * halo_ref[WIDTH + r - k]
        total = term if total is None else total + term
    return total


def high_terms(halo_ref, r):
    total = None
    for k in range(WIDTH - r, WIDTH + 1):
        term = WEIGHTS[k - 1] * halo_ref[r + k - WIDTH]
        total = term if total is None else total + term
    return total


def add_halo(place, parts, halos, outs):
    qx_ref, qy_ref, cx_ref, cy_ref = parts
    far_in, near_in, side_in = halos
    near_even, near_odd = near_in if isinstance(near_in, tuple) else (near_in, near_in)
    far_out, near_out, side_out = outs
    count_y, count_x = qx_ref.shape[1], qy_ref.shape[0]
    block = place.block(count_y)

    def along_x(low_in, high_in, low_out, high_out):
        for r in range(WIDTH):
            low, high = qx_ref[r], qx_ref[WIDTH + r]
            if low_in is not None:
                low = low + cx_ref[r] * low_terms(low_in, r)
            if high_in is not None:
                high = high + cx_ref[WIDTH + r] * high_terms(high_in, r)
            low_out[r], high_out[r] = low, high
        side_out[pl.ds(0, WIDTH)] = low_out[:, pl.ds(block, SIDE)]
        side_out[pl.ds(count_x - WIDTH, WIDTH)] = high_out[:, pl.ds(block, SIDE)]

    inner = pl.ds(WIDTH, count_x - 2 * WIDTH)
    side_out[inner] = qy_ref[inner]

    @pl.when(place.even)
    def _():
        along_x(far_in, near_even, far_out, near_out)

    @pl.when(jnp.logical_not(place.even))
    def _():
        along_x(near_odd, far_in, near_out, far_out)

    def along_y(shifts, masks):
        halo = side_in[...]
        lanes = halo.shape[2]
        line = lax.broadcasted_iota(jnp.int32, (1, SIDE, lanes), 1)
        total = None
        for k in range(1, WIDTH + 1):
            weight = jnp.where(masks(line, k), WEIGHTS[k - 1], 0.0)
            term = weight * pltpu.roll(halo, shifts(k), 1)
            total = term if total is None else total + term
        side_out[...] = side_out[...] + cy_ref[...] * total

    @pl.when(place.y == 0)
    def _():
        along_y(lambda k: SIDE - k, lambda line, k: line >= SIDE - k)

    @pl.when(place.y != 0)
    def _():
        along_y(lambda k: k, lambda line, k: line < k)

    def corners(low_out, high_out):
        low_out[:, pl.ds(block, SIDE)] = side_out[pl.ds(0, WIDTH)]
        high_out[:, pl.ds(block, SIDE)] = side_out[pl.ds(count_x - WIDTH, WIDTH)]

    @pl.when(place.even)
    def _():
        corners(far_out, near_out)

    @pl.when(jnp.logical_not(place.even))
    def _():
        corners(near_out, far_out)


def halo_step(parts, halos):
    count_y, (count_x, _, count_z) = parts[0].shape[1], parts[1].shape
    far, near, side = halos
    nears = near if isinstance(near, tuple) else (near,)

    def kernel(*refs):
        refs = list(refs)
        take = lambda count: [refs.pop(0) for _ in range(count)]
        parts_in, (far_in,), nears_in, (side_in,) = take(4), take(1), take(len(nears)), take(1)
        near_in = tuple(nears_in) if len(nears) == 2 else nears_in[0]
        add_halo(Place(), parts_in, (far_in, near_in, side_in), refs)

    return pl.pallas_call(
        kernel,
        out_shape=face_shapes(count_x, count_y, count_z),
        in_specs=[spec(pltpu.VMEM)] * (6 + len(nears)),
        out_specs=(spec(pltpu.VMEM),) * 3,
        compiler_params=params(8),
        cost_estimate=cost(16 * count_y * count_z, 10, 6),
        name="halo_step",
    )(*parts, far, *nears, side)


def pack_matrix(window, count_z):
    half = count_z // GROUP
    size = GROUP * count_z
    row, column = np.arange(size)[:, None], np.arange(size)[None, :]
    row_b, row_z = row // count_z, row % count_z
    kind = column // count_z
    parity = kind % 2
    lane_b, lane_i = (column % count_z) // half, column % half
    main = (row_b == lane_b) & (row_z == 2 * (half * window + lane_i) + parity)
    wanted_b = (lane_b + (GROUP - 1 if window == 0 else 1)) % GROUP
    wanted_z = 2 * (half * (1 - window) + lane_i) + parity
    useful = lane_i < REACH if window == 0 else lane_i >= half - REACH
    edge = (row_b == wanted_b) & (row_z == wanted_z) & useful
    return np.where(kind < 2, main, edge).astype(np.float32)


def packed(even_ref, matrix_ref):
    count_b, _, count_z = even_ref.shape
    rows = [
        jnp.concatenate([even_ref[b + i] for i in range(GROUP)], axis=1)
        for b in range(0, count_b, GROUP)
    ]
    result = exact_dot(jnp.concatenate(rows, axis=0), matrix_ref[...])
    return [result[:, kind * count_z : (kind + 1) * count_z] for kind in range(4)]


def lag_shifts(lag, is_source):
    parity = lag & 1
    source_shift = -((lag + parity) >> 1)
    receiver_shift = (lag - parity) >> 1
    return (
        parity,
        jnp.where(is_source, source_shift, receiver_shift),
        jnp.where(is_source, receiver_shift, source_shift),
    )


def moved(main, edge, shift):
    count_z = main.shape[1]
    half = count_z // GROUP
    lane = lax.broadcasted_iota(jnp.int32, (1, count_z), 1) % half
    mask = (lane < shift) | (lane >= half + shift)
    return pltpu.roll(jnp.where(mask, edge, main), (count_z - shift) & (count_z - 1), 1)


def pack_own(lags, even, matrix):
    count_b, count_a, count_z = even.shape
    total_rows = count_b // GROUP * count_a
    (count_h,) = lags.shape

    def kernel(lags_ref, even_ref, matrix_ref, out_ref, windows, lag_of, sem):
        copy = pltpu.make_async_copy(lags_ref, lag_of, sem)
        copy.start()
        place = Place()
        for kind, part in enumerate(packed(even_ref, matrix_ref)):
            windows[kind] = part
        copy.wait()
        for h in range(count_h):
            parity, shift, _ = lag_shifts(lag_of[h], place.field == 0)
            out_ref[h] = moved(windows[parity], windows[2 + parity], shift)

    return pl.pallas_call(
        kernel,
        out_shape=shape(count_h, total_rows, count_z),
        in_specs=[spec(pltpu.HBM)] + [spec(pltpu.VMEM)] * 2,
        out_specs=spec(pltpu.VMEM),
        scratch_shapes=[
            pltpu.VMEM((4, total_rows, count_z), F32),
            pltpu.SMEM((count_h,), jnp.int32),
            pltpu.SemaphoreType.DMA,
        ],
        compiler_params=params(8),
        cost_estimate=cost(count_b * count_a * count_z, 1024, 4),
        name="pack_own",
    )(lags, even, matrix)


def edge_slots(count_a, groups, count_z):
    fits = count_z // GROUP // REACH
    slots = []
    for index in range(2 * groups):
        slots.append((index // groups, index % groups, index // fits * count_a, index % fits * REACH))
    return slots, -(-2 * groups // fits) * count_a


def send_into(even_ref, matrix_ref, out_ref):
    count_b, count_a, count_z = even_ref.shape
    groups = count_b // GROUP
    total_rows = groups * count_a
    parts = packed(even_ref, matrix_ref)
    out_ref[pl.ds(0, total_rows), :] = parts[0]
    out_ref[pl.ds(total_rows, total_rows), :] = parts[1]
    slots, _ = edge_slots(count_a, groups, count_z)
    sums = {}
    for parity, g, row, shift in slots:
        part = parts[2 + parity][g * count_a : (g + 1) * count_a]
        part = pltpu.roll(part, shift, 1) if shift else part
        sums[row] = sums[row] + part if row in sums else part
    for row, part in sums.items():
        out_ref[pl.ds(2 * total_rows + row, count_a), :] = part


def sent_shape(count_a, count_b, count_z):
    groups = count_b // GROUP
    _, extra = edge_slots(count_a, groups, count_z)
    return shape(2 * groups * count_a + extra, count_z)


def last_step(flag, even_before, current, parts, near, side, matrix):
    count_x, count_y, count_z = current.shape
    count_a, count_b = count_x // 2, count_y // 2

    def kernel(
        flag_ref, even_ref, current_ref, qx_ref, qy_ref, cx_ref, cy_ref, near_ref, side_ref,
        matrix_ref, final_ref, late_ref, sent_ref, far_out, near_out, side_out,
    ):
        place = Place()
        add_halo(
            place, (qx_ref, qy_ref, cx_ref, cy_ref), (None, near_ref, side_ref),
            (far_out, near_out, side_out),
        )
        low, high = pl.ds(0, WIDTH), pl.ds(count_x - WIDTH, WIDTH)

        @pl.when(place.even)
        def _():
            final_ref[high] = near_out[...]
            final_ref[low] = far_out[...]

        @pl.when(jnp.logical_not(place.even))
        def _():
            final_ref[low] = near_out[...]
            final_ref[high] = far_out[...]

        final_ref[:, pl.ds(place.block(count_y), SIDE)] = side_out[...]
        wants_last = jnp.broadcast_to(flag_ref[0:1, :], (count_a, count_z)) > 0.5
        for b in range(count_b):
            late_ref[b] = jnp.where(
                wants_last, even_rows(final_ref, 0, 0, count_a, b), even_ref[b]
            )
        send_into(late_ref, matrix_ref, sent_ref)

    slab, _, side_shape = face_shapes(count_x, count_y, count_z)
    return pl.pallas_call(
        kernel,
        out_shape=(
            shape(*current.shape),
            shape(count_b, count_a, count_z),
            sent_shape(count_a, count_b, count_z),
        ),
        in_specs=[spec(pltpu.VMEM)] * 10,
        out_specs=(spec(pltpu.VMEM),) * 3,
        scratch_shapes=[
            pltpu.VMEM(slab.shape, F32),
            pltpu.VMEM(slab.shape, F32),
            pltpu.VMEM(side_shape.shape, F32),
        ],
        input_output_aliases={2: 0},
        compiler_params=params(12),
        cost_estimate=cost(count_x * count_y * count_z, 10, 3),
        name="last_step",
    )(flag, even_before, current, *parts, near, side, matrix)


def far_rows(count_b):
    return -(-2 * (count_b // GROUP) // 16) * 16


def last_far(flag, final, late, cx, far, matrix):
    count_x, count_y, count_z = final.shape
    count_b, count_a, _ = late.shape
    rows, pair = far_rows(count_b), WIDTH // 2

    def kernel(
        flag_ref, final_in, late_in, cx_ref, far_ref, matrix_ref, final_ref, late_ref, sent_ref, lhs,
    ):
        place = Place()
        wants_last = jnp.broadcast_to(flag_ref[0:1, :], (1, count_z)) > 0.5
        lhs[...] = jnp.zeros_like(lhs)

        def correct(first_x, first_c, first_a, terms):
            for r in range(WIDTH):
                final_ref[first_x + r] = final_ref[first_x + r] + cx_ref[first_c + r] * terms(
                    far_ref, r
                )
            for b in range(count_b):
                for i in range(pair):
                    value = jnp.where(
                        wants_last,
                        final_ref[first_x + 2 * i, pl.ds(2 * b, 1), :],
                        late_ref[b, pl.ds(first_a + i, 1), :],
                    )
                    late_ref[b, pl.ds(first_a + i, 1), :] = value
                    lanes = pl.ds(b % GROUP * count_z, count_z)
                    lhs[pl.ds(b // GROUP * pair + i, 1), lanes] = value

        @pl.when(place.even)
        def _():
            correct(0, 0, 0, low_terms)

        @pl.when(jnp.logical_not(place.even))
        def _():
            correct(count_x - WIDTH, WIDTH, count_a - pair, high_terms)

        result = exact_dot(lhs[...], matrix_ref[...])
        parts = [result[:, kind * count_z : (kind + 1) * count_z] for kind in range(4)]
        sent_ref[pl.ds(0, rows), :] = parts[0]
        sent_ref[pl.ds(rows, rows), :] = parts[1]
        sent_ref[pl.ds(2 * rows, rows), :] = parts[2] + pltpu.roll(parts[3], REACH, 1)

    return pl.pallas_call(
        kernel,
        out_shape=(shape(*final.shape), shape(*late.shape), shape(3 * rows, count_z)),
        in_specs=[spec(pltpu.VMEM)] * 6,
        out_specs=(spec(pltpu.VMEM),) * 3,
        scratch_shapes=[pltpu.VMEM((rows, GROUP * count_z), F32)],
        input_output_aliases={1: 0, 2: 1},
        compiler_params=params(12),
        cost_estimate=cost(WIDTH * count_y * count_z, 20, 3),
        name="last_far",
    )(flag, final, late, cx, far, matrix)


def write_out(level):
    def kernel(level_ref, out_ref, sem):
        copy = pltpu.make_async_copy(level_ref, out_ref, sem)
        copy.start()
        copy.wait()

    return pl.pallas_call(
        kernel,
        out_shape=shape(*level.shape),
        in_specs=[spec(pltpu.VMEM)],
        out_specs=spec(pltpu.HBM),
        scratch_shapes=[pltpu.SemaphoreType.DMA],
        compiler_params=params(4),
        cost_estimate=cost(level.size, 0, 2),
        name="write_out",
    )(level)


CODE_BITS = 5
PER_CODE = 6


def lag_image(count_a, lags, own, other, extra=None, before=None):
    _, total_rows, count_z = own.shape
    groups = total_rows // count_a
    half = count_z // GROUP
    last = before is not None
    count_h = before.shape[0] if last else lags.shape[0]
    codes = -(-count_h // PER_CODE)
    pair = WIDTH // 2

    def kernel(*refs):
        refs = list(refs)
        take = lambda count: [refs.pop(0) for _ in range(count)]
        lags_ref, own_ref, other_ref = take(3)
        if last:
            extra_ref, before_ref = take(2)
        (out_ref,) = take(1)
        if not last:
            (codes_ref,) = take(1)
        mains, edges = take(2)
        if last:
            store, sem = take(2)
        else:
            store = out_ref
            lag_of, sem = take(2)
        place = Place()
        if last:
            packed_lags = [lags_ref[k : k + 1, :][0, 0] for k in range(codes)]
            mask = (1 << CODE_BITS) - 1
            lag_list = [
                ((packed_lags[h // PER_CODE] >> (h % PER_CODE * CODE_BITS)) & mask) - LAGMAX
                for h in range(count_h)
            ]
        else:
            copy = pltpu.make_async_copy(lags_ref, lag_of, sem)
            copy.start()
        is_source = place.field == 0

        def useful(rows):
            lane = lax.broadcasted_iota(jnp.int32, (rows, count_z), 1) % half
            return jnp.where(is_source, lane, half - 1 - lane) < REACH

        slots, _ = edge_slots(count_a, groups, count_z)
        for parity in range(2):
            mains[parity] = other_ref[pl.ds(parity * total_rows, total_rows), :]
        for parity, g, row, shift in slots:
            part = other_ref[pl.ds(2 * total_rows + row, count_a), :]
            part = pltpu.roll(part, count_z - shift, 1) if shift else part
            edges[parity, pl.ds(g * count_a, count_a), :] = jnp.where(useful(count_a), part, 0.0)
        if last:
            rows = extra_ref.shape[0] // 3
            border = extra_ref[pl.ds(2 * rows, rows), :]
            borders = [
                jnp.where(useful(rows), part, 0.0)
                for part in (border, pltpu.roll(border, count_z - REACH, 1))
            ]

            def overwrite(first_a):
                for g in range(groups):
                    target = pl.ds(g * count_a + first_a, pair)
                    for parity in range(2):
                        mains[parity, target, :] = extra_ref[
                            pl.ds(parity * rows + g * pair, pair), :
                        ]
                        edges[parity, target, :] = borders[parity][g * pair : (g + 1) * pair]

            pl.when(place.even)(lambda: overwrite(0))
            pl.when(jnp.logical_not(place.even))(lambda: overwrite(count_a - pair))
        else:
            copy.wait()
            lag_list = [lag_of[h] for h in range(count_h)]
            for k in range(codes):
                code = jnp.int32(0)
                for h in range(k * PER_CODE, min((k + 1) * PER_CODE, count_h)):
                    code = code | ((lag_list[h] + LAGMAX) << (h % PER_CODE * CODE_BITS))
                codes_ref[k : k + 1, :] = jnp.full((1, count_z), code, jnp.int32)
        for h, lag in enumerate(lag_list):
            parity, own_shift, other_shift = lag_shifts(lag, is_source)
            product = moved(mains[parity], edges[parity], other_shift)
            if last:
                product = product * own_ref[h]
            else:
                product = product * moved(own_ref[parity], own_ref[2 + parity], own_shift)
            for g in range(groups):
                part = product[g * count_a : (g + 1) * count_a]
                lanes = pl.ds(g * count_z, count_z)
                if last:
                    part = part + before_ref[h, :, lanes]
                store[h, :, lanes] = part
            if last:
                pltpu.make_async_copy(store.at[h], out_ref.at[h], sem).start()
        if last:
            pltpu.make_async_copy(store, out_ref, sem).wait()

    image = shape(count_h, count_a, groups * count_z)
    operands = [lags, own, other] + ([extra, before] if last else [])
    scratch = [pltpu.VMEM((2, total_rows, count_z), F32)] * 2
    scratch.append(pltpu.VMEM(image.shape, F32) if last else pltpu.SMEM((count_h,), jnp.int32))
    scratch.append(pltpu.SemaphoreType.DMA)
    return pl.pallas_call(
        kernel,
        out_shape=image if last else (image, shape(8, count_z, dtype=jnp.int32)),
        in_specs=[spec(pltpu.VMEM if last else pltpu.HBM)]
        + [spec(pltpu.VMEM)] * (len(operands) - 1),
        out_specs=spec(pltpu.HBM) if last else (spec(pltpu.VMEM),) * 2,
        scratch_shapes=scratch,
        compiler_params=params(12),
        cost_estimate=cost(count_h * total_rows * count_z, 10, 2),
        name="last_image" if last else "early_image",
    )(*operands)


def body(
    field_now,
    field_prev,
    courant_squared,
    source_cells,
    source_wave,
    receiver_cells,
    receiver_wave,
    snapshot_steps,
    lag_offsets,
):
    count_x, _, count_z = field_now.shape
    loop_size = lax.axis_size("gx")
    half_size = loop_size // 2
    turn = loop_size // 4
    assert lax.axis_size("gy") == 2 and half_size % 2 == 0

    slabs = [(i - turn) % loop_size % half_size for i in range(loop_size)]

    def pairs(odd):
        found = []
        for i, slab in enumerate(slabs):
            if slab % 2 == odd and slab != half_size - 1:
                j = (i + 1) % loop_size
                found += [(i, j), (j, i)]
        return found

    near_pairs, far_pairs = pairs(0), pairs(1)
    across = [(i, (i + half_size) % loop_size) for i in range(loop_size)]

    def send_far(far):
        return lax.ppermute(far, "gx", far_pairs)

    def send_near(near, side):
        near = lax.ppermute(near, "gx", near_pairs)
        return near, lax.ppermute(side, "gy", [(0, 1), (1, 0)])

    def exchange(faces):
        far, near, side = faces
        return (send_far(far), *send_near(near, side))

    def first_exchange(faces):
        far, near, side = faces
        near_even = lax.ppermute(near, "gx", [pair for pair in near_pairs if slabs[pair[0]] % 2])
        far = send_far(far)
        near_odd = lax.ppermute(near, "gx", [pair for pair in near_pairs if not slabs[pair[0]] % 2])
        side = lax.ppermute(side, "gy", [(0, 1), (1, 0)])
        return far, (near_even, near_odd), side

    matrices = jnp.asarray(
        np.stack([pack_matrix(window, count_z) for window in (0, 1)]), dtype=BF16
    )
    raw = (source_cells, source_wave, receiver_cells, receiver_wave)
    field_kept, field_prev, courant_squared, matrices, snapshot_steps, lag_offsets, *raw = (
        pltpu.with_memory_space_constraint(array, pltpu.HBM)
        for array in (
            field_now, field_prev, courant_squared, matrices, snapshot_steps, lag_offsets, *raw
        )
    )
    halos = first_exchange(first_faces(field_kept))
    next1, qx, qy, courant, cx, cy, points, waves, whole0 = inner_step(
        0, raw, None, field_now, None, field_prev, courant_squared
    )
    faces = halo_step((qx, qy, cx, cy), halos)
    halos = exchange(faces)
    next2, qx, qy, whole1, added = inner_step(1, points, waves, next1, faces, whole0, courant)
    faces = halo_step((qx, qy, cx, cy), halos)
    halos = exchange(faces)
    next3, qx, qy, whole2, own_early, sent_early, own_matrix, sent_matrix, flag = inner_step(
        2, points, waves, next2, faces, whole1, courant, snapshot_steps, matrices
    )
    other_early = lax.ppermute(sent_early, "gx", across)
    faces = halo_step((qx, qy, cx, cy), halos)
    far, near, side = exchange(faces)
    next4, qx, qy, even3 = inner_step(3, added, None, next3, faces, whole2, courant)
    final, late, sent_late = last_step(
        flag, even3, next4, (qx, qy, cx, cy), near, side, sent_matrix
    )
    other_late = lax.ppermute(sent_late, "gx", across)
    partial, codes = lag_image(count_x // 2, lag_offsets, own_early, other_early)
    final, late, sent_far = last_far(flag, final, late, cx, far, sent_matrix)
    extra = lax.ppermute(sent_far, "gx", across)
    own_late = pack_own(lag_offsets, late, own_matrix)
    image = lag_image(count_x // 2, codes, own_late, other_late, extra, partial)
    return write_out(final), jnp.transpose(image, (1, 0, 2))


def solution(mesh):
    placed = (
        P(("shots", "gx"), "gy", None),
        P(("shots", "gx"), "gy", None),
        P("gx", "gy", None),
        P(None, "shots"),
        P(None, "shots"),
        P(None, "shots"),
        P(None, "shots"),
        P("shots", None),
        P(),
    )
    return jax.shard_map(
        body,
        mesh=mesh,
        in_specs=placed,
        out_specs=(P(("shots", "gx"), "gy", None), P(("shots", "gx"), None, "gy")),
        check_vma=False,
    )
```

```python
import jax
import jax.numpy as jnp
import numpy as np
from jax import lax
from jax.experimental import pallas as pl
from jax.experimental.pallas import tpu as pltpu
from jax.sharding import PartitionSpec as P

STEPS = 4
WIDTH = 4
LAGMAX = 8
REACH = LAGMAX // 2
GROUP = 4
SIDE = 8

SCALE = 5040.0
BAND = (8064.0, -1008.0, 128.0, -9.0)
CENTRE = 3.0 * (-205.0 / 72.0)
WEIGHTS = (1.6, -0.2, 8.0 / 315.0, -1.0 / 560.0)

F32 = jnp.float32
BF16 = jnp.bfloat16


def shape(*dims, dtype=F32):
    return jax.ShapeDtypeStruct(dims, dtype)


def params(megabytes):
    return pltpu.CompilerParams(vmem_limit_bytes=megabytes << 20)


def spec(space):
    return pl.BlockSpec(memory_space=space)


def cost(count, flops_each, arrays):
    return pl.CostEstimate(
        flops=int(count * flops_each), bytes_accessed=int(4 * count * arrays), transcendentals=0
    )


def split3(values):
    high = values.astype(BF16)
    rest = values - high.astype(F32)
    middle = rest.astype(BF16)
    low = (rest - middle.astype(F32)).astype(BF16)
    return high, middle, low


def exact_dot(values, matrix):
    rows = values.shape[0]
    stacked = jnp.concatenate(split3(values), axis=0)
    result = jnp.dot(stacked, matrix, preferred_element_type=F32)
    return (result[2 * rows :] + result[rows : 2 * rows]) + result[:rows]


class Place:
    def __init__(self):
        loop_size = lax.axis_size("gx")
        self.half = loop_size // 2
        relative = lax.rem(lax.axis_index("gx") + loop_size - loop_size // 4, loop_size)
        self.field = relative // self.half
        self.slab = lax.rem(relative, self.half)
        self.even = lax.rem(self.slab, 2) == 0
        self.y = lax.axis_index("gy")

    def block(self, count_y):
        return pl.multiple_of((1 - self.y) * (count_y - SIDE), SIDE)


def first_faces(field):
    count_x, count_y, count_z = field.shape
    top = count_x - WIDTH

    def kernel(field_ref, far_ref, near_ref, side_ref, sems):
        place = Place()
        far = jnp.where(place.even, 0, top)
        sources = [
            field_ref.at[pl.ds(far, WIDTH)],
            field_ref.at[pl.ds(top - far, WIDTH)],
            field_ref.at[:, pl.ds(place.block(count_y), SIDE)],
        ]
        copies = [
            pltpu.make_async_copy(source, target, sems.at[index])
            for index, (source, target) in enumerate(zip(sources, (far_ref, near_ref, side_ref)))
        ]
        for copy in copies:
            copy.start()
        for copy in copies:
            copy.wait()

    return pl.pallas_call(
        kernel,
        out_shape=face_shapes(count_x, count_y, count_z),
        in_specs=[spec(pltpu.HBM)],
        out_specs=(spec(pltpu.VMEM),) * 3,
        scratch_shapes=[pltpu.SemaphoreType.DMA((3,))],
        compiler_params=params(8),
        name="first_faces",
    )(field)


def face_shapes(count_x, count_y, count_z):
    slab = shape(WIDTH, count_y, count_z)
    return slab, slab, shape(count_x, SIDE, count_z)


def even_rows(level_ref, offset_x, offset_y, count_a, b):
    rows, stride, lanes = level_ref.shape
    flat = level_ref.reshape(rows * stride, lanes)
    start = offset_x * stride + offset_y + 2 * b
    return flat[pl.ds(start, count_a, stride=2 * stride), :]


def inner_step(number, points, waves, current, faces, previous, courant, snapshots=None, matrices=None):
    count_x, count_y, count_z = current.shape
    count_a, count_b = count_x // 2, count_y // 2
    first = faces is None
    last = number == STEPS - 1
    snapshot = number == STEPS // 2
    ahead = number == 1
    if last:
        count_j = 0
    elif first:
        count_j = -(-max(array.shape[1] for array in points) // 128) * 128
    else:
        count_j = points.shape[1]

    def kernel(*refs):
        refs = list(refs)
        take = lambda count: [refs.pop(0) for _ in range(count)]
        if first:
            raw_refs = take(4)
        elif last:
            (added_ref,) = take(1)
        else:
            points_ref, waves_ref = take(2)
        (current_ref,) = take(1)
        if not first:
            far_ref, near_ref, side_ref = take(3)
        previous_ref, courant_ref = take(2)
        if snapshot:
            steps_ref, matrices_ref = take(2)
        next_ref, qx_ref, qy_ref = take(3)
        if first:
            kept_ref, cx_ref, cy_ref, points_ref, waves_ref = take(5)
        if not last:
            (whole_ref,) = take(1)
        if snapshot:
            own_out, sent_out, own_matrix, sent_matrix, flag_ref = take(5)
        if ahead:
            (ahead_ref,) = take(1)
        if last:
            (even_ref,) = take(1)
        padded, zpart, addpart = take(3)
        if last:
            addpart = added_ref
        if first:
            before_ref = take(1)[0]
            raw_refs_in, raw_refs = raw_refs, take(4)
            (sems,) = take(1)
        if snapshot:
            even_ref, wanted, sems = take(3)

        place = Place()
        block = place.block(count_y)
        rows, columns = pl.ds(WIDTH, count_x), pl.ds(SIDE, count_y)
        if first:
            copies = [
                pltpu.make_async_copy(source, target, sems.at[index])
                for index, (source, target) in enumerate(
                    zip(
                        (*raw_refs_in, previous_ref, courant_ref),
                        (*raw_refs, before_ref, kept_ref),
                    )
                )
            ]
            for copy in copies:
                copy.start()
        else:
            before_ref, kept_ref = previous_ref, courant_ref
        if snapshot:
            copies = [
                pltpu.make_async_copy(steps_ref, wanted, sems.at[0]),
                pltpu.make_async_copy(matrices_ref.at[place.field], own_matrix, sems.at[1]),
                pltpu.make_async_copy(matrices_ref.at[1 - place.field], sent_matrix, sems.at[2]),
            ]
            for copy in copies:
                copy.start()

        zero_x = jnp.zeros((WIDTH, count_y + 2 * SIDE, count_z), F32)
        padded[pl.ds(0, WIDTH)] = zero_x
        padded[pl.ds(count_x + WIDTH, WIDTH)] = zero_x
        zero_y = jnp.zeros((count_x, SIDE, count_z), F32)
        padded[rows, pl.ds(0, SIDE)] = zero_y
        padded[rows, pl.ds(count_y + SIDE, SIDE)] = zero_y

        padded[rows, columns] = current_ref[...]
        if not first:
            low, high = pl.ds(WIDTH, WIDTH), pl.ds(count_x, WIDTH)

            @pl.when(place.even)
            def _():
                padded[high, columns] = near_ref[...]
                padded[low, columns] = far_ref[...]

            @pl.when(jnp.logical_not(place.even))
            def _():
                padded[low, columns] = near_ref[...]
                padded[high, columns] = far_ref[...]

            padded[rows, pl.ds(pl.multiple_of(block + SIDE, SIDE), SIDE)] = side_ref[...]

        gap = jnp.abs(
            lax.broadcasted_iota(jnp.int32, (count_z, count_z), 0)
            - lax.broadcasted_iota(jnp.int32, (count_z, count_z), 1)
        )
        band = jnp.zeros((count_z, count_z), F32)
        for offset, weight in enumerate(BAND, 1):
            band = jnp.where(gap == offset, weight, band)
        band = jnp.concatenate([band.astype(BF16)] * 3, axis=0)

        chunk = 8

        def multiply(index, _):
            start = pl.multiple_of(index * chunk, chunk)
            values = padded[pl.ds(start + WIDTH, chunk), columns]
            terms = jnp.concatenate(split3(values.reshape(chunk * count_y, count_z)), axis=1)
            zpart[pl.ds(start, chunk)] = jnp.dot(
                terms, band, preferred_element_type=F32
            ).reshape(chunk, count_y, count_z)
            return 0

        chunks = count_x // chunk
        if first or last:
            lax.fori_loop(0, chunks, multiply, 0)

        if first:
            for copy in copies[:4]:
                copy.wait()
            points_ref[...] = jnp.full(points_ref.shape, -1, jnp.int32)
            waves_ref[...] = jnp.zeros(waves_ref.shape, F32)

            def choose(cells_ref, wave_ref):
                count = cells_ref.shape[1]
                points_ref[pl.ds(0, 3), pl.ds(0, count)] = cells_ref[...]
                waves_ref[pl.ds(0, STEPS), pl.ds(0, count)] = wave_ref[...]

            @pl.when(place.field == 0)
            def _():
                choose(raw_refs[0], raw_refs[1])

            @pl.when(place.field != 0)
            def _():
                choose(raw_refs[2], raw_refs[3])

        if not last:
            px = points_ref[0:1, :] - place.slab * count_x
            py = points_ref[1:2, :] - place.y * count_y
            inside = (px >= 0) & (px < count_x) & (py >= 0) & (py < count_y)
            home = jnp.where(inside, px * count_y + py, -1)
            at_z = (
                lax.broadcasted_iota(jnp.int32, (count_z, count_j), 0) == points_ref[2:3, :]
            )

            def spread_of(step):
                terms = split3(jnp.where(at_z, waves_ref[step : step + 1, :], 0.0))
                return jnp.concatenate(terms, axis=1)

            spreads = [(addpart, spread_of(number))]
            if ahead:
                spreads.append((ahead_ref, spread_of(STEPS - 1)))

        def inject(index, _):
            start = pl.multiple_of(index * chunk, chunk)
            here = start * count_y + lax.broadcasted_iota(
                jnp.int32, (chunk * count_y, count_j), 0
            )
            hit = jnp.where(here == home, 1.0, 0.0).astype(BF16)
            hit = jnp.concatenate([hit] * 3, axis=1)
            for target, spread in spreads:
                added = lax.dot_general(
                    hit, spread, (((1,), (1,)), ((), ())), preferred_element_type=F32
                )
                target[pl.ds(start, chunk)] = added.reshape(chunk, count_y, count_z)
            return 0

        def both(index, _):
            multiply(index, 0)
            return inject(index, 0)

        if not last:
            lax.fori_loop(0, chunks, inject if first else both, 0)
        if first:
            for copy in copies[4:]:
                copy.wait()

        def row(x, _):
            middle = padded[x + WIDTH, columns]
            total = CENTRE * middle + (1.0 / SCALE) * zpart[x]
            for offset, weight in enumerate(WEIGHTS, 1):
                paired = padded[x + WIDTH + offset, columns] + padded[x + WIDTH - offset, columns]
                paired = paired + (
                    padded[x + WIDTH, pl.ds(SIDE + offset, count_y)]
                    + padded[x + WIDTH, pl.ds(SIDE - offset, count_y)]
                )
                total = total + weight * paired
            if not last:
                whole_ref[x] = middle
            next_ref[x] = (2.0 * middle - before_ref[x] + kept_ref[x] * total) + addpart[x]
            return 0

        lax.fori_loop(0, count_x, row, 0, unroll=4)

        qx_ref[pl.ds(0, WIDTH)] = next_ref[pl.ds(0, WIDTH)]
        qx_ref[pl.ds(WIDTH, WIDTH)] = next_ref[pl.ds(count_x - WIDTH, WIDTH)]
        qy_ref[...] = next_ref[:, pl.ds(block, SIDE)]
        if first:
            cx_ref[pl.ds(0, WIDTH)] = kept_ref[pl.ds(0, WIDTH)]
            cx_ref[pl.ds(WIDTH, WIDTH)] = kept_ref[pl.ds(count_x - WIDTH, WIDTH)]
            cy_ref[...] = kept_ref[:, pl.ds(block, SIDE)]
        if last:
            for b in range(count_b):
                even_ref[b] = even_rows(padded, WIDTH, SIDE, count_a, b)
        if snapshot:
            for copy in copies:
                copy.wait()
            flag_ref[...] = jnp.where(
                wanted[place.field, 1] == STEPS, jnp.ones(flag_ref.shape, F32), 0.0
            )
            earlier = wanted[place.field, 0] == number - 1

            @pl.when(earlier)
            def _():
                for b in range(count_b):
                    even_ref[b] = even_rows(previous_ref, 0, 0, count_a, b)

            @pl.when(jnp.logical_not(earlier))
            def _():
                for b in range(count_b):
                    even_ref[b] = even_rows(padded, WIDTH, SIDE, count_a, b)

            for kind, part in enumerate(packed(even_ref, own_matrix)):
                own_out[kind] = part
            send_into(even_ref, sent_matrix, sent_out)

    full = shape(count_x, count_y, count_z)
    slab, side = shape(2 * WIDTH, count_y, count_z), shape(count_x, SIDE, count_z)
    even = shape(count_b, count_a, count_z)
    outs = [full, slab, side]
    if first:
        outs += [full, slab, side, shape(8, count_j, dtype=jnp.int32), shape(8, count_j)]
    if not last:
        outs.append(full)
    if snapshot:
        size = GROUP * count_z
        outs += [
            shape(4, count_b // GROUP * count_a, count_z),
            sent_shape(count_a, count_b, count_z),
            shape(size, size, dtype=BF16),
            shape(size, size, dtype=BF16),
            shape(8, count_z),
        ]
    if ahead:
        outs.append(full)
    if last:
        outs.append(even)
    place_of = spec(pltpu.HBM) if first else spec(pltpu.VMEM)
    if first:
        operands = [*points, current]
    elif last:
        operands = [points, current]
    else:
        operands = [points, waves, current]
    specs = [place_of] * (len(operands) - 1) + [spec(pltpu.VMEM)]
    if not first:
        operands += list(faces)
        specs += [spec(pltpu.VMEM)] * 3
    operands += [previous, courant]
    specs += [place_of] * 2
    scratch = [
        pltpu.VMEM((count_x + 2 * WIDTH, count_y + 2 * SIDE, count_z), F32),
        pltpu.VMEM(full.shape, F32),
        pltpu.VMEM(full.shape, F32),
    ]
    if first:
        scratch.append(pltpu.VMEM(full.shape, F32))
        scratch += [pltpu.VMEM(array.shape, array.dtype) for array in points]
        scratch.append(pltpu.SemaphoreType.DMA((6,)))
    if snapshot:
        operands += [snapshots, matrices]
        specs += [spec(pltpu.HBM)] * 2
        scratch += [
            pltpu.VMEM(even.shape, F32),
            pltpu.SMEM(snapshots.shape, jnp.int32),
            pltpu.SemaphoreType.DMA((3,)),
        ]
    return pl.pallas_call(
        kernel,
        out_shape=tuple(outs),
        in_specs=specs,
        out_specs=(spec(pltpu.VMEM),) * len(outs),
        scratch_shapes=scratch,
        compiler_params=params(20),
        cost_estimate=cost(count_x * count_y * count_z, 60, 6),
    )(*operands)


def low_terms(halo_ref, r):
    total = None
    for k in range(r + 1, WIDTH + 1):
        term = WEIGHTS[k - 1] * halo_ref[WIDTH + r - k]
        total = term if total is None else total + term
    return total


def high_terms(halo_ref, r):
    total = None
    for k in range(WIDTH - r, WIDTH + 1):
        term = WEIGHTS[k - 1] * halo_ref[r + k - WIDTH]
        total = term if total is None else total + term
    return total


def add_halo(place, parts, halos, outs):
    qx_ref, qy_ref, cx_ref, cy_ref = parts
    far_in, near_in, side_in = halos
    far_out, near_out, side_out = outs
    count_y, count_x = qx_ref.shape[1], qy_ref.shape[0]
    block = place.block(count_y)

    def along_x(low_in, high_in, low_out, high_out):
        for r in range(WIDTH):
            low, high = qx_ref[r], qx_ref[WIDTH + r]
            if low_in is not None:
                low = low + cx_ref[r] * low_terms(low_in, r)
            if high_in is not None:
                high = high + cx_ref[WIDTH + r] * high_terms(high_in, r)
            low_out[r], high_out[r] = low, high
        side_out[pl.ds(0, WIDTH)] = low_out[:, pl.ds(block, SIDE)]
        side_out[pl.ds(count_x - WIDTH, WIDTH)] = high_out[:, pl.ds(block, SIDE)]

    inner = pl.ds(WIDTH, count_x - 2 * WIDTH)
    side_out[inner] = qy_ref[inner]

    @pl.when(place.even)
    def _():
        along_x(far_in, near_in, far_out, near_out)

    @pl.when(jnp.logical_not(place.even))
    def _():
        along_x(near_in, far_in, near_out, far_out)

    def along_y(shifts, masks):
        halo = side_in[...]
        lanes = halo.shape[2]
        line = lax.broadcasted_iota(jnp.int32, (1, SIDE, lanes), 1)
        total = None
        for k in range(1, WIDTH + 1):
            weight = jnp.where(masks(line, k), WEIGHTS[k - 1], 0.0)
            term = weight * pltpu.roll(halo, shifts(k), 1)
            total = term if total is None else total + term
        side_out[...] = side_out[...] + cy_ref[...] * total

    @pl.when(place.y == 0)
    def _():
        along_y(lambda k: SIDE - k, lambda line, k: line >= SIDE - k)

    @pl.when(place.y != 0)
    def _():
        along_y(lambda k: k, lambda line, k: line < k)

    def corners(low_out, high_out):
        low_out[:, pl.ds(block, SIDE)] = side_out[pl.ds(0, WIDTH)]
        high_out[:, pl.ds(block, SIDE)] = side_out[pl.ds(count_x - WIDTH, WIDTH)]

    @pl.when(place.even)
    def _():
        corners(far_out, near_out)

    @pl.when(jnp.logical_not(place.even))
    def _():
        corners(near_out, far_out)


def halo_step(parts, halos):
    count_y, (count_x, _, count_z) = parts[0].shape[1], parts[1].shape

    def kernel(*refs):
        add_halo(Place(), refs[:4], refs[4:7], refs[7:])

    return pl.pallas_call(
        kernel,
        out_shape=face_shapes(count_x, count_y, count_z),
        in_specs=[spec(pltpu.VMEM)] * 7,
        out_specs=(spec(pltpu.VMEM),) * 3,
        compiler_params=params(8),
        cost_estimate=cost(16 * count_y * count_z, 10, 6),
        name="halo_step",
    )(*parts, *halos)


def pack_matrix(window, count_z):
    half = count_z // GROUP
    size = GROUP * count_z
    row, column = np.arange(size)[:, None], np.arange(size)[None, :]
    row_b, row_z = row // count_z, row % count_z
    kind = column // count_z
    parity = kind % 2
    lane_b, lane_i = (column % count_z) // half, column % half
    main = (row_b == lane_b) & (row_z == 2 * (half * window + lane_i) + parity)
    wanted_b = (lane_b + (GROUP - 1 if window == 0 else 1)) % GROUP
    wanted_z = 2 * (half * (1 - window) + lane_i) + parity
    useful = lane_i < REACH if window == 0 else lane_i >= half - REACH
    edge = (row_b == wanted_b) & (row_z == wanted_z) & useful
    return np.where(kind < 2, main, edge).astype(np.float32)


def packed(even_ref, matrix_ref):
    count_b, _, count_z = even_ref.shape
    rows = [
        jnp.concatenate([even_ref[b + i] for i in range(GROUP)], axis=1)
        for b in range(0, count_b, GROUP)
    ]
    result = exact_dot(jnp.concatenate(rows, axis=0), matrix_ref[...])
    return [result[:, kind * count_z : (kind + 1) * count_z] for kind in range(4)]


def lag_shifts(lag, is_source):
    parity = lag & 1
    source_shift = -((lag + parity) >> 1)
    receiver_shift = (lag - parity) >> 1
    return (
        parity,
        jnp.where(is_source, source_shift, receiver_shift),
        jnp.where(is_source, receiver_shift, source_shift),
    )


def moved(main, edge, shift):
    count_z = main.shape[1]
    half = count_z // GROUP
    lane = lax.broadcasted_iota(jnp.int32, (1, count_z), 1) % half
    mask = (lane < shift) | (lane >= half + shift)
    return pltpu.roll(jnp.where(mask, edge, main), (count_z - shift) & (count_z - 1), 1)


def pack_own(lags, even, matrix):
    count_b, count_a, count_z = even.shape
    total_rows = count_b // GROUP * count_a
    (count_h,) = lags.shape

    def kernel(lags_ref, even_ref, matrix_ref, out_ref, windows, lag_of, sem):
        copy = pltpu.make_async_copy(lags_ref, lag_of, sem)
        copy.start()
        place = Place()
        for kind, part in enumerate(packed(even_ref, matrix_ref)):
            windows[kind] = part
        copy.wait()
        for h in range(count_h):
            parity, shift, _ = lag_shifts(lag_of[h], place.field == 0)
            out_ref[h] = moved(windows[parity], windows[2 + parity], shift)

    return pl.pallas_call(
        kernel,
        out_shape=shape(count_h, total_rows, count_z),
        in_specs=[spec(pltpu.HBM)] + [spec(pltpu.VMEM)] * 2,
        out_specs=spec(pltpu.VMEM),
        scratch_shapes=[
            pltpu.VMEM((4, total_rows, count_z), F32),
            pltpu.SMEM((count_h,), jnp.int32),
            pltpu.SemaphoreType.DMA,
        ],
        compiler_params=params(8),
        cost_estimate=cost(count_b * count_a * count_z, 1024, 4),
        name="pack_own",
    )(lags, even, matrix)


def edge_slots(count_a, groups, count_z):
    fits = count_z // GROUP // REACH
    slots = []
    for index in range(2 * groups):
        slots.append((index // groups, index % groups, index // fits * count_a, index % fits * REACH))
    return slots, -(-2 * groups // fits) * count_a


def send_into(even_ref, matrix_ref, out_ref):
    count_b, count_a, count_z = even_ref.shape
    groups = count_b // GROUP
    total_rows = groups * count_a
    parts = packed(even_ref, matrix_ref)
    out_ref[pl.ds(0, total_rows), :] = parts[0]
    out_ref[pl.ds(total_rows, total_rows), :] = parts[1]
    slots, _ = edge_slots(count_a, groups, count_z)
    sums = {}
    for parity, g, row, shift in slots:
        part = parts[2 + parity][g * count_a : (g + 1) * count_a]
        part = pltpu.roll(part, shift, 1) if shift else part
        sums[row] = sums[row] + part if row in sums else part
    for row, part in sums.items():
        out_ref[pl.ds(2 * total_rows + row, count_a), :] = part


def sent_shape(count_a, count_b, count_z):
    groups = count_b // GROUP
    _, extra = edge_slots(count_a, groups, count_z)
    return shape(2 * groups * count_a + extra, count_z)


def last_step(flag, even_before, current, parts, near, side, matrix):
    count_x, count_y, count_z = current.shape
    count_a, count_b = count_x // 2, count_y // 2

    def kernel(
        flag_ref, even_ref, current_ref, qx_ref, qy_ref, cx_ref, cy_ref, near_ref, side_ref,
        matrix_ref, final_ref, late_ref, sent_ref, far_out, near_out, side_out,
    ):
        place = Place()
        add_halo(
            place, (qx_ref, qy_ref, cx_ref, cy_ref), (None, near_ref, side_ref),
            (far_out, near_out, side_out),
        )
        low, high = pl.ds(0, WIDTH), pl.ds(count_x - WIDTH, WIDTH)

        @pl.when(place.even)
        def _():
            final_ref[high] = near_out[...]
            final_ref[low] = far_out[...]

        @pl.when(jnp.logical_not(place.even))
        def _():
            final_ref[low] = near_out[...]
            final_ref[high] = far_out[...]

        final_ref[:, pl.ds(place.block(count_y), SIDE)] = side_out[...]
        wants_last = jnp.broadcast_to(flag_ref[0:1, :], (count_a, count_z)) > 0.5
        for b in range(count_b):
            late_ref[b] = jnp.where(
                wants_last, even_rows(final_ref, 0, 0, count_a, b), even_ref[b]
            )
        send_into(late_ref, matrix_ref, sent_ref)

    slab, _, side_shape = face_shapes(count_x, count_y, count_z)
    return pl.pallas_call(
        kernel,
        out_shape=(
            shape(*current.shape),
            shape(count_b, count_a, count_z),
            sent_shape(count_a, count_b, count_z),
        ),
        in_specs=[spec(pltpu.VMEM)] * 10,
        out_specs=(spec(pltpu.VMEM),) * 3,
        scratch_shapes=[
            pltpu.VMEM(slab.shape, F32),
            pltpu.VMEM(slab.shape, F32),
            pltpu.VMEM(side_shape.shape, F32),
        ],
        input_output_aliases={2: 0},
        compiler_params=params(12),
        cost_estimate=cost(count_x * count_y * count_z, 10, 3),
        name="last_step",
    )(flag, even_before, current, *parts, near, side, matrix)


def far_rows(count_b):
    return -(-2 * (count_b // GROUP) // 16) * 16


def last_far(flag, final, late, cx, far, matrix):
    count_x, count_y, count_z = final.shape
    count_b, count_a, _ = late.shape
    rows, pair = far_rows(count_b), WIDTH // 2

    def kernel(
        flag_ref, final_in, late_in, cx_ref, far_ref, matrix_ref, final_ref, late_ref, sent_ref, lhs,
    ):
        place = Place()
        wants_last = jnp.broadcast_to(flag_ref[0:1, :], (1, count_z)) > 0.5
        lhs[...] = jnp.zeros_like(lhs)

        def correct(first_x, first_c, first_a, terms):
            for r in range(WIDTH):
                final_ref[first_x + r] = final_ref[first_x + r] + cx_ref[first_c + r] * terms(
                    far_ref, r
                )
            for b in range(count_b):
                for i in range(pair):
                    value = jnp.where(
                        wants_last,
                        final_ref[first_x + 2 * i, pl.ds(2 * b, 1), :],
                        late_ref[b, pl.ds(first_a + i, 1), :],
                    )
                    late_ref[b, pl.ds(first_a + i, 1), :] = value
                    lanes = pl.ds(b % GROUP * count_z, count_z)
                    lhs[pl.ds(b // GROUP * pair + i, 1), lanes] = value

        @pl.when(place.even)
        def _():
            correct(0, 0, 0, low_terms)

        @pl.when(jnp.logical_not(place.even))
        def _():
            correct(count_x - WIDTH, WIDTH, count_a - pair, high_terms)

        result = exact_dot(lhs[...], matrix_ref[...])
        parts = [result[:, kind * count_z : (kind + 1) * count_z] for kind in range(4)]
        sent_ref[pl.ds(0, rows), :] = parts[0]
        sent_ref[pl.ds(rows, rows), :] = parts[1]
        sent_ref[pl.ds(2 * rows, rows), :] = parts[2] + pltpu.roll(parts[3], REACH, 1)

    return pl.pallas_call(
        kernel,
        out_shape=(shape(*final.shape), shape(*late.shape), shape(3 * rows, count_z)),
        in_specs=[spec(pltpu.VMEM)] * 6,
        out_specs=(spec(pltpu.VMEM),) * 3,
        scratch_shapes=[pltpu.VMEM((rows, GROUP * count_z), F32)],
        input_output_aliases={1: 0, 2: 1},
        compiler_params=params(12),
        cost_estimate=cost(WIDTH * count_y * count_z, 20, 3),
        name="last_far",
    )(flag, final, late, cx, far, matrix)


def write_out(level):
    def kernel(level_ref, out_ref, sem):
        copy = pltpu.make_async_copy(level_ref, out_ref, sem)
        copy.start()
        copy.wait()

    return pl.pallas_call(
        kernel,
        out_shape=shape(*level.shape),
        in_specs=[spec(pltpu.VMEM)],
        out_specs=spec(pltpu.HBM),
        scratch_shapes=[pltpu.SemaphoreType.DMA],
        compiler_params=params(4),
        cost_estimate=cost(level.size, 0, 2),
        name="write_out",
    )(level)


CODE_BITS = 5
PER_CODE = 6


def lag_image(count_a, lags, own, other, extra=None, before=None):
    _, total_rows, count_z = own.shape
    groups = total_rows // count_a
    half = count_z // GROUP
    last = before is not None
    count_h = before.shape[0] if last else lags.shape[0]
    codes = -(-count_h // PER_CODE)
    pair = WIDTH // 2

    def kernel(*refs):
        refs = list(refs)
        take = lambda count: [refs.pop(0) for _ in range(count)]
        lags_ref, own_ref, other_ref = take(3)
        if last:
            extra_ref, before_ref = take(2)
        (out_ref,) = take(1)
        if not last:
            (codes_ref,) = take(1)
        mains, edges = take(2)
        if last:
            store, sem = take(2)
        else:
            store = out_ref
            lag_of, sem = take(2)
        place = Place()
        if last:
            packed_lags = [lags_ref[k : k + 1, :][0, 0] for k in range(codes)]
            mask = (1 << CODE_BITS) - 1
            lag_list = [
                ((packed_lags[h // PER_CODE] >> (h % PER_CODE * CODE_BITS)) & mask) - LAGMAX
                for h in range(count_h)
            ]
        else:
            copy = pltpu.make_async_copy(lags_ref, lag_of, sem)
            copy.start()
        is_source = place.field == 0

        def useful(rows):
            lane = lax.broadcasted_iota(jnp.int32, (rows, count_z), 1) % half
            return jnp.where(is_source, lane, half - 1 - lane) < REACH

        slots, _ = edge_slots(count_a, groups, count_z)
        for parity in range(2):
            mains[parity] = other_ref[pl.ds(parity * total_rows, total_rows), :]
        for parity, g, row, shift in slots:
            part = other_ref[pl.ds(2 * total_rows + row, count_a), :]
            part = pltpu.roll(part, count_z - shift, 1) if shift else part
            edges[parity, pl.ds(g * count_a, count_a), :] = jnp.where(useful(count_a), part, 0.0)
        if last:
            rows = extra_ref.shape[0] // 3
            border = extra_ref[pl.ds(2 * rows, rows), :]
            borders = [
                jnp.where(useful(rows), part, 0.0)
                for part in (border, pltpu.roll(border, count_z - REACH, 1))
            ]

            def overwrite(first_a):
                for g in range(groups):
                    target = pl.ds(g * count_a + first_a, pair)
                    for parity in range(2):
                        mains[parity, target, :] = extra_ref[
                            pl.ds(parity * rows + g * pair, pair), :
                        ]
                        edges[parity, target, :] = borders[parity][g * pair : (g + 1) * pair]

            pl.when(place.even)(lambda: overwrite(0))
            pl.when(jnp.logical_not(place.even))(lambda: overwrite(count_a - pair))
        else:
            copy.wait()
            lag_list = [lag_of[h] for h in range(count_h)]
            for k in range(codes):
                code = jnp.int32(0)
                for h in range(k * PER_CODE, min((k + 1) * PER_CODE, count_h)):
                    code = code | ((lag_list[h] + LAGMAX) << (h % PER_CODE * CODE_BITS))
                codes_ref[k : k + 1, :] = jnp.full((1, count_z), code, jnp.int32)
        for h, lag in enumerate(lag_list):
            parity, own_shift, other_shift = lag_shifts(lag, is_source)
            product = moved(mains[parity], edges[parity], other_shift)
            if last:
                product = product * own_ref[h]
            else:
                product = product * moved(own_ref[parity], own_ref[2 + parity], own_shift)
            for g in range(groups):
                part = product[g * count_a : (g + 1) * count_a]
                lanes = pl.ds(g * count_z, count_z)
                if last:
                    part = part + before_ref[h, :, lanes]
                store[h, :, lanes] = part
            if last:
                pltpu.make_async_copy(store.at[h], out_ref.at[h], sem).start()
        if last:
            pltpu.make_async_copy(store, out_ref, sem).wait()

    image = shape(count_h, count_a, groups * count_z)
    operands = [lags, own, other] + ([extra, before] if last else [])
    scratch = [pltpu.VMEM((2, total_rows, count_z), F32)] * 2
    scratch.append(pltpu.VMEM(image.shape, F32) if last else pltpu.SMEM((count_h,), jnp.int32))
    scratch.append(pltpu.SemaphoreType.DMA)
    return pl.pallas_call(
        kernel,
        out_shape=image if last else (image, shape(8, count_z, dtype=jnp.int32)),
        in_specs=[spec(pltpu.VMEM if last else pltpu.HBM)]
        + [spec(pltpu.VMEM)] * (len(operands) - 1),
        out_specs=spec(pltpu.HBM) if last else (spec(pltpu.VMEM),) * 2,
        scratch_shapes=scratch,
        compiler_params=params(12),
        cost_estimate=cost(count_h * total_rows * count_z, 10, 2),
        name="last_image" if last else "early_image",
    )(*operands)


def body(
    field_now,
    field_prev,
    courant_squared,
    source_cells,
    source_wave,
    receiver_cells,
    receiver_wave,
    snapshot_steps,
    lag_offsets,
):
    count_x, _, count_z = field_now.shape
    loop_size = lax.axis_size("gx")
    half_size = loop_size // 2
    turn = loop_size // 4
    assert lax.axis_size("gy") == 2 and half_size % 2 == 0

    slabs = [(i - turn) % loop_size % half_size for i in range(loop_size)]

    def pairs(odd):
        found = []
        for i, slab in enumerate(slabs):
            if slab % 2 == odd and slab != half_size - 1:
                j = (i + 1) % loop_size
                found += [(i, j), (j, i)]
        return found

    near_pairs, far_pairs = pairs(0), pairs(1)
    across = [(i, (i + half_size) % loop_size) for i in range(loop_size)]

    def send_far(far):
        return lax.ppermute(far, "gx", far_pairs)

    def send_near(near, side):
        near = lax.ppermute(near, "gx", near_pairs)
        return near, lax.ppermute(side, "gy", [(0, 1), (1, 0)])

    def exchange(faces):
        far, near, side = faces
        return (send_far(far), *send_near(near, side))

    matrices = jnp.asarray(
        np.stack([pack_matrix(window, count_z) for window in (0, 1)]), dtype=BF16
    )
    raw = (source_cells, source_wave, receiver_cells, receiver_wave)
    field_kept, field_prev, courant_squared, matrices, snapshot_steps, lag_offsets, *raw = (
        pltpu.with_memory_space_constraint(array, pltpu.HBM)
        for array in (
            field_now, field_prev, courant_squared, matrices, snapshot_steps, lag_offsets, *raw
        )
    )
    halos = exchange(first_faces(field_kept))
    next1, qx, qy, courant, cx, cy, points, waves, whole0 = inner_step(
        0, raw, None, field_now, None, field_prev, courant_squared
    )
    faces = halo_step((qx, qy, cx, cy), halos)
    halos = exchange(faces)
    next2, qx, qy, whole1, added = inner_step(1, points, waves, next1, faces, whole0, courant)
    faces = halo_step((qx, qy, cx, cy), halos)
    halos = exchange(faces)
    next3, qx, qy, whole2, own_early, sent_early, own_matrix, sent_matrix, flag = inner_step(
        2, points, waves, next2, faces, whole1, courant, snapshot_steps, matrices
    )
    other_early = lax.ppermute(sent_early, "gx", across)
    faces = halo_step((qx, qy, cx, cy), halos)
    far, near, side = exchange(faces)
    next4, qx, qy, even3 = inner_step(3, added, None, next3, faces, whole2, courant)
    final, late, sent_late = last_step(
        flag, even3, next4, (qx, qy, cx, cy), near, side, sent_matrix
    )
    other_late = lax.ppermute(sent_late, "gx", across)
    partial, codes = lag_image(count_x // 2, lag_offsets, own_early, other_early)
    final, late, sent_far = last_far(flag, final, late, cx, far, sent_matrix)
    extra = lax.ppermute(sent_far, "gx", across)
    own_late = pack_own(lag_offsets, late, own_matrix)
    image = lag_image(count_x // 2, codes, own_late, other_late, extra, partial)
    return write_out(final), jnp.transpose(image, (1, 0, 2))


def solution(mesh):
    placed = (
        P(("shots", "gx"), "gy", None),
        P(("shots", "gx"), "gy", None),
        P("gx", "gy", None),
        P(None, "shots"),
        P(None, "shots"),
        P(None, "shots"),
        P(None, "shots"),
        P("shots", None),
        P(),
    )
    return jax.shard_map(
        body,
        mesh=mesh,
        in_specs=placed,
        out_specs=(P(("shots", "gx"), "gy", None), P(("shots", "gx"), None, "gy")),
        check_vma=False,
    )
```

```python
import jax
import jax.numpy as jnp
import numpy as np
from jax import lax
from jax.experimental import pallas as pl
from jax.experimental.pallas import tpu as pltpu
from jax.sharding import PartitionSpec as P

STEPS = 4
WIDTH = 4
LAGMAX = 8
REACH = LAGMAX // 2
GROUP = 4
SIDE = 8

SCALE = 5040.0
BAND = (8064.0, -1008.0, 128.0, -9.0)
CENTRE = 3.0 * (-205.0 / 72.0)
WEIGHTS = (1.6, -0.2, 8.0 / 315.0, -1.0 / 560.0)

F32 = jnp.float32
BF16 = jnp.bfloat16


def shape(*dims, dtype=F32):
    return jax.ShapeDtypeStruct(dims, dtype)


def params(megabytes):
    return pltpu.CompilerParams(vmem_limit_bytes=megabytes << 20)


def spec(space):
    return pl.BlockSpec(memory_space=space)


def cost(count, flops_each, arrays):
    return pl.CostEstimate(
        flops=int(count * flops_each), bytes_accessed=int(4 * count * arrays), transcendentals=0
    )


def split3(values):
    high = values.astype(BF16)
    rest = values - high.astype(F32)
    middle = rest.astype(BF16)
    low = (rest - middle.astype(F32)).astype(BF16)
    return high, middle, low


def exact_dot(values, matrix):
    rows = values.shape[0]
    stacked = jnp.concatenate(split3(values), axis=0)
    result = jnp.dot(stacked, matrix, preferred_element_type=F32)
    return (result[2 * rows :] + result[rows : 2 * rows]) + result[:rows]


class Place:
    def __init__(self):
        loop_size = lax.axis_size("gx")
        self.half = loop_size // 2
        relative = lax.rem(lax.axis_index("gx") + loop_size - loop_size // 4, loop_size)
        self.field = relative // self.half
        self.slab = lax.rem(relative, self.half)
        self.even = lax.rem(self.slab, 2) == 0
        self.y = lax.axis_index("gy")

    def block(self, count_y):
        return pl.multiple_of((1 - self.y) * (count_y - SIDE), SIDE)


def first_faces(field):
    count_x, count_y, count_z = field.shape
    top = count_x - WIDTH

    def kernel(field_ref, far_ref, near_ref, side_ref, sems):
        place = Place()
        far = jnp.where(place.even, 0, top)
        sources = [
            field_ref.at[pl.ds(far, WIDTH)],
            field_ref.at[pl.ds(top - far, WIDTH)],
            field_ref.at[:, pl.ds(place.block(count_y), SIDE)],
        ]
        copies = [
            pltpu.make_async_copy(source, target, sems.at[index])
            for index, (source, target) in enumerate(zip(sources, (far_ref, near_ref, side_ref)))
        ]
        for copy in copies:
            copy.start()
        for copy in copies:
            copy.wait()

    return pl.pallas_call(
        kernel,
        out_shape=face_shapes(count_x, count_y, count_z),
        in_specs=[spec(pltpu.HBM)],
        out_specs=(spec(pltpu.VMEM),) * 3,
        scratch_shapes=[pltpu.SemaphoreType.DMA((3,))],
        compiler_params=params(8),
        name="first_faces",
    )(field)


def face_shapes(count_x, count_y, count_z):
    slab = shape(WIDTH, count_y, count_z)
    return slab, slab, shape(count_x, SIDE, count_z)


def even_rows(level_ref, offset_x, offset_y, count_a, b):
    rows, stride, lanes = level_ref.shape
    flat = level_ref.reshape(rows * stride, lanes)
    start = offset_x * stride + offset_y + 2 * b
    return flat[pl.ds(start, count_a, stride=2 * stride), :]


def inner_step(number, points, waves, current, faces, previous, courant, snapshots=None, matrices=None):
    count_x, count_y, count_z = courant.shape
    count_a, count_b = count_x // 2, count_y // 2
    first = faces is None
    last = number == STEPS - 1
    snapshot = number == STEPS // 2
    ahead = number == 1
    if last:
        count_j = 0
    elif first:
        count_j = -(-max(array.shape[1] for array in points) // 128) * 128
    else:
        count_j = points.shape[1]

    def kernel(*refs):
        refs = list(refs)
        take = lambda count: [refs.pop(0) for _ in range(count)]
        if first:
            raw_refs = take(4)
        elif last:
            (added_ref,) = take(1)
        else:
            points_ref, waves_ref = take(2)
        (current_ref,) = take(1)
        if not first:
            far_ref, near_ref, side_ref = take(3)
        previous_ref, courant_ref = take(2)
        if snapshot:
            steps_ref, matrices_ref = take(2)
        padded, next_ref, qx_ref, qy_ref = take(4)
        if first:
            kept_ref, cx_ref, cy_ref, points_ref, waves_ref = take(5)
        if snapshot:
            own_out, sent_out, own_matrix, sent_matrix, flag_ref = take(5)
        if ahead:
            (ahead_ref,) = take(1)
        if last:
            (even_ref,) = take(1)
        zpart, addpart = take(2)
        if last:
            addpart = added_ref
        if first:
            before_ref = take(1)[0]
            raw_refs_in, raw_refs = raw_refs, take(4)
            (sems,) = take(1)
        if snapshot:
            even_ref, wanted, sems = take(3)

        place = Place()
        block = place.block(count_y)
        rows, columns = pl.ds(WIDTH, count_x), pl.ds(SIDE, count_y)
        if first:
            copies = [
                pltpu.make_async_copy(source, target, sems.at[index])
                for index, (source, target) in enumerate(
                    zip(
                        (*raw_refs_in, previous_ref, courant_ref),
                        (*raw_refs, before_ref, kept_ref),
                    )
                )
            ]
            for copy in copies:
                copy.start()
        else:
            before_ref, kept_ref = previous_ref, courant_ref
        if snapshot:
            copies = [
                pltpu.make_async_copy(steps_ref, wanted, sems.at[0]),
                pltpu.make_async_copy(matrices_ref.at[place.field], own_matrix, sems.at[1]),
                pltpu.make_async_copy(matrices_ref.at[1 - place.field], sent_matrix, sems.at[2]),
            ]
            for copy in copies:
                copy.start()

        def clear_border(level_ref):
            zero_x = jnp.zeros((WIDTH, count_y + 2 * SIDE, count_z), F32)
            level_ref[pl.ds(0, WIDTH)] = zero_x
            level_ref[pl.ds(count_x + WIDTH, WIDTH)] = zero_x
            zero_y = jnp.zeros((count_x, SIDE, count_z), F32)
            level_ref[rows, pl.ds(0, SIDE)] = zero_y
            level_ref[rows, pl.ds(count_y + SIDE, SIDE)] = zero_y

        if first:
            clear_border(padded)
            padded[rows, columns] = current_ref[...]
        if not last:
            clear_border(next_ref)
        next_x, next_y = (0, 0) if last else (WIDTH, SIDE)
        before_x, before_y = (0, 0) if first else (WIDTH, SIDE)
        if not first:
            low, high = pl.ds(WIDTH, WIDTH), pl.ds(count_x, WIDTH)

            @pl.when(place.even)
            def _():
                padded[high, columns] = near_ref[...]
                padded[low, columns] = far_ref[...]

            @pl.when(jnp.logical_not(place.even))
            def _():
                padded[low, columns] = near_ref[...]
                padded[high, columns] = far_ref[...]

            padded[rows, pl.ds(pl.multiple_of(block + SIDE, SIDE), SIDE)] = side_ref[...]

        gap = jnp.abs(
            lax.broadcasted_iota(jnp.int32, (count_z, count_z), 0)
            - lax.broadcasted_iota(jnp.int32, (count_z, count_z), 1)
        )
        band = jnp.zeros((count_z, count_z), F32)
        for offset, weight in enumerate(BAND, 1):
            band = jnp.where(gap == offset, weight, band)
        band = jnp.concatenate([band.astype(BF16)] * 3, axis=0)

        chunk = 8

        def multiply(index, _):
            start = pl.multiple_of(index * chunk, chunk)
            values = padded[pl.ds(start + WIDTH, chunk), columns]
            terms = jnp.concatenate(split3(values.reshape(chunk * count_y, count_z)), axis=1)
            zpart[pl.ds(start, chunk)] = jnp.dot(
                terms, band, preferred_element_type=F32
            ).reshape(chunk, count_y, count_z)
            return 0

        chunks = count_x // chunk
        if first or last:
            lax.fori_loop(0, chunks, multiply, 0)

        if first:
            for copy in copies[:4]:
                copy.wait()
            points_ref[...] = jnp.full(points_ref.shape, -1, jnp.int32)
            waves_ref[...] = jnp.zeros(waves_ref.shape, F32)

            def choose(cells_ref, wave_ref):
                count = cells_ref.shape[1]
                points_ref[pl.ds(0, 3), pl.ds(0, count)] = cells_ref[...]
                waves_ref[pl.ds(0, STEPS), pl.ds(0, count)] = wave_ref[...]

            @pl.when(place.field == 0)
            def _():
                choose(raw_refs[0], raw_refs[1])

            @pl.when(place.field != 0)
            def _():
                choose(raw_refs[2], raw_refs[3])

        if not last:
            px = points_ref[0:1, :] - place.slab * count_x
            py = points_ref[1:2, :] - place.y * count_y
            inside = (px >= 0) & (px < count_x) & (py >= 0) & (py < count_y)
            home = jnp.where(inside, px * count_y + py, -1)
            at_z = (
                lax.broadcasted_iota(jnp.int32, (count_z, count_j), 0) == points_ref[2:3, :]
            )

            def spread_of(step):
                terms = split3(jnp.where(at_z, waves_ref[step : step + 1, :], 0.0))
                return jnp.concatenate(terms, axis=1)

            spreads = [(addpart, spread_of(number))]
            if ahead:
                spreads.append((ahead_ref, spread_of(STEPS - 1)))

        def inject(index, _):
            start = pl.multiple_of(index * chunk, chunk)
            here = start * count_y + lax.broadcasted_iota(
                jnp.int32, (chunk * count_y, count_j), 0
            )
            hit = jnp.where(here == home, 1.0, 0.0).astype(BF16)
            hit = jnp.concatenate([hit] * 3, axis=1)
            for target, spread in spreads:
                added = lax.dot_general(
                    hit, spread, (((1,), (1,)), ((), ())), preferred_element_type=F32
                )
                target[pl.ds(start, chunk)] = added.reshape(chunk, count_y, count_z)
            return 0

        def both(index, _):
            multiply(index, 0)
            return inject(index, 0)

        if not last:
            lax.fori_loop(0, chunks, inject if first else both, 0)
        if first:
            for copy in copies[4:]:
                copy.wait()

        depth = 4

        def row_group(index, _):
            x = index * depth
            for y in range(0, count_y, SIDE):
                here, inner = pl.ds(y + SIDE, SIDE), pl.ds(y, SIDE)
                lines = [padded[x + i, here] for i in range(depth + 2 * WIDTH)]
                for j in range(depth):
                    middle = lines[WIDTH + j]
                    total = CENTRE * middle + (1.0 / SCALE) * zpart[x + j, inner]
                    for offset, weight in enumerate(WEIGHTS, 1):
                        paired = lines[WIDTH + j + offset] + lines[WIDTH + j - offset]
                        paired = paired + (
                            padded[x + WIDTH + j, pl.ds(y + SIDE + offset, SIDE)]
                            + padded[x + WIDTH + j, pl.ds(y + SIDE - offset, SIDE)]
                        )
                        total = total + weight * paired
                    old = before_ref[x + j + before_x, pl.ds(y + before_y, SIDE)]
                    value = 2.0 * middle - old + kept_ref[x + j, inner] * total
                    next_ref[x + j + next_x, pl.ds(y + next_y, SIDE)] = (
                        value + addpart[x + j, inner]
                    )
            return 0

        lax.fori_loop(0, count_x // depth, row_group, 0)

        next_columns = pl.ds(next_y, count_y)
        qx_ref[pl.ds(0, WIDTH)] = next_ref[pl.ds(next_x, WIDTH), next_columns]
        qx_ref[pl.ds(WIDTH, WIDTH)] = next_ref[
            pl.ds(next_x + count_x - WIDTH, WIDTH), next_columns
        ]
        qy_ref[...] = next_ref[
            pl.ds(next_x, count_x), pl.ds(pl.multiple_of(block + next_y, SIDE), SIDE)
        ]
        if first:
            cx_ref[pl.ds(0, WIDTH)] = kept_ref[pl.ds(0, WIDTH)]
            cx_ref[pl.ds(WIDTH, WIDTH)] = kept_ref[pl.ds(count_x - WIDTH, WIDTH)]
            cy_ref[...] = kept_ref[:, pl.ds(block, SIDE)]
        if last:
            for b in range(count_b):
                even_ref[b] = even_rows(padded, WIDTH, SIDE, count_a, b)
        if snapshot:
            for copy in copies:
                copy.wait()
            flag_ref[...] = jnp.where(
                wanted[place.field, 1] == STEPS, jnp.ones(flag_ref.shape, F32), 0.0
            )
            earlier = wanted[place.field, 0] == number - 1

            @pl.when(earlier)
            def _():
                for b in range(count_b):
                    even_ref[b] = even_rows(previous_ref, WIDTH, SIDE, count_a, b)

            @pl.when(jnp.logical_not(earlier))
            def _():
                for b in range(count_b):
                    even_ref[b] = even_rows(padded, WIDTH, SIDE, count_a, b)

            for kind, part in enumerate(packed(even_ref, own_matrix)):
                own_out[kind] = part
            send_into(even_ref, sent_matrix, sent_out)

    full = shape(count_x, count_y, count_z)
    slab, side = shape(2 * WIDTH, count_y, count_z), shape(count_x, SIDE, count_z)
    even = shape(count_b, count_a, count_z)
    bordered = shape(count_x + 2 * WIDTH, count_y + 2 * SIDE, count_z)
    outs = [bordered, full if last else bordered, slab, side]
    if first:
        outs += [full, slab, side, shape(8, count_j, dtype=jnp.int32), shape(8, count_j)]
    if snapshot:
        size = GROUP * count_z
        outs += [
            shape(4, count_b // GROUP * count_a, count_z),
            sent_shape(count_a, count_b, count_z),
            shape(size, size, dtype=BF16),
            shape(size, size, dtype=BF16),
            shape(8, count_z),
        ]
    if ahead:
        outs.append(full)
    if last:
        outs.append(even)
    place_of = spec(pltpu.HBM) if first else spec(pltpu.VMEM)
    if first:
        operands = [*points, current]
    elif last:
        operands = [points, current]
    else:
        operands = [points, waves, current]
    aliases = {} if first else {len(operands) - 1: 0}
    specs = [place_of] * (len(operands) - 1) + [spec(pltpu.VMEM)]
    if not first:
        operands += list(faces)
        specs += [spec(pltpu.VMEM)] * 3
    operands += [previous, courant]
    specs += [place_of] * 2
    scratch = [pltpu.VMEM(full.shape, F32)] * 2
    if first:
        scratch.append(pltpu.VMEM(full.shape, F32))
        scratch += [pltpu.VMEM(array.shape, array.dtype) for array in points]
        scratch.append(pltpu.SemaphoreType.DMA((6,)))
    if snapshot:
        operands += [snapshots, matrices]
        specs += [spec(pltpu.HBM)] * 2
        scratch += [
            pltpu.VMEM(even.shape, F32),
            pltpu.SMEM(snapshots.shape, jnp.int32),
            pltpu.SemaphoreType.DMA((3,)),
        ]
    return pl.pallas_call(
        kernel,
        out_shape=tuple(outs),
        in_specs=specs,
        out_specs=(spec(pltpu.VMEM),) * len(outs),
        scratch_shapes=scratch,
        input_output_aliases=aliases,
        compiler_params=params(20),
        cost_estimate=cost(count_x * count_y * count_z, 60, 6),
    )(*operands)


def low_terms(halo_ref, r):
    total = None
    for k in range(r + 1, WIDTH + 1):
        term = WEIGHTS[k - 1] * halo_ref[WIDTH + r - k]
        total = term if total is None else total + term
    return total


def high_terms(halo_ref, r):
    total = None
    for k in range(WIDTH - r, WIDTH + 1):
        term = WEIGHTS[k - 1] * halo_ref[r + k - WIDTH]
        total = term if total is None else total + term
    return total


def add_halo(place, parts, halos, outs):
    qx_ref, qy_ref, cx_ref, cy_ref = parts
    far_in, near_in, side_in = halos
    far_out, near_out, side_out = outs
    count_y, count_x = qx_ref.shape[1], qy_ref.shape[0]
    block = place.block(count_y)

    def along_x(low_in, high_in, low_out, high_out):
        for r in range(WIDTH):
            low, high = qx_ref[r], qx_ref[WIDTH + r]
            if low_in is not None:
                low = low + cx_ref[r] * low_terms(low_in, r)
            if high_in is not None:
                high = high + cx_ref[WIDTH + r] * high_terms(high_in, r)
            low_out[r], high_out[r] = low, high
        side_out[pl.ds(0, WIDTH)] = low_out[:, pl.ds(block, SIDE)]
        side_out[pl.ds(count_x - WIDTH, WIDTH)] = high_out[:, pl.ds(block, SIDE)]

    inner = pl.ds(WIDTH, count_x - 2 * WIDTH)
    side_out[inner] = qy_ref[inner]

    @pl.when(place.even)
    def _():
        along_x(far_in, near_in, far_out, near_out)

    @pl.when(jnp.logical_not(place.even))
    def _():
        along_x(near_in, far_in, near_out, far_out)

    def along_y(shifts, masks):
        halo = side_in[...]
        lanes = halo.shape[2]
        line = lax.broadcasted_iota(jnp.int32, (1, SIDE, lanes), 1)
        total = None
        for k in range(1, WIDTH + 1):
            weight = jnp.where(masks(line, k), WEIGHTS[k - 1], 0.0)
            term = weight * pltpu.roll(halo, shifts(k), 1)
            total = term if total is None else total + term
        side_out[...] = side_out[...] + cy_ref[...] * total

    @pl.when(place.y == 0)
    def _():
        along_y(lambda k: SIDE - k, lambda line, k: line >= SIDE - k)

    @pl.when(place.y != 0)
    def _():
        along_y(lambda k: k, lambda line, k: line < k)

    def corners(low_out, high_out):
        low_out[:, pl.ds(block, SIDE)] = side_out[pl.ds(0, WIDTH)]
        high_out[:, pl.ds(block, SIDE)] = side_out[pl.ds(count_x - WIDTH, WIDTH)]

    @pl.when(place.even)
    def _():
        corners(far_out, near_out)

    @pl.when(jnp.logical_not(place.even))
    def _():
        corners(near_out, far_out)


def halo_step(parts, halos):
    count_y, (count_x, _, count_z) = parts[0].shape[1], parts[1].shape

    def kernel(*refs):
        add_halo(Place(), refs[:4], refs[4:7], refs[7:])

    return pl.pallas_call(
        kernel,
        out_shape=face_shapes(count_x, count_y, count_z),
        in_specs=[spec(pltpu.VMEM)] * 7,
        out_specs=(spec(pltpu.VMEM),) * 3,
        compiler_params=params(8),
        cost_estimate=cost(16 * count_y * count_z, 10, 6),
        name="halo_step",
    )(*parts, *halos)


def pack_matrix(window, count_z):
    half = count_z // GROUP
    size = GROUP * count_z
    row, column = np.arange(size)[:, None], np.arange(size)[None, :]
    row_b, row_z = row // count_z, row % count_z
    kind = column // count_z
    parity = kind % 2
    lane_b, lane_i = (column % count_z) // half, column % half
    main = (row_b == lane_b) & (row_z == 2 * (half * window + lane_i) + parity)
    wanted_b = (lane_b + (GROUP - 1 if window == 0 else 1)) % GROUP
    wanted_z = 2 * (half * (1 - window) + lane_i) + parity
    useful = lane_i < REACH if window == 0 else lane_i >= half - REACH
    edge = (row_b == wanted_b) & (row_z == wanted_z) & useful
    return np.where(kind < 2, main, edge).astype(np.float32)


def packed(even_ref, matrix_ref):
    count_b, _, count_z = even_ref.shape
    rows = [
        jnp.concatenate([even_ref[b + i] for i in range(GROUP)], axis=1)
        for b in range(0, count_b, GROUP)
    ]
    result = exact_dot(jnp.concatenate(rows, axis=0), matrix_ref[...])
    return [result[:, kind * count_z : (kind + 1) * count_z] for kind in range(4)]


def lag_shifts(lag, is_source):
    parity = lag & 1
    source_shift = -((lag + parity) >> 1)
    receiver_shift = (lag - parity) >> 1
    return (
        parity,
        jnp.where(is_source, source_shift, receiver_shift),
        jnp.where(is_source, receiver_shift, source_shift),
    )


def moved(main, edge, shift):
    count_z = main.shape[1]
    half = count_z // GROUP
    lane = lax.broadcasted_iota(jnp.int32, (1, count_z), 1) % half
    mask = (lane < shift) | (lane >= half + shift)
    return pltpu.roll(jnp.where(mask, edge, main), (count_z - shift) & (count_z - 1), 1)


def pack_own(lags, even, matrix):
    count_b, count_a, count_z = even.shape
    total_rows = count_b // GROUP * count_a
    (count_h,) = lags.shape

    def kernel(lags_ref, even_ref, matrix_ref, out_ref, windows, lag_of, sem):
        copy = pltpu.make_async_copy(lags_ref, lag_of, sem)
        copy.start()
        place = Place()
        for kind, part in enumerate(packed(even_ref, matrix_ref)):
            windows[kind] = part
        copy.wait()
        for h in range(count_h):
            parity, shift, _ = lag_shifts(lag_of[h], place.field == 0)
            out_ref[h] = moved(windows[parity], windows[2 + parity], shift)

    return pl.pallas_call(
        kernel,
        out_shape=shape(count_h, total_rows, count_z),
        in_specs=[spec(pltpu.HBM)] + [spec(pltpu.VMEM)] * 2,
        out_specs=spec(pltpu.VMEM),
        scratch_shapes=[
            pltpu.VMEM((4, total_rows, count_z), F32),
            pltpu.SMEM((count_h,), jnp.int32),
            pltpu.SemaphoreType.DMA,
        ],
        compiler_params=params(8),
        cost_estimate=cost(count_b * count_a * count_z, 1024, 4),
        name="pack_own",
    )(lags, even, matrix)


def edge_slots(count_a, groups, count_z):
    fits = count_z // GROUP // REACH
    slots = []
    for index in range(2 * groups):
        slots.append((index // groups, index % groups, index // fits * count_a, index % fits * REACH))
    return slots, -(-2 * groups // fits) * count_a


def send_into(even_ref, matrix_ref, out_ref):
    count_b, count_a, count_z = even_ref.shape
    groups = count_b // GROUP
    total_rows = groups * count_a
    parts = packed(even_ref, matrix_ref)
    out_ref[pl.ds(0, total_rows), :] = parts[0]
    out_ref[pl.ds(total_rows, total_rows), :] = parts[1]
    slots, _ = edge_slots(count_a, groups, count_z)
    sums = {}
    for parity, g, row, shift in slots:
        part = parts[2 + parity][g * count_a : (g + 1) * count_a]
        part = pltpu.roll(part, shift, 1) if shift else part
        sums[row] = sums[row] + part if row in sums else part
    for row, part in sums.items():
        out_ref[pl.ds(2 * total_rows + row, count_a), :] = part


def sent_shape(count_a, count_b, count_z):
    groups = count_b // GROUP
    _, extra = edge_slots(count_a, groups, count_z)
    return shape(2 * groups * count_a + extra, count_z)


def last_step(flag, even_before, current, parts, near, side, matrix):
    count_x, count_y, count_z = current.shape
    count_a, count_b = count_x // 2, count_y // 2

    def kernel(
        flag_ref, even_ref, current_ref, qx_ref, qy_ref, cx_ref, cy_ref, near_ref, side_ref,
        matrix_ref, final_ref, late_ref, sent_ref, far_out, near_out, side_out,
    ):
        place = Place()
        add_halo(
            place, (qx_ref, qy_ref, cx_ref, cy_ref), (None, near_ref, side_ref),
            (far_out, near_out, side_out),
        )
        low, high = pl.ds(0, WIDTH), pl.ds(count_x - WIDTH, WIDTH)

        @pl.when(place.even)
        def _():
            final_ref[high] = near_out[...]
            final_ref[low] = far_out[...]

        @pl.when(jnp.logical_not(place.even))
        def _():
            final_ref[low] = near_out[...]
            final_ref[high] = far_out[...]

        final_ref[:, pl.ds(place.block(count_y), SIDE)] = side_out[...]
        wants_last = jnp.broadcast_to(flag_ref[0:1, :], (count_a, count_z)) > 0.5
        for b in range(count_b):
            late_ref[b] = jnp.where(
                wants_last, even_rows(final_ref, 0, 0, count_a, b), even_ref[b]
            )
        send_into(late_ref, matrix_ref, sent_ref)

    slab, _, side_shape = face_shapes(count_x, count_y, count_z)
    return pl.pallas_call(
        kernel,
        out_shape=(
            shape(*current.shape),
            shape(count_b, count_a, count_z),
            sent_shape(count_a, count_b, count_z),
        ),
        in_specs=[spec(pltpu.VMEM)] * 10,
        out_specs=(spec(pltpu.VMEM),) * 3,
        scratch_shapes=[
            pltpu.VMEM(slab.shape, F32),
            pltpu.VMEM(slab.shape, F32),
            pltpu.VMEM(side_shape.shape, F32),
        ],
        input_output_aliases={2: 0},
        compiler_params=params(12),
        cost_estimate=cost(count_x * count_y * count_z, 10, 3),
        name="last_step",
    )(flag, even_before, current, *parts, near, side, matrix)


def far_rows(count_b):
    return -(-2 * (count_b // GROUP) // 16) * 16


def last_far(flag, final, late, cx, far, matrix):
    count_x, count_y, count_z = final.shape
    count_b, count_a, _ = late.shape
    rows, pair = far_rows(count_b), WIDTH // 2

    def kernel(
        flag_ref, final_in, late_in, cx_ref, far_ref, matrix_ref, final_ref, late_ref, sent_ref, lhs,
    ):
        place = Place()
        wants_last = jnp.broadcast_to(flag_ref[0:1, :], (1, count_z)) > 0.5
        lhs[...] = jnp.zeros_like(lhs)

        def correct(first_x, first_c, first_a, terms):
            for r in range(WIDTH):
                final_ref[first_x + r] = final_ref[first_x + r] + cx_ref[first_c + r] * terms(
                    far_ref, r
                )
            for b in range(count_b):
                for i in range(pair):
                    value = jnp.where(
                        wants_last,
                        final_ref[first_x + 2 * i, pl.ds(2 * b, 1), :],
                        late_ref[b, pl.ds(first_a + i, 1), :],
                    )
                    late_ref[b, pl.ds(first_a + i, 1), :] = value
                    lanes = pl.ds(b % GROUP * count_z, count_z)
                    lhs[pl.ds(b // GROUP * pair + i, 1), lanes] = value

        @pl.when(place.even)
        def _():
            correct(0, 0, 0, low_terms)

        @pl.when(jnp.logical_not(place.even))
        def _():
            correct(count_x - WIDTH, WIDTH, count_a - pair, high_terms)

        result = exact_dot(lhs[...], matrix_ref[...])
        parts = [result[:, kind * count_z : (kind + 1) * count_z] for kind in range(4)]
        sent_ref[pl.ds(0, rows), :] = parts[0]
        sent_ref[pl.ds(rows, rows), :] = parts[1]
        sent_ref[pl.ds(2 * rows, rows), :] = parts[2] + pltpu.roll(parts[3], REACH, 1)

    return pl.pallas_call(
        kernel,
        out_shape=(shape(*final.shape), shape(*late.shape), shape(3 * rows, count_z)),
        in_specs=[spec(pltpu.VMEM)] * 6,
        out_specs=(spec(pltpu.VMEM),) * 3,
        scratch_shapes=[pltpu.VMEM((rows, GROUP * count_z), F32)],
        input_output_aliases={1: 0, 2: 1},
        compiler_params=params(12),
        cost_estimate=cost(WIDTH * count_y * count_z, 20, 3),
        name="last_far",
    )(flag, final, late, cx, far, matrix)


def write_out(level):
    def kernel(level_ref, out_ref, sem):
        copy = pltpu.make_async_copy(level_ref, out_ref, sem)
        copy.start()
        copy.wait()

    return pl.pallas_call(
        kernel,
        out_shape=shape(*level.shape),
        in_specs=[spec(pltpu.VMEM)],
        out_specs=spec(pltpu.HBM),
        scratch_shapes=[pltpu.SemaphoreType.DMA],
        compiler_params=params(4),
        cost_estimate=cost(level.size, 0, 2),
        name="write_out",
    )(level)


CODE_BITS = 5
PER_CODE = 6


def lag_image(count_a, lags, own, other, extra=None, before=None):
    _, total_rows, count_z = own.shape
    groups = total_rows // count_a
    half = count_z // GROUP
    last = before is not None
    count_h = before.shape[0] if last else lags.shape[0]
    codes = -(-count_h // PER_CODE)
    pair = WIDTH // 2

    def kernel(*refs):
        refs = list(refs)
        take = lambda count: [refs.pop(0) for _ in range(count)]
        lags_ref, own_ref, other_ref = take(3)
        if last:
            extra_ref, before_ref = take(2)
        (out_ref,) = take(1)
        if not last:
            (codes_ref,) = take(1)
        mains, edges = take(2)
        if last:
            store, sem = take(2)
        else:
            store = out_ref
            lag_of, sem = take(2)
        place = Place()
        if last:
            packed_lags = [lags_ref[k : k + 1, :][0, 0] for k in range(codes)]
            mask = (1 << CODE_BITS) - 1
            lag_list = [
                ((packed_lags[h // PER_CODE] >> (h % PER_CODE * CODE_BITS)) & mask) - LAGMAX
                for h in range(count_h)
            ]
        else:
            copy = pltpu.make_async_copy(lags_ref, lag_of, sem)
            copy.start()
        is_source = place.field == 0

        def useful(rows):
            lane = lax.broadcasted_iota(jnp.int32, (rows, count_z), 1) % half
            return jnp.where(is_source, lane, half - 1 - lane) < REACH

        slots, _ = edge_slots(count_a, groups, count_z)
        for parity in range(2):
            mains[parity] = other_ref[pl.ds(parity * total_rows, total_rows), :]
        for parity, g, row, shift in slots:
            part = other_ref[pl.ds(2 * total_rows + row, count_a), :]
            part = pltpu.roll(part, count_z - shift, 1) if shift else part
            edges[parity, pl.ds(g * count_a, count_a), :] = jnp.where(useful(count_a), part, 0.0)
        if last:
            rows = extra_ref.shape[0] // 3
            border = extra_ref[pl.ds(2 * rows, rows), :]
            borders = [
                jnp.where(useful(rows), part, 0.0)
                for part in (border, pltpu.roll(border, count_z - REACH, 1))
            ]

            def overwrite(first_a):
                for g in range(groups):
                    target = pl.ds(g * count_a + first_a, pair)
                    for parity in range(2):
                        mains[parity, target, :] = extra_ref[
                            pl.ds(parity * rows + g * pair, pair), :
                        ]
                        edges[parity, target, :] = borders[parity][g * pair : (g + 1) * pair]

            pl.when(place.even)(lambda: overwrite(0))
            pl.when(jnp.logical_not(place.even))(lambda: overwrite(count_a - pair))
        else:
            copy.wait()
            lag_list = [lag_of[h] for h in range(count_h)]
            for k in range(codes):
                code = jnp.int32(0)
                for h in range(k * PER_CODE, min((k + 1) * PER_CODE, count_h)):
                    code = code | ((lag_list[h] + LAGMAX) << (h % PER_CODE * CODE_BITS))
                codes_ref[k : k + 1, :] = jnp.full((1, count_z), code, jnp.int32)
        for h, lag in enumerate(lag_list):
            parity, own_shift, other_shift = lag_shifts(lag, is_source)
            product = moved(mains[parity], edges[parity], other_shift)
            if last:
                product = product * own_ref[h]
            else:
                product = product * moved(own_ref[parity], own_ref[2 + parity], own_shift)
            for g in range(groups):
                part = product[g * count_a : (g + 1) * count_a]
                lanes = pl.ds(g * count_z, count_z)
                if last:
                    part = part + before_ref[h, :, lanes]
                store[h, :, lanes] = part
            if last:
                pltpu.make_async_copy(store.at[h], out_ref.at[h], sem).start()
        if last:
            pltpu.make_async_copy(store, out_ref, sem).wait()

    image = shape(count_h, count_a, groups * count_z)
    operands = [lags, own, other] + ([extra, before] if last else [])
    scratch = [pltpu.VMEM((2, total_rows, count_z), F32)] * 2
    scratch.append(pltpu.VMEM(image.shape, F32) if last else pltpu.SMEM((count_h,), jnp.int32))
    scratch.append(pltpu.SemaphoreType.DMA)
    return pl.pallas_call(
        kernel,
        out_shape=image if last else (image, shape(8, count_z, dtype=jnp.int32)),
        in_specs=[spec(pltpu.VMEM if last else pltpu.HBM)]
        + [spec(pltpu.VMEM)] * (len(operands) - 1),
        out_specs=spec(pltpu.HBM) if last else (spec(pltpu.VMEM),) * 2,
        scratch_shapes=scratch,
        compiler_params=params(12),
        cost_estimate=cost(count_h * total_rows * count_z, 10, 2),
        name="last_image" if last else "early_image",
    )(*operands)


def body(
    field_now,
    field_prev,
    courant_squared,
    source_cells,
    source_wave,
    receiver_cells,
    receiver_wave,
    snapshot_steps,
    lag_offsets,
):
    count_x, _, count_z = field_now.shape
    loop_size = lax.axis_size("gx")
    half_size = loop_size // 2
    turn = loop_size // 4
    assert lax.axis_size("gy") == 2 and half_size % 2 == 0

    slabs = [(i - turn) % loop_size % half_size for i in range(loop_size)]

    def pairs(odd):
        found = []
        for i, slab in enumerate(slabs):
            if slab % 2 == odd and slab != half_size - 1:
                j = (i + 1) % loop_size
                found += [(i, j), (j, i)]
        return found

    near_pairs, far_pairs = pairs(0), pairs(1)
    across = [(i, (i + half_size) % loop_size) for i in range(loop_size)]

    def send_far(far):
        return lax.ppermute(far, "gx", far_pairs)

    def send_near(near, side):
        near = lax.ppermute(near, "gx", near_pairs)
        return near, lax.ppermute(side, "gy", [(0, 1), (1, 0)])

    def exchange(faces):
        far, near, side = faces
        return (send_far(far), *send_near(near, side))

    matrices = jnp.asarray(
        np.stack([pack_matrix(window, count_z) for window in (0, 1)]), dtype=BF16
    )
    raw = (source_cells, source_wave, receiver_cells, receiver_wave)
    field_kept, field_prev, courant_squared, matrices, snapshot_steps, lag_offsets, *raw = (
        pltpu.with_memory_space_constraint(array, pltpu.HBM)
        for array in (
            field_now, field_prev, courant_squared, matrices, snapshot_steps, lag_offsets, *raw
        )
    )
    halos = exchange(first_faces(field_kept))
    whole0, next1, qx, qy, courant, cx, cy, points, waves = inner_step(
        0, raw, None, field_now, None, field_prev, courant_squared
    )
    faces = halo_step((qx, qy, cx, cy), halos)
    halos = exchange(faces)
    whole1, next2, qx, qy, added = inner_step(1, points, waves, next1, faces, whole0, courant)
    faces = halo_step((qx, qy, cx, cy), halos)
    halos = exchange(faces)
    whole2, next3, qx, qy, own_early, sent_early, own_matrix, sent_matrix, flag = inner_step(
        2, points, waves, next2, faces, whole1, courant, snapshot_steps, matrices
    )
    other_early = lax.ppermute(sent_early, "gx", across)
    faces = halo_step((qx, qy, cx, cy), halos)
    far, near, side = exchange(faces)
    _, next4, qx, qy, even3 = inner_step(3, added, None, next3, faces, whole2, courant)
    final, late, sent_late = last_step(
        flag, even3, next4, (qx, qy, cx, cy), near, side, sent_matrix
    )
    other_late = lax.ppermute(sent_late, "gx", across)
    partial, codes = lag_image(count_x // 2, lag_offsets, own_early, other_early)
    final, late, sent_far = last_far(flag, final, late, cx, far, sent_matrix)
    extra = lax.ppermute(sent_far, "gx", across)
    own_late = pack_own(lag_offsets, late, own_matrix)
    image = lag_image(count_x // 2, codes, own_late, other_late, extra, partial)
    return write_out(final), jnp.transpose(image, (1, 0, 2))


def solution(mesh):
    placed = (
        P(("shots", "gx"), "gy", None),
        P(("shots", "gx"), "gy", None),
        P("gx", "gy", None),
        P(None, "shots"),
        P(None, "shots"),
        P(None, "shots"),
        P(None, "shots"),
        P("shots", None),
        P(),
    )
    return jax.shard_map(
        body,
        mesh=mesh,
        in_specs=placed,
        out_specs=(P(("shots", "gx"), "gy", None), P(("shots", "gx"), None, "gy")),
        check_vma=False,
    )
```

```python
import jax
import jax.numpy as jnp
import numpy as np
from jax import lax
from jax.experimental import pallas as pl
from jax.experimental.pallas import tpu as pltpu
from jax.sharding import PartitionSpec as P

STEPS = 4
WIDTH = 4
LAGMAX = 8
REACH = LAGMAX // 2
GROUP = 4
SIDE = 8

SCALE = 5040.0
BAND = (8064.0, -1008.0, 128.0, -9.0)
CENTRE = 3.0 * (-205.0 / 72.0)
WEIGHTS = (1.6, -0.2, 8.0 / 315.0, -1.0 / 560.0)

F32 = jnp.float32
BF16 = jnp.bfloat16


def shape(*dims, dtype=F32):
    return jax.ShapeDtypeStruct(dims, dtype)


def params(megabytes):
    return pltpu.CompilerParams(vmem_limit_bytes=megabytes << 20)


def spec(space):
    return pl.BlockSpec(memory_space=space)


def cost(count, flops_each, arrays):
    return pl.CostEstimate(
        flops=int(count * flops_each), bytes_accessed=int(4 * count * arrays), transcendentals=0
    )


def split3(values):
    high = values.astype(BF16)
    rest = values - high.astype(F32)
    middle = rest.astype(BF16)
    low = (rest - middle.astype(F32)).astype(BF16)
    return high, middle, low


def exact_dot(values, matrix):
    rows = values.shape[0]
    stacked = jnp.concatenate(split3(values), axis=0)
    result = jnp.dot(stacked, matrix, preferred_element_type=F32)
    return (result[2 * rows :] + result[rows : 2 * rows]) + result[:rows]


class Place:
    def __init__(self):
        loop_size = lax.axis_size("gx")
        self.half = loop_size // 2
        relative = lax.rem(lax.axis_index("gx") + loop_size - loop_size // 4, loop_size)
        self.field = relative // self.half
        self.slab = lax.rem(relative, self.half)
        self.even = lax.rem(self.slab, 2) == 0
        self.y = lax.axis_index("gy")

    def block(self, count_y):
        return pl.multiple_of((1 - self.y) * (count_y - SIDE), SIDE)


def first_faces(field):
    count_x, count_y, count_z = field.shape
    top = count_x - WIDTH

    def kernel(field_ref, far_ref, near_ref, side_ref, sems):
        place = Place()
        far = jnp.where(place.even, 0, top)
        sources = [
            field_ref.at[pl.ds(far, WIDTH)],
            field_ref.at[pl.ds(top - far, WIDTH)],
            field_ref.at[:, pl.ds(place.block(count_y), SIDE)],
        ]
        copies = [
            pltpu.make_async_copy(source, target, sems.at[index])
            for index, (source, target) in enumerate(zip(sources, (far_ref, near_ref, side_ref)))
        ]
        for copy in copies:
            copy.start()
        for copy in copies:
            copy.wait()

    return pl.pallas_call(
        kernel,
        out_shape=face_shapes(count_x, count_y, count_z),
        in_specs=[spec(pltpu.HBM)],
        out_specs=(spec(pltpu.VMEM),) * 3,
        scratch_shapes=[pltpu.SemaphoreType.DMA((3,))],
        compiler_params=params(8),
        name="first_faces",
    )(field)


def face_shapes(count_x, count_y, count_z):
    slab = shape(WIDTH, count_y, count_z)
    return slab, slab, shape(count_x, SIDE, count_z)


def even_rows(level_ref, offset_x, offset_y, count_a, b):
    rows, stride, lanes = level_ref.shape
    flat = level_ref.reshape(rows * stride, lanes)
    start = offset_x * stride + offset_y + 2 * b
    return flat[pl.ds(start, count_a, stride=2 * stride), :]


def inner_step(number, points, waves, current, faces, previous, courant, snapshots=None, matrices=None):
    count_x, count_y, count_z = courant.shape
    count_a, count_b = count_x // 2, count_y // 2
    first = faces is None
    last = number == STEPS - 1
    snapshot = number == STEPS // 2
    ahead = number == 1
    if last:
        count_j = 0
    elif first:
        count_j = -(-max(array.shape[1] for array in points) // 128) * 128
    else:
        count_j = points.shape[1]

    def kernel(*refs):
        refs = list(refs)
        take = lambda count: [refs.pop(0) for _ in range(count)]
        if first:
            raw_refs = take(4)
        elif last:
            (added_ref,) = take(1)
        else:
            points_ref, waves_ref = take(2)
        (current_ref,) = take(1)
        if not first:
            far_ref, near_ref, side_ref = take(3)
        previous_ref, courant_ref = take(2)
        if snapshot:
            steps_ref, matrices_ref = take(2)
        padded, next_ref, qx_ref, qy_ref = take(4)
        if first:
            kept_ref, cx_ref, cy_ref, points_ref, waves_ref = take(5)
        if snapshot:
            own_out, sent_out, own_matrix, sent_matrix, flag_ref = take(5)
        if ahead:
            (ahead_ref,) = take(1)
        if last:
            (even_ref,) = take(1)
        zpart, addpart = take(2)
        if last:
            addpart = added_ref
        if first:
            before_ref = take(1)[0]
            raw_refs_in, raw_refs = raw_refs, take(4)
            (sems,) = take(1)
        if snapshot:
            even_ref, wanted, sems = take(3)

        place = Place()
        block = place.block(count_y)
        rows, columns = pl.ds(WIDTH, count_x), pl.ds(SIDE, count_y)
        if first:
            copies = [
                pltpu.make_async_copy(source, target, sems.at[index])
                for index, (source, target) in enumerate(
                    zip(
                        (*raw_refs_in, previous_ref, courant_ref),
                        (*raw_refs, before_ref, kept_ref),
                    )
                )
            ]
            for copy in copies:
                copy.start()
        else:
            before_ref, kept_ref = previous_ref, courant_ref
        if snapshot:
            copies = [
                pltpu.make_async_copy(steps_ref, wanted, sems.at[0]),
                pltpu.make_async_copy(matrices_ref.at[place.field], own_matrix, sems.at[1]),
                pltpu.make_async_copy(matrices_ref.at[1 - place.field], sent_matrix, sems.at[2]),
            ]
            for copy in copies:
                copy.start()

        def clear_border(level_ref):
            zero_x = jnp.zeros((WIDTH, count_y + 2 * SIDE, count_z), F32)
            level_ref[pl.ds(0, WIDTH)] = zero_x
            level_ref[pl.ds(count_x + WIDTH, WIDTH)] = zero_x
            zero_y = jnp.zeros((count_x, SIDE, count_z), F32)
            level_ref[rows, pl.ds(0, SIDE)] = zero_y
            level_ref[rows, pl.ds(count_y + SIDE, SIDE)] = zero_y

        if first:
            clear_border(padded)
            padded[rows, columns] = current_ref[...]
        if not last:
            clear_border(next_ref)
        next_x, next_y = (0, 0) if last else (WIDTH, SIDE)
        before_x, before_y = (0, 0) if first else (WIDTH, SIDE)
        if not first:
            low, high = pl.ds(WIDTH, WIDTH), pl.ds(count_x, WIDTH)

            @pl.when(place.even)
            def _():
                padded[high, columns] = near_ref[...]
                padded[low, columns] = far_ref[...]

            @pl.when(jnp.logical_not(place.even))
            def _():
                padded[low, columns] = near_ref[...]
                padded[high, columns] = far_ref[...]

            padded[rows, pl.ds(pl.multiple_of(block + SIDE, SIDE), SIDE)] = side_ref[...]

        gap = jnp.abs(
            lax.broadcasted_iota(jnp.int32, (count_z, count_z), 0)
            - lax.broadcasted_iota(jnp.int32, (count_z, count_z), 1)
        )
        band = jnp.zeros((count_z, count_z), F32)
        for offset, weight in enumerate(BAND, 1):
            band = jnp.where(gap == offset, weight, band)
        band = jnp.concatenate([band.astype(BF16)] * 3, axis=0)

        chunk = 8

        def multiply(index, _):
            start = pl.multiple_of(index * chunk, chunk)
            values = padded[pl.ds(start + WIDTH, chunk), columns]
            terms = jnp.concatenate(split3(values.reshape(chunk * count_y, count_z)), axis=1)
            zpart[pl.ds(start, chunk)] = jnp.dot(
                terms, band, preferred_element_type=F32
            ).reshape(chunk, count_y, count_z)
            return 0

        chunks = count_x // chunk
        if first or last:
            lax.fori_loop(0, chunks, multiply, 0)

        if first:
            for copy in copies[:4]:
                copy.wait()
            points_ref[...] = jnp.full(points_ref.shape, -1, jnp.int32)
            waves_ref[...] = jnp.zeros(waves_ref.shape, F32)

            def choose(cells_ref, wave_ref):
                count = cells_ref.shape[1]
                points_ref[pl.ds(0, 3), pl.ds(0, count)] = cells_ref[...]
                waves_ref[pl.ds(0, STEPS), pl.ds(0, count)] = wave_ref[...]

            @pl.when(place.field == 0)
            def _():
                choose(raw_refs[0], raw_refs[1])

            @pl.when(place.field != 0)
            def _():
                choose(raw_refs[2], raw_refs[3])

        if not last:
            px = points_ref[0:1, :] - place.slab * count_x
            py = points_ref[1:2, :] - place.y * count_y
            inside = (px >= 0) & (px < count_x) & (py >= 0) & (py < count_y)
            home = jnp.where(inside, px * count_y + py, -1)
            at_z = (
                lax.broadcasted_iota(jnp.int32, (count_z, count_j), 0) == points_ref[2:3, :]
            )

            def spread_of(step):
                terms = split3(jnp.where(at_z, waves_ref[step : step + 1, :], 0.0))
                return jnp.concatenate(terms, axis=1)

            spreads = [(addpart, spread_of(number))]
            if ahead:
                spreads.append((ahead_ref, spread_of(STEPS - 1)))

        def inject(index, _):
            start = pl.multiple_of(index * chunk, chunk)
            here = start * count_y + lax.broadcasted_iota(
                jnp.int32, (chunk * count_y, count_j), 0
            )
            hit = jnp.where(here == home, 1.0, 0.0).astype(BF16)
            hit = jnp.concatenate([hit] * 3, axis=1)
            for target, spread in spreads:
                added = lax.dot_general(
                    hit, spread, (((1,), (1,)), ((), ())), preferred_element_type=F32
                )
                target[pl.ds(start, chunk)] = added.reshape(chunk, count_y, count_z)
            return 0

        def both(index, _):
            multiply(index, 0)
            return inject(index, 0)

        if not last:
            lax.fori_loop(0, chunks, inject if first else both, 0)
        if first:
            for copy in copies[4:]:
                copy.wait()

        depth = 4

        def row_group(index, _):
            x = index * depth
            for y in range(0, count_y, SIDE):
                here, inner = pl.ds(y + SIDE, SIDE), pl.ds(y, SIDE)
                lines = [padded[x + i, here] for i in range(depth + 2 * WIDTH)]
                for j in range(depth):
                    middle = lines[WIDTH + j]
                    total = CENTRE * middle + (1.0 / SCALE) * zpart[x + j, inner]
                    for offset, weight in enumerate(WEIGHTS, 1):
                        paired = lines[WIDTH + j + offset] + lines[WIDTH + j - offset]
                        paired = paired + (
                            padded[x + WIDTH + j, pl.ds(y + SIDE + offset, SIDE)]
                            + padded[x + WIDTH + j, pl.ds(y + SIDE - offset, SIDE)]
                        )
                        total = total + weight * paired
                    old = before_ref[x + j + before_x, pl.ds(y + before_y, SIDE)]
                    value = 2.0 * middle - old + kept_ref[x + j, inner] * total
                    next_ref[x + j + next_x, pl.ds(y + next_y, SIDE)] = (
                        value + addpart[x + j, inner]
                    )
            return 0

        lax.fori_loop(0, count_x // depth, row_group, 0)

        next_columns = pl.ds(next_y, count_y)
        qx_ref[pl.ds(0, WIDTH)] = next_ref[pl.ds(next_x, WIDTH), next_columns]
        qx_ref[pl.ds(WIDTH, WIDTH)] = next_ref[
            pl.ds(next_x + count_x - WIDTH, WIDTH), next_columns
        ]
        qy_ref[...] = next_ref[
            pl.ds(next_x, count_x), pl.ds(pl.multiple_of(block + next_y, SIDE), SIDE)
        ]
        if first:
            cx_ref[pl.ds(0, WIDTH)] = kept_ref[pl.ds(0, WIDTH)]
            cx_ref[pl.ds(WIDTH, WIDTH)] = kept_ref[pl.ds(count_x - WIDTH, WIDTH)]
            cy_ref[...] = kept_ref[:, pl.ds(block, SIDE)]
        if last:
            for b in range(count_b):
                even_ref[b] = even_rows(padded, WIDTH, SIDE, count_a, b)
        if snapshot:
            for copy in copies:
                copy.wait()
            flag_ref[...] = jnp.where(
                wanted[place.field, 1] == STEPS, jnp.ones(flag_ref.shape, F32), 0.0
            )
            earlier = wanted[place.field, 0] == number - 1

            @pl.when(earlier)
            def _():
                for b in range(count_b):
                    even_ref[b] = even_rows(previous_ref, WIDTH, SIDE, count_a, b)

            @pl.when(jnp.logical_not(earlier))
            def _():
                for b in range(count_b):
                    even_ref[b] = even_rows(padded, WIDTH, SIDE, count_a, b)

            for kind, part in enumerate(packed(even_ref, own_matrix)):
                own_out[kind] = part
            send_into(even_ref, sent_matrix, sent_out)

    full = shape(count_x, count_y, count_z)
    slab, side = shape(2 * WIDTH, count_y, count_z), shape(count_x, SIDE, count_z)
    even = shape(count_b, count_a, count_z)
    bordered = shape(count_x + 2 * WIDTH, count_y + 2 * SIDE, count_z)
    outs = [bordered, full if last else bordered, slab, side]
    if first:
        outs += [full, slab, side, shape(8, count_j, dtype=jnp.int32), shape(8, count_j)]
    if snapshot:
        size = GROUP * count_z
        outs += [
            shape(4, count_b // GROUP * count_a, count_z),
            sent_shape(count_a, count_b, count_z),
            shape(size, size, dtype=BF16),
            shape(size, size, dtype=BF16),
            shape(8, count_z),
        ]
    if ahead:
        outs.append(full)
    if last:
        outs.append(even)
    place_of = spec(pltpu.HBM) if first else spec(pltpu.VMEM)
    if first:
        operands = [*points, current]
    elif last:
        operands = [points, current]
    else:
        operands = [points, waves, current]
    aliases = {} if first else {len(operands) - 1: 0}
    specs = [place_of] * (len(operands) - 1) + [spec(pltpu.VMEM)]
    if not first:
        operands += list(faces)
        specs += [spec(pltpu.VMEM)] * 3
    operands += [previous, courant]
    specs += [place_of] * 2
    scratch = [pltpu.VMEM(full.shape, F32)] * 2
    if first:
        scratch.append(pltpu.VMEM(full.shape, F32))
        scratch += [pltpu.VMEM(array.shape, array.dtype) for array in points]
        scratch.append(pltpu.SemaphoreType.DMA((6,)))
    if snapshot:
        operands += [snapshots, matrices]
        specs += [spec(pltpu.HBM)] * 2
        scratch += [
            pltpu.VMEM(even.shape, F32),
            pltpu.SMEM(snapshots.shape, jnp.int32),
            pltpu.SemaphoreType.DMA((3,)),
        ]
    return pl.pallas_call(
        kernel,
        out_shape=tuple(outs),
        in_specs=specs,
        out_specs=(spec(pltpu.VMEM),) * len(outs),
        scratch_shapes=scratch,
        input_output_aliases=aliases,
        compiler_params=params(20),
        cost_estimate=cost(count_x * count_y * count_z, 60, 6),
    )(*operands)


def low_terms(halo_ref, r):
    total = None
    for k in range(r + 1, WIDTH + 1):
        term = WEIGHTS[k - 1] * halo_ref[WIDTH + r - k]
        total = term if total is None else total + term
    return total


def high_terms(halo_ref, r):
    total = None
    for k in range(WIDTH - r, WIDTH + 1):
        term = WEIGHTS[k - 1] * halo_ref[r + k - WIDTH]
        total = term if total is None else total + term
    return total


def add_halo(place, parts, halos, outs):
    qx_ref, qy_ref, cx_ref, cy_ref = parts
    far_in, near_in, side_in = halos
    far_out, near_out, side_out = outs
    count_y, count_x = qx_ref.shape[1], qy_ref.shape[0]
    block = place.block(count_y)

    def along_x(low_in, high_in, low_out, high_out):
        for r in range(WIDTH):
            low, high = qx_ref[r], qx_ref[WIDTH + r]
            if low_in is not None:
                low = low + cx_ref[r] * low_terms(low_in, r)
            if high_in is not None:
                high = high + cx_ref[WIDTH + r] * high_terms(high_in, r)
            low_out[r], high_out[r] = low, high
        side_out[pl.ds(0, WIDTH)] = low_out[:, pl.ds(block, SIDE)]
        side_out[pl.ds(count_x - WIDTH, WIDTH)] = high_out[:, pl.ds(block, SIDE)]

    inner = pl.ds(WIDTH, count_x - 2 * WIDTH)
    side_out[inner] = qy_ref[inner]

    @pl.when(place.even)
    def _():
        along_x(far_in, near_in, far_out, near_out)

    @pl.when(jnp.logical_not(place.even))
    def _():
        along_x(near_in, far_in, near_out, far_out)

    def along_y(shifts, masks):
        halo = side_in[...]
        lanes = halo.shape[2]
        line = lax.broadcasted_iota(jnp.int32, (1, SIDE, lanes), 1)
        total = None
        for k in range(1, WIDTH + 1):
            weight = jnp.where(masks(line, k), WEIGHTS[k - 1], 0.0)
            term = weight * pltpu.roll(halo, shifts(k), 1)
            total = term if total is None else total + term
        side_out[...] = side_out[...] + cy_ref[...] * total

    @pl.when(place.y == 0)
    def _():
        along_y(lambda k: SIDE - k, lambda line, k: line >= SIDE - k)

    @pl.when(place.y != 0)
    def _():
        along_y(lambda k: k, lambda line, k: line < k)

    def corners(low_out, high_out):
        low_out[:, pl.ds(block, SIDE)] = side_out[pl.ds(0, WIDTH)]
        high_out[:, pl.ds(block, SIDE)] = side_out[pl.ds(count_x - WIDTH, WIDTH)]

    @pl.when(place.even)
    def _():
        corners(far_out, near_out)

    @pl.when(jnp.logical_not(place.even))
    def _():
        corners(near_out, far_out)


def halo_step(parts, halos):
    count_y, (count_x, _, count_z) = parts[0].shape[1], parts[1].shape

    def kernel(*refs):
        add_halo(Place(), refs[:4], refs[4:7], refs[7:])

    return pl.pallas_call(
        kernel,
        out_shape=face_shapes(count_x, count_y, count_z),
        in_specs=[spec(pltpu.VMEM)] * 7,
        out_specs=(spec(pltpu.VMEM),) * 3,
        compiler_params=params(8),
        cost_estimate=cost(16 * count_y * count_z, 10, 6),
        name="halo_step",
    )(*parts, *halos)


def pack_matrix(window, count_z):
    half = count_z // GROUP
    size = GROUP * count_z
    row, column = np.arange(size)[:, None], np.arange(size)[None, :]
    row_b, row_z = row // count_z, row % count_z
    kind = column // count_z
    parity = kind % 2
    lane_b, lane_i = (column % count_z) // half, column % half
    main = (row_b == lane_b) & (row_z == 2 * (half * window + lane_i) + parity)
    wanted_b = (lane_b + (GROUP - 1 if window == 0 else 1)) % GROUP
    wanted_z = 2 * (half * (1 - window) + lane_i) + parity
    useful = lane_i < REACH if window == 0 else lane_i >= half - REACH
    edge = (row_b == wanted_b) & (row_z == wanted_z) & useful
    return np.where(kind < 2, main, edge).astype(np.float32)


def packed(even_ref, matrix_ref):
    count_b, _, count_z = even_ref.shape
    rows = [
        jnp.concatenate([even_ref[b + i] for i in range(GROUP)], axis=1)
        for b in range(0, count_b, GROUP)
    ]
    result = exact_dot(jnp.concatenate(rows, axis=0), matrix_ref[...])
    return [result[:, kind * count_z : (kind + 1) * count_z] for kind in range(4)]


def lag_shifts(lag, is_source):
    parity = lag & 1
    source_shift = -((lag + parity) >> 1)
    receiver_shift = (lag - parity) >> 1
    return (
        parity,
        jnp.where(is_source, source_shift, receiver_shift),
        jnp.where(is_source, receiver_shift, source_shift),
    )


def moved(main, edge, shift):
    count_z = main.shape[1]
    half = count_z // GROUP
    lane = lax.broadcasted_iota(jnp.int32, (1, count_z), 1) % half
    mask = (lane < shift) | (lane >= half + shift)
    return pltpu.roll(jnp.where(mask, edge, main), (count_z - shift) & (count_z - 1), 1)


def pack_own(lags, even, matrix):
    count_b, count_a, count_z = even.shape
    total_rows = count_b // GROUP * count_a
    (count_h,) = lags.shape

    def kernel(lags_ref, even_ref, matrix_ref, out_ref, windows, lag_of, sem):
        copy = pltpu.make_async_copy(lags_ref, lag_of, sem)
        copy.start()
        place = Place()
        for kind, part in enumerate(packed(even_ref, matrix_ref)):
            windows[kind] = part
        copy.wait()
        for h in range(count_h):
            parity, shift, _ = lag_shifts(lag_of[h], place.field == 0)
            out_ref[h] = moved(windows[parity], windows[2 + parity], shift)

    return pl.pallas_call(
        kernel,
        out_shape=shape(count_h, total_rows, count_z),
        in_specs=[spec(pltpu.HBM)] + [spec(pltpu.VMEM)] * 2,
        out_specs=spec(pltpu.VMEM),
        scratch_shapes=[
            pltpu.VMEM((4, total_rows, count_z), F32),
            pltpu.SMEM((count_h,), jnp.int32),
            pltpu.SemaphoreType.DMA,
        ],
        compiler_params=params(8),
        cost_estimate=cost(count_b * count_a * count_z, 1024, 4),
        name="pack_own",
    )(lags, even, matrix)


def edge_slots(count_a, groups, count_z):
    fits = count_z // GROUP // REACH
    slots = []
    for index in range(2 * groups):
        slots.append((index // groups, index % groups, index // fits * count_a, index % fits * REACH))
    return slots, -(-2 * groups // fits) * count_a


def edge_sums(parts, count_a, groups, count_z):
    slots, extra = edge_slots(count_a, groups, count_z)
    sums = {}
    for parity, g, row, shift in slots:
        part = parts[2 + parity][g * count_a : (g + 1) * count_a]
        part = pltpu.roll(part, shift, 1) if shift else part
        sums[row] = sums[row] + part if row in sums else part
    return sums, extra


def send_into(even_ref, matrix_ref, out_ref):
    count_b, count_a, count_z = even_ref.shape
    groups = count_b // GROUP
    total_rows = groups * count_a
    parts = packed(even_ref, matrix_ref)
    out_ref[pl.ds(0, total_rows), :] = parts[0]
    out_ref[pl.ds(total_rows, total_rows), :] = parts[1]
    for row, part in edge_sums(parts, count_a, groups, count_z)[0].items():
        out_ref[pl.ds(2 * total_rows + row, count_a), :] = part


def sent_shape(count_a, count_b, count_z):
    groups = count_b // GROUP
    _, extra = edge_slots(count_a, groups, count_z)
    return shape(2 * groups * count_a + extra, count_z)


KEPT = SIDE - WIDTH // 2
FREE = SIDE - KEPT
BATCH = KEPT // FREE + 1


def give_rows(groups):
    tiles = 2 * groups
    return SIDE * tiles, SIDE * (tiles // BATCH * (BATCH - 1))


def give_into(place, even_ref, matrix_ref, out_ref):
    count_b, count_a, count_z = even_ref.shape
    groups = count_b // GROUP
    assert count_a == 2 * SIDE and 2 * groups % BATCH == 0
    parts = packed(even_ref, matrix_ref)
    whole_rows, part_rows = give_rows(groups)
    line = lax.broadcasted_iota(jnp.int32, (SIDE, count_z), 0)

    def store(far_tile, shift):
        fars = []
        for index in range(2 * groups):
            start = index % groups * count_a
            both = [
                parts[index // groups][start + SIDE * tile : start + SIDE * (tile + 1)]
                for tile in range(2)
            ]
            out_ref[pl.ds(SIDE * index, SIDE), :] = both[1 - far_tile]
            fars.append(pltpu.roll(both[far_tile], shift, 0) if shift else both[far_tile])
        row = whole_rows
        for first in range(0, 2 * groups, BATCH):
            *hosts, guest = fars[first : first + BATCH]
            for i, host in enumerate(hosts):
                moved_guest = pltpu.roll(guest, KEPT - FREE * i, 0)
                out_ref[pl.ds(row, SIDE), :] = jnp.where(line < KEPT, host, moved_guest)
                row += SIDE

    pl.when(place.even)(lambda: store(0, KEPT))
    pl.when(jnp.logical_not(place.even))(lambda: store(1, 0))
    for row, part in edge_sums(parts, count_a, groups, count_z)[0].items():
        out_ref[pl.ds(whole_rows + part_rows + row, count_a), :] = part


def take_windows(place, other_ref, mains, groups, count_a):
    count_z = other_ref.shape[1]
    whole_rows, _ = give_rows(groups)
    line = lax.broadcasted_iota(jnp.int32, (SIDE, count_z), 0)

    def load(far_tile, shift):
        fars = []
        row = whole_rows
        for _ in range(0, 2 * groups, BATCH):
            hosts = [other_ref[pl.ds(row + SIDE * i, SIDE), :] for i in range(BATCH - 1)]
            row += SIDE * (BATCH - 1)
            guest = None
            for i, host in enumerate(hosts):
                piece = pltpu.roll(host, (FREE * (i + 1)) % SIDE, 0)
                guest = piece if guest is None else jnp.where(line < FREE * i, guest, piece)
            fars += [*hosts, guest]
        for index, far in enumerate(fars):
            start = index % groups * count_a
            far = pltpu.roll(far, shift, 0) if shift else far
            mains[index // groups, pl.ds(start + SIDE * far_tile, SIDE), :] = far
            mains[index // groups, pl.ds(start + SIDE * (1 - far_tile), SIDE), :] = other_ref[
                pl.ds(SIDE * index, SIDE), :
            ]

    pl.when(place.even)(lambda: load(0, FREE))
    pl.when(jnp.logical_not(place.even))(lambda: load(1, 0))


def given_shape(count_a, count_b, count_z):
    groups = count_b // GROUP
    return shape(sum(give_rows(groups)) + edge_slots(count_a, groups, count_z)[1], count_z)


def last_step(flag, even_before, current, parts, near, side, matrix):
    count_x, count_y, count_z = current.shape
    count_a, count_b = count_x // 2, count_y // 2

    def kernel(
        flag_ref, even_ref, current_ref, qx_ref, qy_ref, cx_ref, cy_ref, near_ref, side_ref,
        matrix_ref, final_ref, late_ref, sent_ref, far_out, near_out, side_out,
    ):
        place = Place()
        add_halo(
            place, (qx_ref, qy_ref, cx_ref, cy_ref), (None, near_ref, side_ref),
            (far_out, near_out, side_out),
        )
        low, high = pl.ds(0, WIDTH), pl.ds(count_x - WIDTH, WIDTH)

        @pl.when(place.even)
        def _():
            final_ref[high] = near_out[...]
            final_ref[low] = far_out[...]

        @pl.when(jnp.logical_not(place.even))
        def _():
            final_ref[low] = near_out[...]
            final_ref[high] = far_out[...]

        final_ref[:, pl.ds(place.block(count_y), SIDE)] = side_out[...]
        wants_last = jnp.broadcast_to(flag_ref[0:1, :], (count_a, count_z)) > 0.5
        for b in range(count_b):
            late_ref[b] = jnp.where(
                wants_last, even_rows(final_ref, 0, 0, count_a, b), even_ref[b]
            )
        give_into(place, late_ref, matrix_ref, sent_ref)

    slab, _, side_shape = face_shapes(count_x, count_y, count_z)
    return pl.pallas_call(
        kernel,
        out_shape=(
            shape(*current.shape),
            shape(count_b, count_a, count_z),
            given_shape(count_a, count_b, count_z),
        ),
        in_specs=[spec(pltpu.VMEM)] * 10,
        out_specs=(spec(pltpu.VMEM),) * 3,
        scratch_shapes=[
            pltpu.VMEM(slab.shape, F32),
            pltpu.VMEM(slab.shape, F32),
            pltpu.VMEM(side_shape.shape, F32),
        ],
        input_output_aliases={2: 0},
        compiler_params=params(12),
        cost_estimate=cost(count_x * count_y * count_z, 10, 3),
        name="last_step",
    )(flag, even_before, current, *parts, near, side, matrix)


def far_rows(count_b):
    return -(-2 * (count_b // GROUP) // 16) * 16


def last_far(flag, final, late, cx, far, matrix):
    count_x, count_y, count_z = final.shape
    count_b, count_a, _ = late.shape
    rows, pair = far_rows(count_b), WIDTH // 2

    def kernel(
        flag_ref, final_in, late_in, cx_ref, far_ref, matrix_ref, final_ref, late_ref, sent_ref, lhs,
    ):
        place = Place()
        wants_last = jnp.broadcast_to(flag_ref[0:1, :], (1, count_z)) > 0.5
        lhs[...] = jnp.zeros_like(lhs)

        def correct(first_x, first_c, first_a, terms):
            for r in range(WIDTH):
                final_ref[first_x + r] = final_ref[first_x + r] + cx_ref[first_c + r] * terms(
                    far_ref, r
                )
            for b in range(count_b):
                for i in range(pair):
                    value = jnp.where(
                        wants_last,
                        final_ref[first_x + 2 * i, pl.ds(2 * b, 1), :],
                        late_ref[b, pl.ds(first_a + i, 1), :],
                    )
                    late_ref[b, pl.ds(first_a + i, 1), :] = value
                    lanes = pl.ds(b % GROUP * count_z, count_z)
                    lhs[pl.ds(b // GROUP * pair + i, 1), lanes] = value

        @pl.when(place.even)
        def _():
            correct(0, 0, 0, low_terms)

        @pl.when(jnp.logical_not(place.even))
        def _():
            correct(count_x - WIDTH, WIDTH, count_a - pair, high_terms)

        result = exact_dot(lhs[...], matrix_ref[...])
        parts = [result[:, kind * count_z : (kind + 1) * count_z] for kind in range(4)]
        sent_ref[pl.ds(0, rows), :] = parts[0]
        sent_ref[pl.ds(rows, rows), :] = parts[1]
        sent_ref[pl.ds(2 * rows, rows), :] = parts[2] + pltpu.roll(parts[3], REACH, 1)

    return pl.pallas_call(
        kernel,
        out_shape=(shape(*final.shape), shape(*late.shape), shape(3 * rows, count_z)),
        in_specs=[spec(pltpu.VMEM)] * 6,
        out_specs=(spec(pltpu.VMEM),) * 3,
        scratch_shapes=[pltpu.VMEM((rows, GROUP * count_z), F32)],
        input_output_aliases={1: 0, 2: 1},
        compiler_params=params(12),
        cost_estimate=cost(WIDTH * count_y * count_z, 20, 3),
        name="last_far",
    )(flag, final, late, cx, far, matrix)


def write_out(level):
    def kernel(level_ref, out_ref, sem):
        copy = pltpu.make_async_copy(level_ref, out_ref, sem)
        copy.start()
        copy.wait()

    return pl.pallas_call(
        kernel,
        out_shape=shape(*level.shape),
        in_specs=[spec(pltpu.VMEM)],
        out_specs=spec(pltpu.HBM),
        scratch_shapes=[pltpu.SemaphoreType.DMA],
        compiler_params=params(4),
        cost_estimate=cost(level.size, 0, 2),
        name="write_out",
    )(level)


CODE_BITS = 5
PER_CODE = 6


def lag_image(count_a, lags, own, other, extra=None, before=None):
    _, total_rows, count_z = own.shape
    groups = total_rows // count_a
    half = count_z // GROUP
    last = before is not None
    count_h = before.shape[0] if last else lags.shape[0]
    codes = -(-count_h // PER_CODE)
    pair = WIDTH // 2

    def kernel(*refs):
        refs = list(refs)
        take = lambda count: [refs.pop(0) for _ in range(count)]
        lags_ref, own_ref, other_ref = take(3)
        if last:
            extra_ref, before_ref = take(2)
        (out_ref,) = take(1)
        if not last:
            (codes_ref,) = take(1)
        mains, edges = take(2)
        if last:
            store, sem = take(2)
        else:
            store = out_ref
            lag_of, sem = take(2)
        place = Place()
        if last:
            packed_lags = [lags_ref[k : k + 1, :][0, 0] for k in range(codes)]
            mask = (1 << CODE_BITS) - 1
            lag_list = [
                ((packed_lags[h // PER_CODE] >> (h % PER_CODE * CODE_BITS)) & mask) - LAGMAX
                for h in range(count_h)
            ]
        else:
            copy = pltpu.make_async_copy(lags_ref, lag_of, sem)
            copy.start()
        is_source = place.field == 0

        def useful(rows):
            lane = lax.broadcasted_iota(jnp.int32, (rows, count_z), 1) % half
            return jnp.where(is_source, lane, half - 1 - lane) < REACH

        slots, _ = edge_slots(count_a, groups, count_z)
        if last:
            take_windows(place, other_ref, mains, groups, count_a)
            edge_row = sum(give_rows(groups))
        else:
            for parity in range(2):
                mains[parity] = other_ref[pl.ds(parity * total_rows, total_rows), :]
            edge_row = 2 * total_rows
        for parity, g, row, shift in slots:
            part = other_ref[pl.ds(edge_row + row, count_a), :]
            part = pltpu.roll(part, count_z - shift, 1) if shift else part
            edges[parity, pl.ds(g * count_a, count_a), :] = jnp.where(useful(count_a), part, 0.0)
        if last:
            rows = extra_ref.shape[0] // 3
            border = extra_ref[pl.ds(2 * rows, rows), :]
            borders = [
                jnp.where(useful(rows), part, 0.0)
                for part in (border, pltpu.roll(border, count_z - REACH, 1))
            ]

            def overwrite(first_a):
                for g in range(groups):
                    target = pl.ds(g * count_a + first_a, pair)
                    for parity in range(2):
                        mains[parity, target, :] = extra_ref[
                            pl.ds(parity * rows + g * pair, pair), :
                        ]
                        edges[parity, target, :] = borders[parity][g * pair : (g + 1) * pair]

            pl.when(place.even)(lambda: overwrite(0))
            pl.when(jnp.logical_not(place.even))(lambda: overwrite(count_a - pair))
        else:
            copy.wait()
            lag_list = [lag_of[h] for h in range(count_h)]
            for k in range(codes):
                code = jnp.int32(0)
                for h in range(k * PER_CODE, min((k + 1) * PER_CODE, count_h)):
                    code = code | ((lag_list[h] + LAGMAX) << (h % PER_CODE * CODE_BITS))
                codes_ref[k : k + 1, :] = jnp.full((1, count_z), code, jnp.int32)
        for h, lag in enumerate(lag_list):
            parity, own_shift, other_shift = lag_shifts(lag, is_source)
            product = moved(mains[parity], edges[parity], other_shift)
            if last:
                product = product * own_ref[h]
            else:
                product = product * moved(own_ref[parity], own_ref[2 + parity], own_shift)
            for g in range(groups):
                part = product[g * count_a : (g + 1) * count_a]
                lanes = pl.ds(g * count_z, count_z)
                if last:
                    part = part + before_ref[h, :, lanes]
                store[h, :, lanes] = part
            if last:
                pltpu.make_async_copy(store.at[h], out_ref.at[h], sem).start()
        if last:
            pltpu.make_async_copy(store, out_ref, sem).wait()

    image = shape(count_h, count_a, groups * count_z)
    operands = [lags, own, other] + ([extra, before] if last else [])
    scratch = [pltpu.VMEM((2, total_rows, count_z), F32)] * 2
    scratch.append(pltpu.VMEM(image.shape, F32) if last else pltpu.SMEM((count_h,), jnp.int32))
    scratch.append(pltpu.SemaphoreType.DMA)
    return pl.pallas_call(
        kernel,
        out_shape=image if last else (image, shape(8, count_z, dtype=jnp.int32)),
        in_specs=[spec(pltpu.VMEM if last else pltpu.HBM)]
        + [spec(pltpu.VMEM)] * (len(operands) - 1),
        out_specs=spec(pltpu.HBM) if last else (spec(pltpu.VMEM),) * 2,
        scratch_shapes=scratch,
        compiler_params=params(12),
        cost_estimate=cost(count_h * total_rows * count_z, 10, 2),
        name="last_image" if last else "early_image",
    )(*operands)


def body(
    field_now,
    field_prev,
    courant_squared,
    source_cells,
    source_wave,
    receiver_cells,
    receiver_wave,
    snapshot_steps,
    lag_offsets,
):
    count_x, _, count_z = field_now.shape
    loop_size = lax.axis_size("gx")
    half_size = loop_size // 2
    turn = loop_size // 4
    assert lax.axis_size("gy") == 2 and half_size % 2 == 0

    slabs = [(i - turn) % loop_size % half_size for i in range(loop_size)]

    def pairs(odd):
        found = []
        for i, slab in enumerate(slabs):
            if slab % 2 == odd and slab != half_size - 1:
                j = (i + 1) % loop_size
                found += [(i, j), (j, i)]
        return found

    near_pairs, far_pairs = pairs(0), pairs(1)
    across = [(i, (i + half_size) % loop_size) for i in range(loop_size)]

    def send_far(far):
        return lax.ppermute(far, "gx", far_pairs)

    def send_near(near, side):
        near = lax.ppermute(near, "gx", near_pairs)
        return near, lax.ppermute(side, "gy", [(0, 1), (1, 0)])

    def exchange(faces):
        far, near, side = faces
        return (send_far(far), *send_near(near, side))

    matrices = jnp.asarray(
        np.stack([pack_matrix(window, count_z) for window in (0, 1)]), dtype=BF16
    )
    raw = (source_cells, source_wave, receiver_cells, receiver_wave)
    field_kept, field_prev, courant_squared, matrices, snapshot_steps, lag_offsets, *raw = (
        pltpu.with_memory_space_constraint(array, pltpu.HBM)
        for array in (
            field_now, field_prev, courant_squared, matrices, snapshot_steps, lag_offsets, *raw
        )
    )
    halos = exchange(first_faces(field_kept))
    whole0, next1, qx, qy, courant, cx, cy, points, waves = inner_step(
        0, raw, None, field_now, None, field_prev, courant_squared
    )
    faces = halo_step((qx, qy, cx, cy), halos)
    halos = exchange(faces)
    whole1, next2, qx, qy, added = inner_step(1, points, waves, next1, faces, whole0, courant)
    faces = halo_step((qx, qy, cx, cy), halos)
    halos = exchange(faces)
    whole2, next3, qx, qy, own_early, sent_early, own_matrix, sent_matrix, flag = inner_step(
        2, points, waves, next2, faces, whole1, courant, snapshot_steps, matrices
    )
    other_early = lax.ppermute(sent_early, "gx", across)
    faces = halo_step((qx, qy, cx, cy), halos)
    far, near, side = exchange(faces)
    _, next4, qx, qy, even3 = inner_step(3, added, None, next3, faces, whole2, courant)
    final, late, sent_late = last_step(
        flag, even3, next4, (qx, qy, cx, cy), near, side, sent_matrix
    )
    other_late = lax.ppermute(sent_late, "gx", across)
    partial, codes = lag_image(count_x // 2, lag_offsets, own_early, other_early)
    final, late, sent_far = last_far(flag, final, late, cx, far, sent_matrix)
    extra = lax.ppermute(sent_far, "gx", across)
    own_late = pack_own(lag_offsets, late, own_matrix)
    image = lag_image(count_x // 2, codes, own_late, other_late, extra, partial)
    return write_out(final), jnp.transpose(image, (1, 0, 2))


def solution(mesh):
    placed = (
        P(("shots", "gx"), "gy", None),
        P(("shots", "gx"), "gy", None),
        P("gx", "gy", None),
        P(None, "shots"),
        P(None, "shots"),
        P(None, "shots"),
        P(None, "shots"),
        P("shots", None),
        P(),
    )
    return jax.shard_map(
        body,
        mesh=mesh,
        in_specs=placed,
        out_specs=(P(("shots", "gx"), "gy", None), P(("shots", "gx"), None, "gy")),
        check_vma=False,
    )
```

```python
import jax
import jax.numpy as jnp
import numpy as np
from jax import lax
from jax.experimental import pallas as pl
from jax.experimental.pallas import tpu as pltpu
from jax.sharding import PartitionSpec as P

STEPS = 4
WIDTH = 4
LAGMAX = 8
REACH = LAGMAX // 2
GROUP = 4
SIDE = 8

SCALE = 5040.0
BAND = (8064.0, -1008.0, 128.0, -9.0)
CENTRE = 3.0 * (-205.0 / 72.0)
WEIGHTS = (1.6, -0.2, 8.0 / 315.0, -1.0 / 560.0)

F32 = jnp.float32
BF16 = jnp.bfloat16


def shape(*dims, dtype=F32):
    return jax.ShapeDtypeStruct(dims, dtype)


def params(megabytes):
    return pltpu.CompilerParams(vmem_limit_bytes=megabytes << 20)


def spec(space):
    return pl.BlockSpec(memory_space=space)


def cost(count, flops_each, arrays):
    return pl.CostEstimate(
        flops=int(count * flops_each), bytes_accessed=int(4 * count * arrays), transcendentals=0
    )


def split3(values):
    high = values.astype(BF16)
    rest = values - high.astype(F32)
    middle = rest.astype(BF16)
    low = (rest - middle.astype(F32)).astype(BF16)
    return high, middle, low


def exact_dot(values, matrix):
    rows = values.shape[0]
    stacked = jnp.concatenate(split3(values), axis=0)
    result = jnp.dot(stacked, matrix, preferred_element_type=F32)
    return (result[2 * rows :] + result[rows : 2 * rows]) + result[:rows]


class Place:
    def __init__(self):
        loop_size = lax.axis_size("gx")
        self.half = loop_size // 2
        relative = lax.rem(lax.axis_index("gx") + loop_size - loop_size // 4, loop_size)
        self.field = relative // self.half
        self.slab = lax.rem(relative, self.half)
        self.even = lax.rem(self.slab, 2) == 0
        self.y = lax.axis_index("gy")

    def block(self, count_y):
        return pl.multiple_of((1 - self.y) * (count_y - SIDE), SIDE)


def first_faces(field):
    count_x, count_y, count_z = field.shape
    top = count_x - WIDTH

    def kernel(field_ref, far_ref, near_ref, side_ref, sems):
        place = Place()
        far = jnp.where(place.even, 0, top)
        sources = [
            field_ref.at[pl.ds(far, WIDTH)],
            field_ref.at[pl.ds(top - far, WIDTH)],
            field_ref.at[:, pl.ds(place.block(count_y), SIDE)],
        ]
        copies = [
            pltpu.make_async_copy(source, target, sems.at[index])
            for index, (source, target) in enumerate(zip(sources, (far_ref, near_ref, side_ref)))
        ]
        for copy in copies:
            copy.start()
        for copy in copies:
            copy.wait()

    return pl.pallas_call(
        kernel,
        out_shape=face_shapes(count_x, count_y, count_z),
        in_specs=[spec(pltpu.HBM)],
        out_specs=(spec(pltpu.VMEM),) * 3,
        scratch_shapes=[pltpu.SemaphoreType.DMA((3,))],
        compiler_params=params(8),
        name="first_faces",
    )(field)


def face_shapes(count_x, count_y, count_z):
    slab = shape(WIDTH, count_y, count_z)
    return slab, slab, shape(count_x, SIDE, count_z)


def even_rows(level_ref, offset_x, offset_y, count_a, b):
    rows, stride, lanes = level_ref.shape
    flat = level_ref.reshape(rows * stride, lanes)
    start = offset_x * stride + offset_y + 2 * b
    return flat[pl.ds(start, count_a, stride=2 * stride), :]


def inner_step(number, points, waves, current, faces, previous, courant, snapshots=None, matrices=None,
    halos=None,
):
    count_x, count_y, count_z = courant.shape
    count_a, count_b = count_x // 2, count_y // 2
    first = faces is None
    last = number == STEPS - 1
    snapshot = number == STEPS // 2
    ahead = number == 1
    if last:
        count_j = 0
    elif first:
        count_j = -(-max(array.shape[1] for array in points) // 128) * 128
    else:
        count_j = points.shape[1]

    def kernel(*refs):
        refs = list(refs)
        take = lambda count: [refs.pop(0) for _ in range(count)]
        if first:
            raw_refs = take(4)
        elif last:
            (added_ref,) = take(1)
        else:
            points_ref, waves_ref = take(2)
        (current_ref,) = take(1)
        if not first:
            far_ref, near_ref, side_ref = take(3)
        previous_ref, courant_ref = take(2)
        if snapshot:
            steps_ref, matrices_ref = take(2)
        if last:
            near_in, side_in, steps_ref, matrix_ref = take(4)
        padded, next_ref = take(2)
        if last:
            late_ref, sent_ref = take(2)
        else:
            qx_ref, qy_ref = take(2)
        if first:
            kept_ref, cx_ref, cy_ref, points_ref, waves_ref = take(5)
        if snapshot:
            own_out, sent_out, own_matrix, sent_matrix, flag_ref = take(5)
        if ahead:
            (ahead_ref,) = take(1)
        zpart, addpart = take(2)
        if last:
            addpart = added_ref
        if first:
            before_ref = take(1)[0]
            raw_refs_in, raw_refs = raw_refs, take(4)
            (sems,) = take(1)
        if snapshot:
            even_ref, wanted, sems = take(3)
        if last:
            wanted, sem = take(2)
            last_copy = pltpu.make_async_copy(steps_ref, wanted, sem)
            last_copy.start()

        place = Place()
        block = place.block(count_y)
        rows, columns = pl.ds(WIDTH, count_x), pl.ds(SIDE, count_y)
        if first:
            copies = [
                pltpu.make_async_copy(source, target, sems.at[index])
                for index, (source, target) in enumerate(
                    zip(
                        (*raw_refs_in, previous_ref, courant_ref),
                        (*raw_refs, before_ref, kept_ref),
                    )
                )
            ]
            for copy in copies:
                copy.start()
        else:
            before_ref, kept_ref = previous_ref, courant_ref
        if snapshot:
            copies = [
                pltpu.make_async_copy(steps_ref, wanted, sems.at[0]),
                pltpu.make_async_copy(matrices_ref.at[place.field], own_matrix, sems.at[1]),
                pltpu.make_async_copy(matrices_ref.at[1 - place.field], sent_matrix, sems.at[2]),
            ]
            for copy in copies:
                copy.start()

        def clear_border(level_ref):
            zero_x = jnp.zeros((WIDTH, count_y + 2 * SIDE, count_z), F32)
            level_ref[pl.ds(0, WIDTH)] = zero_x
            level_ref[pl.ds(count_x + WIDTH, WIDTH)] = zero_x
            zero_y = jnp.zeros((count_x, SIDE, count_z), F32)
            level_ref[rows, pl.ds(0, SIDE)] = zero_y
            level_ref[rows, pl.ds(count_y + SIDE, SIDE)] = zero_y

        if first:
            clear_border(padded)
            padded[rows, columns] = current_ref[...]
        if not last:
            clear_border(next_ref)
        next_x, next_y = (0, 0) if last else (WIDTH, SIDE)
        before_x, before_y = (0, 0) if first else (WIDTH, SIDE)
        if not first:
            low, high = pl.ds(WIDTH, WIDTH), pl.ds(count_x, WIDTH)

            @pl.when(place.even)
            def _():
                padded[high, columns] = near_ref[...]
                padded[low, columns] = far_ref[...]

            @pl.when(jnp.logical_not(place.even))
            def _():
                padded[low, columns] = near_ref[...]
                padded[high, columns] = far_ref[...]

            padded[rows, pl.ds(pl.multiple_of(block + SIDE, SIDE), SIDE)] = side_ref[...]
        if last:
            beside = pl.multiple_of((1 - place.y) * (count_y + SIDE), SIDE)
            padded[rows, pl.ds(beside, SIDE)] = side_in[...]

            @pl.when(place.even)
            def _():
                padded[pl.ds(count_x + WIDTH, WIDTH), columns] = near_in[...]

            @pl.when(jnp.logical_not(place.even))
            def _():
                padded[pl.ds(0, WIDTH), columns] = near_in[...]

        gap = jnp.abs(
            lax.broadcasted_iota(jnp.int32, (count_z, count_z), 0)
            - lax.broadcasted_iota(jnp.int32, (count_z, count_z), 1)
        )
        band = jnp.zeros((count_z, count_z), F32)
        for offset, weight in enumerate(BAND, 1):
            band = jnp.where(gap == offset, weight, band)
        band = jnp.concatenate([band.astype(BF16)] * 3, axis=0)

        chunk = 8

        def multiply(index, _):
            start = pl.multiple_of(index * chunk, chunk)
            values = padded[pl.ds(start + WIDTH, chunk), columns]
            terms = jnp.concatenate(split3(values.reshape(chunk * count_y, count_z)), axis=1)
            zpart[pl.ds(start, chunk)] = jnp.dot(
                terms, band, preferred_element_type=F32
            ).reshape(chunk, count_y, count_z)
            return 0

        chunks = count_x // chunk
        if first or last:
            lax.fori_loop(0, chunks, multiply, 0)

        if first:
            for copy in copies[:4]:
                copy.wait()
            points_ref[...] = jnp.full(points_ref.shape, -1, jnp.int32)
            waves_ref[...] = jnp.zeros(waves_ref.shape, F32)

            def choose(cells_ref, wave_ref):
                count = cells_ref.shape[1]
                points_ref[pl.ds(0, 3), pl.ds(0, count)] = cells_ref[...]
                waves_ref[pl.ds(0, STEPS), pl.ds(0, count)] = wave_ref[...]

            @pl.when(place.field == 0)
            def _():
                choose(raw_refs[0], raw_refs[1])

            @pl.when(place.field != 0)
            def _():
                choose(raw_refs[2], raw_refs[3])

        if not last:
            px = points_ref[0:1, :] - place.slab * count_x
            py = points_ref[1:2, :] - place.y * count_y
            inside = (px >= 0) & (px < count_x) & (py >= 0) & (py < count_y)
            home = jnp.where(inside, px * count_y + py, -1)
            at_z = (
                lax.broadcasted_iota(jnp.int32, (count_z, count_j), 0) == points_ref[2:3, :]
            )

            def spread_of(step):
                terms = split3(jnp.where(at_z, waves_ref[step : step + 1, :], 0.0))
                return jnp.concatenate(terms, axis=1)

            spreads = [(addpart, spread_of(number))]
            if ahead:
                spreads.append((ahead_ref, spread_of(STEPS - 1)))

        def inject(index, _):
            start = pl.multiple_of(index * chunk, chunk)
            here = start * count_y + lax.broadcasted_iota(
                jnp.int32, (chunk * count_y, count_j), 0
            )
            hit = jnp.where(here == home, 1.0, 0.0).astype(BF16)
            hit = jnp.concatenate([hit] * 3, axis=1)
            for target, spread in spreads:
                added = lax.dot_general(
                    hit, spread, (((1,), (1,)), ((), ())), preferred_element_type=F32
                )
                target[pl.ds(start, chunk)] = added.reshape(chunk, count_y, count_z)
            return 0

        def both(index, _):
            multiply(index, 0)
            return inject(index, 0)

        if not last:
            lax.fori_loop(0, chunks, inject if first else both, 0)
        if first:
            for copy in copies[4:]:
                copy.wait()

        depth = 4

        def row_group(index, _):
            x = index * depth
            for y in range(0, count_y, SIDE):
                here, inner = pl.ds(y + SIDE, SIDE), pl.ds(y, SIDE)
                lines = [padded[x + i, here] for i in range(depth + 2 * WIDTH)]
                for j in range(depth):
                    middle = lines[WIDTH + j]
                    total = CENTRE * middle + (1.0 / SCALE) * zpart[x + j, inner]
                    for offset, weight in enumerate(WEIGHTS, 1):
                        paired = lines[WIDTH + j + offset] + lines[WIDTH + j - offset]
                        paired = paired + (
                            padded[x + WIDTH + j, pl.ds(y + SIDE + offset, SIDE)]
                            + padded[x + WIDTH + j, pl.ds(y + SIDE - offset, SIDE)]
                        )
                        total = total + weight * paired
                    old = before_ref[x + j + before_x, pl.ds(y + before_y, SIDE)]
                    value = 2.0 * middle - old + kept_ref[x + j, inner] * total
                    next_ref[x + j + next_x, pl.ds(y + next_y, SIDE)] = (
                        value + addpart[x + j, inner]
                    )
            return 0

        lax.fori_loop(0, count_x // depth, row_group, 0)

        if not last:
            next_columns = pl.ds(next_y, count_y)
            qx_ref[pl.ds(0, WIDTH)] = next_ref[pl.ds(next_x, WIDTH), next_columns]
            qx_ref[pl.ds(WIDTH, WIDTH)] = next_ref[
                pl.ds(next_x + count_x - WIDTH, WIDTH), next_columns
            ]
            qy_ref[...] = next_ref[
                pl.ds(next_x, count_x), pl.ds(pl.multiple_of(block + next_y, SIDE), SIDE)
            ]
        if first:
            cx_ref[pl.ds(0, WIDTH)] = kept_ref[pl.ds(0, WIDTH)]
            cx_ref[pl.ds(WIDTH, WIDTH)] = kept_ref[pl.ds(count_x - WIDTH, WIDTH)]
            cy_ref[...] = kept_ref[:, pl.ds(block, SIDE)]
        if last:
            last_copy.wait()
            wants_last = wanted[place.field, 1] == STEPS

            @pl.when(wants_last)
            def _():
                for b in range(count_b):
                    late_ref[b] = even_rows(next_ref, 0, 0, count_a, b)

            @pl.when(jnp.logical_not(wants_last))
            def _():
                for b in range(count_b):
                    late_ref[b] = even_rows(padded, WIDTH, SIDE, count_a, b)

            give_into(place, late_ref, matrix_ref, sent_ref)
        if snapshot:
            for copy in copies:
                copy.wait()
            flag_ref[...] = jnp.where(
                wanted[place.field, 1] == STEPS, jnp.ones(flag_ref.shape, F32), 0.0
            )
            earlier = wanted[place.field, 0] == number - 1

            @pl.when(earlier)
            def _():
                for b in range(count_b):
                    even_ref[b] = even_rows(previous_ref, WIDTH, SIDE, count_a, b)

            @pl.when(jnp.logical_not(earlier))
            def _():
                for b in range(count_b):
                    even_ref[b] = even_rows(padded, WIDTH, SIDE, count_a, b)

            for kind, part in enumerate(packed(even_ref, own_matrix)):
                own_out[kind] = part
            send_into(even_ref, sent_matrix, sent_out)

    full = shape(count_x, count_y, count_z)
    slab, side = shape(2 * WIDTH, count_y, count_z), shape(count_x, SIDE, count_z)
    even = shape(count_b, count_a, count_z)
    bordered = shape(count_x + 2 * WIDTH, count_y + 2 * SIDE, count_z)
    if last:
        outs = [bordered, full, even, given_shape(count_a, count_b, count_z)]
    else:
        outs = [bordered, bordered, slab, side]
    if first:
        outs += [full, slab, side, shape(8, count_j, dtype=jnp.int32), shape(8, count_j)]
    if snapshot:
        size = GROUP * count_z
        outs += [
            shape(4, count_b // GROUP * count_a, count_z),
            sent_shape(count_a, count_b, count_z),
            shape(size, size, dtype=BF16),
            shape(size, size, dtype=BF16),
            shape(8, count_z),
        ]
    if ahead:
        outs.append(full)
    place_of = spec(pltpu.HBM) if first else spec(pltpu.VMEM)
    if first:
        operands = [*points, current]
    elif last:
        operands = [points, current]
    else:
        operands = [points, waves, current]
    aliases = {} if first else {len(operands) - 1: 0}
    specs = [place_of] * (len(operands) - 1) + [spec(pltpu.VMEM)]
    if not first:
        operands += list(faces)
        specs += [spec(pltpu.VMEM)] * 3
    operands += [previous, courant]
    specs += [place_of] * 2
    scratch = [pltpu.VMEM(full.shape, F32)] * 2
    if first:
        scratch.append(pltpu.VMEM(full.shape, F32))
        scratch += [pltpu.VMEM(array.shape, array.dtype) for array in points]
        scratch.append(pltpu.SemaphoreType.DMA((6,)))
    if last:
        operands += [*halos, snapshots, matrices]
        specs += [spec(pltpu.VMEM)] * 2 + [spec(pltpu.HBM), spec(pltpu.VMEM)]
        scratch += [pltpu.SMEM(snapshots.shape, jnp.int32), pltpu.SemaphoreType.DMA]
    if snapshot:
        operands += [snapshots, matrices]
        specs += [spec(pltpu.HBM)] * 2
        scratch += [
            pltpu.VMEM(even.shape, F32),
            pltpu.SMEM(snapshots.shape, jnp.int32),
            pltpu.SemaphoreType.DMA((3,)),
        ]
    return pl.pallas_call(
        kernel,
        out_shape=tuple(outs),
        in_specs=specs,
        out_specs=(spec(pltpu.VMEM),) * len(outs),
        scratch_shapes=scratch,
        input_output_aliases=aliases,
        compiler_params=params(20),
        cost_estimate=cost(count_x * count_y * count_z, 60, 6),
    )(*operands)


def low_terms(halo_ref, r):
    total = None
    for k in range(r + 1, WIDTH + 1):
        term = WEIGHTS[k - 1] * halo_ref[WIDTH + r - k]
        total = term if total is None else total + term
    return total


def high_terms(halo_ref, r):
    total = None
    for k in range(WIDTH - r, WIDTH + 1):
        term = WEIGHTS[k - 1] * halo_ref[r + k - WIDTH]
        total = term if total is None else total + term
    return total


def add_halo(place, parts, halos, outs):
    qx_ref, qy_ref, cx_ref, cy_ref = parts
    far_in, near_in, side_in = halos
    far_out, near_out, side_out = outs
    count_y, count_x = qx_ref.shape[1], qy_ref.shape[0]
    block = place.block(count_y)

    def along_x(low_in, high_in, low_out, high_out):
        for r in range(WIDTH):
            low, high = qx_ref[r], qx_ref[WIDTH + r]
            if low_in is not None:
                low = low + cx_ref[r] * low_terms(low_in, r)
            if high_in is not None:
                high = high + cx_ref[WIDTH + r] * high_terms(high_in, r)
            low_out[r], high_out[r] = low, high
        side_out[pl.ds(0, WIDTH)] = low_out[:, pl.ds(block, SIDE)]
        side_out[pl.ds(count_x - WIDTH, WIDTH)] = high_out[:, pl.ds(block, SIDE)]

    inner = pl.ds(WIDTH, count_x - 2 * WIDTH)
    side_out[inner] = qy_ref[inner]

    @pl.when(place.even)
    def _():
        along_x(far_in, near_in, far_out, near_out)

    @pl.when(jnp.logical_not(place.even))
    def _():
        along_x(near_in, far_in, near_out, far_out)

    def along_y(shifts, masks):
        halo = side_in[...]
        lanes = halo.shape[2]
        line = lax.broadcasted_iota(jnp.int32, (1, SIDE, lanes), 1)
        total = None
        for k in range(1, WIDTH + 1):
            weight = jnp.where(masks(line, k), WEIGHTS[k - 1], 0.0)
            term = weight * pltpu.roll(halo, shifts(k), 1)
            total = term if total is None else total + term
        side_out[...] = side_out[...] + cy_ref[...] * total

    @pl.when(place.y == 0)
    def _():
        along_y(lambda k: SIDE - k, lambda line, k: line >= SIDE - k)

    @pl.when(place.y != 0)
    def _():
        along_y(lambda k: k, lambda line, k: line < k)

    def corners(low_out, high_out):
        low_out[:, pl.ds(block, SIDE)] = side_out[pl.ds(0, WIDTH)]
        high_out[:, pl.ds(block, SIDE)] = side_out[pl.ds(count_x - WIDTH, WIDTH)]

    @pl.when(place.even)
    def _():
        corners(far_out, near_out)

    @pl.when(jnp.logical_not(place.even))
    def _():
        corners(near_out, far_out)


def halo_step(parts, halos):
    count_y, (count_x, _, count_z) = parts[0].shape[1], parts[1].shape

    def kernel(*refs):
        add_halo(Place(), refs[:4], refs[4:7], refs[7:])

    return pl.pallas_call(
        kernel,
        out_shape=face_shapes(count_x, count_y, count_z),
        in_specs=[spec(pltpu.VMEM)] * 7,
        out_specs=(spec(pltpu.VMEM),) * 3,
        compiler_params=params(8),
        cost_estimate=cost(16 * count_y * count_z, 10, 6),
        name="halo_step",
    )(*parts, *halos)


def pack_matrix(window, count_z):
    half = count_z // GROUP
    size = GROUP * count_z
    row, column = np.arange(size)[:, None], np.arange(size)[None, :]
    row_b, row_z = row // count_z, row % count_z
    kind = column // count_z
    parity = kind % 2
    lane_b, lane_i = (column % count_z) // half, column % half
    main = (row_b == lane_b) & (row_z == 2 * (half * window + lane_i) + parity)
    wanted_b = (lane_b + (GROUP - 1 if window == 0 else 1)) % GROUP
    wanted_z = 2 * (half * (1 - window) + lane_i) + parity
    useful = lane_i < REACH if window == 0 else lane_i >= half - REACH
    edge = (row_b == wanted_b) & (row_z == wanted_z) & useful
    return np.where(kind < 2, main, edge).astype(np.float32)


def packed(even_ref, matrix_ref):
    count_b, _, count_z = even_ref.shape
    rows = [
        jnp.concatenate([even_ref[b + i] for i in range(GROUP)], axis=1)
        for b in range(0, count_b, GROUP)
    ]
    result = exact_dot(jnp.concatenate(rows, axis=0), matrix_ref[...])
    return [result[:, kind * count_z : (kind + 1) * count_z] for kind in range(4)]


def lag_shifts(lag, is_source):
    parity = lag & 1
    source_shift = -((lag + parity) >> 1)
    receiver_shift = (lag - parity) >> 1
    return (
        parity,
        jnp.where(is_source, source_shift, receiver_shift),
        jnp.where(is_source, receiver_shift, source_shift),
    )


def moved(main, edge, shift):
    count_z = main.shape[1]
    half = count_z // GROUP
    lane = lax.broadcasted_iota(jnp.int32, (1, count_z), 1) % half
    mask = (lane < shift) | (lane >= half + shift)
    return pltpu.roll(jnp.where(mask, edge, main), (count_z - shift) & (count_z - 1), 1)


def pack_own(lags, even, matrix):
    count_b, count_a, count_z = even.shape
    total_rows = count_b // GROUP * count_a
    (count_h,) = lags.shape

    def kernel(lags_ref, even_ref, matrix_ref, out_ref, windows, lag_of, sem):
        copy = pltpu.make_async_copy(lags_ref, lag_of, sem)
        copy.start()
        place = Place()
        for kind, part in enumerate(packed(even_ref, matrix_ref)):
            windows[kind] = part
        copy.wait()
        for h in range(count_h):
            parity, shift, _ = lag_shifts(lag_of[h], place.field == 0)
            out_ref[h] = moved(windows[parity], windows[2 + parity], shift)

    return pl.pallas_call(
        kernel,
        out_shape=shape(count_h, total_rows, count_z),
        in_specs=[spec(pltpu.HBM)] + [spec(pltpu.VMEM)] * 2,
        out_specs=spec(pltpu.VMEM),
        scratch_shapes=[
            pltpu.VMEM((4, total_rows, count_z), F32),
            pltpu.SMEM((count_h,), jnp.int32),
            pltpu.SemaphoreType.DMA,
        ],
        compiler_params=params(8),
        cost_estimate=cost(count_b * count_a * count_z, 1024, 4),
        name="pack_own",
    )(lags, even, matrix)


def edge_slots(count_a, groups, count_z):
    fits = count_z // GROUP // REACH
    slots = []
    for index in range(2 * groups):
        slots.append((index // groups, index % groups, index // fits * count_a, index % fits * REACH))
    return slots, -(-2 * groups // fits) * count_a


def edge_sums(parts, count_a, groups, count_z):
    slots, extra = edge_slots(count_a, groups, count_z)
    sums = {}
    for parity, g, row, shift in slots:
        part = parts[2 + parity][g * count_a : (g + 1) * count_a]
        part = pltpu.roll(part, shift, 1) if shift else part
        sums[row] = sums[row] + part if row in sums else part
    return sums, extra


def send_into(even_ref, matrix_ref, out_ref):
    count_b, count_a, count_z = even_ref.shape
    groups = count_b // GROUP
    total_rows = groups * count_a
    parts = packed(even_ref, matrix_ref)
    out_ref[pl.ds(0, total_rows), :] = parts[0]
    out_ref[pl.ds(total_rows, total_rows), :] = parts[1]
    for row, part in edge_sums(parts, count_a, groups, count_z)[0].items():
        out_ref[pl.ds(2 * total_rows + row, count_a), :] = part


def sent_shape(count_a, count_b, count_z):
    groups = count_b // GROUP
    _, extra = edge_slots(count_a, groups, count_z)
    return shape(2 * groups * count_a + extra, count_z)


KEPT = SIDE - WIDTH // 2
FREE = SIDE - KEPT
BATCH = KEPT // FREE + 1


def give_rows(groups):
    tiles = 2 * groups
    return SIDE * tiles, SIDE * (tiles // BATCH * (BATCH - 1))


def give_into(place, even_ref, matrix_ref, out_ref):
    count_b, count_a, count_z = even_ref.shape
    groups = count_b // GROUP
    assert count_a == 2 * SIDE and 2 * groups % BATCH == 0
    parts = packed(even_ref, matrix_ref)
    whole_rows, part_rows = give_rows(groups)
    line = lax.broadcasted_iota(jnp.int32, (SIDE, count_z), 0)

    def store(far_tile, shift):
        fars = []
        for index in range(2 * groups):
            start = index % groups * count_a
            both = [
                parts[index // groups][start + SIDE * tile : start + SIDE * (tile + 1)]
                for tile in range(2)
            ]
            out_ref[pl.ds(SIDE * index, SIDE), :] = both[1 - far_tile]
            fars.append(pltpu.roll(both[far_tile], shift, 0) if shift else both[far_tile])
        row = whole_rows
        for first in range(0, 2 * groups, BATCH):
            *hosts, guest = fars[first : first + BATCH]
            for i, host in enumerate(hosts):
                moved_guest = pltpu.roll(guest, KEPT - FREE * i, 0)
                out_ref[pl.ds(row, SIDE), :] = jnp.where(line < KEPT, host, moved_guest)
                row += SIDE

    pl.when(place.even)(lambda: store(0, KEPT))
    pl.when(jnp.logical_not(place.even))(lambda: store(1, 0))
    for row, part in edge_sums(parts, count_a, groups, count_z)[0].items():
        out_ref[pl.ds(whole_rows + part_rows + row, count_a), :] = part


def take_windows(place, other_ref, mains, groups, count_a):
    count_z = other_ref.shape[1]
    whole_rows, _ = give_rows(groups)
    line = lax.broadcasted_iota(jnp.int32, (SIDE, count_z), 0)

    def load(far_tile, shift):
        fars = []
        row = whole_rows
        for _ in range(0, 2 * groups, BATCH):
            hosts = [other_ref[pl.ds(row + SIDE * i, SIDE), :] for i in range(BATCH - 1)]
            row += SIDE * (BATCH - 1)
            guest = None
            for i, host in enumerate(hosts):
                piece = pltpu.roll(host, (FREE * (i + 1)) % SIDE, 0)
                guest = piece if guest is None else jnp.where(line < FREE * i, guest, piece)
            fars += [*hosts, guest]
        for index, far in enumerate(fars):
            start = index % groups * count_a
            far = pltpu.roll(far, shift, 0) if shift else far
            mains[index // groups, pl.ds(start + SIDE * far_tile, SIDE), :] = far
            mains[index // groups, pl.ds(start + SIDE * (1 - far_tile), SIDE), :] = other_ref[
                pl.ds(SIDE * index, SIDE), :
            ]

    pl.when(place.even)(lambda: load(0, FREE))
    pl.when(jnp.logical_not(place.even))(lambda: load(1, 0))


def given_shape(count_a, count_b, count_z):
    groups = count_b // GROUP
    return shape(sum(give_rows(groups)) + edge_slots(count_a, groups, count_z)[1], count_z)


def far_rows(count_b):
    return -(-2 * (count_b // GROUP) // 16) * 16


def last_far(flag, final, late, cx, far, matrix):
    count_x, count_y, count_z = final.shape
    count_b, count_a, _ = late.shape
    rows, pair = far_rows(count_b), WIDTH // 2

    def kernel(
        flag_ref, final_in, late_in, cx_ref, far_ref, matrix_ref, final_ref, late_ref, sent_ref, lhs,
    ):
        place = Place()
        wants_last = jnp.broadcast_to(flag_ref[0:1, :], (1, count_z)) > 0.5
        lhs[...] = jnp.zeros_like(lhs)

        def correct(first_x, first_c, first_a, terms):
            for r in range(WIDTH):
                final_ref[first_x + r] = final_ref[first_x + r] + cx_ref[first_c + r] * terms(
                    far_ref, r
                )
            for b in range(count_b):
                for i in range(pair):
                    value = jnp.where(
                        wants_last,
                        final_ref[first_x + 2 * i, pl.ds(2 * b, 1), :],
                        late_ref[b, pl.ds(first_a + i, 1), :],
                    )
                    late_ref[b, pl.ds(first_a + i, 1), :] = value
                    lanes = pl.ds(b % GROUP * count_z, count_z)
                    lhs[pl.ds(b // GROUP * pair + i, 1), lanes] = value

        @pl.when(place.even)
        def _():
            correct(0, 0, 0, low_terms)

        @pl.when(jnp.logical_not(place.even))
        def _():
            correct(count_x - WIDTH, WIDTH, count_a - pair, high_terms)

        result = exact_dot(lhs[...], matrix_ref[...])
        parts = [result[:, kind * count_z : (kind + 1) * count_z] for kind in range(4)]
        sent_ref[pl.ds(0, rows), :] = parts[0]
        sent_ref[pl.ds(rows, rows), :] = parts[1]
        sent_ref[pl.ds(2 * rows, rows), :] = parts[2] + pltpu.roll(parts[3], REACH, 1)

    return pl.pallas_call(
        kernel,
        out_shape=(shape(*final.shape), shape(*late.shape), shape(3 * rows, count_z)),
        in_specs=[spec(pltpu.VMEM)] * 6,
        out_specs=(spec(pltpu.VMEM),) * 3,
        scratch_shapes=[pltpu.VMEM((rows, GROUP * count_z), F32)],
        input_output_aliases={1: 0, 2: 1},
        compiler_params=params(12),
        cost_estimate=cost(WIDTH * count_y * count_z, 20, 3),
        name="last_far",
    )(flag, final, late, cx, far, matrix)


def write_out(level):
    def kernel(level_ref, out_ref, sem):
        copy = pltpu.make_async_copy(level_ref, out_ref, sem)
        copy.start()
        copy.wait()

    return pl.pallas_call(
        kernel,
        out_shape=shape(*level.shape),
        in_specs=[spec(pltpu.VMEM)],
        out_specs=spec(pltpu.HBM),
        scratch_shapes=[pltpu.SemaphoreType.DMA],
        compiler_params=params(4),
        cost_estimate=cost(level.size, 0, 2),
        name="write_out",
    )(level)


CODE_BITS = 5
PER_CODE = 6


def lag_image(count_a, lags, own, other, extra=None, before=None):
    _, total_rows, count_z = own.shape
    groups = total_rows // count_a
    half = count_z // GROUP
    last = before is not None
    count_h = before.shape[0] if last else lags.shape[0]
    codes = -(-count_h // PER_CODE)
    pair = WIDTH // 2

    def kernel(*refs):
        refs = list(refs)
        take = lambda count: [refs.pop(0) for _ in range(count)]
        lags_ref, own_ref, other_ref = take(3)
        if last:
            extra_ref, before_ref = take(2)
        (out_ref,) = take(1)
        if not last:
            (codes_ref,) = take(1)
        mains, edges = take(2)
        if last:
            store, sem = take(2)
        else:
            store = out_ref
            lag_of, sem = take(2)
        place = Place()
        if last:
            packed_lags = [lags_ref[k : k + 1, :][0, 0] for k in range(codes)]
            mask = (1 << CODE_BITS) - 1
            lag_list = [
                ((packed_lags[h // PER_CODE] >> (h % PER_CODE * CODE_BITS)) & mask) - LAGMAX
                for h in range(count_h)
            ]
        else:
            copy = pltpu.make_async_copy(lags_ref, lag_of, sem)
            copy.start()
        is_source = place.field == 0

        def useful(rows):
            lane = lax.broadcasted_iota(jnp.int32, (rows, count_z), 1) % half
            return jnp.where(is_source, lane, half - 1 - lane) < REACH

        slots, _ = edge_slots(count_a, groups, count_z)
        if last:
            take_windows(place, other_ref, mains, groups, count_a)
            edge_row = sum(give_rows(groups))
        else:
            for parity in range(2):
                mains[parity] = other_ref[pl.ds(parity * total_rows, total_rows), :]
            edge_row = 2 * total_rows
        for parity, g, row, shift in slots:
            part = other_ref[pl.ds(edge_row + row, count_a), :]
            part = pltpu.roll(part, count_z - shift, 1) if shift else part
            edges[parity, pl.ds(g * count_a, count_a), :] = jnp.where(useful(count_a), part, 0.0)
        if last:
            rows = extra_ref.shape[0] // 3
            border = extra_ref[pl.ds(2 * rows, rows), :]
            borders = [
                jnp.where(useful(rows), part, 0.0)
                for part in (border, pltpu.roll(border, count_z - REACH, 1))
            ]

            def overwrite(first_a):
                for g in range(groups):
                    target = pl.ds(g * count_a + first_a, pair)
                    for parity in range(2):
                        mains[parity, target, :] = extra_ref[
                            pl.ds(parity * rows + g * pair, pair), :
                        ]
                        edges[parity, target, :] = borders[parity][g * pair : (g + 1) * pair]

            pl.when(place.even)(lambda: overwrite(0))
            pl.when(jnp.logical_not(place.even))(lambda: overwrite(count_a - pair))
        else:
            copy.wait()
            lag_list = [lag_of[h] for h in range(count_h)]
            for k in range(codes):
                code = jnp.int32(0)
                for h in range(k * PER_CODE, min((k + 1) * PER_CODE, count_h)):
                    code = code | ((lag_list[h] + LAGMAX) << (h % PER_CODE * CODE_BITS))
                codes_ref[k : k + 1, :] = jnp.full((1, count_z), code, jnp.int32)
        for h, lag in enumerate(lag_list):
            parity, own_shift, other_shift = lag_shifts(lag, is_source)
            product = moved(mains[parity], edges[parity], other_shift)
            if last:
                product = product * own_ref[h]
            else:
                product = product * moved(own_ref[parity], own_ref[2 + parity], own_shift)
            for g in range(groups):
                part = product[g * count_a : (g + 1) * count_a]
                lanes = pl.ds(g * count_z, count_z)
                if last:
                    part = part + before_ref[h, :, lanes]
                store[h, :, lanes] = part
            if last:
                pltpu.make_async_copy(store.at[h], out_ref.at[h], sem).start()
        if last:
            pltpu.make_async_copy(store, out_ref, sem).wait()

    image = shape(count_h, count_a, groups * count_z)
    operands = [lags, own, other] + ([extra, before] if last else [])
    scratch = [pltpu.VMEM((2, total_rows, count_z), F32)] * 2
    scratch.append(pltpu.VMEM(image.shape, F32) if last else pltpu.SMEM((count_h,), jnp.int32))
    scratch.append(pltpu.SemaphoreType.DMA)
    return pl.pallas_call(
        kernel,
        out_shape=image if last else (image, shape(8, count_z, dtype=jnp.int32)),
        in_specs=[spec(pltpu.VMEM if last else pltpu.HBM)]
        + [spec(pltpu.VMEM)] * (len(operands) - 1),
        out_specs=spec(pltpu.HBM) if last else (spec(pltpu.VMEM),) * 2,
        scratch_shapes=scratch,
        compiler_params=params(12),
        cost_estimate=cost(count_h * total_rows * count_z, 10, 2),
        name="last_image" if last else "early_image",
    )(*operands)


def body(
    field_now,
    field_prev,
    courant_squared,
    source_cells,
    source_wave,
    receiver_cells,
    receiver_wave,
    snapshot_steps,
    lag_offsets,
):
    count_x, _, count_z = field_now.shape
    loop_size = lax.axis_size("gx")
    half_size = loop_size // 2
    turn = loop_size // 4
    assert lax.axis_size("gy") == 2 and half_size % 2 == 0

    slabs = [(i - turn) % loop_size % half_size for i in range(loop_size)]

    def pairs(odd):
        found = []
        for i, slab in enumerate(slabs):
            if slab % 2 == odd and slab != half_size - 1:
                j = (i + 1) % loop_size
                found += [(i, j), (j, i)]
        return found

    near_pairs, far_pairs = pairs(0), pairs(1)
    across = [(i, (i + half_size) % loop_size) for i in range(loop_size)]

    def send_far(far):
        return lax.ppermute(far, "gx", far_pairs)

    def send_near(near, side):
        near = lax.ppermute(near, "gx", near_pairs)
        return near, lax.ppermute(side, "gy", [(0, 1), (1, 0)])

    def exchange(faces):
        far, near, side = faces
        return (send_far(far), *send_near(near, side))

    matrices = jnp.asarray(
        np.stack([pack_matrix(window, count_z) for window in (0, 1)]), dtype=BF16
    )
    raw = (source_cells, source_wave, receiver_cells, receiver_wave)
    field_kept, field_prev, courant_squared, matrices, snapshot_steps, lag_offsets, *raw = (
        pltpu.with_memory_space_constraint(array, pltpu.HBM)
        for array in (
            field_now, field_prev, courant_squared, matrices, snapshot_steps, lag_offsets, *raw
        )
    )
    halos = exchange(first_faces(field_kept))
    whole0, next1, qx, qy, courant, cx, cy, points, waves = inner_step(
        0, raw, None, field_now, None, field_prev, courant_squared
    )
    faces = halo_step((qx, qy, cx, cy), halos)
    halos = exchange(faces)
    whole1, next2, qx, qy, added = inner_step(1, points, waves, next1, faces, whole0, courant)
    faces = halo_step((qx, qy, cx, cy), halos)
    halos = exchange(faces)
    whole2, next3, qx, qy, own_early, sent_early, own_matrix, sent_matrix, flag = inner_step(
        2, points, waves, next2, faces, whole1, courant, snapshot_steps, matrices
    )
    other_early = lax.ppermute(sent_early, "gx", across)
    faces = halo_step((qx, qy, cx, cy), halos)
    far, *halos = exchange(faces)
    _, final, late, sent_late = inner_step(
        3, added, None, next3, faces, whole2, courant, snapshot_steps, sent_matrix, halos
    )
    other_late = lax.ppermute(sent_late, "gx", across)
    partial, codes = lag_image(count_x // 2, lag_offsets, own_early, other_early)
    final, late, sent_far = last_far(flag, final, late, cx, far, sent_matrix)
    extra = lax.ppermute(sent_far, "gx", across)
    own_late = pack_own(lag_offsets, late, own_matrix)
    image = lag_image(count_x // 2, codes, own_late, other_late, extra, partial)
    return write_out(final), jnp.transpose(image, (1, 0, 2))


def solution(mesh):
    placed = (
        P(("shots", "gx"), "gy", None),
        P(("shots", "gx"), "gy", None),
        P("gx", "gy", None),
        P(None, "shots"),
        P(None, "shots"),
        P(None, "shots"),
        P(None, "shots"),
        P("shots", None),
        P(),
    )
    return jax.shard_map(
        body,
        mesh=mesh,
        in_specs=placed,
        out_specs=(P(("shots", "gx"), "gy", None), P(("shots", "gx"), None, "gy")),
        check_vma=False,
    )
```

```python
import jax
import jax.numpy as jnp
import numpy as np
from jax import lax
from jax.experimental import pallas as pl
from jax.experimental.pallas import tpu as pltpu
from jax.sharding import PartitionSpec as P

STEPS = 4
WIDTH = 4
LAGMAX = 8
REACH = LAGMAX // 2
GROUP = 4
SIDE = 8

SCALE = 5040.0
BAND = (8064.0, -1008.0, 128.0, -9.0)
CENTRE = 3.0 * (-205.0 / 72.0)
WEIGHTS = (1.6, -0.2, 8.0 / 315.0, -1.0 / 560.0)

F32 = jnp.float32
BF16 = jnp.bfloat16


def shape(*dims, dtype=F32):
    return jax.ShapeDtypeStruct(dims, dtype)


def params(megabytes):
    return pltpu.CompilerParams(vmem_limit_bytes=megabytes << 20)


def spec(space):
    return pl.BlockSpec(memory_space=space)


def cost(count, flops_each, arrays):
    return pl.CostEstimate(
        flops=int(count * flops_each), bytes_accessed=int(4 * count * arrays), transcendentals=0
    )


def split3(values):
    high = values.astype(BF16)
    rest = values - high.astype(F32)
    middle = rest.astype(BF16)
    low = (rest - middle.astype(F32)).astype(BF16)
    return high, middle, low


def exact_dot(values, matrix):
    rows = values.shape[0]
    stacked = jnp.concatenate(split3(values), axis=0)
    result = jnp.dot(stacked, matrix, preferred_element_type=F32)
    return (result[2 * rows :] + result[rows : 2 * rows]) + result[:rows]


class Place:
    def __init__(self):
        loop_size = lax.axis_size("gx")
        self.half = loop_size // 2
        relative = lax.rem(lax.axis_index("gx") + loop_size - loop_size // 4, loop_size)
        self.field = relative // self.half
        self.slab = lax.rem(relative, self.half)
        self.even = lax.rem(self.slab, 2) == 0
        self.y = lax.axis_index("gy")

    def block(self, count_y):
        return pl.multiple_of((1 - self.y) * (count_y - SIDE), SIDE)


def first_faces(field):
    count_x, count_y, count_z = field.shape
    top = count_x - WIDTH

    def kernel(field_ref, far_ref, near_ref, side_ref, sems):
        place = Place()
        far = jnp.where(place.even, 0, top)
        sources = [
            field_ref.at[pl.ds(far, WIDTH)],
            field_ref.at[pl.ds(top - far, WIDTH)],
            field_ref.at[:, pl.ds(place.block(count_y), SIDE)],
        ]
        copies = [
            pltpu.make_async_copy(source, target, sems.at[index])
            for index, (source, target) in enumerate(zip(sources, (far_ref, near_ref, side_ref)))
        ]
        for copy in copies:
            copy.start()
        for copy in copies:
            copy.wait()

    return pl.pallas_call(
        kernel,
        out_shape=face_shapes(count_x, count_y, count_z),
        in_specs=[spec(pltpu.HBM)],
        out_specs=(spec(pltpu.VMEM),) * 3,
        scratch_shapes=[pltpu.SemaphoreType.DMA((3,))],
        compiler_params=params(8),
        name="first_faces",
    )(field)


def face_shapes(count_x, count_y, count_z):
    slab = shape(WIDTH, count_y, count_z)
    return slab, slab, shape(count_x, SIDE, count_z)


def even_rows(level_ref, offset_x, offset_y, count_a, b):
    rows, stride, lanes = level_ref.shape
    flat = level_ref.reshape(rows * stride, lanes)
    start = offset_x * stride + offset_y + 2 * b
    return flat[pl.ds(start, count_a, stride=2 * stride), :]


def inner_step(number, points, waves, current, faces, previous, courant, snapshots=None, matrices=None):
    count_x, count_y, count_z = courant.shape
    count_a, count_b = count_x // 2, count_y // 2
    first = faces is None
    last = number == STEPS - 1
    snapshot = number == STEPS // 2
    ahead = number == 1
    if last:
        count_j = 0
    elif first:
        count_j = -(-max(array.shape[1] for array in points) // 128) * 128
    else:
        count_j = points.shape[1]

    def kernel(*refs):
        refs = list(refs)
        take = lambda count: [refs.pop(0) for _ in range(count)]
        if first:
            raw_refs = take(4)
        elif last:
            (added_ref,) = take(1)
        else:
            points_ref, waves_ref = take(2)
        (current_ref,) = take(1)
        if not first:
            far_ref, near_ref, side_ref = take(3)
        previous_ref, courant_ref = take(2)
        if snapshot:
            steps_ref, matrices_ref = take(2)
        padded, next_ref, qx_ref, qy_ref = take(4)
        if first:
            kept_ref, cx_ref, cy_ref, points_ref, waves_ref = take(5)
        if snapshot:
            own_out, sent_out, own_matrix, sent_matrix, flag_ref = take(5)
        if ahead:
            (ahead_ref,) = take(1)
        if last:
            (even_ref,) = take(1)
        zpart, addpart = take(2)
        if last:
            addpart = added_ref
        if first:
            before_ref = take(1)[0]
            raw_refs_in, raw_refs = raw_refs, take(4)
            (sems,) = take(1)
        if snapshot:
            even_ref, wanted, sems = take(3)

        place = Place()
        block = place.block(count_y)
        rows, columns = pl.ds(WIDTH, count_x), pl.ds(SIDE, count_y)
        if first:
            copies = [
                pltpu.make_async_copy(source, target, sems.at[index])
                for index, (source, target) in enumerate(
                    zip(
                        (*raw_refs_in, previous_ref, courant_ref),
                        (*raw_refs, before_ref, kept_ref),
                    )
                )
            ]
            for copy in copies:
                copy.start()
        else:
            before_ref, kept_ref = previous_ref, courant_ref
        if snapshot:
            copies = [
                pltpu.make_async_copy(steps_ref, wanted, sems.at[0]),
                pltpu.make_async_copy(matrices_ref.at[place.field], own_matrix, sems.at[1]),
                pltpu.make_async_copy(matrices_ref.at[1 - place.field], sent_matrix, sems.at[2]),
            ]
            for copy in copies:
                copy.start()

        def clear_border(level_ref):
            zero_x = jnp.zeros((WIDTH, count_y + 2 * SIDE, count_z), F32)
            level_ref[pl.ds(0, WIDTH)] = zero_x
            level_ref[pl.ds(count_x + WIDTH, WIDTH)] = zero_x
            zero_y = jnp.zeros((count_x, SIDE, count_z), F32)
            level_ref[rows, pl.ds(0, SIDE)] = zero_y
            level_ref[rows, pl.ds(count_y + SIDE, SIDE)] = zero_y

        if first:
            clear_border(padded)
            padded[rows, columns] = current_ref[...]
        if not last:
            clear_border(next_ref)
        next_x, next_y = (0, 0) if last else (WIDTH, SIDE)
        before_x, before_y = (0, 0) if first else (WIDTH, SIDE)
        if not first:
            low, high = pl.ds(WIDTH, WIDTH), pl.ds(count_x, WIDTH)

            @pl.when(place.even)
            def _():
                padded[high, columns] = near_ref[...]
                padded[low, columns] = far_ref[...]

            @pl.when(jnp.logical_not(place.even))
            def _():
                padded[low, columns] = near_ref[...]
                padded[high, columns] = far_ref[...]

            padded[rows, pl.ds(pl.multiple_of(block + SIDE, SIDE), SIDE)] = side_ref[...]

        gap = jnp.abs(
            lax.broadcasted_iota(jnp.int32, (count_z, count_z), 0)
            - lax.broadcasted_iota(jnp.int32, (count_z, count_z), 1)
        )
        band = jnp.zeros((count_z, count_z), F32)
        for offset, weight in enumerate(BAND, 1):
            band = jnp.where(gap == offset, weight, band)
        band = jnp.concatenate([band.astype(BF16)] * 3, axis=0)

        chunk = 8

        def multiply(index, _):
            start = pl.multiple_of(index * chunk, chunk)
            values = padded[pl.ds(start + WIDTH, chunk), columns]
            terms = jnp.concatenate(split3(values.reshape(chunk * count_y, count_z)), axis=1)
            zpart[pl.ds(start, chunk)] = jnp.dot(
                terms, band, preferred_element_type=F32
            ).reshape(chunk, count_y, count_z)
            return 0

        chunks = count_x // chunk
        if first or last:
            lax.fori_loop(0, chunks, multiply, 0)

        if first:
            for copy in copies[:4]:
                copy.wait()
            points_ref[...] = jnp.full(points_ref.shape, -1, jnp.int32)
            waves_ref[...] = jnp.zeros(waves_ref.shape, F32)

            def choose(cells_ref, wave_ref):
                count = cells_ref.shape[1]
                points_ref[pl.ds(0, 3), pl.ds(0, count)] = cells_ref[...]
                waves_ref[pl.ds(0, STEPS), pl.ds(0, count)] = wave_ref[...]

            @pl.when(place.field == 0)
            def _():
                choose(raw_refs[0], raw_refs[1])

            @pl.when(place.field != 0)
            def _():
                choose(raw_refs[2], raw_refs[3])

        if not last:
            px = points_ref[0:1, :] - place.slab * count_x
            py = points_ref[1:2, :] - place.y * count_y
            inside = (px >= 0) & (px < count_x) & (py >= 0) & (py < count_y)
            home = jnp.where(inside, px * count_y + py, -1)
            at_z = (
                lax.broadcasted_iota(jnp.int32, (count_z, count_j), 0) == points_ref[2:3, :]
            )

            def spread_of(step):
                terms = split3(jnp.where(at_z, waves_ref[step : step + 1, :], 0.0))
                return jnp.concatenate(terms, axis=1)

            spreads = [(addpart, spread_of(number))]
            if ahead:
                spreads.append((ahead_ref, spread_of(STEPS - 1)))

        def inject(index, _):
            start = pl.multiple_of(index * chunk, chunk)
            here = start * count_y + lax.broadcasted_iota(
                jnp.int32, (chunk * count_y, count_j), 0
            )
            hit = jnp.where(here == home, 1.0, 0.0).astype(BF16)
            hit = jnp.concatenate([hit] * 3, axis=1)
            for target, spread in spreads:
                added = lax.dot_general(
                    hit, spread, (((1,), (1,)), ((), ())), preferred_element_type=F32
                )
                target[pl.ds(start, chunk)] = added.reshape(chunk, count_y, count_z)
            return 0

        def both(index, _):
            multiply(index, 0)
            return inject(index, 0)

        if not last:
            lax.fori_loop(0, chunks, inject if first else both, 0)
        if first:
            for copy in copies[4:]:
                copy.wait()

        depth = 4

        def row_group(index, _):
            x = index * depth
            for y in range(0, count_y, SIDE):
                here, inner = pl.ds(y + SIDE, SIDE), pl.ds(y, SIDE)
                lines = [padded[x + i, here] for i in range(depth + 2 * WIDTH)]
                for j in range(depth):
                    middle = lines[WIDTH + j]
                    total = CENTRE * middle + (1.0 / SCALE) * zpart[x + j, inner]
                    for offset, weight in enumerate(WEIGHTS, 1):
                        paired = lines[WIDTH + j + offset] + lines[WIDTH + j - offset]
                        paired = paired + (
                            padded[x + WIDTH + j, pl.ds(y + SIDE + offset, SIDE)]
                            + padded[x + WIDTH + j, pl.ds(y + SIDE - offset, SIDE)]
                        )
                        total = total + weight * paired
                    old = before_ref[x + j + before_x, pl.ds(y + before_y, SIDE)]
                    value = 2.0 * middle - old + kept_ref[x + j, inner] * total
                    next_ref[x + j + next_x, pl.ds(y + next_y, SIDE)] = (
                        value + addpart[x + j, inner]
                    )
            return 0

        lax.fori_loop(0, count_x // depth, row_group, 0)

        next_columns = pl.ds(next_y, count_y)
        qx_ref[pl.ds(0, WIDTH)] = next_ref[pl.ds(next_x, WIDTH), next_columns]
        qx_ref[pl.ds(WIDTH, WIDTH)] = next_ref[
            pl.ds(next_x + count_x - WIDTH, WIDTH), next_columns
        ]
        qy_ref[...] = next_ref[
            pl.ds(next_x, count_x), pl.ds(pl.multiple_of(block + next_y, SIDE), SIDE)
        ]
        if first:
            cx_ref[pl.ds(0, WIDTH)] = kept_ref[pl.ds(0, WIDTH)]
            cx_ref[pl.ds(WIDTH, WIDTH)] = kept_ref[pl.ds(count_x - WIDTH, WIDTH)]
            cy_ref[...] = kept_ref[:, pl.ds(block, SIDE)]
        if last:
            for b in range(count_b):
                even_ref[b] = even_rows(padded, WIDTH, SIDE, count_a, b)
        if snapshot:
            for copy in copies:
                copy.wait()
            flag_ref[...] = jnp.where(
                wanted[place.field, 1] == STEPS, jnp.ones(flag_ref.shape, F32), 0.0
            )
            earlier = wanted[place.field, 0] == number - 1

            @pl.when(earlier)
            def _():
                for b in range(count_b):
                    even_ref[b] = even_rows(previous_ref, WIDTH, SIDE, count_a, b)

            @pl.when(jnp.logical_not(earlier))
            def _():
                for b in range(count_b):
                    even_ref[b] = even_rows(padded, WIDTH, SIDE, count_a, b)

            for kind, part in enumerate(packed(even_ref, own_matrix)):
                own_out[kind] = part
            send_into(even_ref, sent_matrix, sent_out)

    full = shape(count_x, count_y, count_z)
    slab, side = shape(2 * WIDTH, count_y, count_z), shape(count_x, SIDE, count_z)
    even = shape(count_b, count_a, count_z)
    bordered = shape(count_x + 2 * WIDTH, count_y + 2 * SIDE, count_z)
    outs = [bordered, full if last else bordered, slab, side]
    if first:
        outs += [full, slab, side, shape(8, count_j, dtype=jnp.int32), shape(8, count_j)]
    if snapshot:
        size = GROUP * count_z
        outs += [
            shape(4, count_b // GROUP * count_a, count_z),
            sent_shape(count_a, count_b, count_z),
            shape(size, size, dtype=BF16),
            shape(size, size, dtype=BF16),
            shape(8, count_z),
        ]
    if ahead:
        outs.append(full)
    if last:
        outs.append(even)
    place_of = spec(pltpu.HBM) if first else spec(pltpu.VMEM)
    if first:
        operands = [*points, current]
    elif last:
        operands = [points, current]
    else:
        operands = [points, waves, current]
    aliases = {} if first else {len(operands) - 1: 0}
    specs = [place_of] * (len(operands) - 1) + [spec(pltpu.VMEM)]
    if not first:
        operands += list(faces)
        specs += [spec(pltpu.VMEM)] * 3
    operands += [previous, courant]
    specs += [place_of] * 2
    scratch = [pltpu.VMEM(full.shape, F32)] * 2
    if first:
        scratch.append(pltpu.VMEM(full.shape, F32))
        scratch += [pltpu.VMEM(array.shape, array.dtype) for array in points]
        scratch.append(pltpu.SemaphoreType.DMA((6,)))
    if snapshot:
        operands += [snapshots, matrices]
        specs += [spec(pltpu.HBM)] * 2
        scratch += [
            pltpu.VMEM(even.shape, F32),
            pltpu.SMEM(snapshots.shape, jnp.int32),
            pltpu.SemaphoreType.DMA((3,)),
        ]
    return pl.pallas_call(
        kernel,
        out_shape=tuple(outs),
        in_specs=specs,
        out_specs=(spec(pltpu.VMEM),) * len(outs),
        scratch_shapes=scratch,
        input_output_aliases=aliases,
        compiler_params=params(20),
        cost_estimate=cost(count_x * count_y * count_z, 60, 6),
    )(*operands)


def low_terms(halo_ref, r):
    total = None
    for k in range(r + 1, WIDTH + 1):
        term = WEIGHTS[k - 1] * halo_ref[WIDTH + r - k]
        total = term if total is None else total + term
    return total


def high_terms(halo_ref, r):
    total = None
    for k in range(WIDTH - r, WIDTH + 1):
        term = WEIGHTS[k - 1] * halo_ref[r + k - WIDTH]
        total = term if total is None else total + term
    return total


def add_halo(place, parts, halos, outs):
    qx_ref, qy_ref, cx_ref, cy_ref = parts
    far_in, near_in, side_in = halos
    far_out, near_out, side_out = outs
    count_y, count_x = qx_ref.shape[1], qy_ref.shape[0]
    block = place.block(count_y)

    def along_x(low_in, high_in, low_out, high_out):
        for r in range(WIDTH):
            low, high = qx_ref[r], qx_ref[WIDTH + r]
            if low_in is not None:
                low = low + cx_ref[r] * low_terms(low_in, r)
            if high_in is not None:
                high = high + cx_ref[WIDTH + r] * high_terms(high_in, r)
            low_out[r], high_out[r] = low, high
        side_out[pl.ds(0, WIDTH)] = low_out[:, pl.ds(block, SIDE)]
        side_out[pl.ds(count_x - WIDTH, WIDTH)] = high_out[:, pl.ds(block, SIDE)]

    inner = pl.ds(WIDTH, count_x - 2 * WIDTH)
    side_out[inner] = qy_ref[inner]

    @pl.when(place.even)
    def _():
        along_x(far_in, near_in, far_out, near_out)

    @pl.when(jnp.logical_not(place.even))
    def _():
        along_x(near_in, far_in, near_out, far_out)

    def along_y(shifts, masks):
        halo = side_in[...]
        depth, lanes = halo.shape[0], halo.shape[2]
        line = lax.broadcasted_iota(jnp.int32, (1, SIDE, lanes), 1)
        total = None
        for k in range(1, WIDTH + 1):
            weight = jnp.where(masks(line, k), WEIGHTS[k - 1], 0.0)
            term = weight * pltpu.roll(halo, shifts(k), 1)
            total = term if total is None else total + term
        side_out[...] = side_out[...] + cy_ref[...] * total

    @pl.when(place.y == 0)
    def _():
        along_y(lambda k: SIDE - k, lambda line, k: line >= SIDE - k)

    @pl.when(place.y != 0)
    def _():
        along_y(lambda k: k, lambda line, k: line < k)

    def corners(low_out, high_out):
        low_out[:, pl.ds(block, SIDE)] = side_out[pl.ds(0, WIDTH)]
        high_out[:, pl.ds(block, SIDE)] = side_out[pl.ds(count_x - WIDTH, WIDTH)]

    @pl.when(place.even)
    def _():
        corners(far_out, near_out)

    @pl.when(jnp.logical_not(place.even))
    def _():
        corners(near_out, far_out)


def halo_step(parts, halos):
    count_y, (count_x, _, count_z) = parts[0].shape[1], parts[1].shape

    def kernel(*refs):
        add_halo(Place(), refs[:4], refs[4:7], refs[7:])

    return pl.pallas_call(
        kernel,
        out_shape=face_shapes(count_x, count_y, count_z),
        in_specs=[spec(pltpu.VMEM)] * 7,
        out_specs=(spec(pltpu.VMEM),) * 3,
        compiler_params=params(8),
        cost_estimate=cost(16 * count_y * count_z, 10, 6),
        name="halo_step",
    )(*parts, *halos)


def pack_matrix(window, count_z):
    half = count_z // GROUP
    size = GROUP * count_z
    row, column = np.arange(size)[:, None], np.arange(size)[None, :]
    row_b, row_z = row // count_z, row % count_z
    kind = column // count_z
    parity = kind % 2
    lane_b, lane_i = (column % count_z) // half, column % half
    main = (row_b == lane_b) & (row_z == 2 * (half * window + lane_i) + parity)
    wanted_b = (lane_b + (GROUP - 1 if window == 0 else 1)) % GROUP
    wanted_z = 2 * (half * (1 - window) + lane_i) + parity
    useful = lane_i < REACH if window == 0 else lane_i >= half - REACH
    edge = (row_b == wanted_b) & (row_z == wanted_z) & useful
    return np.where(kind < 2, main, edge).astype(np.float32)


def packed(even_ref, matrix_ref):
    count_b, _, count_z = even_ref.shape
    rows = [
        jnp.concatenate([even_ref[b + i] for i in range(GROUP)], axis=1)
        for b in range(0, count_b, GROUP)
    ]
    result = exact_dot(jnp.concatenate(rows, axis=0), matrix_ref[...])
    return [result[:, kind * count_z : (kind + 1) * count_z] for kind in range(4)]


def lag_shifts(lag, is_source):
    parity = lag & 1
    source_shift = -((lag + parity) >> 1)
    receiver_shift = (lag - parity) >> 1
    return (
        parity,
        jnp.where(is_source, source_shift, receiver_shift),
        jnp.where(is_source, receiver_shift, source_shift),
    )


def moved(main, edge, shift):
    count_z = main.shape[1]
    half = count_z // GROUP
    lane = lax.broadcasted_iota(jnp.int32, (1, count_z), 1) % half
    mask = (lane < shift) | (lane >= half + shift)
    return pltpu.roll(jnp.where(mask, edge, main), (count_z - shift) & (count_z - 1), 1)


def pack_own(lags, even, matrix):
    count_b, count_a, count_z = even.shape
    total_rows = count_b // GROUP * count_a
    (count_h,) = lags.shape

    def kernel(lags_ref, even_ref, matrix_ref, out_ref, windows, lag_of, sem):
        copy = pltpu.make_async_copy(lags_ref, lag_of, sem)
        copy.start()
        place = Place()
        for kind, part in enumerate(packed(even_ref, matrix_ref)):
            windows[kind] = part
        copy.wait()
        for h in range(count_h):
            parity, shift, _ = lag_shifts(lag_of[h], place.field == 0)
            out_ref[h] = moved(windows[parity], windows[2 + parity], shift)

    return pl.pallas_call(
        kernel,
        out_shape=shape(count_h, total_rows, count_z),
        in_specs=[spec(pltpu.HBM)] + [spec(pltpu.VMEM)] * 2,
        out_specs=spec(pltpu.VMEM),
        scratch_shapes=[
            pltpu.VMEM((4, total_rows, count_z), F32),
            pltpu.SMEM((count_h,), jnp.int32),
            pltpu.SemaphoreType.DMA,
        ],
        compiler_params=params(8),
        cost_estimate=cost(count_b * count_a * count_z, 1024, 4),
        name="pack_own",
    )(lags, even, matrix)


def edge_slots(count_a, groups, count_z):
    fits = count_z // GROUP // REACH
    slots = []
    for index in range(2 * groups):
        slots.append((index // groups, index % groups, index // fits * count_a, index % fits * REACH))
    return slots, -(-2 * groups // fits) * count_a


def edge_sums(parts, count_a, groups, count_z):
    slots, extra = edge_slots(count_a, groups, count_z)
    sums = {}
    for parity, g, row, shift in slots:
        part = parts[2 + parity][g * count_a : (g + 1) * count_a]
        part = pltpu.roll(part, shift, 1) if shift else part
        sums[row] = sums[row] + part if row in sums else part
    return sums, extra


def send_into(even_ref, matrix_ref, out_ref):
    count_b, count_a, count_z = even_ref.shape
    groups = count_b // GROUP
    total_rows = groups * count_a
    parts = packed(even_ref, matrix_ref)
    out_ref[pl.ds(0, total_rows), :] = parts[0]
    out_ref[pl.ds(total_rows, total_rows), :] = parts[1]
    for row, part in edge_sums(parts, count_a, groups, count_z)[0].items():
        out_ref[pl.ds(2 * total_rows + row, count_a), :] = part


def sent_shape(count_a, count_b, count_z):
    groups = count_b // GROUP
    _, extra = edge_slots(count_a, groups, count_z)
    return shape(2 * groups * count_a + extra, count_z)


KEPT = SIDE - WIDTH // 2
FREE = SIDE - KEPT
BATCH = KEPT // FREE + 1


def give_rows(groups):
    tiles = 2 * groups
    return SIDE * tiles, SIDE * (tiles // BATCH * (BATCH - 1))


def give_into(place, even_ref, matrix_ref, out_ref):
    count_b, count_a, count_z = even_ref.shape
    groups = count_b // GROUP
    assert count_a == 2 * SIDE and 2 * groups % BATCH == 0
    parts = packed(even_ref, matrix_ref)
    whole_rows, part_rows = give_rows(groups)
    line = lax.broadcasted_iota(jnp.int32, (SIDE, count_z), 0)

    def store(far_tile, shift):
        fars = []
        for index in range(2 * groups):
            start = index % groups * count_a
            both = [
                parts[index // groups][start + SIDE * tile : start + SIDE * (tile + 1)]
                for tile in range(2)
            ]
            out_ref[pl.ds(SIDE * index, SIDE), :] = both[1 - far_tile]
            fars.append(pltpu.roll(both[far_tile], shift, 0) if shift else both[far_tile])
        row = whole_rows
        for first in range(0, 2 * groups, BATCH):
            *hosts, guest = fars[first : first + BATCH]
            for i, host in enumerate(hosts):
                moved_guest = pltpu.roll(guest, KEPT - FREE * i, 0)
                out_ref[pl.ds(row, SIDE), :] = jnp.where(line < KEPT, host, moved_guest)
                row += SIDE

    pl.when(place.even)(lambda: store(0, KEPT))
    pl.when(jnp.logical_not(place.even))(lambda: store(1, 0))
    for row, part in edge_sums(parts, count_a, groups, count_z)[0].items():
        out_ref[pl.ds(whole_rows + part_rows + row, count_a), :] = part


def take_windows(place, other_ref, mains, groups, count_a):
    count_z = other_ref.shape[1]
    whole_rows, _ = give_rows(groups)
    line = lax.broadcasted_iota(jnp.int32, (SIDE, count_z), 0)

    def load(far_tile, shift):
        fars = []
        row = whole_rows
        for _ in range(0, 2 * groups, BATCH):
            hosts = [other_ref[pl.ds(row + SIDE * i, SIDE), :] for i in range(BATCH - 1)]
            row += SIDE * (BATCH - 1)
            guest = None
            for i, host in enumerate(hosts):
                piece = pltpu.roll(host, (FREE * (i + 1)) % SIDE, 0)
                guest = piece if guest is None else jnp.where(line < FREE * i, guest, piece)
            fars += [*hosts, guest]
        for index, far in enumerate(fars):
            start = index % groups * count_a
            far = pltpu.roll(far, shift, 0) if shift else far
            mains[index // groups, pl.ds(start + SIDE * far_tile, SIDE), :] = far
            mains[index // groups, pl.ds(start + SIDE * (1 - far_tile), SIDE), :] = other_ref[
                pl.ds(SIDE * index, SIDE), :
            ]

    pl.when(place.even)(lambda: load(0, FREE))
    pl.when(jnp.logical_not(place.even))(lambda: load(1, 0))


def given_shape(count_a, count_b, count_z):
    groups = count_b // GROUP
    return shape(sum(give_rows(groups)) + edge_slots(count_a, groups, count_z)[1], count_z)


def last_step(flag, even_before, current, parts, near, side, matrix):
    count_x, count_y, count_z = current.shape
    count_a, count_b = count_x // 2, count_y // 2

    def kernel(
        flag_ref, even_ref, current_ref, qx_ref, qy_ref, cx_ref, cy_ref, near_ref, side_ref,
        matrix_ref, final_ref, late_ref, sent_ref, far_out, near_out, side_out,
    ):
        place = Place()
        add_halo(
            place, (qx_ref, qy_ref, cx_ref, cy_ref), (None, near_ref, side_ref),
            (far_out, near_out, side_out),
        )
        low, high = pl.ds(0, WIDTH), pl.ds(count_x - WIDTH, WIDTH)

        @pl.when(place.even)
        def _():
            final_ref[high] = near_out[...]
            final_ref[low] = far_out[...]

        @pl.when(jnp.logical_not(place.even))
        def _():
            final_ref[low] = near_out[...]
            final_ref[high] = far_out[...]

        final_ref[:, pl.ds(place.block(count_y), SIDE)] = side_out[...]
        wants_last = jnp.broadcast_to(flag_ref[0:1, :], (count_a, count_z)) > 0.5
        for b in range(count_b):
            late_ref[b] = jnp.where(
                wants_last, even_rows(final_ref, 0, 0, count_a, b), even_ref[b]
            )
        give_into(place, late_ref, matrix_ref, sent_ref)

    slab, _, side_shape = face_shapes(count_x, count_y, count_z)
    return pl.pallas_call(
        kernel,
        out_shape=(
            shape(*current.shape),
            shape(count_b, count_a, count_z),
            given_shape(count_a, count_b, count_z),
        ),
        in_specs=[spec(pltpu.VMEM)] * 10,
        out_specs=(spec(pltpu.VMEM),) * 3,
        scratch_shapes=[
            pltpu.VMEM(slab.shape, F32),
            pltpu.VMEM(slab.shape, F32),
            pltpu.VMEM(side_shape.shape, F32),
        ],
        input_output_aliases={2: 0},
        compiler_params=params(12),
        cost_estimate=cost(count_x * count_y * count_z, 10, 3),
        name="last_step",
    )(flag, even_before, current, *parts, near, side, matrix)


def far_rows(count_b):
    return -(-2 * (count_b // GROUP) // 16) * 16


def last_far(flag, final, late, cx, far, matrix):
    count_x, count_y, count_z = final.shape
    count_b, count_a, _ = late.shape
    groups, rows, pair = count_b // GROUP, far_rows(count_b), WIDTH // 2

    def kernel(
        flag_ref, final_in, late_in, cx_ref, far_ref, matrix_ref, final_ref, late_ref, sent_ref, lhs,
    ):
        place = Place()
        wants_last = jnp.broadcast_to(flag_ref[0:1, :], (1, count_z)) > 0.5
        lhs[...] = jnp.zeros_like(lhs)

        def correct(first_x, first_c, first_a, terms):
            for r in range(WIDTH):
                final_ref[first_x + r] = final_ref[first_x + r] + cx_ref[first_c + r] * terms(
                    far_ref, r
                )
            for b in range(count_b):
                for i in range(pair):
                    value = jnp.where(
                        wants_last,
                        final_ref[first_x + 2 * i, pl.ds(2 * b, 1), :],
                        late_ref[b, pl.ds(first_a + i, 1), :],
                    )
                    late_ref[b, pl.ds(first_a + i, 1), :] = value
                    lanes = pl.ds(b % GROUP * count_z, count_z)
                    lhs[pl.ds(b // GROUP * pair + i, 1), lanes] = value

        @pl.when(place.even)
        def _():
            correct(0, 0, 0, low_terms)

        @pl.when(jnp.logical_not(place.even))
        def _():
            correct(count_x - WIDTH, WIDTH, count_a - pair, high_terms)

        result = exact_dot(lhs[...], matrix_ref[...])
        parts = [result[:, kind * count_z : (kind + 1) * count_z] for kind in range(4)]
        sent_ref[pl.ds(0, rows), :] = parts[0]
        sent_ref[pl.ds(rows, rows), :] = parts[1]
        sent_ref[pl.ds(2 * rows, rows), :] = parts[2] + pltpu.roll(parts[3], REACH, 1)

    return pl.pallas_call(
        kernel,
        out_shape=(shape(*final.shape), shape(*late.shape), shape(3 * rows, count_z)),
        in_specs=[spec(pltpu.VMEM)] * 6,
        out_specs=(spec(pltpu.VMEM),) * 3,
        scratch_shapes=[pltpu.VMEM((rows, GROUP * count_z), F32)],
        input_output_aliases={1: 0, 2: 1},
        compiler_params=params(12),
        cost_estimate=cost(WIDTH * count_y * count_z, 20, 3),
        name="last_far",
    )(flag, final, late, cx, far, matrix)


def write_out(level):
    def kernel(level_ref, out_ref, sem):
        copy = pltpu.make_async_copy(level_ref, out_ref, sem)
        copy.start()
        copy.wait()

    return pl.pallas_call(
        kernel,
        out_shape=shape(*level.shape),
        in_specs=[spec(pltpu.VMEM)],
        out_specs=spec(pltpu.HBM),
        scratch_shapes=[pltpu.SemaphoreType.DMA],
        compiler_params=params(4),
        cost_estimate=cost(level.size, 0, 2),
        name="write_out",
    )(level)


class Either:
    def __init__(self, first, second):
        self.both = first, second
        self.shape = first.shape

    def __getitem__(self, index):
        return self.both[0][index] + self.both[1][index]


CODE_BITS = 5
PER_CODE = 6


def lag_image(count_a, lags, own, other, extra=None, before=None):
    _, total_rows, count_z = own.shape
    groups = total_rows // count_a
    half = count_z // GROUP
    last = before is not None
    count_h = before.shape[0] if last else lags.shape[0]
    codes = -(-count_h // PER_CODE)
    pair = WIDTH // 2

    def kernel(*refs):
        refs = list(refs)
        take = lambda count: [refs.pop(0) for _ in range(count)]
        lags_ref, own_ref = take(2)
        other_ref = Either(*take(2)) if last else take(1)[0]
        if last:
            extra_ref, before_ref = take(2)
        (out_ref,) = take(1)
        if not last:
            (codes_ref,) = take(1)
        mains, edges = take(2)
        if last:
            store, sem = take(2)
        else:
            store = out_ref
            lag_of, sem = take(2)
        place = Place()
        if last:
            packed_lags = [lags_ref[k : k + 1, :][0, 0] for k in range(codes)]
            mask = (1 << CODE_BITS) - 1
            lag_list = [
                ((packed_lags[h // PER_CODE] >> (h % PER_CODE * CODE_BITS)) & mask) - LAGMAX
                for h in range(count_h)
            ]
        else:
            copy = pltpu.make_async_copy(lags_ref, lag_of, sem)
            copy.start()
        is_source = place.field == 0

        def useful(rows):
            lane = lax.broadcasted_iota(jnp.int32, (rows, count_z), 1) % half
            return jnp.where(is_source, lane, half - 1 - lane) < REACH

        slots, _ = edge_slots(count_a, groups, count_z)
        if last:
            take_windows(place, other_ref, mains, groups, count_a)
            edge_row = sum(give_rows(groups))
        else:
            for parity in range(2):
                mains[parity] = other_ref[pl.ds(parity * total_rows, total_rows), :]
            edge_row = 2 * total_rows
        for parity, g, row, shift in slots:
            part = other_ref[pl.ds(edge_row + row, count_a), :]
            part = pltpu.roll(part, count_z - shift, 1) if shift else part
            edges[parity, pl.ds(g * count_a, count_a), :] = jnp.where(useful(count_a), part, 0.0)
        if last:
            rows = extra_ref.shape[0] // 3
            border = extra_ref[pl.ds(2 * rows, rows), :]
            borders = [
                jnp.where(useful(rows), part, 0.0)
                for part in (border, pltpu.roll(border, count_z - REACH, 1))
            ]

            def overwrite(first_a):
                for g in range(groups):
                    target = pl.ds(g * count_a + first_a, pair)
                    for parity in range(2):
                        mains[parity, target, :] = extra_ref[
                            pl.ds(parity * rows + g * pair, pair), :
                        ]
                        edges[parity, target, :] = borders[parity][g * pair : (g + 1) * pair]

            pl.when(place.even)(lambda: overwrite(0))
            pl.when(jnp.logical_not(place.even))(lambda: overwrite(count_a - pair))
        else:
            copy.wait()
            lag_list = [lag_of[h] for h in range(count_h)]
            for k in range(codes):
                code = jnp.int32(0)
                for h in range(k * PER_CODE, min((k + 1) * PER_CODE, count_h)):
                    code = code | ((lag_list[h] + LAGMAX) << (h % PER_CODE * CODE_BITS))
                codes_ref[k : k + 1, :] = jnp.full((1, count_z), code, jnp.int32)
        for h, lag in enumerate(lag_list):
            parity, own_shift, other_shift = lag_shifts(lag, is_source)
            product = moved(mains[parity], edges[parity], other_shift)
            if last:
                product = product * own_ref[h]
            else:
                product = product * moved(own_ref[parity], own_ref[2 + parity], own_shift)
            for g in range(groups):
                part = product[g * count_a : (g + 1) * count_a]
                lanes = pl.ds(g * count_z, count_z)
                if last:
                    part = part + before_ref[h, :, lanes]
                store[h, :, lanes] = part
            if last:
                pltpu.make_async_copy(store.at[h], out_ref.at[h], sem).start()
        if last:
            pltpu.make_async_copy(store, out_ref, sem).wait()

    image = shape(count_h, count_a, groups * count_z)
    operands = [lags, own] + ([*other, extra, before] if last else [other])
    scratch = [pltpu.VMEM((2, total_rows, count_z), F32)] * 2
    scratch.append(pltpu.VMEM(image.shape, F32) if last else pltpu.SMEM((count_h,), jnp.int32))
    scratch.append(pltpu.SemaphoreType.DMA)
    return pl.pallas_call(
        kernel,
        out_shape=image if last else (image, shape(8, count_z, dtype=jnp.int32)),
        in_specs=[spec(pltpu.VMEM if last else pltpu.HBM)]
        + [spec(pltpu.VMEM)] * (len(operands) - 1),
        out_specs=spec(pltpu.HBM) if last else (spec(pltpu.VMEM),) * 2,
        scratch_shapes=scratch,
        compiler_params=params(12),
        cost_estimate=cost(count_h * total_rows * count_z, 10, 2),
        name="last_image" if last else "early_image",
    )(*operands)


def body(
    field_now,
    field_prev,
    courant_squared,
    source_cells,
    source_wave,
    receiver_cells,
    receiver_wave,
    snapshot_steps,
    lag_offsets,
):
    count_x, _, count_z = field_now.shape
    loop_size = lax.axis_size("gx")
    half_size = loop_size // 2
    turn = loop_size // 4
    assert lax.axis_size("gy") == 2 and half_size % 2 == 0

    field = ((lax.axis_index("gx") - turn + loop_size) % loop_size) // half_size
    slabs = [(i - turn) % loop_size % half_size for i in range(loop_size)]

    def pairs(odd):
        found = []
        for i, slab in enumerate(slabs):
            if slab % 2 == odd and slab != half_size - 1:
                j = (i + 1) % loop_size
                found += [(i, j), (j, i)]
        return found

    near_pairs, far_pairs = pairs(0), pairs(1)
    across = [(i, (i + half_size) % loop_size) for i in range(loop_size)]
    outer = [pair for pair in across if min(pair) < turn]

    def send_far(far):
        return lax.ppermute(far, "gx", far_pairs)

    def send_near(near, side):
        near = lax.ppermute(near, "gx", near_pairs)
        return near, lax.ppermute(side, "gy", [(0, 1), (1, 0)])

    def exchange(faces):
        far, near, side = faces
        return (send_far(far), *send_near(near, side))

    matrices = jnp.asarray(
        np.stack([pack_matrix(window, count_z) for window in (0, 1)]), dtype=BF16
    )
    raw = (source_cells, source_wave, receiver_cells, receiver_wave)
    field_kept, field_prev, courant_squared, matrices, snapshot_steps, lag_offsets, *raw = (
        pltpu.with_memory_space_constraint(array, pltpu.HBM)
        for array in (
            field_now, field_prev, courant_squared, matrices, snapshot_steps, lag_offsets, *raw
        )
    )
    halos = exchange(first_faces(field_kept))
    whole0, next1, qx, qy, courant, cx, cy, points, waves = inner_step(
        0, raw, None, field_now, None, field_prev, courant_squared
    )
    faces = halo_step((qx, qy, cx, cy), halos)
    halos = exchange(faces)
    whole1, next2, qx, qy, added = inner_step(1, points, waves, next1, faces, whole0, courant)
    faces = halo_step((qx, qy, cx, cy), halos)
    halos = exchange(faces)
    whole2, next3, qx, qy, own_early, sent_early, own_matrix, sent_matrix, flag = inner_step(
        2, points, waves, next2, faces, whole1, courant, snapshot_steps, matrices
    )
    other_early = lax.ppermute(sent_early, "gx", across)
    faces = halo_step((qx, qy, cx, cy), halos)
    far, near, side = exchange(faces)
    _, next4, qx, qy, even3 = inner_step(3, added, None, next3, faces, whole2, courant)
    final, late, sent_late = last_step(
        flag, even3, next4, (qx, qy, cx, cy), near, side, sent_matrix
    )
    first_late = lax.ppermute(sent_late, "gx", outer)
    partial, codes = lag_image(count_x // 2, lag_offsets, own_early, other_early)
    second_late = lax.ppermute(sent_late, "gx", [p for p in across if p not in outer])
    final, late, sent_far = last_far(flag, final, late, cx, far, sent_matrix)
    extra = lax.ppermute(sent_far, "gx", across)
    own_late = pack_own(lag_offsets, late, own_matrix)
    image = lag_image(count_x // 2, codes, own_late, (first_late, second_late), extra, partial)
    return write_out(final), jnp.transpose(image, (1, 0, 2))


def solution(mesh):
    placed = (
        P(("shots", "gx"), "gy", None),
        P(("shots", "gx"), "gy", None),
        P("gx", "gy", None),
        P(None, "shots"),
        P(None, "shots"),
        P(None, "shots"),
        P(None, "shots"),
        P("shots", None),
        P(),
    )
    return jax.shard_map(
        body,
        mesh=mesh,
        in_specs=placed,
        out_specs=(P(("shots", "gx"), "gy", None), P(("shots", "gx"), None, "gy")),
        check_vma=False,
    )
```

```python
import jax
import jax.numpy as jnp
import numpy as np
from jax import lax
from jax.experimental import pallas as pl
from jax.experimental.pallas import tpu as pltpu
from jax.sharding import PartitionSpec as P

STEPS = 4
WIDTH = 4
LAGMAX = 8
REACH = LAGMAX // 2
GROUP = 4
SIDE = 8

SCALE = 5040.0
BAND = (8064.0, -1008.0, 128.0, -9.0)
CENTRE = 3.0 * (-205.0 / 72.0)
WEIGHTS = (1.6, -0.2, 8.0 / 315.0, -1.0 / 560.0)

F32 = jnp.float32
BF16 = jnp.bfloat16


def shape(*dims, dtype=F32):
    return jax.ShapeDtypeStruct(dims, dtype)


def params(megabytes):
    return pltpu.CompilerParams(vmem_limit_bytes=megabytes << 20)


def spec(space):
    return pl.BlockSpec(memory_space=space)


def cost(count, flops_each, arrays):
    return pl.CostEstimate(
        flops=int(count * flops_each), bytes_accessed=int(4 * count * arrays), transcendentals=0
    )


def split3(values):
    high = values.astype(BF16)
    rest = values - high.astype(F32)
    middle = rest.astype(BF16)
    low = (rest - middle.astype(F32)).astype(BF16)
    return high, middle, low


def exact_dot(values, matrix):
    rows = values.shape[0]
    stacked = jnp.concatenate(split3(values), axis=0)
    result = jnp.dot(stacked, matrix, preferred_element_type=F32)
    return (result[2 * rows :] + result[rows : 2 * rows]) + result[:rows]


class Place:
    def __init__(self):
        loop_size = lax.axis_size("gx")
        self.half = loop_size // 2
        relative = lax.rem(lax.axis_index("gx") + loop_size - loop_size // 4, loop_size)
        self.field = relative // self.half
        self.slab = lax.rem(relative, self.half)
        self.even = lax.rem(self.slab, 2) == 0
        self.y = lax.axis_index("gy")

    def block(self, count_y):
        return pl.multiple_of((1 - self.y) * (count_y - SIDE), SIDE)


def first_faces(field):
    count_x, count_y, count_z = field.shape
    top = count_x - WIDTH

    def kernel(field_ref, far_ref, near_ref, side_ref, sems):
        place = Place()
        far = jnp.where(place.even, 0, top)
        sources = [
            field_ref.at[pl.ds(far, WIDTH)],
            field_ref.at[pl.ds(top - far, WIDTH)],
            field_ref.at[:, pl.ds(place.block(count_y), SIDE)],
        ]
        copies = [
            pltpu.make_async_copy(source, target, sems.at[index])
            for index, (source, target) in enumerate(zip(sources, (far_ref, near_ref, side_ref)))
        ]
        for copy in copies:
            copy.start()
        for copy in copies:
            copy.wait()

    return pl.pallas_call(
        kernel,
        out_shape=face_shapes(count_x, count_y, count_z),
        in_specs=[spec(pltpu.HBM)],
        out_specs=(spec(pltpu.VMEM),) * 3,
        scratch_shapes=[pltpu.SemaphoreType.DMA((3,))],
        compiler_params=params(8),
        name="first_faces",
    )(field)


def face_shapes(count_x, count_y, count_z):
    slab = shape(WIDTH, count_y, count_z)
    return slab, slab, shape(count_x, SIDE, count_z)


def even_rows(level_ref, offset_x, offset_y, count_a, b):
    rows, stride, lanes = level_ref.shape
    flat = level_ref.reshape(rows * stride, lanes)
    start = offset_x * stride + offset_y + 2 * b
    return flat[pl.ds(start, count_a, stride=2 * stride), :]


def inner_step(number, points, waves, current, faces, previous, courant, snapshots=None, matrices=None):
    count_x, count_y, count_z = courant.shape
    count_a, count_b = count_x // 2, count_y // 2
    first = faces is None
    last = number == STEPS - 1
    snapshot = number == STEPS // 2
    ahead = number == 1
    if last:
        count_j = 0
    elif first:
        count_j = -(-max(array.shape[1] for array in points) // 128) * 128
    else:
        count_j = points.shape[1]

    def kernel(*refs):
        refs = list(refs)
        take = lambda count: [refs.pop(0) for _ in range(count)]
        if first:
            raw_refs = take(4)
        elif last:
            (added_ref,) = take(1)
        else:
            points_ref, waves_ref = take(2)
        (current_ref,) = take(1)
        if not first:
            far_ref, near_ref, side_ref = take(3)
        previous_ref, courant_ref = take(2)
        if snapshot:
            steps_ref, matrices_ref = take(2)
        padded, next_ref, qx_ref, qy_ref = take(4)
        if first:
            kept_ref, cx_ref, cy_ref, points_ref, waves_ref = take(5)
        if snapshot:
            own_out, sent_out, own_matrix, sent_matrix, flag_ref = take(5)
        if ahead:
            (ahead_ref,) = take(1)
        zpart, addpart = take(2)
        if last:
            addpart = added_ref
        if first:
            before_ref = take(1)[0]
            raw_refs_in, raw_refs = raw_refs, take(4)
            (sems,) = take(1)
        if snapshot:
            even_ref, wanted, sems = take(3)

        place = Place()
        block = place.block(count_y)
        rows, columns = pl.ds(WIDTH, count_x), pl.ds(SIDE, count_y)
        if first:
            copies = [
                pltpu.make_async_copy(source, target, sems.at[index])
                for index, (source, target) in enumerate(
                    zip(
                        (*raw_refs_in, previous_ref, courant_ref),
                        (*raw_refs, before_ref, kept_ref),
                    )
                )
            ]
            for copy in copies:
                copy.start()
        else:
            before_ref, kept_ref = previous_ref, courant_ref
        if snapshot:
            copies = [
                pltpu.make_async_copy(steps_ref, wanted, sems.at[0]),
                pltpu.make_async_copy(matrices_ref.at[place.field], own_matrix, sems.at[1]),
                pltpu.make_async_copy(matrices_ref.at[1 - place.field], sent_matrix, sems.at[2]),
            ]
            for copy in copies:
                copy.start()

        def clear_border(level_ref):
            zero_x = jnp.zeros((WIDTH, count_y + 2 * SIDE, count_z), F32)
            level_ref[pl.ds(0, WIDTH)] = zero_x
            level_ref[pl.ds(count_x + WIDTH, WIDTH)] = zero_x
            zero_y = jnp.zeros((count_x, SIDE, count_z), F32)
            level_ref[rows, pl.ds(0, SIDE)] = zero_y
            level_ref[rows, pl.ds(count_y + SIDE, SIDE)] = zero_y

        if first:
            clear_border(padded)
            padded[rows, columns] = current_ref[...]
        if not last:
            clear_border(next_ref)
        next_x, next_y = (0, 0) if last else (WIDTH, SIDE)
        before_x, before_y = (0, 0) if first else (WIDTH, SIDE)
        if not first:
            low, high = pl.ds(WIDTH, WIDTH), pl.ds(count_x, WIDTH)

            @pl.when(place.even)
            def _():
                padded[high, columns] = near_ref[...]
                padded[low, columns] = far_ref[...]

            @pl.when(jnp.logical_not(place.even))
            def _():
                padded[low, columns] = near_ref[...]
                padded[high, columns] = far_ref[...]

            padded[rows, pl.ds(pl.multiple_of(block + SIDE, SIDE), SIDE)] = side_ref[...]

        gap = jnp.abs(
            lax.broadcasted_iota(jnp.int32, (count_z, count_z), 0)
            - lax.broadcasted_iota(jnp.int32, (count_z, count_z), 1)
        )
        band = jnp.zeros((count_z, count_z), F32)
        for offset, weight in enumerate(BAND, 1):
            band = jnp.where(gap == offset, weight, band)
        band = jnp.concatenate([band.astype(BF16)] * 3, axis=0)

        chunk = 8

        def multiply(index, _):
            start = pl.multiple_of(index * chunk, chunk)
            values = padded[pl.ds(start + WIDTH, chunk), columns]
            terms = jnp.concatenate(split3(values.reshape(chunk * count_y, count_z)), axis=1)
            zpart[pl.ds(start, chunk)] = jnp.dot(
                terms, band, preferred_element_type=F32
            ).reshape(chunk, count_y, count_z)
            return 0

        chunks = count_x // chunk
        if first or last:
            lax.fori_loop(0, chunks, multiply, 0)

        if first:
            for copy in copies[:4]:
                copy.wait()
            points_ref[...] = jnp.full(points_ref.shape, -1, jnp.int32)
            waves_ref[...] = jnp.zeros(waves_ref.shape, F32)

            def choose(cells_ref, wave_ref):
                count = cells_ref.shape[1]
                points_ref[pl.ds(0, 3), pl.ds(0, count)] = cells_ref[...]
                waves_ref[pl.ds(0, STEPS), pl.ds(0, count)] = wave_ref[...]

            @pl.when(place.field == 0)
            def _():
                choose(raw_refs[0], raw_refs[1])

            @pl.when(place.field != 0)
            def _():
                choose(raw_refs[2], raw_refs[3])

        if not last:
            px = points_ref[0:1, :] - place.slab * count_x
            py = points_ref[1:2, :] - place.y * count_y
            inside = (px >= 0) & (px < count_x) & (py >= 0) & (py < count_y)
            home = jnp.where(inside, px * count_y + py, -1)
            at_z = (
                lax.broadcasted_iota(jnp.int32, (count_z, count_j), 0) == points_ref[2:3, :]
            )

            def spread_of(step):
                terms = split3(jnp.where(at_z, waves_ref[step : step + 1, :], 0.0))
                return jnp.concatenate(terms, axis=1)

            spreads = [(addpart, spread_of(number))]
            if ahead:
                spreads.append((ahead_ref, spread_of(STEPS - 1)))

        def inject(index, _):
            start = pl.multiple_of(index * chunk, chunk)
            here = start * count_y + lax.broadcasted_iota(
                jnp.int32, (chunk * count_y, count_j), 0
            )
            hit = jnp.where(here == home, 1.0, 0.0).astype(BF16)
            hit = jnp.concatenate([hit] * 3, axis=1)
            for target, spread in spreads:
                added = lax.dot_general(
                    hit, spread, (((1,), (1,)), ((), ())), preferred_element_type=F32
                )
                target[pl.ds(start, chunk)] = added.reshape(chunk, count_y, count_z)
            return 0

        def both(index, _):
            multiply(index, 0)
            return inject(index, 0)

        if not last:
            lax.fori_loop(0, chunks, inject if first else both, 0)
        if first:
            for copy in copies[4:]:
                copy.wait()

        depth = 4

        def row_group(index, _):
            x = index * depth
            for y in range(0, count_y, SIDE):
                here, inner = pl.ds(y + SIDE, SIDE), pl.ds(y, SIDE)
                lines = [padded[x + i, here] for i in range(depth + 2 * WIDTH)]
                for j in range(depth):
                    middle = lines[WIDTH + j]
                    total = CENTRE * middle + (1.0 / SCALE) * zpart[x + j, inner]
                    for offset, weight in enumerate(WEIGHTS, 1):
                        paired = lines[WIDTH + j + offset] + lines[WIDTH + j - offset]
                        paired = paired + (
                            padded[x + WIDTH + j, pl.ds(y + SIDE + offset, SIDE)]
                            + padded[x + WIDTH + j, pl.ds(y + SIDE - offset, SIDE)]
                        )
                        total = total + weight * paired
                    old = before_ref[x + j + before_x, pl.ds(y + before_y, SIDE)]
                    value = 2.0 * middle - old + kept_ref[x + j, inner] * total
                    next_ref[x + j + next_x, pl.ds(y + next_y, SIDE)] = (
                        value + addpart[x + j, inner]
                    )
            return 0

        lax.fori_loop(0, count_x // depth, row_group, 0)

        next_columns = pl.ds(next_y, count_y)
        qx_ref[pl.ds(0, WIDTH)] = next_ref[pl.ds(next_x, WIDTH), next_columns]
        qx_ref[pl.ds(WIDTH, WIDTH)] = next_ref[
            pl.ds(next_x + count_x - WIDTH, WIDTH), next_columns
        ]
        qy_ref[...] = next_ref[
            pl.ds(next_x, count_x), pl.ds(pl.multiple_of(block + next_y, SIDE), SIDE)
        ]
        if first:
            cx_ref[pl.ds(0, WIDTH)] = kept_ref[pl.ds(0, WIDTH)]
            cx_ref[pl.ds(WIDTH, WIDTH)] = kept_ref[pl.ds(count_x - WIDTH, WIDTH)]
            cy_ref[...] = kept_ref[:, pl.ds(block, SIDE)]
        if snapshot:
            for copy in copies:
                copy.wait()
            flag_ref[...] = jnp.where(
                wanted[place.field, 1] == STEPS, jnp.ones(flag_ref.shape, F32), 0.0
            )
            earlier = wanted[place.field, 0] == number - 1

            @pl.when(earlier)
            def _():
                for b in range(count_b):
                    even_ref[b] = even_rows(previous_ref, WIDTH, SIDE, count_a, b)

            @pl.when(jnp.logical_not(earlier))
            def _():
                for b in range(count_b):
                    even_ref[b] = even_rows(padded, WIDTH, SIDE, count_a, b)

            for kind, part in enumerate(packed(even_ref, own_matrix)):
                own_out[kind] = part
            send_into(even_ref, sent_matrix, sent_out)

    full = shape(count_x, count_y, count_z)
    slab, side = shape(2 * WIDTH, count_y, count_z), shape(count_x, SIDE, count_z)
    even = shape(count_b, count_a, count_z)
    bordered = shape(count_x + 2 * WIDTH, count_y + 2 * SIDE, count_z)
    outs = [bordered, full if last else bordered, slab, side]
    if first:
        outs += [full, slab, side, shape(8, count_j, dtype=jnp.int32), shape(8, count_j)]
    if snapshot:
        size = GROUP * count_z
        outs += [
            shape(4, count_b // GROUP * count_a, count_z),
            sent_shape(count_a, count_b, count_z),
            shape(size, size, dtype=BF16),
            shape(size, size, dtype=BF16),
            shape(8, count_z),
        ]
    if ahead:
        outs.append(full)
    place_of = spec(pltpu.HBM) if first else spec(pltpu.VMEM)
    if first:
        operands = [*points, current]
    elif last:
        operands = [points, current]
    else:
        operands = [points, waves, current]
    aliases = {} if first else {len(operands) - 1: 0}
    specs = [place_of] * (len(operands) - 1) + [spec(pltpu.VMEM)]
    if not first:
        operands += list(faces)
        specs += [spec(pltpu.VMEM)] * 3
    operands += [previous, courant]
    specs += [place_of] * 2
    scratch = [pltpu.VMEM(full.shape, F32)] * 2
    if first:
        scratch.append(pltpu.VMEM(full.shape, F32))
        scratch += [pltpu.VMEM(array.shape, array.dtype) for array in points]
        scratch.append(pltpu.SemaphoreType.DMA((6,)))
    if snapshot:
        operands += [snapshots, matrices]
        specs += [spec(pltpu.HBM)] * 2
        scratch += [
            pltpu.VMEM(even.shape, F32),
            pltpu.SMEM(snapshots.shape, jnp.int32),
            pltpu.SemaphoreType.DMA((3,)),
        ]
    return pl.pallas_call(
        kernel,
        out_shape=tuple(outs),
        in_specs=specs,
        out_specs=(spec(pltpu.VMEM),) * len(outs),
        scratch_shapes=scratch,
        input_output_aliases=aliases,
        compiler_params=params(20),
        cost_estimate=cost(count_x * count_y * count_z, 60, 6),
    )(*operands)


def low_terms(halo_ref, r):
    total = None
    for k in range(r + 1, WIDTH + 1):
        term = WEIGHTS[k - 1] * halo_ref[WIDTH + r - k]
        total = term if total is None else total + term
    return total


def high_terms(halo_ref, r):
    total = None
    for k in range(WIDTH - r, WIDTH + 1):
        term = WEIGHTS[k - 1] * halo_ref[r + k - WIDTH]
        total = term if total is None else total + term
    return total


def add_halo(place, parts, halos, outs):
    qx_ref, qy_ref, cx_ref, cy_ref = parts
    far_in, near_in, side_in = halos
    far_out, near_out, side_out = outs
    count_y, count_x = qx_ref.shape[1], qy_ref.shape[0]
    block = place.block(count_y)

    def along_x(low_in, high_in, low_out, high_out):
        for r in range(WIDTH):
            low, high = qx_ref[r], qx_ref[WIDTH + r]
            if low_in is not None:
                low = low + cx_ref[r] * low_terms(low_in, r)
            if high_in is not None:
                high = high + cx_ref[WIDTH + r] * high_terms(high_in, r)
            low_out[r], high_out[r] = low, high
        side_out[pl.ds(0, WIDTH)] = low_out[:, pl.ds(block, SIDE)]
        side_out[pl.ds(count_x - WIDTH, WIDTH)] = high_out[:, pl.ds(block, SIDE)]

    inner = pl.ds(WIDTH, count_x - 2 * WIDTH)
    side_out[inner] = qy_ref[inner]

    @pl.when(place.even)
    def _():
        along_x(far_in, near_in, far_out, near_out)

    @pl.when(jnp.logical_not(place.even))
    def _():
        along_x(near_in, far_in, near_out, far_out)

    def along_y(shifts, masks):
        halo = side_in[...]
        lanes = halo.shape[2]
        line = lax.broadcasted_iota(jnp.int32, (1, SIDE, lanes), 1)
        total = None
        for k in range(1, WIDTH + 1):
            weight = jnp.where(masks(line, k), WEIGHTS[k - 1], 0.0)
            term = weight * pltpu.roll(halo, shifts(k), 1)
            total = term if total is None else total + term
        side_out[...] = side_out[...] + cy_ref[...] * total

    @pl.when(place.y == 0)
    def _():
        along_y(lambda k: SIDE - k, lambda line, k: line >= SIDE - k)

    @pl.when(place.y != 0)
    def _():
        along_y(lambda k: k, lambda line, k: line < k)

    def corners(low_out, high_out):
        low_out[:, pl.ds(block, SIDE)] = side_out[pl.ds(0, WIDTH)]
        high_out[:, pl.ds(block, SIDE)] = side_out[pl.ds(count_x - WIDTH, WIDTH)]

    @pl.when(place.even)
    def _():
        corners(far_out, near_out)

    @pl.when(jnp.logical_not(place.even))
    def _():
        corners(near_out, far_out)


def halo_step(parts, halos):
    count_y, (count_x, _, count_z) = parts[0].shape[1], parts[1].shape

    def kernel(*refs):
        add_halo(Place(), refs[:4], refs[4:7], refs[7:])

    return pl.pallas_call(
        kernel,
        out_shape=face_shapes(count_x, count_y, count_z),
        in_specs=[spec(pltpu.VMEM)] * 7,
        out_specs=(spec(pltpu.VMEM),) * 3,
        compiler_params=params(8),
        cost_estimate=cost(16 * count_y * count_z, 10, 6),
        name="halo_step",
    )(*parts, *halos)


def pack_matrix(window, count_z):
    half = count_z // GROUP
    size = GROUP * count_z
    row, column = np.arange(size)[:, None], np.arange(size)[None, :]
    row_b, row_z = row // count_z, row % count_z
    kind = column // count_z
    parity = kind % 2
    lane_b, lane_i = (column % count_z) // half, column % half
    main = (row_b == lane_b) & (row_z == 2 * (half * window + lane_i) + parity)
    wanted_b = (lane_b + (GROUP - 1 if window == 0 else 1)) % GROUP
    wanted_z = 2 * (half * (1 - window) + lane_i) + parity
    useful = lane_i < REACH if window == 0 else lane_i >= half - REACH
    edge = (row_b == wanted_b) & (row_z == wanted_z) & useful
    return np.where(kind < 2, main, edge).astype(np.float32)


def packed(even_ref, matrix_ref):
    count_b, _, count_z = even_ref.shape
    rows = [
        jnp.concatenate([even_ref[b + i] for i in range(GROUP)], axis=1)
        for b in range(0, count_b, GROUP)
    ]
    result = exact_dot(jnp.concatenate(rows, axis=0), matrix_ref[...])
    return [result[:, kind * count_z : (kind + 1) * count_z] for kind in range(4)]


def lag_shifts(lag, is_source):
    parity = lag & 1
    source_shift = -((lag + parity) >> 1)
    receiver_shift = (lag - parity) >> 1
    return (
        parity,
        jnp.where(is_source, source_shift, receiver_shift),
        jnp.where(is_source, receiver_shift, source_shift),
    )


def moved(main, edge, shift):
    count_z = main.shape[1]
    half = count_z // GROUP
    lane = lax.broadcasted_iota(jnp.int32, (1, count_z), 1) % half
    mask = (lane < shift) | (lane >= half + shift)
    return pltpu.roll(jnp.where(mask, edge, main), (count_z - shift) & (count_z - 1), 1)


def pack_own(lags, even, matrix):
    count_b, count_a, count_z = even.shape
    total_rows = count_b // GROUP * count_a
    (count_h,) = lags.shape

    def kernel(lags_ref, even_ref, matrix_ref, out_ref, windows, lag_of, sem):
        copy = pltpu.make_async_copy(lags_ref, lag_of, sem)
        copy.start()
        place = Place()
        for kind, part in enumerate(packed(even_ref, matrix_ref)):
            windows[kind] = part
        copy.wait()
        for h in range(count_h):
            parity, shift, _ = lag_shifts(lag_of[h], place.field == 0)
            out_ref[h] = moved(windows[parity], windows[2 + parity], shift)

    return pl.pallas_call(
        kernel,
        out_shape=shape(count_h, total_rows, count_z),
        in_specs=[spec(pltpu.HBM)] + [spec(pltpu.VMEM)] * 2,
        out_specs=spec(pltpu.VMEM),
        scratch_shapes=[
            pltpu.VMEM((4, total_rows, count_z), F32),
            pltpu.SMEM((count_h,), jnp.int32),
            pltpu.SemaphoreType.DMA,
        ],
        compiler_params=params(8),
        cost_estimate=cost(count_b * count_a * count_z, 1024, 4),
        name="pack_own",
    )(lags, even, matrix)


def edge_slots(count_a, groups, count_z):
    fits = count_z // GROUP // REACH
    slots = []
    for index in range(2 * groups):
        slots.append((index // groups, index % groups, index // fits * count_a, index % fits * REACH))
    return slots, -(-2 * groups // fits) * count_a


def edge_sums(parts, count_a, groups, count_z):
    slots, extra = edge_slots(count_a, groups, count_z)
    sums = {}
    for parity, g, row, shift in slots:
        part = parts[2 + parity][g * count_a : (g + 1) * count_a]
        part = pltpu.roll(part, shift, 1) if shift else part
        sums[row] = sums[row] + part if row in sums else part
    return sums, extra


def send_into(even_ref, matrix_ref, out_ref):
    count_b, count_a, count_z = even_ref.shape
    groups = count_b // GROUP
    total_rows = groups * count_a
    parts = packed(even_ref, matrix_ref)
    out_ref[pl.ds(0, total_rows), :] = parts[0]
    out_ref[pl.ds(total_rows, total_rows), :] = parts[1]
    for row, part in edge_sums(parts, count_a, groups, count_z)[0].items():
        out_ref[pl.ds(2 * total_rows + row, count_a), :] = part


def sent_shape(count_a, count_b, count_z):
    groups = count_b // GROUP
    _, extra = edge_slots(count_a, groups, count_z)
    return shape(2 * groups * count_a + extra, count_z)


KEPT = SIDE - WIDTH // 2
FREE = SIDE - KEPT
BATCH = KEPT // FREE + 1


def give_rows(groups):
    tiles = 2 * groups
    return SIDE * tiles, SIDE * (tiles // BATCH * (BATCH - 1))


def give_into(place, even_ref, matrix_ref, out_ref):
    count_b, count_a, count_z = even_ref.shape
    groups = count_b // GROUP
    assert count_a == 2 * SIDE and 2 * groups % BATCH == 0
    parts = packed(even_ref, matrix_ref)
    whole_rows, part_rows = give_rows(groups)
    line = lax.broadcasted_iota(jnp.int32, (SIDE, count_z), 0)

    def store(far_tile, shift):
        fars = []
        for index in range(2 * groups):
            start = index % groups * count_a
            both = [
                parts[index // groups][start + SIDE * tile : start + SIDE * (tile + 1)]
                for tile in range(2)
            ]
            out_ref[pl.ds(SIDE * index, SIDE), :] = both[1 - far_tile]
            fars.append(pltpu.roll(both[far_tile], shift, 0) if shift else both[far_tile])
        row = whole_rows
        for first in range(0, 2 * groups, BATCH):
            *hosts, guest = fars[first : first + BATCH]
            for i, host in enumerate(hosts):
                moved_guest = pltpu.roll(guest, KEPT - FREE * i, 0)
                out_ref[pl.ds(row, SIDE), :] = jnp.where(line < KEPT, host, moved_guest)
                row += SIDE

    pl.when(place.even)(lambda: store(0, KEPT))
    pl.when(jnp.logical_not(place.even))(lambda: store(1, 0))
    for row, part in edge_sums(parts, count_a, groups, count_z)[0].items():
        out_ref[pl.ds(whole_rows + part_rows + row, count_a), :] = part


def take_windows(place, other_ref, mains, groups, count_a):
    count_z = other_ref.shape[1]
    whole_rows, _ = give_rows(groups)
    line = lax.broadcasted_iota(jnp.int32, (SIDE, count_z), 0)

    def load(far_tile, shift):
        fars = []
        row = whole_rows
        for _ in range(0, 2 * groups, BATCH):
            hosts = [other_ref[pl.ds(row + SIDE * i, SIDE), :] for i in range(BATCH - 1)]
            row += SIDE * (BATCH - 1)
            guest = None
            for i, host in enumerate(hosts):
                piece = pltpu.roll(host, (FREE * (i + 1)) % SIDE, 0)
                guest = piece if guest is None else jnp.where(line < FREE * i, guest, piece)
            fars += [*hosts, guest]
        for index, far in enumerate(fars):
            start = index % groups * count_a
            far = pltpu.roll(far, shift, 0) if shift else far
            mains[index // groups, pl.ds(start + SIDE * far_tile, SIDE), :] = far
            mains[index // groups, pl.ds(start + SIDE * (1 - far_tile), SIDE), :] = other_ref[
                pl.ds(SIDE * index, SIDE), :
            ]

    pl.when(place.even)(lambda: load(0, FREE))
    pl.when(jnp.logical_not(place.even))(lambda: load(1, 0))


def given_shape(count_a, count_b, count_z):
    groups = count_b // GROUP
    return shape(sum(give_rows(groups)) + edge_slots(count_a, groups, count_z)[1], count_z)


def last_step(flag, before, current, parts, near, side, matrix):
    count_x, count_y, count_z = current.shape
    count_a, count_b = count_x // 2, count_y // 2

    def kernel(
        flag_ref, before_ref, current_ref, qx_ref, qy_ref, cx_ref, cy_ref, near_ref, side_ref,
        matrix_ref, final_ref, late_ref, sent_ref, far_out, near_out, side_out,
    ):
        place = Place()
        add_halo(
            place, (qx_ref, qy_ref, cx_ref, cy_ref), (None, near_ref, side_ref),
            (far_out, near_out, side_out),
        )
        low, high = pl.ds(0, WIDTH), pl.ds(count_x - WIDTH, WIDTH)

        @pl.when(place.even)
        def _():
            final_ref[high] = near_out[...]
            final_ref[low] = far_out[...]

        @pl.when(jnp.logical_not(place.even))
        def _():
            final_ref[low] = near_out[...]
            final_ref[high] = far_out[...]

        final_ref[:, pl.ds(place.block(count_y), SIDE)] = side_out[...]
        wants_last = flag_ref[0:1, :][0, 0] > 0.5

        @pl.when(wants_last)
        def _():
            for b in range(count_b):
                late_ref[b] = even_rows(final_ref, 0, 0, count_a, b)

        @pl.when(jnp.logical_not(wants_last))
        def _():
            for b in range(count_b):
                late_ref[b] = even_rows(before_ref, WIDTH, SIDE, count_a, b)

        give_into(place, late_ref, matrix_ref, sent_ref)

    slab, _, side_shape = face_shapes(count_x, count_y, count_z)
    return pl.pallas_call(
        kernel,
        out_shape=(
            shape(*current.shape),
            shape(count_b, count_a, count_z),
            given_shape(count_a, count_b, count_z),
        ),
        in_specs=[spec(pltpu.VMEM)] * 10,
        out_specs=(spec(pltpu.VMEM),) * 3,
        scratch_shapes=[
            pltpu.VMEM(slab.shape, F32),
            pltpu.VMEM(slab.shape, F32),
            pltpu.VMEM(side_shape.shape, F32),
        ],
        input_output_aliases={2: 0},
        compiler_params=params(12),
        cost_estimate=cost(count_x * count_y * count_z, 10, 3),
        name="last_step",
    )(flag, before, current, *parts, near, side, matrix)


def far_rows(count_b):
    return -(-2 * (count_b // GROUP) // 16) * 16


def last_far(flag, final, late, cx, far, matrix):
    count_x, count_y, count_z = final.shape
    count_b, count_a, _ = late.shape
    rows, pair = far_rows(count_b), WIDTH // 2

    def kernel(
        flag_ref, final_in, late_in, cx_ref, far_ref, matrix_ref, final_ref, late_ref, sent_ref, lhs,
    ):
        place = Place()
        wants_last = jnp.broadcast_to(flag_ref[0:1, :], (1, count_z)) > 0.5
        lhs[...] = jnp.zeros_like(lhs)

        def correct(first_x, first_c, first_a, terms):
            for r in range(WIDTH):
                final_ref[first_x + r] = final_ref[first_x + r] + cx_ref[first_c + r] * terms(
                    far_ref, r
                )
            for b in range(count_b):
                for i in range(pair):
                    value = jnp.where(
                        wants_last,
                        final_ref[first_x + 2 * i, pl.ds(2 * b, 1), :],
                        late_ref[b, pl.ds(first_a + i, 1), :],
                    )
                    late_ref[b, pl.ds(first_a + i, 1), :] = value
                    lanes = pl.ds(b % GROUP * count_z, count_z)
                    lhs[pl.ds(b // GROUP * pair + i, 1), lanes] = value

        @pl.when(place.even)
        def _():
            correct(0, 0, 0, low_terms)

        @pl.when(jnp.logical_not(place.even))
        def _():
            correct(count_x - WIDTH, WIDTH, count_a - pair, high_terms)

        result = exact_dot(lhs[...], matrix_ref[...])
        parts = [result[:, kind * count_z : (kind + 1) * count_z] for kind in range(4)]
        sent_ref[pl.ds(0, rows), :] = parts[0]
        sent_ref[pl.ds(rows, rows), :] = parts[1]
        sent_ref[pl.ds(2 * rows, rows), :] = parts[2] + pltpu.roll(parts[3], REACH, 1)

    return pl.pallas_call(
        kernel,
        out_shape=(shape(*final.shape), shape(*late.shape), shape(3 * rows, count_z)),
        in_specs=[spec(pltpu.VMEM)] * 6,
        out_specs=(spec(pltpu.VMEM),) * 3,
        scratch_shapes=[pltpu.VMEM((rows, GROUP * count_z), F32)],
        input_output_aliases={1: 0, 2: 1},
        compiler_params=params(12),
        cost_estimate=cost(WIDTH * count_y * count_z, 20, 3),
        name="last_far",
    )(flag, final, late, cx, far, matrix)


def write_out(level):
    def kernel(level_ref, out_ref, sem):
        copy = pltpu.make_async_copy(level_ref, out_ref, sem)
        copy.start()
        copy.wait()

    return pl.pallas_call(
        kernel,
        out_shape=shape(*level.shape),
        in_specs=[spec(pltpu.VMEM)],
        out_specs=spec(pltpu.HBM),
        scratch_shapes=[pltpu.SemaphoreType.DMA],
        compiler_params=params(4),
        cost_estimate=cost(level.size, 0, 2),
        name="write_out",
    )(level)


CODE_BITS = 5
PER_CODE = 6


def lag_image(count_a, lags, own, other, extra=None, before=None):
    _, total_rows, count_z = own.shape
    groups = total_rows // count_a
    half = count_z // GROUP
    last = before is not None
    count_h = before.shape[0] if last else lags.shape[0]
    codes = -(-count_h // PER_CODE)
    pair = WIDTH // 2

    def kernel(*refs):
        refs = list(refs)
        take = lambda count: [refs.pop(0) for _ in range(count)]
        lags_ref, own_ref, other_ref = take(3)
        if last:
            extra_ref, before_ref = take(2)
        (out_ref,) = take(1)
        if not last:
            (codes_ref,) = take(1)
        mains, edges = take(2)
        if last:
            store, sem = take(2)
        else:
            store = out_ref
            lag_of, sem = take(2)
        place = Place()
        if last:
            packed_lags = [lags_ref[k : k + 1, :][0, 0] for k in range(codes)]
            mask = (1 << CODE_BITS) - 1
            lag_list = [
                ((packed_lags[h // PER_CODE] >> (h % PER_CODE * CODE_BITS)) & mask) - LAGMAX
                for h in range(count_h)
            ]
        else:
            copy = pltpu.make_async_copy(lags_ref, lag_of, sem)
            copy.start()
        is_source = place.field == 0

        def useful(rows):
            lane = lax.broadcasted_iota(jnp.int32, (rows, count_z), 1) % half
            return jnp.where(is_source, lane, half - 1 - lane) < REACH

        slots, _ = edge_slots(count_a, groups, count_z)
        if last:
            take_windows(place, other_ref, mains, groups, count_a)
            edge_row = sum(give_rows(groups))
        else:
            for parity in range(2):
                mains[parity] = other_ref[pl.ds(parity * total_rows, total_rows), :]
            edge_row = 2 * total_rows
        for parity, g, row, shift in slots:
            part = other_ref[pl.ds(edge_row + row, count_a), :]
            part = pltpu.roll(part, count_z - shift, 1) if shift else part
            edges[parity, pl.ds(g * count_a, count_a), :] = jnp.where(useful(count_a), part, 0.0)
        if last:
            rows = extra_ref.shape[0] // 3
            border = extra_ref[pl.ds(2 * rows, rows), :]
            borders = [
                jnp.where(useful(rows), part, 0.0)
                for part in (border, pltpu.roll(border, count_z - REACH, 1))
            ]

            def overwrite(first_a):
                for g in range(groups):
                    target = pl.ds(g * count_a + first_a, pair)
                    for parity in range(2):
                        mains[parity, target, :] = extra_ref[
                            pl.ds(parity * rows + g * pair, pair), :
                        ]
                        edges[parity, target, :] = borders[parity][g * pair : (g + 1) * pair]

            pl.when(place.even)(lambda: overwrite(0))
            pl.when(jnp.logical_not(place.even))(lambda: overwrite(count_a - pair))
        else:
            copy.wait()
            lag_list = [lag_of[h] for h in range(count_h)]
            for k in range(codes):
                code = jnp.int32(0)
                for h in range(k * PER_CODE, min((k + 1) * PER_CODE, count_h)):
                    code = code | ((lag_list[h] + LAGMAX) << (h % PER_CODE * CODE_BITS))
                codes_ref[k : k + 1, :] = jnp.full((1, count_z), code, jnp.int32)
        for h, lag in enumerate(lag_list):
            parity, own_shift, other_shift = lag_shifts(lag, is_source)
            product = moved(mains[parity], edges[parity], other_shift)
            if last:
                product = product * own_ref[h]
            else:
                product = product * moved(own_ref[parity], own_ref[2 + parity], own_shift)
            for g in range(groups):
                part = product[g * count_a : (g + 1) * count_a]
                lanes = pl.ds(g * count_z, count_z)
                if last:
                    part = part + before_ref[h, :, lanes]
                store[h, :, lanes] = part
            if last:
                pltpu.make_async_copy(store.at[h], out_ref.at[h], sem).start()
        if last:
            pltpu.make_async_copy(store, out_ref, sem).wait()

    image = shape(count_h, count_a, groups * count_z)
    operands = [lags, own, other] + ([extra, before] if last else [])
    scratch = [pltpu.VMEM((2, total_rows, count_z), F32)] * 2
    scratch.append(pltpu.VMEM(image.shape, F32) if last else pltpu.SMEM((count_h,), jnp.int32))
    scratch.append(pltpu.SemaphoreType.DMA)
    return pl.pallas_call(
        kernel,
        out_shape=image if last else (image, shape(8, count_z, dtype=jnp.int32)),
        in_specs=[spec(pltpu.VMEM if last else pltpu.HBM)]
        + [spec(pltpu.VMEM)] * (len(operands) - 1),
        out_specs=spec(pltpu.HBM) if last else (spec(pltpu.VMEM),) * 2,
        scratch_shapes=scratch,
        compiler_params=params(12),
        cost_estimate=cost(count_h * total_rows * count_z, 10, 2),
        name="last_image" if last else "early_image",
    )(*operands)


def body(
    field_now,
    field_prev,
    courant_squared,
    source_cells,
    source_wave,
    receiver_cells,
    receiver_wave,
    snapshot_steps,
    lag_offsets,
):
    count_x, _, count_z = field_now.shape
    loop_size = lax.axis_size("gx")
    half_size = loop_size // 2
    turn = loop_size // 4
    assert lax.axis_size("gy") == 2 and half_size % 2 == 0

    slabs = [(i - turn) % loop_size % half_size for i in range(loop_size)]

    def pairs(odd):
        found = []
        for i, slab in enumerate(slabs):
            if slab % 2 == odd and slab != half_size - 1:
                j = (i + 1) % loop_size
                found += [(i, j), (j, i)]
        return found

    near_pairs, far_pairs = pairs(0), pairs(1)
    across = [(i, (i + half_size) % loop_size) for i in range(loop_size)]

    def send_far(far):
        return lax.ppermute(far, "gx", far_pairs)

    def send_near(near, side):
        near = lax.ppermute(near, "gx", near_pairs)
        return near, lax.ppermute(side, "gy", [(0, 1), (1, 0)])

    def exchange(faces):
        far, near, side = faces
        return (send_far(far), *send_near(near, side))

    matrices = jnp.asarray(
        np.stack([pack_matrix(window, count_z) for window in (0, 1)]), dtype=BF16
    )
    raw = (source_cells, source_wave, receiver_cells, receiver_wave)
    field_kept, field_prev, courant_squared, matrices, snapshot_steps, lag_offsets, *raw = (
        pltpu.with_memory_space_constraint(array, pltpu.HBM)
        for array in (
            field_now, field_prev, courant_squared, matrices, snapshot_steps, lag_offsets, *raw
        )
    )
    halos = exchange(first_faces(field_kept))
    whole0, next1, qx, qy, courant, cx, cy, points, waves = inner_step(
        0, raw, None, field_now, None, field_prev, courant_squared
    )
    faces = halo_step((qx, qy, cx, cy), halos)
    halos = exchange(faces)
    whole1, next2, qx, qy, added = inner_step(1, points, waves, next1, faces, whole0, courant)
    faces = halo_step((qx, qy, cx, cy), halos)
    halos = exchange(faces)
    whole2, next3, qx, qy, own_early, sent_early, own_matrix, sent_matrix, flag = inner_step(
        2, points, waves, next2, faces, whole1, courant, snapshot_steps, matrices
    )
    other_early = lax.ppermute(sent_early, "gx", across)
    faces = halo_step((qx, qy, cx, cy), halos)
    far, near, side = exchange(faces)
    whole3, next4, qx, qy = inner_step(3, added, None, next3, faces, whole2, courant)
    final, late, sent_late = last_step(
        flag, whole3, next4, (qx, qy, cx, cy), near, side, sent_matrix
    )
    other_late = lax.ppermute(sent_late, "gx", across)
    partial, codes = lag_image(count_x // 2, lag_offsets, own_early, other_early)
    final, late, sent_far = last_far(flag, final, late, cx, far, sent_matrix)
    extra = lax.ppermute(sent_far, "gx", across)
    own_late = pack_own(lag_offsets, late, own_matrix)
    image = lag_image(count_x // 2, codes, own_late, other_late, extra, partial)
    return write_out(final), jnp.transpose(image, (1, 0, 2))


def solution(mesh):
    placed = (
        P(("shots", "gx"), "gy", None),
        P(("shots", "gx"), "gy", None),
        P("gx", "gy", None),
        P(None, "shots"),
        P(None, "shots"),
        P(None, "shots"),
        P(None, "shots"),
        P("shots", None),
        P(),
    )
    return jax.shard_map(
        body,
        mesh=mesh,
        in_specs=placed,
        out_specs=(P(("shots", "gx"), "gy", None), P(("shots", "gx"), None, "gy")),
        check_vma=False,
    )
```
